32 devices in a mesh: expert: 8 (over z, y), tensor: 4 (over x, core).
Axes of the slice: x: 2, y: 2, z: 4, core: 2. Of those that a mesh axis runs over, the one named last changes fastest.
Arguments:
- hidden_in: bfloat16 [2048, 2048], P('expert'), may hold values from -6 to 6
- cotangent: bfloat16 [2048, 2048], P('expert'), may hold values from -6 to 6
- layout: int32 [2048], P('expert'), may hold values from 0 to 2047, each once
- seq_lengths: int32 [3], replicated, may hold values from 1 to 960, 1920 in all
- expert_ids: int32 [2048, 8], P('expert'), may hold values from 0 to 15, all different within a row; in each aligned block of 256 rows (0 to 255, 256 to 511, ...) at most 256 rows name the same one
- drop_rank: int32 [2048], P('expert'), may hold values from 0 to 2047, each once
- norm1_gain: float32 [2048], replicated, may hold values from 0.5 to 1.5
- w_query: bfloat16 [2048, 4096], P(None, 'tensor'), may hold values from -0.125 to 0.125
- key_weight: bfloat16 [2048, 512], P(None, 'tensor'), may hold values from -0.125 to 0.125
- value_weight: bfloat16 [2048, 512], P(None, 'tensor'), may hold values from -0.125 to 0.125
- query_gain: float32 [128], replicated, may hold values from 0.5 to 1.5
- key_gain: float32 [128], replicated, may hold values from 0.5 to 1.5
- w_out: bfloat16 [4096, 2048], P('tensor'), may hold values from -1.5 to 1.5
- norm2_gain: float32 [2048], replicated, may hold values from 0.5 to 1.5
- w_router: bfloat16 [2048, 16], replicated, may hold values from -0.0625 to 0.0625
- w_gate: bfloat16 [16, 2048, 768], P('expert', None, 'tensor'), may hold values from -0.125 to 0.125
- w_up: bfloat16 [16, 2048, 768], P('expert', None, 'tensor'), may hold values from -0.125 to 0.125
- w_down: bfloat16 [16, 768, 2048], P('expert', 'tensor'), may hold values from -0.875 to 0.875
Outputs:
- out_hidden: bfloat16 [2048, 2048], P('expert')
- grad_hidden: bfloat16 [2048, 2048], P('expert')
- grad_norm1: float32 [2048], replicated
- grad_query: float32 [2048, 4096], P(None, 'tensor')
- grad_key: float32 [2048, 512], P(None, 'tensor')
- grad_value: float32 [2048, 512], P(None, 'tensor')
- grad_query_gain: float32 [128], replicated
- grad_key_gain: float32 [128], replicated
- grad_out: float32 [4096, 2048], P('tensor')
- grad_norm2: float32 [2048], replicated
- grad_router: float32 [2048, 16], replicated
- grad_gate: float32 [16, 2048, 768], P('expert', None, 'tensor')
- grad_up: float32 [16, 2048, 768], P('expert', None, 'tensor')
- grad_down: float32 [16, 768, 2048], P('expert', 'tensor')
The draws below stay inside these ranges and needn't reach their ends.
Inputs may be any that keep to these rules, and one draw needn't show every extreme that they name: `layout`: each place of the packed order is held by exactly one row. `seq_lengths`: the sequences lie one after another from place 0 and their lengths add up to 1920; places from 1920 on are padding; the longest has exactly 960. `expert_ids`: each row names 8 different experts; the 256 rows of one device name one expert at most 256 times, a bound that some block reaches. `drop_rank`: each value appears once.
All inputs are finite; a program needn't handle non-finite values.
Results may differ from the reference program's by a relative error of at most 0.024.
Values may be sent and summed in bfloat16 or wider, within the bound.
A program may use at most 320 MiB of HBM per device.

```python
import math
from functools import partial
import jax
import jax.numpy as jnp
import numpy as np
from jax import lax

MODEL_DIMENSION = 2048
QUERY_HEADS = 32
KEY_VALUE_HEADS = 4
HEAD_SIZE = 128
FF = 768
TOPK = 8
TOK_DEV = 256
EXPERTS = 16
TOKEN_TOTAL = 2048
VALID = 1920
LONGEST = 960
SEQS = 3
SLOT = 256
CAP = 1280
N_TENSOR = 4


def shard_levels(key, dims, split, smallest, top_value):
    level, own = 1.0, jax.random.fold_in(key, 6)
    for axis_at, blocks in split:
        draws = jnp.exp(jax.random.uniform(jax.random.fold_in(own, axis_at), (blocks,), jnp.float32, smallest / len(split), top_value / len(split)))
        level = level * jnp.repeat(draws, dims[axis_at] // blocks).reshape([-1 if axis == axis_at else 1 for axis in range(len(dims))])
    return level


def profile(amount, total, reach, lean):
    portions = [(1 << 20) // math.isqrt(rank ** lean) + 1 for rank in range(2, amount + 1)]
    surplus, counts = total - reach - (amount - 1), [1] * (amount - 1)
    while surplus > 0:
        candidates = [i for i in range(amount - 1) if counts[i] < reach]
        mass, left = sum([portions[i] for i in candidates]), surplus
        for i in candidates:
            addition = min(reach - counts[i], max(1, left * portions[i] // mass), surplus)
            counts[i] = counts[i] + addition
            surplus = surplus - addition
    return np.array([reach] + counts)


def ragged(stream_key, count, total, reach, skew):
    if count == 2:
        one = jax.random.randint(stream_key, (), max(1, total - reach), min(reach, total - 1) + 1)
        return jnp.stack([one, total - one])
    tallies = jnp.asarray(profile(count, total, reach, skew), jnp.int32)
    couples = (count - 1) // 2
    donor, taker = tallies[1:1 + 2 * couples:2], tallies[2:2 + 2 * couples:2]
    margin = jnp.minimum(donor - 1, reach - taker)
    moved = jax.random.randint(jax.random.fold_in(stream_key, 1), (couples,), 0, 1 << 20) % (margin + 1)
    tallies = tallies.at[1:1 + 2 * couples:2].set(donor - moved).at[2:2 + 2 * couples:2].set(taker + moved)
    return tallies[jax.random.permutation(jax.random.fold_in(stream_key, 2), count)]


def assign_block(own_key, own, number, rows, number_of, top, bound, skew):
    sequence = jax.random.permutation(own_key, number_of)
    packed, usual = portions_of(number_of, rows * top, bound, skew, True), portions_of(number_of, rows * top, bound, skew, False)
    places = jnp.arange(number_of)

    def named(tallies, rotation):
        used = int((tallies > 0).sum())
        fixed = max(1, used // 4)
        moved = fixed + (places - fixed + rotation * (used - fixed)) % max(1, number_of - fixed)
        return jnp.zeros((number_of,), jnp.int32).at[sequence[jnp.where(places < fixed, places, moved)]].set(jnp.asarray(tallies, jnp.int32))

    tallies = jnp.where(number % 4 == 0, named(packed, number // 4), named(usual, number - number // 4 - 1))
    mixed = jax.random.permutation(jax.random.fold_in(own, 3), number_of)
    donor, taker = mixed[0:number_of // 2 * 2:2], mixed[1:number_of // 2 * 2:2]
    margin = jnp.minimum(tallies[donor] - 1, bound - tallies[taker]) // 2
    margin = jnp.where((donor == sequence[0]) | (taker == sequence[0]) | (tallies[taker] == 0), 0, jnp.maximum(margin, 0))
    moved = jax.random.randint(jax.random.fold_in(own, 4), (number_of // 2,), 0, 1 << 20) % (margin + 1)
    tallies = tallies.at[donor].add(-moved).at[taker].add(moved)
    items = jnp.searchsorted(jnp.cumsum(tallies), jnp.arange(rows * top), side="right").astype(jnp.int32)
    listing = items.reshape(top, rows).T
    listing = listing[jax.random.permutation(jax.random.fold_in(own, 1), rows)]
    rotation = jax.random.randint(jax.random.fold_in(own, 2), (rows, 1), 0, top)
    return jnp.take_along_axis(listing, (jnp.arange(top)[None, :] + rotation) % top, axis=1)


def portions_of(count, total, limit, skew, full):
    weights = [(1 << 20) // math.isqrt(standing ** skew) + 1 for standing in range(1, count + 1)]
    largest = limit if full else min(limit, max(-(-total // count), total * weights[0] // sum(weights)))
    least = 1 if total - largest >= count - 1 else 0
    holding, surplus = [largest] + [least] * (count - 1), total - largest - least * (count - 1)
    while surplus > 0:
        candidates = [i for i in range(1, count) if holding[i] < largest] or [i for i in range(1, count) if holding[i] < limit]
        mass, remaining = sum([weights[i] for i in candidates]), surplus
        for i in candidates:
            more = min(limit - holding[i], max(1, remaining * weights[i] // mass), surplus)
            holding[i] = holding[i] + more
            surplus = surplus - more
    return np.array(holding)


def bell_draw(own_key, dims, width, most, shards=(), kind=jnp.bfloat16):
    drawn = jax.random.normal(own_key, dims, jnp.float32) * width
    if len(shards) > 0:
        drawn = shard_levels(own_key, dims, shards, -0.22, 0.18) * drawn
    return jnp.clip(drawn, min=-most, max=most).astype(kind)


def setup_inputs(seed: int = 0) -> dict:
    seeds = jax.random.split(jax.random.key(seed), 19)
    hidden_in = bell_draw(seeds[0], (TOKEN_TOTAL, MODEL_DIMENSION), 1.0, 6.0, ((0, 8),))
    cotangent = bell_draw(seeds[1], (TOKEN_TOTAL, MODEL_DIMENSION), 1.0, 6.0, ((0, 8),))
    layout = jax.random.permutation(seeds[2], TOKEN_TOTAL).astype(jnp.int32)
    seq_lengths = ragged(seeds[3], SEQS, VALID, LONGEST, 2).astype(jnp.int32)
    expert_ids_keys = jax.random.split(jax.random.fold_in(seeds[4], 1), TOKEN_TOTAL // TOK_DEV)
    expert_ids_turns = jax.random.permutation(jax.random.fold_in(seeds[4], 3), TOKEN_TOTAL // TOK_DEV)
    expert_ids = jax.vmap(lambda own, number: assign_block(jax.random.fold_in(seeds[4], 2), own, number, TOK_DEV, EXPERTS, TOPK, SLOT, 1))(expert_ids_keys, expert_ids_turns).reshape((TOKEN_TOTAL, TOPK))
    drop_rank = jax.random.permutation(seeds[5], TOKEN_TOTAL).astype(jnp.int32)
    norm1_gain = jnp.clip(1.0 + 0.1 * jax.random.normal(seeds[6], (MODEL_DIMENSION,), jnp.float32), 0.5, 1.5)
    w_query = bell_draw(seeds[7], (MODEL_DIMENSION, QUERY_HEADS * HEAD_SIZE), MODEL_DIMENSION ** -0.5, 0.125, ((1, 4),))
    key_weight = bell_draw(seeds[8], (MODEL_DIMENSION, KEY_VALUE_HEADS * HEAD_SIZE), MODEL_DIMENSION ** -0.5, 0.125, ((1, 4),))
    value_weight = bell_draw(seeds[9], (MODEL_DIMENSION, KEY_VALUE_HEADS * HEAD_SIZE), MODEL_DIMENSION ** -0.5, 0.125, ((1, 4),))
    query_gain = jnp.clip(1.0 + 0.1 * jax.random.normal(seeds[10], (HEAD_SIZE,), jnp.float32), 0.5, 1.5)
    key_gain = jnp.clip(1.0 + 0.1 * jax.random.normal(seeds[11], (HEAD_SIZE,), jnp.float32), 0.5, 1.5)
    w_out = bell_draw(seeds[12], (QUERY_HEADS * HEAD_SIZE, MODEL_DIMENSION), (max(QUERY_HEADS * HEAD_SIZE // 256, 2)) ** -0.5, 1.5, ((0, 4),))
    norm2_gain = jnp.clip(1.0 + 0.1 * jax.random.normal(seeds[13], (MODEL_DIMENSION,), jnp.float32), 0.5, 1.5)
    w_router = bell_draw(seeds[14], (MODEL_DIMENSION, EXPERTS), (4 * MODEL_DIMENSION) ** -0.5, 0.0625)
    w_gate = bell_draw(seeds[15], (EXPERTS, MODEL_DIMENSION, FF), MODEL_DIMENSION ** -0.5, 0.125, ((0, 8), (2, 4)))
    w_up = bell_draw(seeds[16], (EXPERTS, MODEL_DIMENSION, FF), MODEL_DIMENSION ** -0.5, 0.125, ((0, 8), (2, 4)))
    w_down = bell_draw(seeds[17], (EXPERTS, FF, MODEL_DIMENSION), (FF // 16) ** -0.5, 0.875, ((0, 8), (1, 4)))
    return dict(hidden_in=hidden_in, cotangent=cotangent, layout=layout, seq_lengths=seq_lengths, expert_ids=expert_ids, drop_rank=drop_rank, norm1_gain=norm1_gain, w_query=w_query, key_weight=key_weight, value_weight=value_weight, query_gain=query_gain, key_gain=key_gain, w_out=w_out, norm2_gain=norm2_gain, w_router=w_router, w_gate=w_gate, w_up=w_up, w_down=w_down)


@jax.custom_vjp
def reduced_precision(v):
    return lax.optimization_barrier(v.astype(jnp.bfloat16)).astype(jnp.float32)

@jax.custom_vjp
def reduced_precision_backward(v):
    return v

def low_keep(v):
    return (reduced_precision(v), None)

def low_pass(kept, grad):
    return (grad,)

def back_keep(v):
    return (v, None)

def back_low(kept, grad):
    return (reduced_precision(grad),)
reduced_precision.defvjp(low_keep, low_pass)
reduced_precision_backward.defvjp(back_keep, back_low)
EPS = 1e-06
THETA = 1000000.0
NEG = -1e+30
HIGH = lax.Precision.HIGHEST

def product_highest_precision(left, right):
    return jnp.dot(left, right, precision=HIGH, preferred_element_type=jnp.float32)

def norm_rows(value_matrix, gain):
    return value_matrix * lax.rsqrt(lax.optimization_barrier(jnp.mean(value_matrix * value_matrix, axis=-1, keepdims=True)) + EPS) * gain

def rotary(value_matrix, position):
    half_dim = value_matrix.shape[-1] // 2
    inverse = THETA ** (-(jnp.arange(half_dim, dtype=jnp.float32) * 2.0) / value_matrix.shape[-1])
    angles = position.astype(jnp.float32)[:, None] * inverse[None, :]
    cosine_table = jnp.concatenate([jnp.cos(angles), jnp.cos(angles)], axis=-1)[:, None, :]
    sine_table = jnp.concatenate([jnp.sin(angles), jnp.sin(angles)], axis=-1)[:, None, :]
    turned = jnp.concatenate([-value_matrix[..., half_dim:], value_matrix[..., :half_dim]], axis=-1)
    return value_matrix * cosine_table + turned * sine_table

def shape_queries(linear, gain, position):
    head_dim = gain.shape[0]
    shaped = linear.reshape(linear.shape[0], linear.shape[1] // head_dim, head_dim)
    return rotary(norm_rows(shaped, gain), position) * head_dim ** (-0.5)

def shape_keys(linear, gain, position):
    head_dim = gain.shape[0]
    shaped = linear.reshape(linear.shape[0], linear.shape[1] // head_dim, head_dim)
    return rotary(norm_rows(shaped, gain), position)

def token_tables(token_position, seq_lengths):
    bounds = jnp.cumsum(seq_lengths).astype(jnp.int32)
    passed = token_position[:, None] >= bounds[None, :]
    segment_ids = lax.optimization_barrier(jnp.sum(passed.astype(jnp.int32), axis=1)).astype(jnp.int32)
    opening = lax.optimization_barrier(jnp.max(jnp.where(passed, bounds[None, :], 0), axis=1)).astype(jnp.int32)
    return (segment_ids, (token_position - opening).astype(jnp.int32))

def visible(query_segment, query_place, key_segment, key_place):
    return (query_segment[:, None] == key_segment[None, :]) & (key_place[None, :] <= query_place[:, None])

def layer(hidden, norm1_gain, w_query, key_weight, value_weight, query_gain, key_gain, w_out, norm2_gain, w_router, w_gate, w_up, w_down, tables):
    segment_ids, position, token_position, expert_ids, kept_pair, target, source = tables
    first_normalized = reduced_precision(norm_rows(hidden, norm1_gain))
    query_lin = reduced_precision_backward(product_highest_precision(first_normalized, w_query))
    key_lin = reduced_precision_backward(product_highest_precision(first_normalized, key_weight))
    value_matrix = reduced_precision(reduced_precision_backward(product_highest_precision(first_normalized, value_weight))).reshape(TOKEN_TOTAL, KEY_VALUE_HEADS, HEAD_SIZE)
    query_matrix = reduced_precision(shape_queries(query_lin, query_gain, position))
    key_rows = reduced_precision(shape_keys(key_lin, key_gain, position))
    heads_per_group = QUERY_HEADS // KEY_VALUE_HEADS
    rows_per_block = min(512, TOKEN_TOTAL)
    count_of_blocks = TOKEN_TOTAL // rows_per_block

    def attend_rows(operands):
        query_block, segment_block, place_block = operands
        scores = reduced_precision_backward(jnp.einsum('qhgd,khd->hgqk', query_block, key_rows, precision=HIGH))
        allowed = visible(segment_block, place_block, segment_ids, token_position)
        scores = jnp.where(allowed[None, None], scores, NEG)
        probability = reduced_precision(jax.nn.softmax(scores, axis=-1))
        return jnp.einsum('hgqk,khd->qhgd', probability, value_matrix, precision=HIGH)
    attention_output = lax.map(jax.checkpoint(attend_rows), (query_matrix.reshape(count_of_blocks, rows_per_block, KEY_VALUE_HEADS, heads_per_group, HEAD_SIZE), segment_ids.reshape(count_of_blocks, rows_per_block), token_position.reshape(count_of_blocks, rows_per_block)))
    attention_output = reduced_precision(reduced_precision_backward(attention_output.reshape(TOKEN_TOTAL, QUERY_HEADS * HEAD_SIZE)))
    residual = hidden + reduced_precision_backward(product_highest_precision(attention_output, w_out))
    normed2 = reduced_precision(norm_rows(residual, norm2_gain))
    logits = reduced_precision_backward(product_highest_precision(normed2, w_router))
    gate_weights = jax.nn.softmax(jnp.take_along_axis(logits, expert_ids, axis=1), axis=1) * kept_pair
    padded = jnp.concatenate([normed2, jnp.zeros((1, MODEL_DIMENSION), jnp.float32)], axis=0)
    entries = padded[source].reshape(EXPERTS, CAP, MODEL_DIMENSION)
    group_width = FF // N_TENSOR
    returned = jnp.zeros((EXPERTS, CAP, MODEL_DIMENSION), jnp.float32)
    for group_index in range(N_TENSOR):
        lower_col = group_index * group_width
        upper_col = lower_col + group_width
        group_entries = reduced_precision_backward(entries)
        gate_lin = reduced_precision_backward(jnp.einsum('ecd,edf->ecf', group_entries, w_gate[:, :, lower_col:upper_col], precision=HIGH))
        up_lin = reduced_precision_backward(jnp.einsum('ecd,edf->ecf', group_entries, w_up[:, :, lower_col:upper_col], precision=HIGH))
        activation = reduced_precision(jax.nn.silu(gate_lin) * up_lin)
        returned = returned + reduced_precision(reduced_precision_backward(jnp.einsum('ecf,efd->ecd', activation, w_down[:, lower_col:upper_col, :], precision=HIGH)))
    flattened = jnp.concatenate([returned.reshape(EXPERTS * CAP, MODEL_DIMENSION), jnp.zeros((1, MODEL_DIMENSION), jnp.float32)], axis=0)
    pair_out = flattened[target].reshape(TOKEN_TOTAL, TOPK, MODEL_DIMENSION)
    return residual + lax.optimization_barrier(jnp.sum(gate_weights[:, :, None] * pair_out, axis=1))

def reference(hidden_in, cotangent, layout, seq_lengths, expert_ids, drop_rank, norm1_gain, w_query, key_weight, value_weight, query_gain, key_gain, w_out, norm2_gain, w_router, w_gate, w_up, w_down):
    token_position = layout.astype(jnp.int32)
    chosen_ids = expert_ids.astype(jnp.int32)
    rank_order = drop_rank.astype(jnp.int32)
    segment_ids, position = token_tables(token_position, seq_lengths.astype(jnp.int32))
    valid = segment_ids < SEQS
    expert_range = jnp.arange(EXPERTS, dtype=jnp.int32)
    picks = (jnp.any(chosen_ids[:, :, None] == expert_range, axis=1) & valid[:, None]).astype(jnp.int32)
    ranked = jnp.zeros((TOKEN_TOTAL, EXPERTS), jnp.int32).at[rank_order].set(picks)
    earlier = (jnp.cumsum(ranked, axis=0) - ranked).astype(jnp.int32)[rank_order]
    global_slot = jnp.take_along_axis(earlier, chosen_ids, axis=1).astype(jnp.int32)
    kept_mask = (global_slot < CAP) & valid[:, None]
    target = jnp.where(kept_mask, chosen_ids * CAP + global_slot, EXPERTS * CAP).reshape(-1).astype(jnp.int32)
    pair_token = jnp.repeat(jnp.arange(TOKEN_TOTAL, dtype=jnp.int32), TOPK)
    source = jnp.full((EXPERTS * CAP,), TOKEN_TOTAL, jnp.int32).at[target].set(pair_token, mode='drop')
    tables = (segment_ids, position, token_position, chosen_ids, kept_mask.astype(jnp.float32), target, source)
    layer_fn = partial(layer, tables=tables)
    out_hidden, pullback = jax.vjp(layer_fn, hidden_in.astype(jnp.float32), norm1_gain.astype(jnp.float32), w_query.astype(jnp.float32), key_weight.astype(jnp.float32), value_weight.astype(jnp.float32), query_gain.astype(jnp.float32), key_gain.astype(jnp.float32), w_out.astype(jnp.float32), norm2_gain.astype(jnp.float32), w_router.astype(jnp.float32), w_gate.astype(jnp.float32), w_up.astype(jnp.float32), w_down.astype(jnp.float32))
    grads = pullback(cotangent.astype(jnp.float32))
    return (out_hidden.astype(jnp.bfloat16), grads[0].astype(jnp.bfloat16), grads[1], grads[2], grads[3], grads[4], grads[5], grads[6], grads[7], grads[8], grads[9], grads[10], grads[11], grads[12])
```

```python
from functools import partial
import math

import jax
import jax.numpy as jnp
from jax import lax
from jax.sharding import PartitionSpec as P

TOPK = 8
CAP = 1280


EPS = 1e-06
THETA = 1000000.0
NEG = -1e30


def norm_rows(value_matrix, gain):
    return (
        value_matrix
        * lax.rsqrt(jnp.mean(value_matrix * value_matrix, axis=-1, keepdims=True) + EPS)
        * gain
    )


def rotary(value_matrix, position):
    half_dim = value_matrix.shape[-1] // 2
    inverse = THETA ** (-(jnp.arange(half_dim, dtype=jnp.float32) * 2.0) / value_matrix.shape[-1])
    angles = position.astype(jnp.float32)[:, None] * inverse[None, :]
    cosine_table = jnp.concatenate([jnp.cos(angles), jnp.cos(angles)], axis=-1)[:, None, :]
    sine_table = jnp.concatenate([jnp.sin(angles), jnp.sin(angles)], axis=-1)[:, None, :]
    turned = jnp.concatenate([-value_matrix[..., half_dim:], value_matrix[..., :half_dim]], axis=-1)
    return value_matrix * cosine_table + turned * sine_table


def shape_queries(linear, gain, position):
    head_dim = gain.shape[0]
    shaped = linear.reshape(linear.shape[0], linear.shape[1] // head_dim, head_dim)
    return rotary(norm_rows(shaped, gain), position) * head_dim ** (-0.5)


def shape_keys(linear, gain, position):
    head_dim = gain.shape[0]
    shaped = linear.reshape(linear.shape[0], linear.shape[1] // head_dim, head_dim)
    return rotary(norm_rows(shaped, gain), position)


def token_tables(token_position, seq_lengths):
    bounds = jnp.cumsum(seq_lengths)
    passed = token_position[:, None] >= bounds[None, :]
    segment_ids = jnp.sum(passed.astype(jnp.int32), axis=1)
    opening = jnp.max(jnp.where(passed, bounds[None, :], 0), axis=1)
    return (segment_ids, (token_position - opening).astype(jnp.int32))


def visible(query_segment, query_place, key_segment, key_place):
    return (query_segment[:, None] == key_segment[None, :]) & (
        key_place[None, :] <= query_place[:, None]
    )


def deliver(payload, slot_ids):
    return (
        lax.all_to_all(payload, "expert", split_axis=0, concat_axis=0, tiled=True),
        lax.all_to_all(slot_ids, "expert", split_axis=0, concat_axis=0, tiled=True),
    )


def bring_back(payload):
    return lax.all_to_all(payload, "expert", split_axis=0, concat_axis=0, tiled=True)


def expert_forward(entry_rows, w_gate, w_up, w_down):
    gate_lin = jnp.einsum("gesd,edf->gesf", entry_rows, w_gate, preferred_element_type=jnp.float32)
    up_lin = jnp.einsum("gesd,edf->gesf", entry_rows, w_up, preferred_element_type=jnp.float32)
    activation = (jax.nn.silu(gate_lin) * up_lin).astype(jnp.bfloat16)
    expert_out = jnp.einsum(
        "gesf,efd->gesd", activation, w_down, preferred_element_type=jnp.float32
    ).astype(jnp.bfloat16)
    return (gate_lin, up_lin, activation, expert_out)


def expert_backward(entry_rows, gate_lin, up_lin, activation, grad_in, w_gate, w_up, w_down):
    grad_down = jnp.einsum(
        "gesf,gesd->efd", activation, grad_in, preferred_element_type=jnp.float32
    )
    grad_act = jnp.einsum("gesd,efd->gesf", grad_in, w_down, preferred_element_type=jnp.float32)
    sigmoid = jax.nn.sigmoid(gate_lin)
    grad_gate_lin = (grad_act * up_lin * sigmoid * (1.0 + gate_lin * (1.0 - sigmoid))).astype(
        jnp.bfloat16
    )
    grad_up_lin = (grad_act * gate_lin * sigmoid).astype(jnp.bfloat16)
    grad_w_gate = jnp.einsum(
        "gesd,gesf->edf", entry_rows, grad_gate_lin, preferred_element_type=jnp.float32
    )
    grad_w_up = jnp.einsum(
        "gesd,gesf->edf", entry_rows, grad_up_lin, preferred_element_type=jnp.float32
    )
    grad_entry = jnp.einsum(
        "gesf,edf->gesd", grad_gate_lin, w_gate, preferred_element_type=jnp.float32
    )
    grad_entry = (
        grad_entry
        + jnp.einsum("gesf,edf->gesd", grad_up_lin, w_up, preferred_element_type=jnp.float32)
    ).astype(jnp.bfloat16)
    return (grad_entry, grad_w_gate, grad_w_up, grad_down)


def per_device(
    hidden_in,
    cotangent,
    layout,
    seq_lengths,
    expert_ids,
    drop_rank,
    norm1_gain,
    w_query,
    key_weight,
    value_weight,
    query_gain,
    key_gain,
    w_out,
    norm2_gain,
    w_router,
    w_gate,
    w_up,
    w_down,
):
    tok_rows = hidden_in.shape[0]
    model_width = hidden_in.shape[1]
    head_dim = query_gain.shape[0]
    local_heads = w_query.shape[1] // head_dim
    expert_count = w_router.shape[1]
    local_count = w_gate.shape[0]
    group_count = lax.axis_size("expert")
    slot_count = 2 * tok_rows * TOPK // expert_count
    seq_count = seq_lengths.shape[0]
    expert_range = jnp.arange(expert_count, dtype=jnp.int32)
    hidden = hidden_in.astype(jnp.float32)
    segment_ids, position = token_tables(layout, seq_lengths)
    valid = segment_ids < seq_count
    first_normalized = norm_rows(hidden, norm1_gain)
    normed1_low = first_normalized.astype(jnp.bfloat16)
    query_lin = jnp.dot(normed1_low, w_query, preferred_element_type=jnp.float32)
    key_lin = jnp.dot(normed1_low, key_weight, preferred_element_type=jnp.float32)
    value_lin = jnp.dot(normed1_low, value_weight, preferred_element_type=jnp.float32)
    query_shaped = shape_queries(query_lin, query_gain, position).astype(jnp.bfloat16)
    query_total = local_heads * tok_rows
    query_rows = jnp.transpose(query_shaped, (1, 0, 2)).reshape(query_total, head_dim)
    key_rows = (
        shape_keys(key_lin, key_gain, position).astype(jnp.bfloat16).reshape(tok_rows, head_dim)
    )
    value_rows = value_lin.astype(jnp.bfloat16)
    all_keys, all_values, all_place, all_ids, all_rank = (
        lax.all_gather(key_rows, "expert", axis=0, tiled=True),
        lax.all_gather(value_rows, "expert", axis=0, tiled=True),
        lax.all_gather(layout, "expert", axis=0, tiled=True),
        lax.all_gather(expert_ids, "expert", axis=0, tiled=True),
        lax.all_gather(drop_rank, "expert", axis=0, tiled=True),
    )
    all_segment = token_tables(all_place, seq_lengths)[0]
    rows_per_block = math.gcd(512, query_total)
    count_of_blocks = query_total // rows_per_block
    query_segment = jnp.tile(segment_ids, local_heads)
    query_place = jnp.tile(layout, local_heads)

    def attend_block(operands):
        query_block, segment_block, place_block = operands
        scores = jnp.einsum("qd,kd->qk", query_block, all_keys, preferred_element_type=jnp.float32)
        scores = jnp.where(visible(segment_block, place_block, all_segment, all_place), scores, NEG)
        highest = jnp.max(scores, axis=1, keepdims=True)
        weights = jnp.exp(scores - highest)
        totals = jnp.sum(weights, axis=1, keepdims=True)
        probability = (weights / totals).astype(jnp.bfloat16)
        mixed_out = jnp.dot(probability, all_values, preferred_element_type=jnp.float32)
        return (mixed_out, (highest + jnp.log(totals))[:, 0])

    attention_output, log_totals = lax.map(
        attend_block,
        (
            query_rows.reshape(count_of_blocks, rows_per_block, head_dim),
            query_segment.reshape(count_of_blocks, rows_per_block),
            query_place.reshape(count_of_blocks, rows_per_block),
        ),
    )
    attention_output = attention_output.reshape(local_heads, tok_rows, head_dim).astype(
        jnp.bfloat16
    )
    att_cat = jnp.transpose(attention_output, (1, 0, 2)).reshape(tok_rows, local_heads * head_dim)
    branch_part = jnp.dot(att_cat, w_out, preferred_element_type=jnp.float32)
    branch = lax.psum(branch_part, "tensor")
    residual = hidden + branch
    normed2 = norm_rows(residual, norm2_gain)
    normed2_low = normed2.astype(jnp.bfloat16)
    logits = jnp.dot(normed2_low, w_router, preferred_element_type=jnp.float32)
    soft_gate = jax.nn.softmax(jnp.take_along_axis(logits, expert_ids, axis=1), axis=1)
    picks = jnp.any(expert_ids[:, :, None] == expert_range, axis=1) & valid[:, None]
    all_valid = all_segment < seq_count
    all_picks = jnp.any(all_ids[:, :, None] == expert_range, axis=1) & all_valid[:, None]
    earlier = (all_rank[None, :] < drop_rank[:, None]).astype(jnp.bfloat16)
    before_counts = jnp.dot(
        earlier, all_picks.astype(jnp.bfloat16), preferred_element_type=jnp.float32
    )
    global_slot = jnp.take_along_axis(before_counts, expert_ids, axis=1).astype(jnp.int32)
    kept_mask = (global_slot < CAP) & valid[:, None]
    gate_weight = soft_gate * kept_mask.astype(jnp.float32)
    lower_rows = (jnp.arange(tok_rows)[None, :] < jnp.arange(tok_rows)[:, None]).astype(
        jnp.bfloat16
    )
    local_counts = jnp.dot(
        lower_rows, picks.astype(jnp.bfloat16), preferred_element_type=jnp.float32
    )
    local_slot = jnp.take_along_axis(local_counts, expert_ids, axis=1).astype(jnp.int32)
    pair_count = tok_rows * TOPK
    dump_index = expert_count * slot_count
    target = jnp.where(kept_mask, expert_ids * slot_count + local_slot, dump_index)
    pair_index = jnp.arange(pair_count, dtype=jnp.int32)
    slot_pair = (
        jnp.full((dump_index,), pair_count, jnp.int32)
        .at[target.reshape(-1)]
        .set(pair_index, mode="drop")
    )
    slot_token = jnp.where(slot_pair < pair_count, slot_pair // TOPK, tok_rows)
    slot_global = (
        jnp.full((dump_index,), -1, jnp.int32)
        .at[target.reshape(-1)]
        .set(global_slot.reshape(-1), mode="drop")
    )
    padded_rows = jnp.concatenate([normed2_low, jnp.zeros((1, model_width), jnp.bfloat16)], axis=0)
    send_rows = padded_rows[slot_token].reshape(group_count, local_count, slot_count, model_width)
    send_slot = slot_global.reshape(group_count, local_count, slot_count)
    received, received_slot = deliver(send_rows, send_slot)
    gate_lin, up_lin, activation, expert_out = expert_forward(received, w_gate, w_up, w_down)
    returned = bring_back(expert_out)
    returned_flat = jnp.concatenate(
        [returned.reshape(dump_index, model_width), jnp.zeros((1, model_width), returned.dtype)],
        axis=0,
    )
    pair_out = returned_flat[target]
    moe_part = jnp.sum(gate_weight[:, :, None] * pair_out, axis=1)
    moe_branch = lax.psum(moe_part.astype(jnp.bfloat16), "tensor").astype(jnp.float32)
    out_hidden = (residual + moe_branch).astype(jnp.bfloat16)
    grad_y = cotangent.astype(jnp.float32)
    gate_dot = jnp.sum(grad_y[:, None, :] * pair_out, axis=2)
    pair_grads = (
        (gate_weight[:, :, None] * grad_y[:, None, :])
        .astype(jnp.bfloat16)
        .reshape(pair_count, model_width)
    )
    pair_grads = jnp.concatenate([pair_grads, jnp.zeros((1, model_width), jnp.bfloat16)], axis=0)
    send_grad = pair_grads[slot_pair].reshape(group_count, local_count, slot_count, model_width)
    grad_received, grad_slot = deliver(send_grad, send_slot)
    grad_entry, grad_w_gate, grad_w_up, grad_w_down = expert_backward(
        received, gate_lin, up_lin, activation, grad_received, w_gate, w_up, w_down
    )
    grad_returned = bring_back(grad_entry)
    grad_flat = jnp.concatenate(
        [
            grad_returned.reshape(dump_index, model_width),
            jnp.zeros((1, model_width), grad_returned.dtype),
        ],
        axis=0,
    )
    grad_normed2_part = jnp.sum(grad_flat[target], axis=1, dtype=jnp.float32)
    grad_normed2_exp, gate_dot = lax.psum((grad_normed2_part, gate_dot), "tensor")
    grad_soft = gate_dot * kept_mask.astype(jnp.float32)
    grad_chosen = soft_gate * (grad_soft - jnp.sum(soft_gate * grad_soft, axis=1, keepdims=True))
    grad_logits = jnp.sum(
        grad_chosen[:, :, None] * (expert_ids[:, :, None] == expert_range).astype(jnp.float32),
        axis=1,
    ).astype(jnp.bfloat16)
    grad_w_router = jnp.einsum(
        "td,te->de", normed2_low, grad_logits, preferred_element_type=jnp.float32
    )
    grad_normed2 = grad_normed2_exp + jnp.einsum(
        "te,de->td", grad_logits, w_router, preferred_element_type=jnp.float32
    )
    norm2_pull = jax.vjp(norm_rows, residual, norm2_gain)[1]
    grad_resid_norm, grad_norm2 = norm2_pull(grad_normed2)
    grad_residual = grad_y + grad_resid_norm
    grad_residual_low = grad_residual.astype(jnp.bfloat16)
    grad_w_out = jnp.einsum(
        "tc,td->cd", att_cat, grad_residual_low, preferred_element_type=jnp.float32
    )
    grad_att_cat = jnp.einsum(
        "td,cd->tc", grad_residual_low, w_out, preferred_element_type=jnp.float32
    ).astype(jnp.bfloat16)
    grad_att_rows = jnp.transpose(
        grad_att_cat.reshape(tok_rows, local_heads, head_dim), (1, 0, 2)
    ).reshape(query_total, head_dim)

    def query_grad_block(operands):
        query_block, segment_block, place_block, grad_block, log_block = operands
        scores = jnp.einsum("qd,kd->qk", query_block, all_keys, preferred_element_type=jnp.float32)
        scores = jnp.where(visible(segment_block, place_block, all_segment, all_place), scores, NEG)
        probability = jnp.exp(scores - log_block[:, None])
        grad_prob = jnp.einsum(
            "qd,kd->qk", grad_block, all_values, preferred_element_type=jnp.float32
        )
        delta_row = jnp.sum(probability * grad_prob, axis=1)
        grad_scores = (probability * (grad_prob - delta_row[:, None])).astype(jnp.bfloat16)
        return (jnp.dot(grad_scores, all_keys, preferred_element_type=jnp.float32), delta_row)

    grad_query_rows, deltas = lax.map(
        query_grad_block,
        (
            query_rows.reshape(count_of_blocks, rows_per_block, head_dim),
            query_segment.reshape(count_of_blocks, rows_per_block),
            query_place.reshape(count_of_blocks, rows_per_block),
            grad_att_rows.reshape(count_of_blocks, rows_per_block, head_dim),
            log_totals,
        ),
    )
    log_flat = log_totals.reshape(query_total)
    delta_flat = deltas.reshape(query_total)
    key_block = math.gcd(lax.axis_size("expert") * tok_rows, 2048)

    def one_block(offset):
        key_part = lax.dynamic_slice_in_dim(all_keys, offset, key_block, 0)
        value_part = lax.dynamic_slice_in_dim(all_values, offset, key_block, 0)
        segment_part = lax.dynamic_slice_in_dim(all_segment, offset, key_block, 0)
        place_part = lax.dynamic_slice_in_dim(all_place, offset, key_block, 0)
        scores = jnp.einsum("qd,kd->qk", query_rows, key_part, preferred_element_type=jnp.float32)
        scores = jnp.where(
            visible(query_segment, query_place, segment_part, place_part), scores, NEG
        )
        probability = jnp.exp(scores - log_flat[:, None])
        grad_value = jnp.einsum(
            "qk,qd->kd",
            probability.astype(jnp.bfloat16),
            grad_att_rows,
            preferred_element_type=jnp.float32,
        )
        grad_prob = jnp.einsum(
            "qd,kd->qk", grad_att_rows, value_part, preferred_element_type=jnp.float32
        )
        grad_scores = (probability * (grad_prob - delta_flat[:, None])).astype(jnp.bfloat16)
        grad_key = jnp.einsum(
            "qk,qd->kd", grad_scores, query_rows, preferred_element_type=jnp.float32
        )
        return jnp.concatenate([grad_key, grad_value], axis=1)

    stacked = lax.map(
        one_block,
        jnp.arange(lax.axis_size("expert") * tok_rows // key_block, dtype=jnp.int32) * key_block,
    )
    key_value_grad = lax.psum_scatter(
        stacked.reshape(lax.axis_size("expert") * tok_rows, 2 * head_dim).astype(jnp.bfloat16),
        "expert",
        scatter_dimension=0,
        tiled=True,
    ).astype(jnp.float32)
    grad_key_post = key_value_grad[:, :head_dim].reshape(tok_rows, 1, head_dim)
    grad_values_low = key_value_grad[:, head_dim:].astype(jnp.bfloat16)
    grad_query_tok = jnp.transpose(
        grad_query_rows.reshape(local_heads, tok_rows, head_dim), (1, 0, 2)
    )
    query_pull = jax.vjp(partial(shape_queries, position=position), query_lin, query_gain)[1]
    grad_query_lin, grad_qgain_part = query_pull(grad_query_tok)
    key_pull = jax.vjp(partial(shape_keys, position=position), key_lin, key_gain)[1]
    grad_key_lin, grad_kgain_part = key_pull(grad_key_post)
    grad_query_low = grad_query_lin.astype(jnp.bfloat16)
    grad_key_low = grad_key_lin.astype(jnp.bfloat16)
    grad_w_query = jnp.einsum(
        "td,tc->dc", normed1_low, grad_query_low, preferred_element_type=jnp.float32
    )
    grad_w_key = jnp.einsum(
        "td,tc->dc", normed1_low, grad_key_low, preferred_element_type=jnp.float32
    )
    grad_w_value = jnp.einsum(
        "td,tc->dc", normed1_low, grad_values_low, preferred_element_type=jnp.float32
    )
    grad_normed1_part = jnp.einsum(
        "tc,dc->td", grad_query_low, w_query, preferred_element_type=jnp.float32
    )
    grad_normed1_part = grad_normed1_part + jnp.einsum(
        "tc,dc->td", grad_key_low, key_weight, preferred_element_type=jnp.float32
    )
    grad_normed1_part = grad_normed1_part + jnp.einsum(
        "tc,dc->td", grad_values_low, value_weight, preferred_element_type=jnp.float32
    )
    grad_normed1, grad_qgain_part, grad_kgain_part = (
        lax.psum(grad_normed1_part.astype(jnp.bfloat16), "tensor").astype(jnp.float32),
        lax.psum(grad_qgain_part.astype(jnp.bfloat16), "tensor").astype(jnp.float32),
        lax.psum(grad_kgain_part.astype(jnp.bfloat16), "tensor").astype(jnp.float32),
    )
    norm1_pull = jax.vjp(norm_rows, hidden, norm1_gain)[1]
    grad_hidden_norm, grad_norm1 = norm1_pull(grad_normed1)
    grad_hidden = (grad_residual + grad_hidden_norm).astype(jnp.bfloat16)
    summed = (
        lax.psum(grad_norm1.astype(jnp.bfloat16), "expert").astype(jnp.float32),
        lax.psum(grad_w_query.astype(jnp.bfloat16), "expert").astype(jnp.float32),
        lax.psum(grad_w_key.astype(jnp.bfloat16), "expert").astype(jnp.float32),
        lax.psum(grad_w_value.astype(jnp.bfloat16), "expert").astype(jnp.float32),
        lax.psum(grad_qgain_part.astype(jnp.bfloat16), "expert").astype(jnp.float32),
        lax.psum(grad_kgain_part.astype(jnp.bfloat16), "expert").astype(jnp.float32),
        lax.psum(grad_w_out.astype(jnp.bfloat16), "expert").astype(jnp.float32),
        lax.psum(grad_norm2.astype(jnp.bfloat16), "expert").astype(jnp.float32),
        lax.psum(grad_w_router.astype(jnp.bfloat16), "expert").astype(jnp.float32),
    )
    return (
        out_hidden,
        grad_hidden,
        summed[0],
        summed[1],
        summed[2],
        summed[3],
        summed[4],
        summed[5],
        summed[6],
        summed[7],
        summed[8],
        grad_w_gate,
        grad_w_up,
        grad_w_down,
    )


def all_tokens(layout, expert_ids, drop_rank):
    packed = jnp.concatenate([layout[None], drop_rank[None], expert_ids.T], axis=0)
    gathered = lax.all_gather(packed, "expert", axis=1, tiled=True)
    return gathered[0], gathered[1], gathered[2:]


BOTH = ("expert", "tensor")


def gather_rows(rows):
    return lax.all_gather(rows, BOTH, axis=0, tiled=True)


def scatter_rows(partial_rows):
    return lax.psum_scatter(partial_rows, BOTH, scatter_dimension=0, tiled=True)


def head_device(
    hidden_in,
    cotangent,
    layout,
    seq_lengths,
    expert_ids,
    drop_rank,
    norm1_gain,
    w_query,
    key_weight,
    value_weight,
    query_gain,
    key_gain,
    w_out,
    norm2_gain,
    w_router,
    w_gate,
    w_up,
    w_down,
):
    f32, bf16 = jnp.float32, jnp.bfloat16
    tok_rows, model_width = hidden_in.shape
    head_dim = query_gain.shape[0]
    expert_count = w_router.shape[1]
    local_count, _, ff_local = w_gate.shape
    groups = lax.axis_size("expert")
    tensor_size = lax.axis_size("tensor")
    total_rows = groups * tok_rows
    own_rows = tok_rows // tensor_size
    seq_count = seq_lengths.shape[0]
    group = lax.axis_index("expert")
    part = lax.axis_index("tensor")

    def own(rows):
        return lax.dynamic_slice_in_dim(rows, part * own_rows, own_rows, 0)

    place, rank, ids_t = all_tokens(layout, expert_ids, drop_rank)
    segment, position = token_tables(place, seq_lengths)
    valid = segment < seq_count
    hidden_all = gather_rows(own(hidden_in))
    grad_y_all = gather_rows(own(cotangent))

    head_query = lax.dynamic_slice_in_dim(w_query, group * head_dim, head_dim, 1)
    head_out = lax.dynamic_slice_in_dim(w_out, group * head_dim, head_dim, 0)
    qkv_weight = jnp.concatenate([head_query, key_weight, value_weight], axis=1)
    normed1 = norm_rows(hidden_all.astype(f32), norm1_gain).astype(bf16)
    lin = jnp.dot(normed1, qkv_weight, preferred_element_type=f32)
    query_lin, key_lin = lin[:, :head_dim], lin[:, head_dim : 2 * head_dim]
    values = lin[:, 2 * head_dim :].astype(bf16)
    queries, query_pull = jax.vjp(
        lambda v, g: shape_queries(v, g, position)[:, 0], query_lin, query_gain
    )
    keys, key_pull = jax.vjp(lambda v, g: shape_keys(v, g, position)[:, 0], key_lin, key_gain)
    queries, keys = queries.astype(bf16), keys.astype(bf16)
    allowed = visible(segment, place, segment, place)
    scores = jnp.einsum("qd,kd->qk", queries, keys, preferred_element_type=f32)
    scores = jnp.where(allowed, scores, NEG)
    probability = jax.nn.softmax(scores, axis=1)
    attended = jnp.dot(probability.astype(bf16), values, preferred_element_type=f32).astype(bf16)
    att_rows = lax.all_to_all(attended, "expert", split_axis=0, concat_axis=0, tiled=True)
    att_rows = jnp.transpose(att_rows.reshape(groups, tok_rows, head_dim), (1, 0, 2)).reshape(
        tok_rows, groups * head_dim
    )
    branch_part = jnp.dot(att_rows, w_out, preferred_element_type=f32)
    branch = lax.psum_scatter(
        branch_part.astype(bf16), "tensor", scatter_dimension=0, tiled=True
    ).astype(f32)
    residual = own(hidden_in).astype(f32) + branch
    normed2, norm2_pull = jax.vjp(norm_rows, residual, norm2_gain)
    normed2 = normed2.astype(bf16)
    normed2_all = gather_rows(normed2)

    expert_range = jnp.arange(expert_count, dtype=jnp.int32)
    chosen = jnp.any(ids_t[:, :, None] == expert_range, axis=0)
    picks = (chosen & valid[:, None]).astype(bf16)
    earlier = (rank[None, :] < rank[:, None]).astype(bf16)
    slot = jnp.dot(earlier, picks, preferred_element_type=f32)
    kept = chosen & valid[:, None] & (slot < CAP)

    def gates(rows, picked):
        logits = jnp.dot(rows, w_router, preferred_element_type=f32)
        return jax.nn.softmax(jnp.where(picked, logits, -jnp.inf), axis=1)

    gate_weight = jnp.where(kept, gates(normed2_all, chosen), 0.0)
    gate_local = lax.dynamic_slice_in_dim(gate_weight, group * local_count, local_count, 1)
    kept_local = lax.dynamic_slice_in_dim(kept, group * local_count, local_count, 1)

    weight_in = jnp.concatenate([w_gate, w_up], axis=0)
    weight_in = jnp.transpose(weight_in, (1, 0, 2)).reshape(model_width, -1)
    weight_down = w_down.reshape(local_count * ff_local, model_width)
    wide = local_count * ff_local
    lin2 = jnp.dot(normed2_all, weight_in, preferred_element_type=f32)
    gate_lin, up_lin = lin2[:, :wide], lin2[:, wide:]
    sigmoid = jax.nn.sigmoid(gate_lin)
    silu = gate_lin * sigmoid
    spread = jnp.repeat(gate_local, ff_local, axis=1)
    activation = (silu * up_lin).astype(bf16).astype(f32)
    weighted = (activation * spread).astype(bf16)
    out_part = jnp.dot(weighted, weight_down, preferred_element_type=f32)
    grad_down = jnp.einsum("rf,rd->fd", weighted, grad_y_all, preferred_element_type=f32)
    grad_mid = jnp.einsum("rd,fd->rf", grad_y_all, weight_down, preferred_element_type=f32)
    dots = jnp.sum((activation * grad_mid).reshape(total_rows, local_count, ff_local), axis=2)
    dots = jnp.where(kept_local, dots, 0.0)
    grad_act = grad_mid * spread
    grad_gate_lin = (grad_act * up_lin * sigmoid * (1.0 + gate_lin * (1.0 - sigmoid))).astype(bf16)
    grad_up_lin = (grad_act * silu).astype(bf16)
    grad_lin2 = jnp.concatenate([grad_gate_lin, grad_up_lin], axis=1)
    grad_in = jnp.einsum("rd,rf->df", normed2_all, grad_lin2, preferred_element_type=f32)
    grad_in = jnp.transpose(
        grad_in.reshape(model_width, 2 * local_count, ff_local), (1, 0, 2)
    )
    grad_normed2_part = jnp.einsum(
        "rf,df->rd", grad_lin2, weight_in, preferred_element_type=f32
    )
    dots_wide = jnp.zeros((total_rows, head_dim), f32)
    dots_wide = lax.dynamic_update_slice(dots_wide, dots, (0, group * local_count))
    back = scatter_rows(
        jnp.concatenate([grad_normed2_part, dots_wide], axis=1).astype(bf16)
    ).astype(f32)
    moe_branch = scatter_rows(out_part.astype(bf16)).astype(f32)
    out_own = (residual + moe_branch).astype(bf16)

    start = group * tok_rows + part * own_rows
    chosen_own = lax.dynamic_slice_in_dim(chosen, start, own_rows, 0)
    soft_own = gates(normed2, chosen_own)
    grad_soft = back[:, model_width : model_width + expert_count]
    grad_logits = (
        soft_own * (grad_soft - jnp.sum(soft_own * grad_soft, axis=1, keepdims=True))
    ).astype(bf16)
    grad_router = jnp.einsum("td,te->de", normed2, grad_logits, preferred_element_type=f32)
    grad_normed2 = back[:, :model_width] + jnp.einsum(
        "te,de->td", grad_logits, w_router, preferred_element_type=f32
    )
    grad_resid_norm, grad_norm2 = norm2_pull(grad_normed2)
    grad_residual = own(cotangent).astype(f32) + grad_resid_norm
    grad_residual_all = gather_rows(grad_residual.astype(bf16))

    grad_out = jnp.einsum("rc,rd->cd", attended, grad_residual_all, preferred_element_type=f32)
    grad_att = jnp.einsum(
        "rd,cd->rc", grad_residual_all, head_out, preferred_element_type=f32
    ).astype(bf16)
    grad_prob = jnp.einsum("qd,kd->qk", grad_att, values, preferred_element_type=f32)
    delta = jnp.sum(probability * grad_prob, axis=1, keepdims=True)
    grad_scores = (probability * (grad_prob - delta)).astype(bf16)
    grad_queries = jnp.dot(grad_scores, keys, preferred_element_type=f32)
    grad_keys = jnp.einsum("qk,qd->kd", grad_scores, queries, preferred_element_type=f32)
    grad_values = jnp.einsum(
        "qk,qd->kd", probability.astype(bf16), grad_att, preferred_element_type=f32
    )
    grad_query_lin, grad_qgain = query_pull(grad_queries)
    grad_key_lin, grad_kgain = key_pull(grad_keys)
    grad_lin = jnp.concatenate([grad_query_lin, grad_key_lin, grad_values], axis=1).astype(bf16)
    grad_qkv = jnp.einsum("td,tc->dc", normed1, grad_lin, preferred_element_type=f32)
    grad_normed1_part = jnp.einsum(
        "tc,dc->td", grad_lin, qkv_weight, preferred_element_type=f32
    )
    grad_normed1 = scatter_rows(grad_normed1_part.astype(bf16)).astype(f32)
    norm1_pull = jax.vjp(norm_rows, own(hidden_in).astype(f32), norm1_gain)[1]
    grad_hidden_norm, grad_norm1 = norm1_pull(grad_normed1)
    grad_hidden_own = (grad_residual + grad_hidden_norm).astype(bf16)
    ends = lax.all_gather(
        jnp.concatenate([out_own, grad_hidden_own], axis=1), "tensor", axis=0, tiled=True
    )
    grad_query = lax.all_gather(
        grad_qkv[:, :head_dim].astype(bf16), "expert", axis=1, tiled=True
    ).astype(f32)
    grad_out = lax.all_gather(grad_out.astype(bf16), "expert", axis=0, tiled=True).astype(f32)
    grad_kv = lax.psum(grad_qkv[:, head_dim:].astype(bf16), "expert").astype(f32)
    grad_norm1, grad_norm2, grad_qgain, grad_kgain, grad_router = lax.psum(
        (grad_norm1, grad_norm2, grad_qgain, grad_kgain, grad_router), BOTH
    )
    grad_down = grad_down.reshape(local_count, ff_local, model_width)
    return (
        ends[:, :model_width],
        ends[:, model_width:],
        grad_norm1,
        grad_query,
        grad_kv[:, :head_dim],
        grad_kv[:, head_dim:],
        grad_qgain,
        grad_kgain,
        grad_out,
        grad_norm2,
        grad_router,
        grad_in[:local_count],
        grad_in[local_count:],
        grad_down,
    )


def solution(mesh):
    groups = mesh.shape["expert"]

    def device_fn(*operands):
        heads = operands[7].shape[1] // operands[10].shape[0]
        one_head = heads == groups and operands[8].shape[1] == operands[10].shape[0]
        return (head_device if one_head else per_device)(*operands)

    return jax.shard_map(
        device_fn,
        mesh=mesh,
        in_specs=(
            P("expert", None),
            P("expert", None),
            P("expert"),
            P(),
            P("expert", None),
            P("expert"),
            P(),
            P(None, "tensor"),
            P(None, "tensor"),
            P(None, "tensor"),
            P(),
            P(),
            P("tensor", None),
            P(),
            P(),
            P("expert", None, "tensor"),
            P("expert", None, "tensor"),
            P("expert", "tensor", None),
        ),
        out_specs=(
            P("expert", None),
            P("expert", None),
            P(),
            P(None, "tensor"),
            P(None, "tensor"),
            P(None, "tensor"),
            P(),
            P(),
            P("tensor", None),
            P(),
            P(),
            P("expert", None, "tensor"),
            P("expert", None, "tensor"),
            P("expert", "tensor", None),
        ),
        check_vma=False,
    )
```

```python
from functools import partial
import math

import jax
import jax.numpy as jnp
from jax import lax
from jax.experimental import pallas as pl
from jax.experimental.pallas import tpu as pltpu
from jax.sharding import PartitionSpec as P

TOPK = 8
CAP = 1280


EPS = 1e-06
THETA = 1000000.0
NEG = -1e30


def norm_rows(value_matrix, gain):
    return (
        value_matrix
        * lax.rsqrt(jnp.mean(value_matrix * value_matrix, axis=-1, keepdims=True) + EPS)
        * gain
    )


def rotary(value_matrix, position):
    half_dim = value_matrix.shape[-1] // 2
    inverse = THETA ** (-(jnp.arange(half_dim, dtype=jnp.float32) * 2.0) / value_matrix.shape[-1])
    angles = position.astype(jnp.float32)[:, None] * inverse[None, :]
    cosine_table = jnp.concatenate([jnp.cos(angles), jnp.cos(angles)], axis=-1)[:, None, :]
    sine_table = jnp.concatenate([jnp.sin(angles), jnp.sin(angles)], axis=-1)[:, None, :]
    turned = jnp.concatenate([-value_matrix[..., half_dim:], value_matrix[..., :half_dim]], axis=-1)
    return value_matrix * cosine_table + turned * sine_table


def shape_queries(linear, gain, position):
    head_dim = gain.shape[0]
    shaped = linear.reshape(linear.shape[0], linear.shape[1] // head_dim, head_dim)
    return rotary(norm_rows(shaped, gain), position) * head_dim ** (-0.5)


def shape_keys(linear, gain, position):
    head_dim = gain.shape[0]
    shaped = linear.reshape(linear.shape[0], linear.shape[1] // head_dim, head_dim)
    return rotary(norm_rows(shaped, gain), position)


def token_tables(token_position, seq_lengths):
    bounds = jnp.cumsum(seq_lengths)
    passed = token_position[:, None] >= bounds[None, :]
    segment_ids = jnp.sum(passed.astype(jnp.int32), axis=1)
    opening = jnp.max(jnp.where(passed, bounds[None, :], 0), axis=1)
    return (segment_ids, (token_position - opening).astype(jnp.int32))


def visible(query_segment, query_place, key_segment, key_place):
    return (query_segment[:, None] == key_segment[None, :]) & (
        key_place[None, :] <= query_place[:, None]
    )


def deliver(payload, slot_ids):
    return (
        lax.all_to_all(payload, "expert", split_axis=0, concat_axis=0, tiled=True),
        lax.all_to_all(slot_ids, "expert", split_axis=0, concat_axis=0, tiled=True),
    )


def bring_back(payload):
    return lax.all_to_all(payload, "expert", split_axis=0, concat_axis=0, tiled=True)


def expert_forward(entry_rows, w_gate, w_up, w_down):
    gate_lin = jnp.einsum("gesd,edf->gesf", entry_rows, w_gate, preferred_element_type=jnp.float32)
    up_lin = jnp.einsum("gesd,edf->gesf", entry_rows, w_up, preferred_element_type=jnp.float32)
    activation = (jax.nn.silu(gate_lin) * up_lin).astype(jnp.bfloat16)
    expert_out = jnp.einsum(
        "gesf,efd->gesd", activation, w_down, preferred_element_type=jnp.float32
    ).astype(jnp.bfloat16)
    return (gate_lin, up_lin, activation, expert_out)


def expert_backward(entry_rows, gate_lin, up_lin, activation, grad_in, w_gate, w_up, w_down):
    grad_down = jnp.einsum(
        "gesf,gesd->efd", activation, grad_in, preferred_element_type=jnp.float32
    )
    grad_act = jnp.einsum("gesd,efd->gesf", grad_in, w_down, preferred_element_type=jnp.float32)
    sigmoid = jax.nn.sigmoid(gate_lin)
    grad_gate_lin = (grad_act * up_lin * sigmoid * (1.0 + gate_lin * (1.0 - sigmoid))).astype(
        jnp.bfloat16
    )
    grad_up_lin = (grad_act * gate_lin * sigmoid).astype(jnp.bfloat16)
    grad_w_gate = jnp.einsum(
        "gesd,gesf->edf", entry_rows, grad_gate_lin, preferred_element_type=jnp.float32
    )
    grad_w_up = jnp.einsum(
        "gesd,gesf->edf", entry_rows, grad_up_lin, preferred_element_type=jnp.float32
    )
    grad_entry = jnp.einsum(
        "gesf,edf->gesd", grad_gate_lin, w_gate, preferred_element_type=jnp.float32
    )
    grad_entry = (
        grad_entry
        + jnp.einsum("gesf,edf->gesd", grad_up_lin, w_up, preferred_element_type=jnp.float32)
    ).astype(jnp.bfloat16)
    return (grad_entry, grad_w_gate, grad_w_up, grad_down)


def per_device(
    hidden_in,
    cotangent,
    layout,
    seq_lengths,
    expert_ids,
    drop_rank,
    norm1_gain,
    w_query,
    key_weight,
    value_weight,
    query_gain,
    key_gain,
    w_out,
    norm2_gain,
    w_router,
    w_gate,
    w_up,
    w_down,
):
    tok_rows = hidden_in.shape[0]
    model_width = hidden_in.shape[1]
    head_dim = query_gain.shape[0]
    local_heads = w_query.shape[1] // head_dim
    expert_count = w_router.shape[1]
    local_count = w_gate.shape[0]
    group_count = lax.axis_size("expert")
    slot_count = 2 * tok_rows * TOPK // expert_count
    seq_count = seq_lengths.shape[0]
    expert_range = jnp.arange(expert_count, dtype=jnp.int32)
    hidden = hidden_in.astype(jnp.float32)
    segment_ids, position = token_tables(layout, seq_lengths)
    valid = segment_ids < seq_count
    first_normalized = norm_rows(hidden, norm1_gain)
    normed1_low = first_normalized.astype(jnp.bfloat16)
    query_lin = jnp.dot(normed1_low, w_query, preferred_element_type=jnp.float32)
    key_lin = jnp.dot(normed1_low, key_weight, preferred_element_type=jnp.float32)
    value_lin = jnp.dot(normed1_low, value_weight, preferred_element_type=jnp.float32)
    query_shaped = shape_queries(query_lin, query_gain, position).astype(jnp.bfloat16)
    query_total = local_heads * tok_rows
    query_rows = jnp.transpose(query_shaped, (1, 0, 2)).reshape(query_total, head_dim)
    key_rows = (
        shape_keys(key_lin, key_gain, position).astype(jnp.bfloat16).reshape(tok_rows, head_dim)
    )
    value_rows = value_lin.astype(jnp.bfloat16)
    all_keys, all_values, all_place, all_ids, all_rank = (
        lax.all_gather(key_rows, "expert", axis=0, tiled=True),
        lax.all_gather(value_rows, "expert", axis=0, tiled=True),
        lax.all_gather(layout, "expert", axis=0, tiled=True),
        lax.all_gather(expert_ids, "expert", axis=0, tiled=True),
        lax.all_gather(drop_rank, "expert", axis=0, tiled=True),
    )
    all_segment = token_tables(all_place, seq_lengths)[0]
    rows_per_block = math.gcd(512, query_total)
    count_of_blocks = query_total // rows_per_block
    query_segment = jnp.tile(segment_ids, local_heads)
    query_place = jnp.tile(layout, local_heads)

    def attend_block(operands):
        query_block, segment_block, place_block = operands
        scores = jnp.einsum("qd,kd->qk", query_block, all_keys, preferred_element_type=jnp.float32)
        scores = jnp.where(visible(segment_block, place_block, all_segment, all_place), scores, NEG)
        highest = jnp.max(scores, axis=1, keepdims=True)
        weights = jnp.exp(scores - highest)
        totals = jnp.sum(weights, axis=1, keepdims=True)
        probability = (weights / totals).astype(jnp.bfloat16)
        mixed_out = jnp.dot(probability, all_values, preferred_element_type=jnp.float32)
        return (mixed_out, (highest + jnp.log(totals))[:, 0])

    attention_output, log_totals = lax.map(
        attend_block,
        (
            query_rows.reshape(count_of_blocks, rows_per_block, head_dim),
            query_segment.reshape(count_of_blocks, rows_per_block),
            query_place.reshape(count_of_blocks, rows_per_block),
        ),
    )
    attention_output = attention_output.reshape(local_heads, tok_rows, head_dim).astype(
        jnp.bfloat16
    )
    att_cat = jnp.transpose(attention_output, (1, 0, 2)).reshape(tok_rows, local_heads * head_dim)
    branch_part = jnp.dot(att_cat, w_out, preferred_element_type=jnp.float32)
    branch = lax.psum(branch_part, "tensor")
    residual = hidden + branch
    normed2 = norm_rows(residual, norm2_gain)
    normed2_low = normed2.astype(jnp.bfloat16)
    logits = jnp.dot(normed2_low, w_router, preferred_element_type=jnp.float32)
    soft_gate = jax.nn.softmax(jnp.take_along_axis(logits, expert_ids, axis=1), axis=1)
    picks = jnp.any(expert_ids[:, :, None] == expert_range, axis=1) & valid[:, None]
    all_valid = all_segment < seq_count
    all_picks = jnp.any(all_ids[:, :, None] == expert_range, axis=1) & all_valid[:, None]
    earlier = (all_rank[None, :] < drop_rank[:, None]).astype(jnp.bfloat16)
    before_counts = jnp.dot(
        earlier, all_picks.astype(jnp.bfloat16), preferred_element_type=jnp.float32
    )
    global_slot = jnp.take_along_axis(before_counts, expert_ids, axis=1).astype(jnp.int32)
    kept_mask = (global_slot < CAP) & valid[:, None]
    gate_weight = soft_gate * kept_mask.astype(jnp.float32)
    lower_rows = (jnp.arange(tok_rows)[None, :] < jnp.arange(tok_rows)[:, None]).astype(
        jnp.bfloat16
    )
    local_counts = jnp.dot(
        lower_rows, picks.astype(jnp.bfloat16), preferred_element_type=jnp.float32
    )
    local_slot = jnp.take_along_axis(local_counts, expert_ids, axis=1).astype(jnp.int32)
    pair_count = tok_rows * TOPK
    dump_index = expert_count * slot_count
    target = jnp.where(kept_mask, expert_ids * slot_count + local_slot, dump_index)
    pair_index = jnp.arange(pair_count, dtype=jnp.int32)
    slot_pair = (
        jnp.full((dump_index,), pair_count, jnp.int32)
        .at[target.reshape(-1)]
        .set(pair_index, mode="drop")
    )
    slot_token = jnp.where(slot_pair < pair_count, slot_pair // TOPK, tok_rows)
    slot_global = (
        jnp.full((dump_index,), -1, jnp.int32)
        .at[target.reshape(-1)]
        .set(global_slot.reshape(-1), mode="drop")
    )
    padded_rows = jnp.concatenate([normed2_low, jnp.zeros((1, model_width), jnp.bfloat16)], axis=0)
    send_rows = padded_rows[slot_token].reshape(group_count, local_count, slot_count, model_width)
    send_slot = slot_global.reshape(group_count, local_count, slot_count)
    received, received_slot = deliver(send_rows, send_slot)
    gate_lin, up_lin, activation, expert_out = expert_forward(received, w_gate, w_up, w_down)
    returned = bring_back(expert_out)
    returned_flat = jnp.concatenate(
        [returned.reshape(dump_index, model_width), jnp.zeros((1, model_width), returned.dtype)],
        axis=0,
    )
    pair_out = returned_flat[target]
    moe_part = jnp.sum(gate_weight[:, :, None] * pair_out, axis=1)
    moe_branch = lax.psum(moe_part.astype(jnp.bfloat16), "tensor").astype(jnp.float32)
    out_hidden = (residual + moe_branch).astype(jnp.bfloat16)
    grad_y = cotangent.astype(jnp.float32)
    gate_dot = jnp.sum(grad_y[:, None, :] * pair_out, axis=2)
    pair_grads = (
        (gate_weight[:, :, None] * grad_y[:, None, :])
        .astype(jnp.bfloat16)
        .reshape(pair_count, model_width)
    )
    pair_grads = jnp.concatenate([pair_grads, jnp.zeros((1, model_width), jnp.bfloat16)], axis=0)
    send_grad = pair_grads[slot_pair].reshape(group_count, local_count, slot_count, model_width)
    grad_received, grad_slot = deliver(send_grad, send_slot)
    grad_entry, grad_w_gate, grad_w_up, grad_w_down = expert_backward(
        received, gate_lin, up_lin, activation, grad_received, w_gate, w_up, w_down
    )
    grad_returned = bring_back(grad_entry)
    grad_flat = jnp.concatenate(
        [
            grad_returned.reshape(dump_index, model_width),
            jnp.zeros((1, model_width), grad_returned.dtype),
        ],
        axis=0,
    )
    grad_normed2_part = jnp.sum(grad_flat[target], axis=1, dtype=jnp.float32)
    grad_normed2_exp, gate_dot = lax.psum((grad_normed2_part, gate_dot), "tensor")
    grad_soft = gate_dot * kept_mask.astype(jnp.float32)
    grad_chosen = soft_gate * (grad_soft - jnp.sum(soft_gate * grad_soft, axis=1, keepdims=True))
    grad_logits = jnp.sum(
        grad_chosen[:, :, None] * (expert_ids[:, :, None] == expert_range).astype(jnp.float32),
        axis=1,
    ).astype(jnp.bfloat16)
    grad_w_router = jnp.einsum(
        "td,te->de", normed2_low, grad_logits, preferred_element_type=jnp.float32
    )
    grad_normed2 = grad_normed2_exp + jnp.einsum(
        "te,de->td", grad_logits, w_router, preferred_element_type=jnp.float32
    )
    norm2_pull = jax.vjp(norm_rows, residual, norm2_gain)[1]
    grad_resid_norm, grad_norm2 = norm2_pull(grad_normed2)
    grad_residual = grad_y + grad_resid_norm
    grad_residual_low = grad_residual.astype(jnp.bfloat16)
    grad_w_out = jnp.einsum(
        "tc,td->cd", att_cat, grad_residual_low, preferred_element_type=jnp.float32
    )
    grad_att_cat = jnp.einsum(
        "td,cd->tc", grad_residual_low, w_out, preferred_element_type=jnp.float32
    ).astype(jnp.bfloat16)
    grad_att_rows = jnp.transpose(
        grad_att_cat.reshape(tok_rows, local_heads, head_dim), (1, 0, 2)
    ).reshape(query_total, head_dim)

    def query_grad_block(operands):
        query_block, segment_block, place_block, grad_block, log_block = operands
        scores = jnp.einsum("qd,kd->qk", query_block, all_keys, preferred_element_type=jnp.float32)
        scores = jnp.where(visible(segment_block, place_block, all_segment, all_place), scores, NEG)
        probability = jnp.exp(scores - log_block[:, None])
        grad_prob = jnp.einsum(
            "qd,kd->qk", grad_block, all_values, preferred_element_type=jnp.float32
        )
        delta_row = jnp.sum(probability * grad_prob, axis=1)
        grad_scores = (probability * (grad_prob - delta_row[:, None])).astype(jnp.bfloat16)
        return (jnp.dot(grad_scores, all_keys, preferred_element_type=jnp.float32), delta_row)

    grad_query_rows, deltas = lax.map(
        query_grad_block,
        (
            query_rows.reshape(count_of_blocks, rows_per_block, head_dim),
            query_segment.reshape(count_of_blocks, rows_per_block),
            query_place.reshape(count_of_blocks, rows_per_block),
            grad_att_rows.reshape(count_of_blocks, rows_per_block, head_dim),
            log_totals,
        ),
    )
    log_flat = log_totals.reshape(query_total)
    delta_flat = deltas.reshape(query_total)
    key_block = math.gcd(lax.axis_size("expert") * tok_rows, 2048)

    def one_block(offset):
        key_part = lax.dynamic_slice_in_dim(all_keys, offset, key_block, 0)
        value_part = lax.dynamic_slice_in_dim(all_values, offset, key_block, 0)
        segment_part = lax.dynamic_slice_in_dim(all_segment, offset, key_block, 0)
        place_part = lax.dynamic_slice_in_dim(all_place, offset, key_block, 0)
        scores = jnp.einsum("qd,kd->qk", query_rows, key_part, preferred_element_type=jnp.float32)
        scores = jnp.where(
            visible(query_segment, query_place, segment_part, place_part), scores, NEG
        )
        probability = jnp.exp(scores - log_flat[:, None])
        grad_value = jnp.einsum(
            "qk,qd->kd",
            probability.astype(jnp.bfloat16),
            grad_att_rows,
            preferred_element_type=jnp.float32,
        )
        grad_prob = jnp.einsum(
            "qd,kd->qk", grad_att_rows, value_part, preferred_element_type=jnp.float32
        )
        grad_scores = (probability * (grad_prob - delta_flat[:, None])).astype(jnp.bfloat16)
        grad_key = jnp.einsum(
            "qk,qd->kd", grad_scores, query_rows, preferred_element_type=jnp.float32
        )
        return jnp.concatenate([grad_key, grad_value], axis=1)

    stacked = lax.map(
        one_block,
        jnp.arange(lax.axis_size("expert") * tok_rows // key_block, dtype=jnp.int32) * key_block,
    )
    key_value_grad = lax.psum_scatter(
        stacked.reshape(lax.axis_size("expert") * tok_rows, 2 * head_dim).astype(jnp.bfloat16),
        "expert",
        scatter_dimension=0,
        tiled=True,
    ).astype(jnp.float32)
    grad_key_post = key_value_grad[:, :head_dim].reshape(tok_rows, 1, head_dim)
    grad_values_low = key_value_grad[:, head_dim:].astype(jnp.bfloat16)
    grad_query_tok = jnp.transpose(
        grad_query_rows.reshape(local_heads, tok_rows, head_dim), (1, 0, 2)
    )
    query_pull = jax.vjp(partial(shape_queries, position=position), query_lin, query_gain)[1]
    grad_query_lin, grad_qgain_part = query_pull(grad_query_tok)
    key_pull = jax.vjp(partial(shape_keys, position=position), key_lin, key_gain)[1]
    grad_key_lin, grad_kgain_part = key_pull(grad_key_post)
    grad_query_low = grad_query_lin.astype(jnp.bfloat16)
    grad_key_low = grad_key_lin.astype(jnp.bfloat16)
    grad_w_query = jnp.einsum(
        "td,tc->dc", normed1_low, grad_query_low, preferred_element_type=jnp.float32
    )
    grad_w_key = jnp.einsum(
        "td,tc->dc", normed1_low, grad_key_low, preferred_element_type=jnp.float32
    )
    grad_w_value = jnp.einsum(
        "td,tc->dc", normed1_low, grad_values_low, preferred_element_type=jnp.float32
    )
    grad_normed1_part = jnp.einsum(
        "tc,dc->td", grad_query_low, w_query, preferred_element_type=jnp.float32
    )
    grad_normed1_part = grad_normed1_part + jnp.einsum(
        "tc,dc->td", grad_key_low, key_weight, preferred_element_type=jnp.float32
    )
    grad_normed1_part = grad_normed1_part + jnp.einsum(
        "tc,dc->td", grad_values_low, value_weight, preferred_element_type=jnp.float32
    )
    grad_normed1, grad_qgain_part, grad_kgain_part = (
        lax.psum(grad_normed1_part.astype(jnp.bfloat16), "tensor").astype(jnp.float32),
        lax.psum(grad_qgain_part.astype(jnp.bfloat16), "tensor").astype(jnp.float32),
        lax.psum(grad_kgain_part.astype(jnp.bfloat16), "tensor").astype(jnp.float32),
    )
    norm1_pull = jax.vjp(norm_rows, hidden, norm1_gain)[1]
    grad_hidden_norm, grad_norm1 = norm1_pull(grad_normed1)
    grad_hidden = (grad_residual + grad_hidden_norm).astype(jnp.bfloat16)
    summed = (
        lax.psum(grad_norm1.astype(jnp.bfloat16), "expert").astype(jnp.float32),
        lax.psum(grad_w_query.astype(jnp.bfloat16), "expert").astype(jnp.float32),
        lax.psum(grad_w_key.astype(jnp.bfloat16), "expert").astype(jnp.float32),
        lax.psum(grad_w_value.astype(jnp.bfloat16), "expert").astype(jnp.float32),
        lax.psum(grad_qgain_part.astype(jnp.bfloat16), "expert").astype(jnp.float32),
        lax.psum(grad_kgain_part.astype(jnp.bfloat16), "expert").astype(jnp.float32),
        lax.psum(grad_w_out.astype(jnp.bfloat16), "expert").astype(jnp.float32),
        lax.psum(grad_norm2.astype(jnp.bfloat16), "expert").astype(jnp.float32),
        lax.psum(grad_w_router.astype(jnp.bfloat16), "expert").astype(jnp.float32),
    )
    return (
        out_hidden,
        grad_hidden,
        summed[0],
        summed[1],
        summed[2],
        summed[3],
        summed[4],
        summed[5],
        summed[6],
        summed[7],
        summed[8],
        grad_w_gate,
        grad_w_up,
        grad_w_down,
    )


def all_tokens(layout, expert_ids, drop_rank):
    packed = jnp.concatenate([layout[None], drop_rank[None], expert_ids.T], axis=0)
    gathered = lax.all_gather(packed, "expert", axis=1, tiled=True)
    return gathered[0], gathered[1], gathered[2:]


BOTH = ("expert", "tensor")


MESH = pl.DeviceIdType.MESH
FAR_FIRST = (3, -3, 2, -2, 1, -1, 0)


class Spot:
    def __init__(self):
        group, part = lax.axis_index("expert"), lax.axis_index("tensor")
        self.z, self.y = group // 2, group % 2
        self.x, self.c = part // 2, part % 2

    def has(self, dz):
        return (self.z + dz >= 0) & (self.z + dz <= 3)

    def device(self, dz=0, dy=0, dx=0, dc=0):
        y = 1 - self.y if dy else self.y
        x = 1 - self.x if dx else self.x
        c = 1 - self.c if dc else self.c
        return ((self.z + dz) * 2 + y, x * 2 + c)

    def rows(self, dz, dy, dx, dc, count):
        group, part = self.device(dz, dy, dx, dc)
        return pl.ds(pl.multiple_of((group * 4 + part) * count, count), count)

    def greet(self):
        barrier = pltpu.get_barrier_semaphore()
        for step in ((0, 1, 0, 0), (0, 0, 1, 0), (0, 0, 0, 1)):
            pl.semaphore_signal(barrier, inc=1, device_id=self.device(*step), device_id_type=MESH)
        for dz in (1, -1):

            @pl.when(self.has(dz))
            def _(dz=dz):
                pl.semaphore_signal(
                    barrier, inc=1, device_id=self.device(dz), device_id_type=MESH
                )

        inner = jnp.where((self.z > 0) & (self.z < 3), 1, 0)
        pl.semaphore_wait(barrier, 4 + inner)


def when_has(spot, dz, action):
    if dz == 0:
        action()
    else:
        pl.when(spot.has(dz))(action)


def gather_kernel(src, out, recv, z_send, y_send, x_send, c_send, c_recv, local_sem):
    count, width = src.shape
    half = width // 2
    first, second, whole = pl.ds(0, half), pl.ds(half, half), pl.ds(0, width)
    spot = Spot()
    local = pltpu.make_async_copy(src, out.at[spot.rows(0, 0, 0, 0, count), :], local_sem)
    local.start()
    spot.greet()

    def send(dz, dy, dx, columns, send_sem, recv_sem, device):
        place = out.at[spot.rows(dz, dy, dx, 0, count), columns]
        own = dz == 0 and dy == 0 and dx == 0
        copy = pltpu.make_async_remote_copy(
            src_ref=src.at[:, columns] if own else place,
            dst_ref=place,
            send_sem=send_sem,
            recv_sem=recv_sem,
            device_id=device,
            device_id_type=MESH,
        )
        copy.start()

    def await_bytes(rows, columns, sem):
        view = out.at[pl.ds(0, rows), columns]
        pltpu.make_async_copy(view, view, sem).wait()

    to_y, to_x, to_c = spot.device(0, 1), spot.device(0, 0, 1), spot.device(0, 0, 0, 1)

    def spread(dz):
        if dz <= 0:

            @pl.when(spot.has(1))
            def _():
                send(dz, 0, 0, whole, z_send.at[dz + 3, 0], recv.at[0, dz + 2], spot.device(1))

        if dz >= 0:

            @pl.when(spot.has(-1))
            def _():
                send(dz, 0, 0, whole, z_send.at[dz + 3, 1], recv.at[0, dz + 4], spot.device(-1))

        send(dz, 0, 0, whole, y_send, recv.at[1, dz + 3], to_y)
        send(dz, 0, 0, whole, x_send, recv.at[2, dz + 3], to_x)
        send(dz, 0, 0, whole, c_send, c_recv, to_c)

    def take_z(dz):
        def action():
            await_bytes(count, whole, recv.at[0, dz + 3])
            spread(dz)

        when_has(spot, dz, action)

    def take_yx(dz):
        def action():
            await_bytes(count, whole, recv.at[1, dz + 3])
            send(dz, 1, 0, first, x_send, recv.at[3, dz + 3], to_x)
            send(dz, 1, 0, whole, c_send, c_recv, to_c)
            await_bytes(count, whole, recv.at[2, dz + 3])
            send(dz, 0, 1, second, y_send, recv.at[4, dz + 3], to_y)
            send(dz, 0, 1, whole, c_send, c_recv, to_c)

        when_has(spot, dz, action)

    def take_diagonal(dz):
        def action():
            await_bytes(count, first, recv.at[3, dz + 3])
            await_bytes(count, second, recv.at[4, dz + 3])
            send(dz, 1, 1, whole, c_send, c_recv, to_c)

        when_has(spot, dz, action)

    spread(0)
    for dz in (1, -1):
        take_z(dz)
    take_yx(0)
    for dz in (2, -2):
        take_z(dz)
    for dz in (1, -1):
        take_yx(dz)
    take_diagonal(0)
    for dz in (3, -3):
        take_z(dz)
    for dz in (2, -2):
        take_yx(dz)
    for dz in (1, -1):
        take_diagonal(dz)
    for dz in (3, -3):
        take_yx(dz)
    for dz in (2, -2, 3, -3):
        take_diagonal(dz)

    await_bytes(16 * count, whole, c_recv)
    await_bytes(16 * count, whole, c_send)
    await_bytes(6 * count, whole, y_send)
    await_bytes(6 * count, whole, x_send)
    for dz in range(-3, 4):
        for side, step in ((0, 1), (1, -1)):
            if dz * step <= 0:

                @pl.when(spot.has(dz) & spot.has(step))
                def _(dz=dz, side=side):
                    await_bytes(count, whole, z_send.at[dz + 3, side])

    local.wait()


def gather_rows(rows):
    count, width = rows.shape
    dma = pltpu.SemaphoreType.DMA
    return pl.pallas_call(
        gather_kernel,
        out_shape=jax.ShapeDtypeStruct((32 * count, width), rows.dtype),
        in_specs=[pl.BlockSpec(memory_space=pl.ANY)],
        out_specs=pl.BlockSpec(memory_space=pl.ANY),
        scratch_shapes=[dma((5, 7)), dma((7, 2)), dma, dma, dma, dma, dma],
        compiler_params=pltpu.CompilerParams(collective_id=0, has_side_effects=True),
        name="gather_rows",
    )(rows)


def scatter_kernel(
    part, out, held, from_a, from_b, from_y, from_x, from_below, from_above,
    c_recv, recv, z_send, y_send, x_send, c_send,
):
    count, width = out.shape
    half = 1024
    first, second, whole = pl.ds(0, half), pl.ds(half, width - half), pl.ds(0, width)
    spot = Spot()
    spot.greet()
    to_y, to_x, to_c = spot.device(0, 1), spot.device(0, 0, 1), spot.device(0, 0, 0, 1)

    def send(src, dst, send_sem, recv_sem, device):
        pltpu.make_async_remote_copy(
            src_ref=src, dst_ref=dst, send_sem=send_sem, recv_sem=recv_sem,
            device_id=device, device_id_type=MESH,
        ).start()

    def arrive(view, sem):
        pltpu.make_async_copy(view, view, sem).wait()

    def add(into, *terms):
        @pl.loop(0, count // 16)
        def _(step):
            rows = pl.ds(pl.multiple_of(step * 16, 16), 16)
            total = into[rows, :].astype(jnp.float32)
            for term in terms:
                total = total + term[rows, :].astype(jnp.float32)
            into[rows, :] = total.astype(into.dtype)

    groups = ((1, 1), (1, 0), (0, 1), (0, 0))
    for dy, dx in groups:
        for dz in FAR_FIRST:

            def action(dz=dz, dy=dy, dx=dx):
                send(
                    part.at[spot.rows(dz, dy, dx, 1, count), :],
                    held.at[spot.z + dz, dy, dx],
                    c_send, c_recv.at[dz + 3, dy, dx], to_c,
                )

            when_has(spot, dz, action)

    def merge(dz, dy, dx, *terms):
        mine = held.at[spot.z + dz, dy, dx]
        arrive(mine, c_recv.at[dz + 3, dy, dx])
        add(mine, part.at[spot.rows(dz, dy, dx, 0, count), :])
        return mine

    for dz in FAR_FIRST:

        def action(dz=dz):
            far = spot.z + dz
            mine = merge(dz, 1, 1)
            send(mine.at[:, first], from_a.at[far], x_send, recv.at[0, dz + 3], to_x)
            send(mine.at[:, second], from_b.at[far], y_send, recv.at[1, dz + 3], to_y)

        when_has(spot, dz, action)
    for dz in FAR_FIRST:

        def action(dz=dz):
            far = spot.z + dz
            mine = merge(dz, 1, 0)
            arrive(from_a.at[far], recv.at[0, dz + 3])
            add(mine.at[:, first], from_a.at[far])
            send(mine, from_y.at[far], y_send, recv.at[2, dz + 3], to_y)
            mine = merge(dz, 0, 1)
            arrive(from_b.at[far], recv.at[1, dz + 3])
            add(mine.at[:, second], from_b.at[far])
            send(mine, from_x.at[far], x_send, recv.at[3, dz + 3], to_x)

        when_has(spot, dz, action)
    for dz in FAR_FIRST:

        def action(dz=dz):
            far = spot.z + dz
            mine = merge(dz, 0, 0)
            arrive(from_y.at[far], recv.at[2, dz + 3])
            arrive(from_x.at[far], recv.at[3, dz + 3])
            add(mine, from_y.at[far], from_x.at[far])
            if dz >= 0:

                @pl.when(spot.has(-1))
                def _():
                    arrive(from_below.at[far], recv.at[4, dz + 3])
                    add(mine, from_below.at[far])

            if dz <= 0:

                @pl.when(spot.has(1))
                def _():
                    arrive(from_above.at[far], recv.at[5, dz + 3])
                    add(mine, from_above.at[far])

            if dz > 0:
                send(mine, from_below.at[far], z_send.at[dz + 3], recv.at[4, dz + 2],
                     spot.device(1))
            if dz < 0:
                send(mine, from_above.at[far], z_send.at[dz + 3], recv.at[5, dz + 4],
                     spot.device(-1))
            if dz == 0:
                out[...] = mine[...].astype(out.dtype)

        when_has(spot, dz, action)

    def await_rows(rows, sem):
        view = part.at[pl.ds(0, rows), :]
        pltpu.make_async_copy(view, view, sem).wait()

    await_rows(16 * count, c_send)
    for columns, other, sem in ((second, first, y_send), (first, second, x_send)):
        view = part.at[pl.ds(0, 4 * count), columns]
        whole_view = part.at[pl.ds(0, 4 * count), :]
        pltpu.make_async_copy(view, view, sem).wait()
        pltpu.make_async_copy(whole_view, whole_view, sem).wait()
    for dz in FAR_FIRST[:-1]:

        def action(dz=dz):
            await_rows(count, z_send.at[dz + 3])

        when_has(spot, dz, action)


def scatter_rows(partial_rows, ident):
    total, width = partial_rows.shape
    count = total // 32
    dma, bf16 = pltpu.SemaphoreType.DMA, jnp.bfloat16
    line = pltpu.VMEM((4, count, width), bf16)
    return pl.pallas_call(
        scatter_kernel,
        out_shape=jax.ShapeDtypeStruct((count, width), jnp.float32),
        in_specs=[pl.BlockSpec(memory_space=pltpu.VMEM)],
        out_specs=pl.BlockSpec(memory_space=pltpu.VMEM),
        scratch_shapes=[
            pltpu.VMEM((4, 2, 2, count, width), bf16),
            pltpu.VMEM((4, count, 1024), bf16),
            pltpu.VMEM((4, count, width - 1024), bf16),
            line, line, line, line,
            dma((7, 2, 2)), dma((6, 7)), dma((7,)), dma, dma, dma,
        ],
        compiler_params=pltpu.CompilerParams(
            collective_id=ident, has_side_effects=True, vmem_limit_bytes=40 << 20
        ),
        name="scatter_rows",
    )(partial_rows)


def head_device(
    hidden_in,
    cotangent,
    layout,
    seq_lengths,
    expert_ids,
    drop_rank,
    norm1_gain,
    w_query,
    key_weight,
    value_weight,
    query_gain,
    key_gain,
    w_out,
    norm2_gain,
    w_router,
    w_gate,
    w_up,
    w_down,
):
    f32, bf16 = jnp.float32, jnp.bfloat16
    tok_rows, model_width = hidden_in.shape
    head_dim = query_gain.shape[0]
    expert_count = w_router.shape[1]
    local_count, _, ff_local = w_gate.shape
    groups = lax.axis_size("expert")
    tensor_size = lax.axis_size("tensor")
    total_rows = groups * tok_rows
    own_rows = tok_rows // tensor_size
    seq_count = seq_lengths.shape[0]
    group = lax.axis_index("expert")
    part = lax.axis_index("tensor")

    def own(rows):
        return lax.dynamic_slice_in_dim(rows, part * own_rows, own_rows, 0)

    place, rank, ids_t = all_tokens(layout, expert_ids, drop_rank)
    segment, position = token_tables(place, seq_lengths)
    valid = segment < seq_count
    hidden_all = gather_rows(own(hidden_in))
    grad_y_all = gather_rows(own(cotangent))

    head_query = lax.dynamic_slice_in_dim(w_query, group * head_dim, head_dim, 1)
    head_out = lax.dynamic_slice_in_dim(w_out, group * head_dim, head_dim, 0)
    qkv_weight = jnp.concatenate([head_query, key_weight, value_weight], axis=1)
    normed1 = norm_rows(hidden_all.astype(f32), norm1_gain).astype(bf16)
    lin = jnp.dot(normed1, qkv_weight, preferred_element_type=f32)
    query_lin, key_lin = lin[:, :head_dim], lin[:, head_dim : 2 * head_dim]
    values = lin[:, 2 * head_dim :].astype(bf16)
    queries, query_pull = jax.vjp(
        lambda v, g: shape_queries(v, g, position)[:, 0], query_lin, query_gain
    )
    keys, key_pull = jax.vjp(lambda v, g: shape_keys(v, g, position)[:, 0], key_lin, key_gain)
    queries, keys = queries.astype(bf16), keys.astype(bf16)
    allowed = visible(segment, place, segment, place)
    scores = jnp.einsum("qd,kd->qk", queries, keys, preferred_element_type=f32)
    scores = jnp.where(allowed, scores, NEG)
    probability = jax.nn.softmax(scores, axis=1)
    attended = jnp.dot(probability.astype(bf16), values, preferred_element_type=f32).astype(bf16)
    att_rows = lax.all_to_all(attended, "expert", split_axis=0, concat_axis=0, tiled=True)
    att_rows = jnp.transpose(att_rows.reshape(groups, tok_rows, head_dim), (1, 0, 2)).reshape(
        tok_rows, groups * head_dim
    )
    branch_part = jnp.dot(att_rows, w_out, preferred_element_type=f32)
    branch = lax.psum_scatter(
        branch_part.astype(bf16), "tensor", scatter_dimension=0, tiled=True
    ).astype(f32)
    residual = own(hidden_in).astype(f32) + branch
    normed2, norm2_pull = jax.vjp(norm_rows, residual, norm2_gain)
    normed2 = normed2.astype(bf16)
    normed2_all = gather_rows(normed2)

    expert_range = jnp.arange(expert_count, dtype=jnp.int32)
    chosen = jnp.any(ids_t[:, :, None] == expert_range, axis=0)
    picks = (chosen & valid[:, None]).astype(bf16)
    earlier = (rank[None, :] < rank[:, None]).astype(bf16)
    slot = jnp.dot(earlier, picks, preferred_element_type=f32)
    kept = chosen & valid[:, None] & (slot < CAP)

    def gates(rows, picked):
        logits = jnp.dot(rows, w_router, preferred_element_type=f32)
        return jax.nn.softmax(jnp.where(picked, logits, -jnp.inf), axis=1)

    gate_weight = jnp.where(kept, gates(normed2_all, chosen), 0.0)
    gate_local = lax.dynamic_slice_in_dim(gate_weight, group * local_count, local_count, 1)
    kept_local = lax.dynamic_slice_in_dim(kept, group * local_count, local_count, 1)

    weight_in = jnp.concatenate([w_gate, w_up], axis=0)
    weight_in = jnp.transpose(weight_in, (1, 0, 2)).reshape(model_width, -1)
    weight_down = w_down.reshape(local_count * ff_local, model_width)
    wide = local_count * ff_local
    lin2 = jnp.dot(normed2_all, weight_in, preferred_element_type=f32)
    gate_lin, up_lin = lin2[:, :wide], lin2[:, wide:]
    sigmoid = jax.nn.sigmoid(gate_lin)
    silu = gate_lin * sigmoid
    spread = jnp.repeat(gate_local, ff_local, axis=1)
    activation = (silu * up_lin).astype(bf16).astype(f32)
    weighted = (activation * spread).astype(bf16)
    out_part = jnp.dot(weighted, weight_down, preferred_element_type=f32)
    grad_down = jnp.einsum("rf,rd->fd", weighted, grad_y_all, preferred_element_type=f32)
    grad_mid = jnp.einsum("rd,fd->rf", grad_y_all, weight_down, preferred_element_type=f32)
    dots = jnp.sum((activation * grad_mid).reshape(total_rows, local_count, ff_local), axis=2)
    dots = jnp.where(kept_local, dots, 0.0)
    grad_act = grad_mid * spread
    grad_gate_lin = (grad_act * up_lin * sigmoid * (1.0 + gate_lin * (1.0 - sigmoid))).astype(bf16)
    grad_up_lin = (grad_act * silu).astype(bf16)
    grad_lin2 = jnp.concatenate([grad_gate_lin, grad_up_lin], axis=1)
    grad_in = jnp.einsum("rd,rf->df", normed2_all, grad_lin2, preferred_element_type=f32)
    grad_in = jnp.transpose(
        grad_in.reshape(model_width, 2 * local_count, ff_local), (1, 0, 2)
    )
    grad_normed2_part = jnp.einsum(
        "rf,df->rd", grad_lin2, weight_in, preferred_element_type=f32
    )
    dots_wide = jnp.zeros((total_rows, head_dim), f32)
    dots_wide = lax.dynamic_update_slice(dots_wide, dots, (0, group * local_count))
    back = scatter_rows(
        jnp.concatenate([grad_normed2_part, dots_wide], axis=1).astype(bf16),
        1,
    )
    moe_branch = scatter_rows(out_part.astype(bf16), 2)
    out_own = (residual + moe_branch).astype(bf16)

    start = group * tok_rows + part * own_rows
    chosen_own = lax.dynamic_slice_in_dim(chosen, start, own_rows, 0)
    soft_own = gates(normed2, chosen_own)
    grad_soft = back[:, model_width : model_width + expert_count]
    grad_logits = (
        soft_own * (grad_soft - jnp.sum(soft_own * grad_soft, axis=1, keepdims=True))
    ).astype(bf16)
    grad_router = jnp.einsum("td,te->de", normed2, grad_logits, preferred_element_type=f32)
    grad_normed2 = back[:, :model_width] + jnp.einsum(
        "te,de->td", grad_logits, w_router, preferred_element_type=f32
    )
    grad_resid_norm, grad_norm2 = norm2_pull(grad_normed2)
    grad_residual = own(cotangent).astype(f32) + grad_resid_norm
    grad_residual_all = gather_rows(grad_residual.astype(bf16))

    grad_out = jnp.einsum("rc,rd->cd", attended, grad_residual_all, preferred_element_type=f32)
    grad_att = jnp.einsum(
        "rd,cd->rc", grad_residual_all, head_out, preferred_element_type=f32
    ).astype(bf16)
    grad_prob = jnp.einsum("qd,kd->qk", grad_att, values, preferred_element_type=f32)
    delta = jnp.sum(probability * grad_prob, axis=1, keepdims=True)
    grad_scores = (probability * (grad_prob - delta)).astype(bf16)
    grad_queries = jnp.dot(grad_scores, keys, preferred_element_type=f32)
    grad_keys = jnp.einsum("qk,qd->kd", grad_scores, queries, preferred_element_type=f32)
    grad_values = jnp.einsum(
        "qk,qd->kd", probability.astype(bf16), grad_att, preferred_element_type=f32
    )
    grad_query_lin, grad_qgain = query_pull(grad_queries)
    grad_key_lin, grad_kgain = key_pull(grad_keys)
    grad_lin = jnp.concatenate([grad_query_lin, grad_key_lin, grad_values], axis=1).astype(bf16)
    grad_qkv = jnp.einsum("td,tc->dc", normed1, grad_lin, preferred_element_type=f32)
    grad_normed1_part = jnp.einsum(
        "tc,dc->td", grad_lin, qkv_weight, preferred_element_type=f32
    )
    grad_normed1 = scatter_rows(grad_normed1_part.astype(bf16), 2)
    norm1_pull = jax.vjp(norm_rows, own(hidden_in).astype(f32), norm1_gain)[1]
    grad_hidden_norm, grad_norm1 = norm1_pull(grad_normed1)
    grad_hidden_own = (grad_residual + grad_hidden_norm).astype(bf16)
    ends = lax.all_gather(
        jnp.concatenate([out_own, grad_hidden_own], axis=1), "tensor", axis=0, tiled=True
    )
    grad_query = lax.all_gather(
        grad_qkv[:, :head_dim].astype(bf16), "expert", axis=1, tiled=True
    ).astype(f32)
    grad_out = lax.all_gather(grad_out.astype(bf16), "expert", axis=0, tiled=True).astype(f32)
    grad_kv = lax.psum(grad_qkv[:, head_dim:].astype(bf16), "expert").astype(f32)
    grad_norm1, grad_norm2, grad_qgain, grad_kgain, grad_router = lax.psum(
        (grad_norm1, grad_norm2, grad_qgain, grad_kgain, grad_router), BOTH
    )
    grad_down = grad_down.reshape(local_count, ff_local, model_width)
    return (
        ends[:, :model_width],
        ends[:, model_width:],
        grad_norm1,
        grad_query,
        grad_kv[:, :head_dim],
        grad_kv[:, head_dim:],
        grad_qgain,
        grad_kgain,
        grad_out,
        grad_norm2,
        grad_router,
        grad_in[:local_count],
        grad_in[local_count:],
        grad_down,
    )


def solution(mesh):
    groups = mesh.shape["expert"]

    def device_fn(*operands):
        heads = operands[7].shape[1] // operands[10].shape[0]
        one_head = heads == groups == 8 and operands[8].shape[1] == operands[10].shape[0]
        one_head = one_head and mesh.shape["tensor"] == 4
        return (head_device if one_head else per_device)(*operands)

    return jax.shard_map(
        device_fn,
        mesh=mesh,
        in_specs=(
            P("expert", None),
            P("expert", None),
            P("expert"),
            P(),
            P("expert", None),
            P("expert"),
            P(),
            P(None, "tensor"),
            P(None, "tensor"),
            P(None, "tensor"),
            P(),
            P(),
            P("tensor", None),
            P(),
            P(),
            P("expert", None, "tensor"),
            P("expert", None, "tensor"),
            P("expert", "tensor", None),
        ),
        out_specs=(
            P("expert", None),
            P("expert", None),
            P(),
            P(None, "tensor"),
            P(None, "tensor"),
            P(None, "tensor"),
            P(),
            P(),
            P("tensor", None),
            P(),
            P(),
            P("expert", None, "tensor"),
            P("expert", None, "tensor"),
            P("expert", "tensor", None),
        ),
        check_vma=False,
    )
```

```python
from functools import partial
import math

import jax
import jax.numpy as jnp
from jax import lax
from jax.experimental import pallas as pl
from jax.experimental.pallas import tpu as pltpu
from jax.sharding import PartitionSpec as P

TOPK = 8
CAP = 1280


EPS = 1e-06
THETA = 1000000.0
NEG = -1e30


def norm_rows(value_matrix, gain):
    return (
        value_matrix
        * lax.rsqrt(jnp.mean(value_matrix * value_matrix, axis=-1, keepdims=True) + EPS)
        * gain
    )


def rotary(value_matrix, position):
    half_dim = value_matrix.shape[-1] // 2
    inverse = THETA ** (-(jnp.arange(half_dim, dtype=jnp.float32) * 2.0) / value_matrix.shape[-1])
    angles = position.astype(jnp.float32)[:, None] * inverse[None, :]
    cosine_table = jnp.concatenate([jnp.cos(angles), jnp.cos(angles)], axis=-1)[:, None, :]
    sine_table = jnp.concatenate([jnp.sin(angles), jnp.sin(angles)], axis=-1)[:, None, :]
    turned = jnp.concatenate([-value_matrix[..., half_dim:], value_matrix[..., :half_dim]], axis=-1)
    return value_matrix * cosine_table + turned * sine_table


def shape_queries(linear, gain, position):
    head_dim = gain.shape[0]
    shaped = linear.reshape(linear.shape[0], linear.shape[1] // head_dim, head_dim)
    return rotary(norm_rows(shaped, gain), position) * head_dim ** (-0.5)


def shape_keys(linear, gain, position):
    head_dim = gain.shape[0]
    shaped = linear.reshape(linear.shape[0], linear.shape[1] // head_dim, head_dim)
    return rotary(norm_rows(shaped, gain), position)


def token_tables(token_position, seq_lengths):
    bounds = jnp.cumsum(seq_lengths)
    passed = token_position[:, None] >= bounds[None, :]
    segment_ids = jnp.sum(passed.astype(jnp.int32), axis=1)
    opening = jnp.max(jnp.where(passed, bounds[None, :], 0), axis=1)
    return (segment_ids, (token_position - opening).astype(jnp.int32))


def visible(query_segment, query_place, key_segment, key_place):
    return (query_segment[:, None] == key_segment[None, :]) & (
        key_place[None, :] <= query_place[:, None]
    )


def deliver(payload, slot_ids):
    return (
        lax.all_to_all(payload, "expert", split_axis=0, concat_axis=0, tiled=True),
        lax.all_to_all(slot_ids, "expert", split_axis=0, concat_axis=0, tiled=True),
    )


def bring_back(payload):
    return lax.all_to_all(payload, "expert", split_axis=0, concat_axis=0, tiled=True)


def expert_forward(entry_rows, w_gate, w_up, w_down):
    gate_lin = jnp.einsum("gesd,edf->gesf", entry_rows, w_gate, preferred_element_type=jnp.float32)
    up_lin = jnp.einsum("gesd,edf->gesf", entry_rows, w_up, preferred_element_type=jnp.float32)
    activation = (jax.nn.silu(gate_lin) * up_lin).astype(jnp.bfloat16)
    expert_out = jnp.einsum(
        "gesf,efd->gesd", activation, w_down, preferred_element_type=jnp.float32
    ).astype(jnp.bfloat16)
    return (gate_lin, up_lin, activation, expert_out)


def expert_backward(entry_rows, gate_lin, up_lin, activation, grad_in, w_gate, w_up, w_down):
    grad_down = jnp.einsum(
        "gesf,gesd->efd", activation, grad_in, preferred_element_type=jnp.float32
    )
    grad_act = jnp.einsum("gesd,efd->gesf", grad_in, w_down, preferred_element_type=jnp.float32)
    sigmoid = jax.nn.sigmoid(gate_lin)
    grad_gate_lin = (grad_act * up_lin * sigmoid * (1.0 + gate_lin * (1.0 - sigmoid))).astype(
        jnp.bfloat16
    )
    grad_up_lin = (grad_act * gate_lin * sigmoid).astype(jnp.bfloat16)
    grad_w_gate = jnp.einsum(
        "gesd,gesf->edf", entry_rows, grad_gate_lin, preferred_element_type=jnp.float32
    )
    grad_w_up = jnp.einsum(
        "gesd,gesf->edf", entry_rows, grad_up_lin, preferred_element_type=jnp.float32
    )
    grad_entry = jnp.einsum(
        "gesf,edf->gesd", grad_gate_lin, w_gate, preferred_element_type=jnp.float32
    )
    grad_entry = (
        grad_entry
        + jnp.einsum("gesf,edf->gesd", grad_up_lin, w_up, preferred_element_type=jnp.float32)
    ).astype(jnp.bfloat16)
    return (grad_entry, grad_w_gate, grad_w_up, grad_down)


def per_device(
    hidden_in,
    cotangent,
    layout,
    seq_lengths,
    expert_ids,
    drop_rank,
    norm1_gain,
    w_query,
    key_weight,
    value_weight,
    query_gain,
    key_gain,
    w_out,
    norm2_gain,
    w_router,
    w_gate,
    w_up,
    w_down,
):
    tok_rows = hidden_in.shape[0]
    model_width = hidden_in.shape[1]
    head_dim = query_gain.shape[0]
    local_heads = w_query.shape[1] // head_dim
    expert_count = w_router.shape[1]
    local_count = w_gate.shape[0]
    group_count = lax.axis_size("expert")
    slot_count = 2 * tok_rows * TOPK // expert_count
    seq_count = seq_lengths.shape[0]
    expert_range = jnp.arange(expert_count, dtype=jnp.int32)
    hidden = hidden_in.astype(jnp.float32)
    segment_ids, position = token_tables(layout, seq_lengths)
    valid = segment_ids < seq_count
    first_normalized = norm_rows(hidden, norm1_gain)
    normed1_low = first_normalized.astype(jnp.bfloat16)
    query_lin = jnp.dot(normed1_low, w_query, preferred_element_type=jnp.float32)
    key_lin = jnp.dot(normed1_low, key_weight, preferred_element_type=jnp.float32)
    value_lin = jnp.dot(normed1_low, value_weight, preferred_element_type=jnp.float32)
    query_shaped = shape_queries(query_lin, query_gain, position).astype(jnp.bfloat16)
    query_total = local_heads * tok_rows
    query_rows = jnp.transpose(query_shaped, (1, 0, 2)).reshape(query_total, head_dim)
    key_rows = (
        shape_keys(key_lin, key_gain, position).astype(jnp.bfloat16).reshape(tok_rows, head_dim)
    )
    value_rows = value_lin.astype(jnp.bfloat16)
    all_keys, all_values, all_place, all_ids, all_rank = (
        lax.all_gather(key_rows, "expert", axis=0, tiled=True),
        lax.all_gather(value_rows, "expert", axis=0, tiled=True),
        lax.all_gather(layout, "expert", axis=0, tiled=True),
        lax.all_gather(expert_ids, "expert", axis=0, tiled=True),
        lax.all_gather(drop_rank, "expert", axis=0, tiled=True),
    )
    all_segment = token_tables(all_place, seq_lengths)[0]
    rows_per_block = math.gcd(512, query_total)
    count_of_blocks = query_total // rows_per_block
    query_segment = jnp.tile(segment_ids, local_heads)
    query_place = jnp.tile(layout, local_heads)

    def attend_block(operands):
        query_block, segment_block, place_block = operands
        scores = jnp.einsum("qd,kd->qk", query_block, all_keys, preferred_element_type=jnp.float32)
        scores = jnp.where(visible(segment_block, place_block, all_segment, all_place), scores, NEG)
        highest = jnp.max(scores, axis=1, keepdims=True)
        weights = jnp.exp(scores - highest)
        totals = jnp.sum(weights, axis=1, keepdims=True)
        probability = (weights / totals).astype(jnp.bfloat16)
        mixed_out = jnp.dot(probability, all_values, preferred_element_type=jnp.float32)
        return (mixed_out, (highest + jnp.log(totals))[:, 0])

    attention_output, log_totals = lax.map(
        attend_block,
        (
            query_rows.reshape(count_of_blocks, rows_per_block, head_dim),
            query_segment.reshape(count_of_blocks, rows_per_block),
            query_place.reshape(count_of_blocks, rows_per_block),
        ),
    )
    attention_output = attention_output.reshape(local_heads, tok_rows, head_dim).astype(
        jnp.bfloat16
    )
    att_cat = jnp.transpose(attention_output, (1, 0, 2)).reshape(tok_rows, local_heads * head_dim)
    branch_part = jnp.dot(att_cat, w_out, preferred_element_type=jnp.float32)
    branch = lax.psum(branch_part, "tensor")
    residual = hidden + branch
    normed2 = norm_rows(residual, norm2_gain)
    normed2_low = normed2.astype(jnp.bfloat16)
    logits = jnp.dot(normed2_low, w_router, preferred_element_type=jnp.float32)
    soft_gate = jax.nn.softmax(jnp.take_along_axis(logits, expert_ids, axis=1), axis=1)
    picks = jnp.any(expert_ids[:, :, None] == expert_range, axis=1) & valid[:, None]
    all_valid = all_segment < seq_count
    all_picks = jnp.any(all_ids[:, :, None] == expert_range, axis=1) & all_valid[:, None]
    earlier = (all_rank[None, :] < drop_rank[:, None]).astype(jnp.bfloat16)
    before_counts = jnp.dot(
        earlier, all_picks.astype(jnp.bfloat16), preferred_element_type=jnp.float32
    )
    global_slot = jnp.take_along_axis(before_counts, expert_ids, axis=1).astype(jnp.int32)
    kept_mask = (global_slot < CAP) & valid[:, None]
    gate_weight = soft_gate * kept_mask.astype(jnp.float32)
    lower_rows = (jnp.arange(tok_rows)[None, :] < jnp.arange(tok_rows)[:, None]).astype(
        jnp.bfloat16
    )
    local_counts = jnp.dot(
        lower_rows, picks.astype(jnp.bfloat16), preferred_element_type=jnp.float32
    )
    local_slot = jnp.take_along_axis(local_counts, expert_ids, axis=1).astype(jnp.int32)
    pair_count = tok_rows * TOPK
    dump_index = expert_count * slot_count
    target = jnp.where(kept_mask, expert_ids * slot_count + local_slot, dump_index)
    pair_index = jnp.arange(pair_count, dtype=jnp.int32)
    slot_pair = (
        jnp.full((dump_index,), pair_count, jnp.int32)
        .at[target.reshape(-1)]
        .set(pair_index, mode="drop")
    )
    slot_token = jnp.where(slot_pair < pair_count, slot_pair // TOPK, tok_rows)
    slot_global = (
        jnp.full((dump_index,), -1, jnp.int32)
        .at[target.reshape(-1)]
        .set(global_slot.reshape(-1), mode="drop")
    )
    padded_rows = jnp.concatenate([normed2_low, jnp.zeros((1, model_width), jnp.bfloat16)], axis=0)
    send_rows = padded_rows[slot_token].reshape(group_count, local_count, slot_count, model_width)
    send_slot = slot_global.reshape(group_count, local_count, slot_count)
    received, received_slot = deliver(send_rows, send_slot)
    gate_lin, up_lin, activation, expert_out = expert_forward(received, w_gate, w_up, w_down)
    returned = bring_back(expert_out)
    returned_flat = jnp.concatenate(
        [returned.reshape(dump_index, model_width), jnp.zeros((1, model_width), returned.dtype)],
        axis=0,
    )
    pair_out = returned_flat[target]
    moe_part = jnp.sum(gate_weight[:, :, None] * pair_out, axis=1)
    moe_branch = lax.psum(moe_part.astype(jnp.bfloat16), "tensor").astype(jnp.float32)
    out_hidden = (residual + moe_branch).astype(jnp.bfloat16)
    grad_y = cotangent.astype(jnp.float32)
    gate_dot = jnp.sum(grad_y[:, None, :] * pair_out, axis=2)
    pair_grads = (
        (gate_weight[:, :, None] * grad_y[:, None, :])
        .astype(jnp.bfloat16)
        .reshape(pair_count, model_width)
    )
    pair_grads = jnp.concatenate([pair_grads, jnp.zeros((1, model_width), jnp.bfloat16)], axis=0)
    send_grad = pair_grads[slot_pair].reshape(group_count, local_count, slot_count, model_width)
    grad_received, grad_slot = deliver(send_grad, send_slot)
    grad_entry, grad_w_gate, grad_w_up, grad_w_down = expert_backward(
        received, gate_lin, up_lin, activation, grad_received, w_gate, w_up, w_down
    )
    grad_returned = bring_back(grad_entry)
    grad_flat = jnp.concatenate(
        [
            grad_returned.reshape(dump_index, model_width),
            jnp.zeros((1, model_width), grad_returned.dtype),
        ],
        axis=0,
    )
    grad_normed2_part = jnp.sum(grad_flat[target], axis=1, dtype=jnp.float32)
    grad_normed2_exp, gate_dot = lax.psum((grad_normed2_part, gate_dot), "tensor")
    grad_soft = gate_dot * kept_mask.astype(jnp.float32)
    grad_chosen = soft_gate * (grad_soft - jnp.sum(soft_gate * grad_soft, axis=1, keepdims=True))
    grad_logits = jnp.sum(
        grad_chosen[:, :, None] * (expert_ids[:, :, None] == expert_range).astype(jnp.float32),
        axis=1,
    ).astype(jnp.bfloat16)
    grad_w_router = jnp.einsum(
        "td,te->de", normed2_low, grad_logits, preferred_element_type=jnp.float32
    )
    grad_normed2 = grad_normed2_exp + jnp.einsum(
        "te,de->td", grad_logits, w_router, preferred_element_type=jnp.float32
    )
    norm2_pull = jax.vjp(norm_rows, residual, norm2_gain)[1]
    grad_resid_norm, grad_norm2 = norm2_pull(grad_normed2)
    grad_residual = grad_y + grad_resid_norm
    grad_residual_low = grad_residual.astype(jnp.bfloat16)
    grad_w_out = jnp.einsum(
        "tc,td->cd", att_cat, grad_residual_low, preferred_element_type=jnp.float32
    )
    grad_att_cat = jnp.einsum(
        "td,cd->tc", grad_residual_low, w_out, preferred_element_type=jnp.float32
    ).astype(jnp.bfloat16)
    grad_att_rows = jnp.transpose(
        grad_att_cat.reshape(tok_rows, local_heads, head_dim), (1, 0, 2)
    ).reshape(query_total, head_dim)

    def query_grad_block(operands):
        query_block, segment_block, place_block, grad_block, log_block = operands
        scores = jnp.einsum("qd,kd->qk", query_block, all_keys, preferred_element_type=jnp.float32)
        scores = jnp.where(visible(segment_block, place_block, all_segment, all_place), scores, NEG)
        probability = jnp.exp(scores - log_block[:, None])
        grad_prob = jnp.einsum(
            "qd,kd->qk", grad_block, all_values, preferred_element_type=jnp.float32
        )
        delta_row = jnp.sum(probability * grad_prob, axis=1)
        grad_scores = (probability * (grad_prob - delta_row[:, None])).astype(jnp.bfloat16)
        return (jnp.dot(grad_scores, all_keys, preferred_element_type=jnp.float32), delta_row)

    grad_query_rows, deltas = lax.map(
        query_grad_block,
        (
            query_rows.reshape(count_of_blocks, rows_per_block, head_dim),
            query_segment.reshape(count_of_blocks, rows_per_block),
            query_place.reshape(count_of_blocks, rows_per_block),
            grad_att_rows.reshape(count_of_blocks, rows_per_block, head_dim),
            log_totals,
        ),
    )
    log_flat = log_totals.reshape(query_total)
    delta_flat = deltas.reshape(query_total)
    key_block = math.gcd(lax.axis_size("expert") * tok_rows, 2048)

    def one_block(offset):
        key_part = lax.dynamic_slice_in_dim(all_keys, offset, key_block, 0)
        value_part = lax.dynamic_slice_in_dim(all_values, offset, key_block, 0)
        segment_part = lax.dynamic_slice_in_dim(all_segment, offset, key_block, 0)
        place_part = lax.dynamic_slice_in_dim(all_place, offset, key_block, 0)
        scores = jnp.einsum("qd,kd->qk", query_rows, key_part, preferred_element_type=jnp.float32)
        scores = jnp.where(
            visible(query_segment, query_place, segment_part, place_part), scores, NEG
        )
        probability = jnp.exp(scores - log_flat[:, None])
        grad_value = jnp.einsum(
            "qk,qd->kd",
            probability.astype(jnp.bfloat16),
            grad_att_rows,
            preferred_element_type=jnp.float32,
        )
        grad_prob = jnp.einsum(
            "qd,kd->qk", grad_att_rows, value_part, preferred_element_type=jnp.float32
        )
        grad_scores = (probability * (grad_prob - delta_flat[:, None])).astype(jnp.bfloat16)
        grad_key = jnp.einsum(
            "qk,qd->kd", grad_scores, query_rows, preferred_element_type=jnp.float32
        )
        return jnp.concatenate([grad_key, grad_value], axis=1)

    stacked = lax.map(
        one_block,
        jnp.arange(lax.axis_size("expert") * tok_rows // key_block, dtype=jnp.int32) * key_block,
    )
    key_value_grad = lax.psum_scatter(
        stacked.reshape(lax.axis_size("expert") * tok_rows, 2 * head_dim).astype(jnp.bfloat16),
        "expert",
        scatter_dimension=0,
        tiled=True,
    ).astype(jnp.float32)
    grad_key_post = key_value_grad[:, :head_dim].reshape(tok_rows, 1, head_dim)
    grad_values_low = key_value_grad[:, head_dim:].astype(jnp.bfloat16)
    grad_query_tok = jnp.transpose(
        grad_query_rows.reshape(local_heads, tok_rows, head_dim), (1, 0, 2)
    )
    query_pull = jax.vjp(partial(shape_queries, position=position), query_lin, query_gain)[1]
    grad_query_lin, grad_qgain_part = query_pull(grad_query_tok)
    key_pull = jax.vjp(partial(shape_keys, position=position), key_lin, key_gain)[1]
    grad_key_lin, grad_kgain_part = key_pull(grad_key_post)
    grad_query_low = grad_query_lin.astype(jnp.bfloat16)
    grad_key_low = grad_key_lin.astype(jnp.bfloat16)
    grad_w_query = jnp.einsum(
        "td,tc->dc", normed1_low, grad_query_low, preferred_element_type=jnp.float32
    )
    grad_w_key = jnp.einsum(
        "td,tc->dc", normed1_low, grad_key_low, preferred_element_type=jnp.float32
    )
    grad_w_value = jnp.einsum(
        "td,tc->dc", normed1_low, grad_values_low, preferred_element_type=jnp.float32
    )
    grad_normed1_part = jnp.einsum(
        "tc,dc->td", grad_query_low, w_query, preferred_element_type=jnp.float32
    )
    grad_normed1_part = grad_normed1_part + jnp.einsum(
        "tc,dc->td", grad_key_low, key_weight, preferred_element_type=jnp.float32
    )
    grad_normed1_part = grad_normed1_part + jnp.einsum(
        "tc,dc->td", grad_values_low, value_weight, preferred_element_type=jnp.float32
    )
    grad_normed1, grad_qgain_part, grad_kgain_part = (
        lax.psum(grad_normed1_part.astype(jnp.bfloat16), "tensor").astype(jnp.float32),
        lax.psum(grad_qgain_part.astype(jnp.bfloat16), "tensor").astype(jnp.float32),
        lax.psum(grad_kgain_part.astype(jnp.bfloat16), "tensor").astype(jnp.float32),
    )
    norm1_pull = jax.vjp(norm_rows, hidden, norm1_gain)[1]
    grad_hidden_norm, grad_norm1 = norm1_pull(grad_normed1)
    grad_hidden = (grad_residual + grad_hidden_norm).astype(jnp.bfloat16)
    summed = (
        lax.psum(grad_norm1.astype(jnp.bfloat16), "expert").astype(jnp.float32),
        lax.psum(grad_w_query.astype(jnp.bfloat16), "expert").astype(jnp.float32),
        lax.psum(grad_w_key.astype(jnp.bfloat16), "expert").astype(jnp.float32),
        lax.psum(grad_w_value.astype(jnp.bfloat16), "expert").astype(jnp.float32),
        lax.psum(grad_qgain_part.astype(jnp.bfloat16), "expert").astype(jnp.float32),
        lax.psum(grad_kgain_part.astype(jnp.bfloat16), "expert").astype(jnp.float32),
        lax.psum(grad_w_out.astype(jnp.bfloat16), "expert").astype(jnp.float32),
        lax.psum(grad_norm2.astype(jnp.bfloat16), "expert").astype(jnp.float32),
        lax.psum(grad_w_router.astype(jnp.bfloat16), "expert").astype(jnp.float32),
    )
    return (
        out_hidden,
        grad_hidden,
        summed[0],
        summed[1],
        summed[2],
        summed[3],
        summed[4],
        summed[5],
        summed[6],
        summed[7],
        summed[8],
        grad_w_gate,
        grad_w_up,
        grad_w_down,
    )


MESH = pl.DeviceIdType.MESH
FAR_FIRST = (3, -3, 2, -2, 1, -1, 0)


class Spot:
    def __init__(self):
        group, part = lax.axis_index("expert"), lax.axis_index("tensor")
        self.z, self.y = group // 2, group % 2
        self.x, self.c = part // 2, part % 2

    def has(self, dz):
        return (self.z + dz >= 0) & (self.z + dz <= 3)

    def device(self, dz=0, dy=0, dx=0, dc=0):
        y = 1 - self.y if dy else self.y
        x = 1 - self.x if dx else self.x
        c = 1 - self.c if dc else self.c
        return ((self.z + dz) * 2 + y, x * 2 + c)

    def rows(self, dz, dy, dx, dc, count):
        group, part = self.device(dz, dy, dx, dc)
        return pl.ds(pl.multiple_of((group * 4 + part) * count, count), count)

    def greet(self):
        barrier = pltpu.get_barrier_semaphore()
        for step in ((0, 1, 0, 0), (0, 0, 1, 0), (0, 0, 0, 1)):
            pl.semaphore_signal(barrier, inc=1, device_id=self.device(*step), device_id_type=MESH)
        for dz in (1, -1):

            @pl.when(self.has(dz))
            def _(dz=dz):
                pl.semaphore_signal(
                    barrier, inc=1, device_id=self.device(dz), device_id_type=MESH
                )

        inner = jnp.where((self.z > 0) & (self.z < 3), 1, 0)
        pl.semaphore_wait(barrier, 4 + inner)


def when_has(spot, dz, action):
    if dz == 0:
        action()
    else:
        pl.when(spot.has(dz))(action)


def gather_body(
    spot, src, out, recv, z_send, y_send, x_send, c_send, c_recv, local_sem, also=lambda *_: None
):
    count, width = src.shape
    half = width // 2
    first, second, whole = pl.ds(0, half), pl.ds(half, half), pl.ds(0, width)
    local = pltpu.make_async_copy(src, out.at[spot.rows(0, 0, 0, 0, count), :], local_sem)
    local.start()

    def send(dz, dy, dx, columns, send_sem, recv_sem, device):
        place = out.at[spot.rows(dz, dy, dx, 0, count), columns]
        own = dz == 0 and dy == 0 and dx == 0
        copy = pltpu.make_async_remote_copy(
            src_ref=src.at[:, columns] if own else place,
            dst_ref=place,
            send_sem=send_sem,
            recv_sem=recv_sem,
            device_id=device,
            device_id_type=MESH,
        )
        copy.start()

    def await_bytes(rows, columns, sem):
        view = out.at[pl.ds(0, rows), columns]
        pltpu.make_async_copy(view, view, sem).wait()

    to_y, to_x, to_c = spot.device(0, 1), spot.device(0, 0, 1), spot.device(0, 0, 0, 1)

    def spread(dz):
        also("spread", dz)
        if dz <= 0:

            @pl.when(spot.has(1))
            def _():
                send(dz, 0, 0, whole, z_send.at[dz + 3, 0], recv.at[0, dz + 2], spot.device(1))

        if dz >= 0:

            @pl.when(spot.has(-1))
            def _():
                send(dz, 0, 0, whole, z_send.at[dz + 3, 1], recv.at[0, dz + 4], spot.device(-1))

        send(dz, 0, 0, whole, y_send, recv.at[1, dz + 3], to_y)
        send(dz, 0, 0, whole, x_send, recv.at[2, dz + 3], to_x)
        send(dz, 0, 0, whole, c_send, c_recv, to_c)

    def take_z(dz):
        def action():
            await_bytes(count, whole, recv.at[0, dz + 3])
            also("take", dz)
            spread(dz)

        when_has(spot, dz, action)

    def take_yx(dz):
        def action():
            await_bytes(count, whole, recv.at[1, dz + 3])
            send(dz, 1, 0, first, x_send, recv.at[3, dz + 3], to_x)
            send(dz, 1, 0, whole, c_send, c_recv, to_c)
            await_bytes(count, whole, recv.at[2, dz + 3])
            send(dz, 0, 1, second, y_send, recv.at[4, dz + 3], to_y)
            send(dz, 0, 1, whole, c_send, c_recv, to_c)

        when_has(spot, dz, action)

    def take_diagonal(dz):
        def action():
            await_bytes(count, first, recv.at[3, dz + 3])
            await_bytes(count, second, recv.at[4, dz + 3])
            send(dz, 1, 1, whole, c_send, c_recv, to_c)

        when_has(spot, dz, action)

    spread(0)
    for dz in (1, -1):
        take_z(dz)
    take_yx(0)
    for dz in (2, -2):
        take_z(dz)
    for dz in (1, -1):
        take_yx(dz)
    take_diagonal(0)
    for dz in (3, -3):
        take_z(dz)
    for dz in (2, -2):
        take_yx(dz)
    for dz in (1, -1):
        take_diagonal(dz)
    for dz in (3, -3):
        take_yx(dz)
    for dz in (2, -2, 3, -3):
        take_diagonal(dz)

    await_bytes(16 * count, whole, c_recv)
    await_bytes(16 * count, whole, c_send)
    await_bytes(6 * count, whole, y_send)
    await_bytes(6 * count, whole, x_send)
    for dz in range(-3, 4):
        for side, step in ((0, 1), (1, -1)):
            if dz * step <= 0:

                @pl.when(spot.has(dz) & spot.has(step))
                def _(dz=dz, side=side):
                    await_bytes(count, whole, z_send.at[dz + 3, side])

    local.wait()


GATHER_SEMS = ((5, 7), (7, 2), None, None, None, None, None)


def dma_sems(shapes):
    return [pltpu.SemaphoreType.DMA(shape) if shape else pltpu.SemaphoreType.DMA for shape in shapes]


def gather_kernel(src, out, *sems):
    spot = Spot()
    spot.greet()
    gather_body(spot, src, out, *sems)


def gather_tagged_kernel(src, tag, out, tag_out, *refs):
    sems, (tag_z, tag_y, tag_z_send, tag_y_send, tag_local) = refs[:7], refs[7:]
    spot = Spot()

    def place(dz, dy):
        return tag_out.at[spot.device(dz, dy)[0]]

    own = pltpu.make_async_copy(tag, place(0, 0), tag_local)
    own.start()
    spot.greet()

    def also(what, dz):
        here = place(dz, 0)
        source = tag if dz == 0 else here
        if what == "take":
            arrive(here, tag_z.at[dz + 3])
            return
        if dz <= 0:

            @pl.when(spot.has(1))
            def _():
                push(source, here, tag_z_send.at[dz + 3, 0], tag_z.at[dz + 2], spot.device(1))

        if dz >= 0:

            @pl.when(spot.has(-1))
            def _():
                push(source, here, tag_z_send.at[dz + 3, 1], tag_z.at[dz + 4], spot.device(-1))

        push(source, here, tag_y_send.at[dz + 3], tag_y.at[dz + 3], spot.device(0, 1))

    gather_body(spot, src, out, *sems, also=also)
    for dz in range(-3, 4):

        def action(dz=dz):
            arrive(place(dz, 1), tag_y.at[dz + 3])
            arrive(place(dz, 0), tag_y_send.at[dz + 3])
            for side, step in ((0, 1), (1, -1)):
                if dz * step <= 0:

                    @pl.when(spot.has(step))
                    def _():
                        arrive(place(dz, 0), tag_z_send.at[dz + 3, side])

        when_has(spot, dz, action)
    own.wait()


def gather_rows(rows, tag=None):
    count, width = rows.shape
    hbm = pl.BlockSpec(memory_space=pl.ANY)
    shape = jax.ShapeDtypeStruct((32 * count, width), rows.dtype)
    if tag is None:
        return pl.pallas_call(
            gather_kernel,
            out_shape=shape,
            in_specs=[hbm],
            out_specs=hbm,
            scratch_shapes=dma_sems(GATHER_SEMS),
            compiler_params=pltpu.CompilerParams(collective_id=0, has_side_effects=True),
            name="gather_rows",
        )(rows)
    return pl.pallas_call(
        gather_tagged_kernel,
        out_shape=(shape, jax.ShapeDtypeStruct((8,) + tag.shape, tag.dtype)),
        in_specs=[hbm, hbm],
        out_specs=(hbm, hbm),
        scratch_shapes=dma_sems(GATHER_SEMS + ((7,), (7,), (7, 2), (7,), None)),
        compiler_params=pltpu.CompilerParams(collective_id=1, has_side_effects=True),
        name="gather_tagged",
    )(rows, tag)


def add_into(into, chunk, *terms):
    @pl.loop(0, into.shape[0] // chunk)
    def _(step):
        rows = pl.ds(pl.multiple_of(step * chunk, chunk), chunk)
        total = into[rows, :].astype(jnp.float32)
        for term in terms:
            total = total + term[rows, :].astype(jnp.float32)
        into[rows, :] = total.astype(into.dtype)


def push(src, dst, send_sem, recv_sem, device):
    pltpu.make_async_remote_copy(
        src_ref=src,
        dst_ref=dst,
        send_sem=send_sem,
        recv_sem=recv_sem,
        device_id=device,
        device_id_type=MESH,
    ).start()


def arrive(view, sem):
    pltpu.make_async_copy(view, view, sem).wait()


def scatter_kernel(split, with_kv, *refs):
    refs = list(refs)
    part = refs.pop(0)
    kv_part = refs.pop(0) if with_kv else None
    out = refs.pop(0)
    kv_out = refs.pop(0) if with_kv else None
    held, from_a, from_b, from_y, from_x, from_below, from_above = refs[:7]
    c_recv, recv, z_send, half_send, y_send, x_send, c_send = refs[7:14]
    if with_kv:
        kv_held, kv_y, kv_below, kv_above, kv_recv, kv_z_send, kv_send = refs[14:]
    count, width = out.shape
    first, second, whole = pl.ds(0, split), pl.ds(split, width - split), pl.ds(0, width)
    spot = Spot()
    spot.greet()
    to_y, to_x, to_c = spot.device(0, 1), spot.device(0, 0, 1), spot.device(0, 0, 0, 1)
    groups = ((1, 1), (1, 0), (0, 1), (0, 0))
    for dy, dx in groups:
        for dz in FAR_FIRST:

            def action(dz=dz, dy=dy, dx=dx):
                push(
                    part.at[spot.rows(dz, dy, dx, 1, count), :],
                    held.at[spot.z + dz, dy, dx],
                    c_send,
                    c_recv.at[dz + 3, dy, dx],
                    to_c,
                )

            when_has(spot, dz, action)

    def kv_rows(dz, dy):
        group, _ = spot.device(dz, dy)
        return pl.ds(pl.multiple_of(group * 256, 256), 256)

    if with_kv:
        for dz in FAR_FIRST:

            def action(dz=dz):
                push(
                    kv_part.at[kv_rows(dz, 1), :],
                    kv_y.at[spot.z + dz],
                    kv_send,
                    kv_recv.at[0, dz + 3],
                    to_y,
                )

            when_has(spot, dz, action)

    def merge(dz, dy, dx):
        mine = held.at[spot.z + dz, dy, dx]
        arrive(mine, c_recv.at[dz + 3, dy, dx])
        add_into(mine, 16, part.at[spot.rows(dz, dy, dx, 0, count), :])
        return mine

    for dz in FAR_FIRST:

        def action(dz=dz):
            far = spot.z + dz
            mine = merge(dz, 1, 1)
            push(mine.at[:, first], from_a.at[far], half_send.at[0], recv.at[0, dz + 3], to_x)
            push(mine.at[:, second], from_b.at[far], half_send.at[1], recv.at[1, dz + 3], to_y)

        when_has(spot, dz, action)

    def line(dz, mine, chunk, below, above, sems, sends):
        far = spot.z + dz
        if dz >= 0:

            @pl.when(spot.has(-1))
            def _():
                arrive(below.at[far], sems[0].at[dz + 3])
                add_into(mine, chunk, below.at[far])

        if dz <= 0:

            @pl.when(spot.has(1))
            def _():
                arrive(above.at[far], sems[1].at[dz + 3])
                add_into(mine, chunk, above.at[far])

        if dz > 0:
            push(mine, below.at[far], sends.at[dz + 3], sems[0].at[dz + 2], spot.device(1))
        if dz < 0:
            push(mine, above.at[far], sends.at[dz + 3], sems[1].at[dz + 4], spot.device(-1))

    for dz in FAR_FIRST:

        def action(dz=dz):
            far = spot.z + dz
            mine = merge(dz, 1, 0)
            arrive(from_a.at[far], recv.at[0, dz + 3])
            add_into(mine.at[:, first], 16, from_a.at[far])
            push(mine, from_y.at[far], y_send, recv.at[2, dz + 3], to_y)
            mine = merge(dz, 0, 1)
            arrive(from_b.at[far], recv.at[1, dz + 3])
            add_into(mine.at[:, second], 16, from_b.at[far])
            push(mine, from_x.at[far], x_send, recv.at[3, dz + 3], to_x)
            if with_kv:
                kv_mine = kv_held.at[far]
                kv_mine[...] = kv_part[kv_rows(dz, 0), :]
                arrive(kv_y.at[far], kv_recv.at[0, dz + 3])
                add_into(kv_mine, 64, kv_y.at[far])
                line(
                    dz, kv_mine, 64, kv_below, kv_above,
                    (kv_recv.at[1], kv_recv.at[2]), kv_z_send,
                )

        when_has(spot, dz, action)
    for dz in FAR_FIRST:

        def action(dz=dz):
            far = spot.z + dz
            mine = merge(dz, 0, 0)
            arrive(from_y.at[far], recv.at[2, dz + 3])
            arrive(from_x.at[far], recv.at[3, dz + 3])
            add_into(mine, 16, from_y.at[far], from_x.at[far])
            line(dz, mine, 16, from_below, from_above, (recv.at[4], recv.at[5]), z_send)
            if dz == 0:
                out[...] = mine[...].astype(out.dtype)
                if with_kv:
                    kv_out[...] = kv_held[far].astype(kv_out.dtype)

        when_has(spot, dz, action)

    def await_view(rows, columns, sem):
        view = part.at[pl.ds(0, rows), columns]
        pltpu.make_async_copy(view, view, sem).wait()

    await_view(16 * count, whole, c_send)
    await_view(4 * count, whole, y_send)
    await_view(4 * count, whole, x_send)
    arrive(from_a, half_send.at[0])
    arrive(from_b, half_send.at[1])
    if with_kv:
        view = kv_part.at[pl.ds(0, 1024), :]
        pltpu.make_async_copy(view, view, kv_send).wait()
    for dz in FAR_FIRST[:-1]:

        def action(dz=dz):
            await_view(count, whole, z_send.at[dz + 3])
            if with_kv:
                view = kv_part.at[pl.ds(0, 256), :]
                pltpu.make_async_copy(view, view, kv_z_send.at[dz + 3]).wait()

        when_has(spot, dz, action)


def scatter_rows(partial_rows, ident, kv_partial=None):
    total, width = partial_rows.shape
    count = total // 32
    with_kv = kv_partial is not None
    dma, bf16 = pltpu.SemaphoreType.DMA, jnp.bfloat16
    split = 1536 if with_kv else 1024
    line = pltpu.VMEM((4, count, width), bf16)
    scratch = [
        pltpu.VMEM((4, 2, 2, count, width), bf16),
        pltpu.VMEM((4, count, split), bf16),
        pltpu.VMEM((4, count, width - split), bf16),
        line, line, line, line,
        dma((7, 2, 2)), dma((6, 7)), dma((7,)), dma((2,)), dma, dma, dma,
    ]
    vmem = pl.BlockSpec(memory_space=pltpu.VMEM)
    out_shape = jax.ShapeDtypeStruct((count, width), jnp.float32)
    if with_kv:
        kv_line = pltpu.VMEM((4, 256, kv_partial.shape[1]), bf16)
        scratch += [kv_line, kv_line, kv_line, kv_line, dma((3, 7)), dma((7,)), dma]
        out_shape = (out_shape, jax.ShapeDtypeStruct((256, kv_partial.shape[1]), bf16))
    return pl.pallas_call(
        partial(scatter_kernel, split, with_kv),
        out_shape=out_shape,
        in_specs=[vmem] * (2 if with_kv else 1),
        out_specs=(vmem, vmem) if with_kv else vmem,
        scratch_shapes=scratch,
        compiler_params=pltpu.CompilerParams(
            collective_id=ident, has_side_effects=True, vmem_limit_bytes=48 << 20
        ),
        name="scatter_rows_kv" if with_kv else "scatter_rows",
    )(*((partial_rows, kv_partial) if with_kv else (partial_rows,)))


def finish_kernel(
    query, kv, small, ends, query_out, kv_out, small_out, ends_out,
    z_recv, y_recv, x_recv, z_send, total_send, total_recv, local_sem,
):
    spot = Spot()
    dim = query.shape[1]
    few, many = small.shape[0], ends.shape[0]

    def query_at(dz, dy):
        group, _ = spot.device(dz, dy)
        return query_out.at[:, pl.ds(pl.multiple_of(group * dim, dim), dim)]

    def kv_at(dz, dy):
        group, _ = spot.device(dz, dy)
        return kv_out.at[pl.ds(pl.multiple_of(group * 256, 256), 256), :]

    def small_at(dz, dy, dx, dc):
        return small_out.at[spot.rows(dz, dy, dx, dc, few), :]

    def ends_at(dx, dc):
        _, part = spot.device(0, 0, dx, dc)
        return ends_out.at[pl.ds(pl.multiple_of(part * many, many), many), :]

    locals_ = [
        pltpu.make_async_copy(query, query_at(0, 0), local_sem.at[0]),
        pltpu.make_async_copy(kv, kv_at(0, 0), local_sem.at[1]),
        pltpu.make_async_copy(small, small_at(0, 0, 0, 0), local_sem.at[2]),
        pltpu.make_async_copy(ends, ends_at(0, 0), local_sem.at[3]),
    ]
    for copy in locals_:
        copy.start()
    spot.greet()
    to_y, to_x, to_c = spot.device(0, 1), spot.device(0, 0, 1), spot.device(0, 0, 0, 1)

    def spread(dz):
        own = dz == 0
        goods = (
            (small if own else small_at(dz, 0, 0, 0), small_at(dz, 0, 0, 0)),
            (kv if own else kv_at(dz, 0), kv_at(dz, 0)),
            (query if own else query_at(dz, 0), query_at(dz, 0)),
        )
        for kind, (src, dst) in enumerate(goods):
            if dz <= 0:

                @pl.when(spot.has(1))
                def _(kind=kind, src=src, dst=dst):
                    push(src, dst, z_send.at[kind, dz + 3, 0], z_recv.at[kind, dz + 2],
                         spot.device(1))

            if dz >= 0:

                @pl.when(spot.has(-1))
                def _(kind=kind, src=src, dst=dst):
                    push(src, dst, z_send.at[kind, dz + 3, 1], z_recv.at[kind, dz + 4],
                         spot.device(-1))

            push(src, dst, total_send.at[kind], y_recv.at[kind, dz + 3], to_y)
        src, dst = goods[0]
        push(src, dst, total_send.at[3], x_recv.at[dz + 3, 0], to_x)
        push(src, dst, total_send.at[4], total_recv.at[0], to_c)

    push(ends, ends_at(0, 0), total_send.at[5], total_recv.at[1], to_x)
    push(ends, ends_at(0, 0), total_send.at[6], total_recv.at[2], to_c)
    spread(0)
    for step in (1, 2, 3):
        for dz in (step, -step):

            def action(dz=dz):
                for kind, dst in enumerate((small_at(dz, 0, 0, 0), kv_at(dz, 0), query_at(dz, 0))):
                    arrive(dst, z_recv.at[kind, dz + 3])
                spread(dz)

            when_has(spot, dz, action)
    arrive(ends_at(1, 0), total_recv.at[1])
    push(ends_at(1, 0), ends_at(1, 0), total_send.at[6], total_recv.at[2], to_c)
    for dz in (0, 1, -1, 2, -2, 3, -3):

        def action(dz=dz):
            place = small_at(dz, 1, 0, 0)
            arrive(place, y_recv.at[0, dz + 3])
            push(place, place, total_send.at[3], x_recv.at[dz + 3, 1], to_x)
            push(place, place, total_send.at[4], total_recv.at[0], to_c)
            place = small_at(dz, 0, 1, 0)
            arrive(place, x_recv.at[dz + 3, 0])
            push(place, place, total_send.at[4], total_recv.at[0], to_c)

        when_has(spot, dz, action)
    for dz in (0, 1, -1, 2, -2, 3, -3):

        def action(dz=dz):
            place = small_at(dz, 1, 1, 0)
            arrive(place, x_recv.at[dz + 3, 1])
            push(place, place, total_send.at[4], total_recv.at[0], to_c)
            arrive(kv_at(dz, 1), y_recv.at[1, dz + 3])
            arrive(query_at(dz, 1), y_recv.at[2, dz + 3])

        when_has(spot, dz, action)

    def drain(ref, rows, sem):
        view = ref.at[pl.ds(0, rows), :]
        pltpu.make_async_copy(view, view, sem).wait()

    drain(small_out, 16 * few, total_recv.at[0])
    drain(ends_out, 2 * many, total_recv.at[2])
    drain(small_out, 4 * few, total_send.at[0])
    drain(kv_out, 4 * 256, total_send.at[1])
    half = query_out.at[:, pl.ds(0, 4 * dim)]
    pltpu.make_async_copy(half, half, total_send.at[2]).wait()
    drain(small_out, 8 * few, total_send.at[3])
    drain(small_out, 16 * few, total_send.at[4])
    drain(ends_out, many, total_send.at[5])
    drain(ends_out, 2 * many, total_send.at[6])
    for dz in range(-3, 4):
        for side, step in ((0, 1), (1, -1)):
            if dz * step <= 0:

                @pl.when(spot.has(dz) & spot.has(step))
                def _(dz=dz, side=side):
                    places = (small_at(dz, 0, 0, 0), kv_at(dz, 0), query_at(dz, 0))
                    for kind, place in enumerate(places):
                        arrive(place, z_send.at[kind, dz + 3, side])

    for copy in locals_:
        copy.wait()


def finish(query, kv, small, ends, ident):
    dma, shape = pltpu.SemaphoreType.DMA, jax.ShapeDtypeStruct
    hbm = pl.BlockSpec(memory_space=pl.ANY)
    return pl.pallas_call(
        finish_kernel,
        out_shape=(
            shape((query.shape[0], 8 * query.shape[1]), query.dtype),
            shape((8 * kv.shape[0], kv.shape[1]), kv.dtype),
            shape((32 * small.shape[0], small.shape[1]), small.dtype),
            shape((4 * ends.shape[0], ends.shape[1]), ends.dtype),
        ),
        in_specs=[hbm] * 4,
        out_specs=(hbm,) * 4,
        scratch_shapes=[
            dma((3, 7)), dma((3, 7)), dma((7, 2)), dma((3, 7, 2)), dma((7,)), dma((3,)), dma((4,)),
        ],
        compiler_params=pltpu.CompilerParams(collective_id=ident, has_side_effects=True),
        name="finish",
    )(query, kv, small, ends)


F32, BF16 = jnp.float32, jnp.bfloat16
VMEM_SPEC = pl.BlockSpec(memory_space=pltpu.VMEM)
HBM_SPEC = pl.BlockSpec(memory_space=pl.ANY)


def mxu(left, right, left_dim=1, right_dim=0):
    return lax.dot_general(
        left, right, (((left_dim,), (right_dim,)), ((), ())), preferred_element_type=F32
    )


def head_norm(lin):
    root = lax.rsqrt(jnp.mean(lin * lin, axis=-1, keepdims=True) + EPS)
    return lin * root, root


def project_kernel(
    which, hidden, gain, w_query, w_key, w_value, q_gain, k_gain, cosine, sine,
    normed, queries, keys, values, lin_out, weight,
):
    dim = w_query.shape[1]

    @pl.when(pl.program_id(0) == 0)
    def _():
        weight[:, :dim] = w_query[...]
        weight[:, dim : 2 * dim] = w_key[...]
        weight[:, 2 * dim :] = w_value[...]

    rows = hidden[...].astype(F32)
    scaled = rows * lax.rsqrt(jnp.mean(rows * rows, axis=-1, keepdims=True) + EPS) * gain[...]
    normed[...] = scaled.astype(BF16)
    lin = mxu(normed[...], weight[...])
    lin_out[...] = lin[:, : 2 * dim]
    values[...] = lin[:, 2 * dim :].astype(BF16)
    for at, head_gain, scale, out in ((0, q_gain, dim**-0.5, queries), (dim, k_gain, 1.0, keys)):
        plain, _ = head_norm(lin[:, at : at + dim])
        plain = plain * head_gain[...]
        turned = pltpu.roll(plain, dim // 2, 1)
        out[...] = ((plain * cosine[...] + turned * sine[...]) * scale).astype(BF16)


def project(group, hidden, gain, w_query, w_key, w_value, q_gain, k_gain, cosine, sine):
    total, width = hidden.shape
    dim = w_key.shape[1]
    rows = 256
    block = lambda columns: pl.BlockSpec((rows, columns), lambda i, _: (i, 0))
    fixed = lambda shape: pl.BlockSpec(shape, lambda i, _: (0, 0))
    shape = jax.ShapeDtypeStruct
    return pl.pallas_call(
        project_kernel,
        grid_spec=pltpu.PrefetchScalarGridSpec(
            num_scalar_prefetch=1,
            grid=(total // rows,),
            in_specs=[
                block(width), fixed((1, width)),
                pl.BlockSpec((width, dim), lambda i, which: (0, which[0])),
                fixed((width, dim)), fixed((width, dim)), fixed((1, dim)), fixed((1, dim)),
                block(dim), block(dim),
            ],
            out_specs=[block(width), block(dim), block(dim), block(dim), block(2 * dim)],
            scratch_shapes=[pltpu.VMEM((width, 3 * dim), BF16)],
        ),
        out_shape=[
            shape((total, width), BF16), shape((total, dim), BF16), shape((total, dim), BF16),
            shape((total, dim), BF16), shape((total, 2 * dim), F32),
        ],
        compiler_params=pltpu.CompilerParams(vmem_limit_bytes=40 << 20),
        name="project",
    )(group, hidden, gain, w_query, w_key, w_value, q_gain, k_gain, cosine, sine)


def attend_kernel(
    queries, keys, values, place_column, place_row, open_row,
    attended, log_total, att_rows, send_sem, recv_sem, local_sem,
):
    group, part = lax.axis_index("expert"), lax.axis_index("tensor")
    dim = queries.shape[1]
    rows = 256
    barrier = pltpu.get_barrier_semaphore()

    @pl.loop(1, 8)
    def _(step):
        pl.semaphore_signal(
            barrier, inc=1, device_id=((group + step) % 8, part), device_id_type=MESH
        )

    pl.semaphore_wait(barrier, 7)
    mine = att_rows.at[:, pl.ds(pl.multiple_of(group * dim, dim), dim)]

    def copy_of(step):
        target = (group + step) % 8
        block = attended.at[pl.ds(pl.multiple_of(target * rows, rows), rows), :]
        return pltpu.make_async_remote_copy(
            src_ref=block,
            dst_ref=mine,
            send_sem=send_sem.at[step],
            recv_sem=recv_sem.at[step],
            device_id=(target, part),
            device_id_type=MESH,
        )

    def block_of(step):
        at = pl.multiple_of((group + step) % 8 * rows, rows)
        here = pl.ds(at, rows)
        scores = mxu(keys[...], queries[here, :], 1, 1)
        seen = (place_column[...] <= place_row[:, here]) & (place_column[...] >= open_row[:, here])
        scores = jnp.where(seen, scores, NEG)
        highest = jnp.max(scores, axis=0, keepdims=True)
        weights = jnp.exp(scores - highest)
        totals = jnp.sum(weights, axis=0, keepdims=True)
        probability = (weights * (1.0 / totals)).astype(BF16)
        mixed = mxu(values[...], probability, 0, 0)
        attended[here, :] = mixed.T.astype(BF16)
        log_total[:, here] = highest + jnp.log(totals)

    @pl.loop(1, 8)
    def _(step):
        block_of(step)
        copy_of(step).start()

    block_of(0)
    own = attended.at[pl.ds(pl.multiple_of(group * rows, rows), rows), :]
    local = pltpu.make_async_copy(own, mine, local_sem)
    local.start()

    @pl.loop(1, 8)
    def _(step):
        copy_of(step).wait_send()
        source = (group + 8 - step) % 8
        there = att_rows.at[:, pl.ds(pl.multiple_of(source * dim, dim), dim)]
        pltpu.make_async_copy(there, there, recv_sem.at[step]).wait()

    local.wait()


def attend(queries, keys, values, place_column, place_row, open_row):
    total, dim = queries.shape
    shape = jax.ShapeDtypeStruct
    return pl.pallas_call(
        attend_kernel,
        out_shape=(
            shape((total, dim), BF16), shape((1, total), F32), shape((total // 8, 8 * dim), BF16),
        ),
        in_specs=[VMEM_SPEC] * 6,
        out_specs=(VMEM_SPEC, VMEM_SPEC, HBM_SPEC),
        scratch_shapes=dma_sems(((8,), (8,), None)),
        compiler_params=pltpu.CompilerParams(
            collective_id=6, has_side_effects=True, vmem_limit_bytes=40 << 20
        ),
        name="attend",
    )(queries, keys, values, place_column, place_row, open_row)


def branch_kernel(
    att_rows, w_out, hidden, gain, residual, normed, normed_all,
    partial_sum, from_core, to_x_sum, from_x, tensor_sems, *sems,
):
    count, width = hidden.shape
    spot = Spot()

    @pl.loop(0, width // 256)
    def _(step):
        columns = pl.ds(pl.multiple_of(step * 256, 256), 256)
        partial_sum[:, columns] = mxu(att_rows[...], w_out[:, columns]).astype(BF16)

    spot.greet()

    def rows(dx, dc):
        _, part = spot.device(0, 0, dx, dc)
        return partial_sum.at[pl.ds(pl.multiple_of(part * count, count), count), :]

    to_x, to_c = spot.device(0, 0, 1), spot.device(0, 0, 0, 1)
    for dx in (1, 0):
        push(rows(dx, 1), from_core.at[dx], tensor_sems.at[dx], tensor_sems.at[2 + dx], to_c)
    arrive(from_core.at[1], tensor_sems.at[3])
    to_x_sum[...] = (rows(1, 0)[...].astype(F32) + from_core[1].astype(F32)).astype(BF16)
    push(to_x_sum, from_x, tensor_sems.at[4], tensor_sems.at[5], to_x)
    arrive(from_core.at[0], tensor_sems.at[2])
    arrive(from_x, tensor_sems.at[5])
    branch = rows(0, 0)[...].astype(F32) + from_core[0].astype(F32) + from_x[...].astype(F32)
    total = hidden[...].astype(F32) + branch
    residual[...] = total
    root = lax.rsqrt(jnp.mean(total * total, axis=-1, keepdims=True) + EPS)
    normed[...] = (total * root * gain[...]).astype(BF16)
    for at, view in ((0, from_core.at[0]), (1, from_core.at[1]), (4, from_x)):
        arrive(view, tensor_sems.at[at])
    gather_body(spot, normed, normed_all, *sems)


def branch_rows(att_rows, w_out, hidden, gain):
    count, width = hidden.shape
    shape = jax.ShapeDtypeStruct
    return pl.pallas_call(
        branch_kernel,
        out_shape=(
            shape((count, width), F32), shape((count, width), BF16),
            shape((32 * count, width), BF16),
        ),
        in_specs=[VMEM_SPEC] * 4,
        out_specs=(VMEM_SPEC, VMEM_SPEC, HBM_SPEC),
        scratch_shapes=[
            pltpu.VMEM((4 * count, width), BF16), pltpu.VMEM((2, count, width), BF16),
            pltpu.VMEM((count, width), BF16), pltpu.VMEM((count, width), BF16),
        ]
        + dma_sems(((6,),) + GATHER_SEMS),
        compiler_params=pltpu.CompilerParams(
            collective_id=7, has_side_effects=True, vmem_limit_bytes=40 << 20
        ),
        name="branch",
    )(att_rows, w_out, hidden, gain)


def attend_back_kernel(
    which, grad_rows, w_out, queries, query_lin, cosine, sine, place_row, open_row, log_total,
    keys, values, place_column, lin, k_gain, q_gain, cosine_all, sine_all,
    grad_lin, grad_q_gain, grad_k_gain, grad_keys, grad_values,
):
    step = pl.program_id(0)
    rows, dim = queries.shape
    here = pl.ds(pl.multiple_of(step * rows, rows), rows)

    @pl.when(step == 0)
    def _():
        grad_keys[...] = jnp.zeros_like(grad_keys)
        grad_values[...] = jnp.zeros_like(grad_values)
        grad_q_gain[...] = jnp.zeros_like(grad_q_gain)

    def unshape(grad, plain, gain, cos, sin):
        grad = grad * cos + pltpu.roll(grad * sin, dim // 2, 1)
        normed, root = head_norm(plain)
        gain_part = jnp.sum(grad * normed, axis=0, keepdims=True)
        grad = grad * gain
        return root * (grad - normed * jnp.mean(grad * normed, axis=-1, keepdims=True)), gain_part

    grad_att = mxu(grad_rows[...], w_out[...], 1, 1).astype(BF16)
    scores = mxu(keys[...], queries[...], 1, 1)
    seen = (place_column[...] <= place_row[...]) & (place_column[...] >= open_row[...])
    probability = jnp.exp(jnp.where(seen, scores - log_total[...], NEG))
    grad_prob = mxu(values[...], grad_att, 1, 1)
    delta = jnp.sum(probability * grad_prob, axis=0, keepdims=True)
    grad_scores = (probability * (grad_prob - delta)).astype(BF16)
    grad_values[...] += mxu(probability.astype(BF16), grad_att)
    grad_keys[...] += mxu(grad_scores, queries[...])
    grad_query = mxu(grad_scores, keys[...], 0, 0) * dim**-0.5
    grad_query, gain_part = unshape(
        grad_query, query_lin[...], q_gain[...], cosine[...], sine[...]
    )
    grad_q_gain[...] += gain_part
    grad_lin[here, :dim] = grad_query.astype(BF16)

    @pl.when(step == pl.num_programs(0) - 1)
    def _():
        grad_key, key_part = unshape(
            grad_keys[...], lin[:, dim:], k_gain[...], cosine_all[...], sine_all[...]
        )
        grad_lin[:, dim : 2 * dim] = grad_key.astype(BF16)
        grad_lin[:, 2 * dim :] = grad_values[...].astype(BF16)
        grad_k_gain[...] = key_part


def attend_back(
    group, grad_rows, w_out, queries, lin, cosine, sine, place_row, open_row, log_total,
    keys, values, place_column, k_gain, q_gain,
):
    total, width = grad_rows.shape
    dim = keys.shape[1]
    rows = 256
    block = lambda columns: pl.BlockSpec((rows, columns), lambda i, _: (i, 0))
    across = pl.BlockSpec((1, rows), lambda i, _: (0, i))
    fixed = lambda shape: pl.BlockSpec(shape, lambda i, _: (0, 0))
    shape = jax.ShapeDtypeStruct
    return pl.pallas_call(
        attend_back_kernel,
        grid_spec=pltpu.PrefetchScalarGridSpec(
            num_scalar_prefetch=1,
            grid=(total // rows,),
            in_specs=[
                block(width), pl.BlockSpec((dim, width), lambda i, which: (which[0], 0)),
                block(dim), block(dim), block(dim), block(dim), across, across, across,
                fixed((total, dim)), fixed((total, dim)), fixed((total, 1)),
                fixed((total, 2 * dim)), fixed((1, dim)), fixed((1, dim)),
                fixed((total, dim)), fixed((total, dim)),
            ],
            out_specs=[fixed((total, 3 * dim)), fixed((1, dim)), fixed((1, dim))],
            scratch_shapes=[pltpu.VMEM((total, dim), F32), pltpu.VMEM((total, dim), F32)],
        ),
        out_shape=[shape((total, 3 * dim), BF16), shape((1, dim), F32), shape((1, dim), F32)],
        compiler_params=pltpu.CompilerParams(vmem_limit_bytes=48 << 20),
        name="attend_back",
    )(
        group, grad_rows, w_out, queries, lin, cosine, sine, place_row, open_row, log_total,
        keys, values, place_column, lin, k_gain, q_gain, cosine, sine,
    )


def head_device(
    hidden_in,
    cotangent,
    layout,
    seq_lengths,
    expert_ids,
    drop_rank,
    norm1_gain,
    w_query,
    key_weight,
    value_weight,
    query_gain,
    key_gain,
    w_out,
    norm2_gain,
    w_router,
    w_gate,
    w_up,
    w_down,
):
    f32, bf16 = jnp.float32, jnp.bfloat16
    tok_rows, model_width = hidden_in.shape
    head_dim = query_gain.shape[0]
    expert_count = w_router.shape[1]
    local_count, _, ff_local = w_gate.shape
    groups = lax.axis_size("expert")
    tensor_size = lax.axis_size("tensor")
    total_rows = groups * tok_rows
    own_rows = tok_rows // tensor_size
    seq_count = seq_lengths.shape[0]
    group = lax.axis_index("expert")
    part = lax.axis_index("tensor")

    def own(rows):
        return lax.dynamic_slice_in_dim(rows, part * own_rows, own_rows, 0)

    which = jnp.reshape(group, (1,))
    tag = jnp.concatenate(
        [layout[None], drop_rank[None], expert_ids.T, jnp.zeros((6, tok_rows), jnp.int32)], axis=0
    )
    hidden_all, tags = gather_rows(own(hidden_in), tag)
    tags = jnp.transpose(tags, (1, 0, 2)).reshape(16, total_rows)
    place, rank, ids_t = tags[0], tags[1], tags[2:10]
    segment, position = token_tables(place, seq_lengths)
    valid = segment < seq_count
    cotangent_late, _ = lax.optimization_barrier((own(cotangent), tags))
    grad_y_all = lax.all_gather(cotangent_late, ("expert", "tensor"), axis=0, tiled=True)

    half_dim = head_dim // 2
    inverse = THETA ** (-(jnp.arange(half_dim, dtype=f32) * 2.0) / head_dim)
    angles = position.astype(f32)[:, None] * inverse[None, :]
    cosine, sine = jnp.cos(angles), jnp.sin(angles)
    cosine = jnp.concatenate([cosine, cosine], axis=1)
    sine = jnp.concatenate([-sine, sine], axis=1)
    q_gain, k_gain = query_gain[None], key_gain[None]
    normed1, queries, keys, values, lin = project(
        which, hidden_all, norm1_gain[None], w_query, key_weight, value_weight, q_gain, k_gain,
        cosine, sine,
    )
    place_row, open_row = place[None], (place - position)[None]
    place_column = place[:, None]
    attended, log_total, att_rows = attend(
        queries, keys, values, place_column, place_row, open_row
    )
    residual, normed2, normed2_all = branch_rows(
        att_rows, w_out, own(hidden_in), norm2_gain[None]
    )

    expert_range = jnp.arange(expert_count, dtype=jnp.int32)
    chosen = jnp.any(ids_t[:, :, None] == expert_range, axis=0)
    picks = (chosen & valid[:, None]).astype(bf16)
    earlier = (rank[None, :] < rank[:, None]).astype(bf16)
    slot = jnp.dot(earlier, picks, preferred_element_type=f32)
    kept = chosen & valid[:, None] & (slot < CAP)

    def gates(rows, picked):
        logits = jnp.dot(rows, w_router, preferred_element_type=f32)
        return jax.nn.softmax(jnp.where(picked, logits, -jnp.inf), axis=1)

    gate_weight = jnp.where(kept, gates(normed2_all, chosen), 0.0)
    gate_local = lax.dynamic_slice_in_dim(gate_weight, group * local_count, local_count, 1)
    kept_local = lax.dynamic_slice_in_dim(kept, group * local_count, local_count, 1)

    weight_in = jnp.concatenate([w_gate, w_up], axis=0)
    weight_in = jnp.transpose(weight_in, (1, 0, 2)).reshape(model_width, -1)
    weight_down = w_down.reshape(local_count * ff_local, model_width)
    wide = local_count * ff_local
    lin2 = jnp.dot(normed2_all, weight_in, preferred_element_type=f32)
    gate_lin, up_lin = lin2[:, :wide], lin2[:, wide:]
    sigmoid = jax.nn.sigmoid(gate_lin)
    silu = gate_lin * sigmoid
    spread = jnp.repeat(gate_local, ff_local, axis=1)
    activation = (silu * up_lin).astype(bf16).astype(f32)
    weighted = (activation * spread).astype(bf16)
    out_part = jnp.dot(weighted, weight_down, preferred_element_type=f32)
    grad_down = jnp.einsum("rf,rd->fd", weighted, grad_y_all, preferred_element_type=f32)
    grad_mid = jnp.einsum("rd,fd->rf", grad_y_all, weight_down, preferred_element_type=f32)
    dots = jnp.sum((activation * grad_mid).reshape(total_rows, local_count, ff_local), axis=2)
    dots = jnp.where(kept_local, dots, 0.0)
    grad_act = grad_mid * spread
    grad_gate_lin = (grad_act * up_lin * sigmoid * (1.0 + gate_lin * (1.0 - sigmoid))).astype(bf16)
    grad_up_lin = (grad_act * silu).astype(bf16)
    grad_lin2 = jnp.concatenate([grad_gate_lin, grad_up_lin], axis=1)
    grad_in = jnp.einsum("rd,rf->df", normed2_all, grad_lin2, preferred_element_type=f32)
    grad_in = jnp.transpose(
        grad_in.reshape(model_width, 2 * local_count, ff_local), (1, 0, 2)
    )
    grad_normed2_part = jnp.einsum(
        "rf,df->rd", grad_lin2, weight_in, preferred_element_type=f32
    )
    dots_wide = jnp.zeros((total_rows, head_dim), f32)
    dots_wide = lax.dynamic_update_slice(dots_wide, dots, (0, group * local_count))
    back = scatter_rows(
        jnp.concatenate([grad_normed2_part, dots_wide], axis=1).astype(bf16),
        2,
    )
    moe_branch = scatter_rows(out_part.astype(bf16), 4)
    out_own = (residual + moe_branch).astype(bf16)

    start = group * tok_rows + part * own_rows
    chosen_own = lax.dynamic_slice_in_dim(chosen, start, own_rows, 0)
    soft_own = gates(normed2, chosen_own)
    grad_soft = back[:, model_width : model_width + expert_count]
    grad_logits = (
        soft_own * (grad_soft - jnp.sum(soft_own * grad_soft, axis=1, keepdims=True))
    ).astype(bf16)
    grad_router = jnp.einsum("td,te->de", normed2, grad_logits, preferred_element_type=f32)
    grad_normed2 = back[:, :model_width] + jnp.einsum(
        "te,de->td", grad_logits, w_router, preferred_element_type=f32
    )
    norm2_pull = jax.vjp(norm_rows, residual, norm2_gain)[1]
    grad_resid_norm, grad_norm2 = norm2_pull(grad_normed2)
    grad_residual = own(cotangent).astype(f32) + grad_resid_norm
    grad_residual_all = gather_rows(grad_residual.astype(bf16))

    grad_out = jnp.einsum(
        "rc,rd->cd", attended, grad_residual_all, preferred_element_type=f32
    ).astype(bf16)
    grad_out_all = lax.all_gather(grad_out, "expert", axis=0, tiled=True)
    grad_residual_all, _ = lax.optimization_barrier((grad_residual_all, grad_out))
    grad_lin, grad_qgain, grad_kgain = attend_back(
        which, grad_residual_all, w_out, queries, lin, cosine, sine, place_row, open_row,
        log_total, keys, values, place_column, k_gain, q_gain,
    )
    head_query = lax.dynamic_slice_in_dim(w_query, group * head_dim, head_dim, 1)
    qkv_weight = jnp.concatenate([head_query, key_weight, value_weight], axis=1)
    grad_normed1_part = jnp.einsum(
        "tc,dc->td", grad_lin, qkv_weight, preferred_element_type=f32
    )
    grad_qkv = jnp.einsum(
        "td,tc->dc", normed1, grad_lin, preferred_element_type=f32
    ).astype(bf16)
    extra = jnp.zeros((model_width, head_dim), f32)
    router_rows = lax.dynamic_update_slice(extra, grad_router, (0, 0))
    extra = lax.dynamic_update_slice(router_rows, grad_norm2[:, None], (0, expert_count))
    extra = lax.dynamic_update_slice(extra, grad_qgain.T, (0, expert_count + 1))
    extra = lax.dynamic_update_slice(extra, grad_kgain.T, (0, expert_count + 2))
    reduced, kv_own = scatter_rows(
        jnp.concatenate([grad_normed1_part, extra], axis=1).astype(bf16),
        3,
        grad_qkv[:, head_dim:],
    )
    norm1_pull = jax.vjp(norm_rows, own(hidden_in).astype(f32), norm1_gain)[1]
    grad_hidden_norm, grad_norm1 = norm1_pull(reduced[:, :model_width])
    grad_hidden_own = (grad_residual + grad_hidden_norm).astype(bf16)
    extra_rows = own_rows * head_dim // model_width
    small = jnp.concatenate(
        [
            grad_norm1[None],
            reduced[:, model_width:].reshape(extra_rows, model_width),
            jnp.zeros((15 - extra_rows, model_width), f32),
        ],
        axis=0,
    ).astype(bf16)
    grad_query, grad_kv, small, ends = finish(
        grad_qkv[:, :head_dim], kv_own, small, jnp.concatenate([out_own, grad_hidden_own], axis=1), 5
    )
    grad_query, grad_kv, grad_out = (v.astype(f32) for v in (grad_query, grad_kv, grad_out_all))
    small = small.reshape(groups * tensor_size, 16, model_width).astype(f32)
    grad_norm1 = jnp.sum(small[:, 0], axis=0)
    extra = small[:, 1 : 1 + extra_rows].reshape(model_width, head_dim)
    grad_router = extra[:, :expert_count]
    grad_norm2 = extra[:, expert_count]
    grad_qgain, grad_kgain = extra[:head_dim, expert_count + 1], extra[:head_dim, expert_count + 2]
    grad_down = grad_down.reshape(local_count, ff_local, model_width)
    return (
        ends[:, :model_width],
        ends[:, model_width:],
        grad_norm1,
        grad_query,
        grad_kv[:, :head_dim],
        grad_kv[:, head_dim:],
        grad_qgain,
        grad_kgain,
        grad_out,
        grad_norm2,
        grad_router,
        grad_in[:local_count],
        grad_in[local_count:],
        grad_down,
    )


def solution(mesh):
    groups = mesh.shape["expert"]

    def device_fn(*operands):
        heads = operands[7].shape[1] // operands[10].shape[0]
        one_head = heads == groups == 8 and operands[8].shape[1] == operands[10].shape[0]
        one_head = one_head and mesh.shape["tensor"] == 4
        return (head_device if one_head else per_device)(*operands)

    return jax.shard_map(
        device_fn,
        mesh=mesh,
        in_specs=(
            P("expert", None),
            P("expert", None),
            P("expert"),
            P(),
            P("expert", None),
            P("expert"),
            P(),
            P(None, "tensor"),
            P(None, "tensor"),
            P(None, "tensor"),
            P(),
            P(),
            P("tensor", None),
            P(),
            P(),
            P("expert", None, "tensor"),
            P("expert", None, "tensor"),
            P("expert", "tensor", None),
        ),
        out_specs=(
            P("expert", None),
            P("expert", None),
            P(),
            P(None, "tensor"),
            P(None, "tensor"),
            P(None, "tensor"),
            P(),
            P(),
            P("tensor", None),
            P(),
            P(),
            P("expert", None, "tensor"),
            P("expert", None, "tensor"),
            P("expert", "tensor", None),
        ),
        check_vma=False,
    )
```

```python
from functools import partial
import math

import jax
import jax.numpy as jnp
from jax import lax
from jax.experimental import pallas as pl
from jax.experimental.pallas import tpu as pltpu
from jax.sharding import PartitionSpec as P

TOPK = 8
CAP = 1280


EPS = 1e-06
THETA = 1000000.0
NEG = -1e30


def norm_rows(value_matrix, gain):
    return (
        value_matrix
        * lax.rsqrt(jnp.mean(value_matrix * value_matrix, axis=-1, keepdims=True) + EPS)
        * gain
    )


def rotary(value_matrix, position):
    half_dim = value_matrix.shape[-1] // 2
    inverse = THETA ** (-(jnp.arange(half_dim, dtype=jnp.float32) * 2.0) / value_matrix.shape[-1])
    angles = position.astype(jnp.float32)[:, None] * inverse[None, :]
    cosine_table = jnp.concatenate([jnp.cos(angles), jnp.cos(angles)], axis=-1)[:, None, :]
    sine_table = jnp.concatenate([jnp.sin(angles), jnp.sin(angles)], axis=-1)[:, None, :]
    turned = jnp.concatenate([-value_matrix[..., half_dim:], value_matrix[..., :half_dim]], axis=-1)
    return value_matrix * cosine_table + turned * sine_table


def shape_queries(linear, gain, position):
    head_dim = gain.shape[0]
    shaped = linear.reshape(linear.shape[0], linear.shape[1] // head_dim, head_dim)
    return rotary(norm_rows(shaped, gain), position) * head_dim ** (-0.5)


def shape_keys(linear, gain, position):
    head_dim = gain.shape[0]
    shaped = linear.reshape(linear.shape[0], linear.shape[1] // head_dim, head_dim)
    return rotary(norm_rows(shaped, gain), position)


def token_tables(token_position, seq_lengths):
    bounds = jnp.cumsum(seq_lengths)
    passed = token_position[:, None] >= bounds[None, :]
    segment_ids = jnp.sum(passed.astype(jnp.int32), axis=1)
    opening = jnp.max(jnp.where(passed, bounds[None, :], 0), axis=1)
    return (segment_ids, (token_position - opening).astype(jnp.int32))


def visible(query_segment, query_place, key_segment, key_place):
    return (query_segment[:, None] == key_segment[None, :]) & (
        key_place[None, :] <= query_place[:, None]
    )


def deliver(payload, slot_ids):
    return (
        lax.all_to_all(payload, "expert", split_axis=0, concat_axis=0, tiled=True),
        lax.all_to_all(slot_ids, "expert", split_axis=0, concat_axis=0, tiled=True),
    )


def bring_back(payload):
    return lax.all_to_all(payload, "expert", split_axis=0, concat_axis=0, tiled=True)


def expert_forward(entry_rows, w_gate, w_up, w_down):
    gate_lin = jnp.einsum("gesd,edf->gesf", entry_rows, w_gate, preferred_element_type=jnp.float32)
    up_lin = jnp.einsum("gesd,edf->gesf", entry_rows, w_up, preferred_element_type=jnp.float32)
    activation = (jax.nn.silu(gate_lin) * up_lin).astype(jnp.bfloat16)
    expert_out = jnp.einsum(
        "gesf,efd->gesd", activation, w_down, preferred_element_type=jnp.float32
    ).astype(jnp.bfloat16)
    return (gate_lin, up_lin, activation, expert_out)


def expert_backward(entry_rows, gate_lin, up_lin, activation, grad_in, w_gate, w_up, w_down):
    grad_down = jnp.einsum(
        "gesf,gesd->efd", activation, grad_in, preferred_element_type=jnp.float32
    )
    grad_act = jnp.einsum("gesd,efd->gesf", grad_in, w_down, preferred_element_type=jnp.float32)
    sigmoid = jax.nn.sigmoid(gate_lin)
    grad_gate_lin = (grad_act * up_lin * sigmoid * (1.0 + gate_lin * (1.0 - sigmoid))).astype(
        jnp.bfloat16
    )
    grad_up_lin = (grad_act * gate_lin * sigmoid).astype(jnp.bfloat16)
    grad_w_gate = jnp.einsum(
        "gesd,gesf->edf", entry_rows, grad_gate_lin, preferred_element_type=jnp.float32
    )
    grad_w_up = jnp.einsum(
        "gesd,gesf->edf", entry_rows, grad_up_lin, preferred_element_type=jnp.float32
    )
    grad_entry = jnp.einsum(
        "gesf,edf->gesd", grad_gate_lin, w_gate, preferred_element_type=jnp.float32
    )
    grad_entry = (
        grad_entry
        + jnp.einsum("gesf,edf->gesd", grad_up_lin, w_up, preferred_element_type=jnp.float32)
    ).astype(jnp.bfloat16)
    return (grad_entry, grad_w_gate, grad_w_up, grad_down)


def per_device(
    hidden_in,
    cotangent,
    layout,
    seq_lengths,
    expert_ids,
    drop_rank,
    norm1_gain,
    w_query,
    key_weight,
    value_weight,
    query_gain,
    key_gain,
    w_out,
    norm2_gain,
    w_router,
    w_gate,
    w_up,
    w_down,
):
    tok_rows = hidden_in.shape[0]
    model_width = hidden_in.shape[1]
    head_dim = query_gain.shape[0]
    local_heads = w_query.shape[1] // head_dim
    expert_count = w_router.shape[1]
    local_count = w_gate.shape[0]
    group_count = lax.axis_size("expert")
    slot_count = 2 * tok_rows * TOPK // expert_count
    seq_count = seq_lengths.shape[0]
    expert_range = jnp.arange(expert_count, dtype=jnp.int32)
    hidden = hidden_in.astype(jnp.float32)
    segment_ids, position = token_tables(layout, seq_lengths)
    valid = segment_ids < seq_count
    first_normalized = norm_rows(hidden, norm1_gain)
    normed1_low = first_normalized.astype(jnp.bfloat16)
    query_lin = jnp.dot(normed1_low, w_query, preferred_element_type=jnp.float32)
    key_lin = jnp.dot(normed1_low, key_weight, preferred_element_type=jnp.float32)
    value_lin = jnp.dot(normed1_low, value_weight, preferred_element_type=jnp.float32)
    query_shaped = shape_queries(query_lin, query_gain, position).astype(jnp.bfloat16)
    query_total = local_heads * tok_rows
    query_rows = jnp.transpose(query_shaped, (1, 0, 2)).reshape(query_total, head_dim)
    key_rows = (
        shape_keys(key_lin, key_gain, position).astype(jnp.bfloat16).reshape(tok_rows, head_dim)
    )
    value_rows = value_lin.astype(jnp.bfloat16)
    all_keys, all_values, all_place, all_ids, all_rank = (
        lax.all_gather(key_rows, "expert", axis=0, tiled=True),
        lax.all_gather(value_rows, "expert", axis=0, tiled=True),
        lax.all_gather(layout, "expert", axis=0, tiled=True),
        lax.all_gather(expert_ids, "expert", axis=0, tiled=True),
        lax.all_gather(drop_rank, "expert", axis=0, tiled=True),
    )
    all_segment = token_tables(all_place, seq_lengths)[0]
    rows_per_block = math.gcd(512, query_total)
    count_of_blocks = query_total // rows_per_block
    query_segment = jnp.tile(segment_ids, local_heads)
    query_place = jnp.tile(layout, local_heads)

    def attend_block(operands):
        query_block, segment_block, place_block = operands
        scores = jnp.einsum("qd,kd->qk", query_block, all_keys, preferred_element_type=jnp.float32)
        scores = jnp.where(visible(segment_block, place_block, all_segment, all_place), scores, NEG)
        highest = jnp.max(scores, axis=1, keepdims=True)
        weights = jnp.exp(scores - highest)
        totals = jnp.sum(weights, axis=1, keepdims=True)
        probability = (weights / totals).astype(jnp.bfloat16)
        mixed_out = jnp.dot(probability, all_values, preferred_element_type=jnp.float32)
        return (mixed_out, (highest + jnp.log(totals))[:, 0])

    attention_output, log_totals = lax.map(
        attend_block,
        (
            query_rows.reshape(count_of_blocks, rows_per_block, head_dim),
            query_segment.reshape(count_of_blocks, rows_per_block),
            query_place.reshape(count_of_blocks, rows_per_block),
        ),
    )
    attention_output = attention_output.reshape(local_heads, tok_rows, head_dim).astype(
        jnp.bfloat16
    )
    att_cat = jnp.transpose(attention_output, (1, 0, 2)).reshape(tok_rows, local_heads * head_dim)
    branch_part = jnp.dot(att_cat, w_out, preferred_element_type=jnp.float32)
    branch = lax.psum(branch_part, "tensor")
    residual = hidden + branch
    normed2 = norm_rows(residual, norm2_gain)
    normed2_low = normed2.astype(jnp.bfloat16)
    logits = jnp.dot(normed2_low, w_router, preferred_element_type=jnp.float32)
    soft_gate = jax.nn.softmax(jnp.take_along_axis(logits, expert_ids, axis=1), axis=1)
    picks = jnp.any(expert_ids[:, :, None] == expert_range, axis=1) & valid[:, None]
    all_valid = all_segment < seq_count
    all_picks = jnp.any(all_ids[:, :, None] == expert_range, axis=1) & all_valid[:, None]
    earlier = (all_rank[None, :] < drop_rank[:, None]).astype(jnp.bfloat16)
    before_counts = jnp.dot(
        earlier, all_picks.astype(jnp.bfloat16), preferred_element_type=jnp.float32
    )
    global_slot = jnp.take_along_axis(before_counts, expert_ids, axis=1).astype(jnp.int32)
    kept_mask = (global_slot < CAP) & valid[:, None]
    gate_weight = soft_gate * kept_mask.astype(jnp.float32)
    lower_rows = (jnp.arange(tok_rows)[None, :] < jnp.arange(tok_rows)[:, None]).astype(
        jnp.bfloat16
    )
    local_counts = jnp.dot(
        lower_rows, picks.astype(jnp.bfloat16), preferred_element_type=jnp.float32
    )
    local_slot = jnp.take_along_axis(local_counts, expert_ids, axis=1).astype(jnp.int32)
    pair_count = tok_rows * TOPK
    dump_index = expert_count * slot_count
    target = jnp.where(kept_mask, expert_ids * slot_count + local_slot, dump_index)
    pair_index = jnp.arange(pair_count, dtype=jnp.int32)
    slot_pair = (
        jnp.full((dump_index,), pair_count, jnp.int32)
        .at[target.reshape(-1)]
        .set(pair_index, mode="drop")
    )
    slot_token = jnp.where(slot_pair < pair_count, slot_pair // TOPK, tok_rows)
    slot_global = (
        jnp.full((dump_index,), -1, jnp.int32)
        .at[target.reshape(-1)]
        .set(global_slot.reshape(-1), mode="drop")
    )
    padded_rows = jnp.concatenate([normed2_low, jnp.zeros((1, model_width), jnp.bfloat16)], axis=0)
    send_rows = padded_rows[slot_token].reshape(group_count, local_count, slot_count, model_width)
    send_slot = slot_global.reshape(group_count, local_count, slot_count)
    received, received_slot = deliver(send_rows, send_slot)
    gate_lin, up_lin, activation, expert_out = expert_forward(received, w_gate, w_up, w_down)
    returned = bring_back(expert_out)
    returned_flat = jnp.concatenate(
        [returned.reshape(dump_index, model_width), jnp.zeros((1, model_width), returned.dtype)],
        axis=0,
    )
    pair_out = returned_flat[target]
    moe_part = jnp.sum(gate_weight[:, :, None] * pair_out, axis=1)
    moe_branch = lax.psum(moe_part.astype(jnp.bfloat16), "tensor").astype(jnp.float32)
    out_hidden = (residual + moe_branch).astype(jnp.bfloat16)
    grad_y = cotangent.astype(jnp.float32)
    gate_dot = jnp.sum(grad_y[:, None, :] * pair_out, axis=2)
    pair_grads = (
        (gate_weight[:, :, None] * grad_y[:, None, :])
        .astype(jnp.bfloat16)
        .reshape(pair_count, model_width)
    )
    pair_grads = jnp.concatenate([pair_grads, jnp.zeros((1, model_width), jnp.bfloat16)], axis=0)
    send_grad = pair_grads[slot_pair].reshape(group_count, local_count, slot_count, model_width)
    grad_received, grad_slot = deliver(send_grad, send_slot)
    grad_entry, grad_w_gate, grad_w_up, grad_w_down = expert_backward(
        received, gate_lin, up_lin, activation, grad_received, w_gate, w_up, w_down
    )
    grad_returned = bring_back(grad_entry)
    grad_flat = jnp.concatenate(
        [
            grad_returned.reshape(dump_index, model_width),
            jnp.zeros((1, model_width), grad_returned.dtype),
        ],
        axis=0,
    )
    grad_normed2_part = jnp.sum(grad_flat[target], axis=1, dtype=jnp.float32)
    grad_normed2_exp, gate_dot = lax.psum((grad_normed2_part, gate_dot), "tensor")
    grad_soft = gate_dot * kept_mask.astype(jnp.float32)
    grad_chosen = soft_gate * (grad_soft - jnp.sum(soft_gate * grad_soft, axis=1, keepdims=True))
    grad_logits = jnp.sum(
        grad_chosen[:, :, None] * (expert_ids[:, :, None] == expert_range).astype(jnp.float32),
        axis=1,
    ).astype(jnp.bfloat16)
    grad_w_router = jnp.einsum(
        "td,te->de", normed2_low, grad_logits, preferred_element_type=jnp.float32
    )
    grad_normed2 = grad_normed2_exp + jnp.einsum(
        "te,de->td", grad_logits, w_router, preferred_element_type=jnp.float32
    )
    norm2_pull = jax.vjp(norm_rows, residual, norm2_gain)[1]
    grad_resid_norm, grad_norm2 = norm2_pull(grad_normed2)
    grad_residual = grad_y + grad_resid_norm
    grad_residual_low = grad_residual.astype(jnp.bfloat16)
    grad_w_out = jnp.einsum(
        "tc,td->cd", att_cat, grad_residual_low, preferred_element_type=jnp.float32
    )
    grad_att_cat = jnp.einsum(
        "td,cd->tc", grad_residual_low, w_out, preferred_element_type=jnp.float32
    ).astype(jnp.bfloat16)
    grad_att_rows = jnp.transpose(
        grad_att_cat.reshape(tok_rows, local_heads, head_dim), (1, 0, 2)
    ).reshape(query_total, head_dim)

    def query_grad_block(operands):
        query_block, segment_block, place_block, grad_block, log_block = operands
        scores = jnp.einsum("qd,kd->qk", query_block, all_keys, preferred_element_type=jnp.float32)
        scores = jnp.where(visible(segment_block, place_block, all_segment, all_place), scores, NEG)
        probability = jnp.exp(scores - log_block[:, None])
        grad_prob = jnp.einsum(
            "qd,kd->qk", grad_block, all_values, preferred_element_type=jnp.float32
        )
        delta_row = jnp.sum(probability * grad_prob, axis=1)
        grad_scores = (probability * (grad_prob - delta_row[:, None])).astype(jnp.bfloat16)
        return (jnp.dot(grad_scores, all_keys, preferred_element_type=jnp.float32), delta_row)

    grad_query_rows, deltas = lax.map(
        query_grad_block,
        (
            query_rows.reshape(count_of_blocks, rows_per_block, head_dim),
            query_segment.reshape(count_of_blocks, rows_per_block),
            query_place.reshape(count_of_blocks, rows_per_block),
            grad_att_rows.reshape(count_of_blocks, rows_per_block, head_dim),
            log_totals,
        ),
    )
    log_flat = log_totals.reshape(query_total)
    delta_flat = deltas.reshape(query_total)
    key_block = math.gcd(lax.axis_size("expert") * tok_rows, 2048)

    def one_block(offset):
        key_part = lax.dynamic_slice_in_dim(all_keys, offset, key_block, 0)
        value_part = lax.dynamic_slice_in_dim(all_values, offset, key_block, 0)
        segment_part = lax.dynamic_slice_in_dim(all_segment, offset, key_block, 0)
        place_part = lax.dynamic_slice_in_dim(all_place, offset, key_block, 0)
        scores = jnp.einsum("qd,kd->qk", query_rows, key_part, preferred_element_type=jnp.float32)
        scores = jnp.where(
            visible(query_segment, query_place, segment_part, place_part), scores, NEG
        )
        probability = jnp.exp(scores - log_flat[:, None])
        grad_value = jnp.einsum(
            "qk,qd->kd",
            probability.astype(jnp.bfloat16),
            grad_att_rows,
            preferred_element_type=jnp.float32,
        )
        grad_prob = jnp.einsum(
            "qd,kd->qk", grad_att_rows, value_part, preferred_element_type=jnp.float32
        )
        grad_scores = (probability * (grad_prob - delta_flat[:, None])).astype(jnp.bfloat16)
        grad_key = jnp.einsum(
            "qk,qd->kd", grad_scores, query_rows, preferred_element_type=jnp.float32
        )
        return jnp.concatenate([grad_key, grad_value], axis=1)

    stacked = lax.map(
        one_block,
        jnp.arange(lax.axis_size("expert") * tok_rows // key_block, dtype=jnp.int32) * key_block,
    )
    key_value_grad = lax.psum_scatter(
        stacked.reshape(lax.axis_size("expert") * tok_rows, 2 * head_dim).astype(jnp.bfloat16),
        "expert",
        scatter_dimension=0,
        tiled=True,
    ).astype(jnp.float32)
    grad_key_post = key_value_grad[:, :head_dim].reshape(tok_rows, 1, head_dim)
    grad_values_low = key_value_grad[:, head_dim:].astype(jnp.bfloat16)
    grad_query_tok = jnp.transpose(
        grad_query_rows.reshape(local_heads, tok_rows, head_dim), (1, 0, 2)
    )
    query_pull = jax.vjp(partial(shape_queries, position=position), query_lin, query_gain)[1]
    grad_query_lin, grad_qgain_part = query_pull(grad_query_tok)
    key_pull = jax.vjp(partial(shape_keys, position=position), key_lin, key_gain)[1]
    grad_key_lin, grad_kgain_part = key_pull(grad_key_post)
    grad_query_low = grad_query_lin.astype(jnp.bfloat16)
    grad_key_low = grad_key_lin.astype(jnp.bfloat16)
    grad_w_query = jnp.einsum(
        "td,tc->dc", normed1_low, grad_query_low, preferred_element_type=jnp.float32
    )
    grad_w_key = jnp.einsum(
        "td,tc->dc", normed1_low, grad_key_low, preferred_element_type=jnp.float32
    )
    grad_w_value = jnp.einsum(
        "td,tc->dc", normed1_low, grad_values_low, preferred_element_type=jnp.float32
    )
    grad_normed1_part = jnp.einsum(
        "tc,dc->td", grad_query_low, w_query, preferred_element_type=jnp.float32
    )
    grad_normed1_part = grad_normed1_part + jnp.einsum(
        "tc,dc->td", grad_key_low, key_weight, preferred_element_type=jnp.float32
    )
    grad_normed1_part = grad_normed1_part + jnp.einsum(
        "tc,dc->td", grad_values_low, value_weight, preferred_element_type=jnp.float32
    )
    grad_normed1, grad_qgain_part, grad_kgain_part = (
        lax.psum(grad_normed1_part.astype(jnp.bfloat16), "tensor").astype(jnp.float32),
        lax.psum(grad_qgain_part.astype(jnp.bfloat16), "tensor").astype(jnp.float32),
        lax.psum(grad_kgain_part.astype(jnp.bfloat16), "tensor").astype(jnp.float32),
    )
    norm1_pull = jax.vjp(norm_rows, hidden, norm1_gain)[1]
    grad_hidden_norm, grad_norm1 = norm1_pull(grad_normed1)
    grad_hidden = (grad_residual + grad_hidden_norm).astype(jnp.bfloat16)
    summed = (
        lax.psum(grad_norm1.astype(jnp.bfloat16), "expert").astype(jnp.float32),
        lax.psum(grad_w_query.astype(jnp.bfloat16), "expert").astype(jnp.float32),
        lax.psum(grad_w_key.astype(jnp.bfloat16), "expert").astype(jnp.float32),
        lax.psum(grad_w_value.astype(jnp.bfloat16), "expert").astype(jnp.float32),
        lax.psum(grad_qgain_part.astype(jnp.bfloat16), "expert").astype(jnp.float32),
        lax.psum(grad_kgain_part.astype(jnp.bfloat16), "expert").astype(jnp.float32),
        lax.psum(grad_w_out.astype(jnp.bfloat16), "expert").astype(jnp.float32),
        lax.psum(grad_norm2.astype(jnp.bfloat16), "expert").astype(jnp.float32),
        lax.psum(grad_w_router.astype(jnp.bfloat16), "expert").astype(jnp.float32),
    )
    return (
        out_hidden,
        grad_hidden,
        summed[0],
        summed[1],
        summed[2],
        summed[3],
        summed[4],
        summed[5],
        summed[6],
        summed[7],
        summed[8],
        grad_w_gate,
        grad_w_up,
        grad_w_down,
    )


MESH = pl.DeviceIdType.MESH
FAR_FIRST = (3, -3, 2, -2, 1, -1, 0)


class Spot:
    def __init__(self):
        group, part = lax.axis_index("expert"), lax.axis_index("tensor")
        self.z, self.y = group // 2, group % 2
        self.x, self.c = part // 2, part % 2

    def has(self, dz):
        return (self.z + dz >= 0) & (self.z + dz <= 3)

    def device(self, dz=0, dy=0, dx=0, dc=0):
        y = 1 - self.y if dy else self.y
        x = 1 - self.x if dx else self.x
        c = 1 - self.c if dc else self.c
        return ((self.z + dz) * 2 + y, x * 2 + c)

    def rows(self, dz, dy, dx, dc, count):
        group, part = self.device(dz, dy, dx, dc)
        return pl.ds(pl.multiple_of((group * 4 + part) * count, count), count)

    def greet(self):
        barrier = pltpu.get_barrier_semaphore()
        for step in ((0, 1, 0, 0), (0, 0, 1, 0), (0, 0, 0, 1)):
            pl.semaphore_signal(barrier, inc=1, device_id=self.device(*step), device_id_type=MESH)
        for dz in (1, -1):

            @pl.when(self.has(dz))
            def _(dz=dz):
                pl.semaphore_signal(
                    barrier, inc=1, device_id=self.device(dz), device_id_type=MESH
                )

        inner = jnp.where((self.z > 0) & (self.z < 3), 1, 0)
        pl.semaphore_wait(barrier, 4 + inner)


def when_has(spot, dz, action):
    if dz == 0:
        action()
    else:
        pl.when(spot.has(dz))(action)


def gather_body(
    spot, src, out, recv, z_send, y_send, x_send, c_send, c_recv, local_sem, also=lambda *_: None
):
    count, width = src.shape
    half = width // 2
    first, second, whole = pl.ds(0, half), pl.ds(half, half), pl.ds(0, width)
    local = pltpu.make_async_copy(src, out.at[spot.rows(0, 0, 0, 0, count), :], local_sem)
    local.start()

    def send(dz, dy, dx, columns, send_sem, recv_sem, device):
        place = out.at[spot.rows(dz, dy, dx, 0, count), columns]
        own = dz == 0 and dy == 0 and dx == 0
        copy = pltpu.make_async_remote_copy(
            src_ref=src.at[:, columns] if own else place,
            dst_ref=place,
            send_sem=send_sem,
            recv_sem=recv_sem,
            device_id=device,
            device_id_type=MESH,
        )
        copy.start()

    def await_bytes(rows, columns, sem):
        view = out.at[pl.ds(0, rows), columns]
        pltpu.make_async_copy(view, view, sem).wait()

    to_y, to_x, to_c = spot.device(0, 1), spot.device(0, 0, 1), spot.device(0, 0, 0, 1)

    def spread(dz):
        also("spread", dz)
        if dz <= 0:

            @pl.when(spot.has(1))
            def _():
                send(dz, 0, 0, whole, z_send.at[dz + 3, 0], recv.at[0, dz + 2], spot.device(1))

        if dz >= 0:

            @pl.when(spot.has(-1))
            def _():
                send(dz, 0, 0, whole, z_send.at[dz + 3, 1], recv.at[0, dz + 4], spot.device(-1))

        send(dz, 0, 0, whole, y_send, recv.at[1, dz + 3], to_y)
        send(dz, 0, 0, whole, x_send, recv.at[2, dz + 3], to_x)
        send(dz, 0, 0, whole, c_send, c_recv, to_c)

    def take_z(dz):
        def action():
            await_bytes(count, whole, recv.at[0, dz + 3])
            also("take", dz)
            spread(dz)

        when_has(spot, dz, action)

    def take_yx(dz):
        def action():
            await_bytes(count, whole, recv.at[1, dz + 3])
            send(dz, 1, 0, first, x_send, recv.at[3, dz + 3], to_x)
            send(dz, 1, 0, whole, c_send, c_recv, to_c)
            await_bytes(count, whole, recv.at[2, dz + 3])
            send(dz, 0, 1, second, y_send, recv.at[4, dz + 3], to_y)
            send(dz, 0, 1, whole, c_send, c_recv, to_c)

        when_has(spot, dz, action)

    def take_diagonal(dz):
        def action():
            await_bytes(count, first, recv.at[3, dz + 3])
            await_bytes(count, second, recv.at[4, dz + 3])
            send(dz, 1, 1, whole, c_send, c_recv, to_c)

        when_has(spot, dz, action)

    spread(0)
    for dz in (1, -1):
        take_z(dz)
    take_yx(0)
    for dz in (2, -2):
        take_z(dz)
    for dz in (1, -1):
        take_yx(dz)
    take_diagonal(0)
    for dz in (3, -3):
        take_z(dz)
    for dz in (2, -2):
        take_yx(dz)
    for dz in (1, -1):
        take_diagonal(dz)
    for dz in (3, -3):
        take_yx(dz)
    for dz in (2, -2, 3, -3):
        take_diagonal(dz)

    await_bytes(16 * count, whole, c_recv)
    await_bytes(16 * count, whole, c_send)
    await_bytes(6 * count, whole, y_send)
    await_bytes(6 * count, whole, x_send)
    for dz in range(-3, 4):
        for side, step in ((0, 1), (1, -1)):
            if dz * step <= 0:

                @pl.when(spot.has(dz) & spot.has(step))
                def _(dz=dz, side=side):
                    await_bytes(count, whole, z_send.at[dz + 3, side])

    local.wait()


GATHER_SEMS = ((5, 7), (7, 2), None, None, None, None, None)


def dma_sems(shapes):
    return [pltpu.SemaphoreType.DMA(shape) if shape else pltpu.SemaphoreType.DMA for shape in shapes]


def gather_kernel(src, out, *sems):
    spot = Spot()
    spot.greet()
    gather_body(spot, src, out, *sems)


def gather_tagged_kernel(src, tag, out, tag_out, *refs):
    sems, (tag_z, tag_y, tag_z_send, tag_y_send, tag_local) = refs[:7], refs[7:]
    spot = Spot()

    def place(dz, dy):
        return tag_out.at[spot.device(dz, dy)[0]]

    own = pltpu.make_async_copy(tag, place(0, 0), tag_local)
    own.start()
    spot.greet()

    def also(what, dz):
        here = place(dz, 0)
        source = tag if dz == 0 else here
        if what == "take":
            arrive(here, tag_z.at[dz + 3])
            return
        if dz <= 0:

            @pl.when(spot.has(1))
            def _():
                push(source, here, tag_z_send.at[dz + 3, 0], tag_z.at[dz + 2], spot.device(1))

        if dz >= 0:

            @pl.when(spot.has(-1))
            def _():
                push(source, here, tag_z_send.at[dz + 3, 1], tag_z.at[dz + 4], spot.device(-1))

        push(source, here, tag_y_send.at[dz + 3], tag_y.at[dz + 3], spot.device(0, 1))

    gather_body(spot, src, out, *sems, also=also)
    for dz in range(-3, 4):

        def action(dz=dz):
            arrive(place(dz, 1), tag_y.at[dz + 3])
            arrive(place(dz, 0), tag_y_send.at[dz + 3])
            for side, step in ((0, 1), (1, -1)):
                if dz * step <= 0:

                    @pl.when(spot.has(step))
                    def _():
                        arrive(place(dz, 0), tag_z_send.at[dz + 3, side])

        when_has(spot, dz, action)
    own.wait()


def gather_rows(rows, tag=None):
    count, width = rows.shape
    hbm = pl.BlockSpec(memory_space=pl.ANY)
    shape = jax.ShapeDtypeStruct((32 * count, width), rows.dtype)
    if tag is None:
        return pl.pallas_call(
            gather_kernel,
            out_shape=shape,
            in_specs=[hbm],
            out_specs=hbm,
            scratch_shapes=dma_sems(GATHER_SEMS),
            compiler_params=pltpu.CompilerParams(collective_id=0, has_side_effects=True),
            name="gather_rows",
        )(rows)
    return pl.pallas_call(
        gather_tagged_kernel,
        out_shape=(shape, jax.ShapeDtypeStruct((8,) + tag.shape, tag.dtype)),
        in_specs=[hbm, hbm],
        out_specs=(hbm, hbm),
        scratch_shapes=dma_sems(GATHER_SEMS + ((7,), (7,), (7, 2), (7,), None)),
        compiler_params=pltpu.CompilerParams(collective_id=1, has_side_effects=True),
        name="gather_tagged",
    )(rows, tag)


def add_into(into, chunk, *terms):
    @pl.loop(0, into.shape[0] // chunk)
    def _(step):
        rows = pl.ds(pl.multiple_of(step * chunk, chunk), chunk)
        total = into[rows, :].astype(jnp.float32)
        for term in terms:
            total = total + term[rows, :].astype(jnp.float32)
        into[rows, :] = total.astype(into.dtype)


def push(src, dst, send_sem, recv_sem, device):
    pltpu.make_async_remote_copy(
        src_ref=src,
        dst_ref=dst,
        send_sem=send_sem,
        recv_sem=recv_sem,
        device_id=device,
        device_id_type=MESH,
    ).start()


def arrive(view, sem):
    pltpu.make_async_copy(view, view, sem).wait()


def scatter_kernel(split, with_kv, *refs):
    refs = list(refs)
    part = refs.pop(0)
    kv_part = refs.pop(0) if with_kv else None
    out = refs.pop(0)
    kv_out = refs.pop(0) if with_kv else None
    held, from_a, from_b, from_y, from_x, from_below, from_above = refs[:7]
    c_recv, recv, z_send, half_send, y_send, x_send, c_send = refs[7:14]
    if with_kv:
        kv_held, kv_y, kv_below, kv_above, kv_recv, kv_z_send, kv_send = refs[14:]
    count, width = out.shape
    first, second, whole = pl.ds(0, split), pl.ds(split, width - split), pl.ds(0, width)
    spot = Spot()
    spot.greet()
    to_y, to_x, to_c = spot.device(0, 1), spot.device(0, 0, 1), spot.device(0, 0, 0, 1)
    groups = ((1, 1), (1, 0), (0, 1), (0, 0))
    for dy, dx in groups:
        for dz in FAR_FIRST:

            def action(dz=dz, dy=dy, dx=dx):
                push(
                    part.at[spot.rows(dz, dy, dx, 1, count), :],
                    held.at[spot.z + dz, dy, dx],
                    c_send,
                    c_recv.at[dz + 3, dy, dx],
                    to_c,
                )

            when_has(spot, dz, action)

    def kv_rows(dz, dy):
        group, _ = spot.device(dz, dy)
        return pl.ds(pl.multiple_of(group * 256, 256), 256)

    if with_kv:
        for dz in FAR_FIRST:

            def action(dz=dz):
                push(
                    kv_part.at[kv_rows(dz, 1), :],
                    kv_y.at[spot.z + dz],
                    kv_send,
                    kv_recv.at[0, dz + 3],
                    to_y,
                )

            when_has(spot, dz, action)

    def merge(dz, dy, dx):
        mine = held.at[spot.z + dz, dy, dx]
        arrive(mine, c_recv.at[dz + 3, dy, dx])
        add_into(mine, 16, part.at[spot.rows(dz, dy, dx, 0, count), :])
        return mine

    for dz in FAR_FIRST:

        def action(dz=dz):
            far = spot.z + dz
            mine = merge(dz, 1, 1)
            push(mine.at[:, first], from_a.at[far], half_send.at[0], recv.at[0, dz + 3], to_x)
            push(mine.at[:, second], from_b.at[far], half_send.at[1], recv.at[1, dz + 3], to_y)

        when_has(spot, dz, action)

    def line(dz, mine, chunk, below, above, sems, sends):
        far = spot.z + dz
        if dz >= 0:

            @pl.when(spot.has(-1))
            def _():
                arrive(below.at[far], sems[0].at[dz + 3])
                add_into(mine, chunk, below.at[far])

        if dz <= 0:

            @pl.when(spot.has(1))
            def _():
                arrive(above.at[far], sems[1].at[dz + 3])
                add_into(mine, chunk, above.at[far])

        if dz > 0:
            push(mine, below.at[far], sends.at[dz + 3], sems[0].at[dz + 2], spot.device(1))
        if dz < 0:
            push(mine, above.at[far], sends.at[dz + 3], sems[1].at[dz + 4], spot.device(-1))

    for dz in FAR_FIRST:

        def action(dz=dz):
            far = spot.z + dz
            mine = merge(dz, 1, 0)
            arrive(from_a.at[far], recv.at[0, dz + 3])
            add_into(mine.at[:, first], 16, from_a.at[far])
            push(mine, from_y.at[far], y_send, recv.at[2, dz + 3], to_y)
            mine = merge(dz, 0, 1)
            arrive(from_b.at[far], recv.at[1, dz + 3])
            add_into(mine.at[:, second], 16, from_b.at[far])
            push(mine, from_x.at[far], x_send, recv.at[3, dz + 3], to_x)
            if with_kv:
                kv_mine = kv_held.at[far]
                kv_mine[...] = kv_part[kv_rows(dz, 0), :]
                arrive(kv_y.at[far], kv_recv.at[0, dz + 3])
                add_into(kv_mine, 64, kv_y.at[far])
                line(
                    dz, kv_mine, 64, kv_below, kv_above,
                    (kv_recv.at[1], kv_recv.at[2]), kv_z_send,
                )

        when_has(spot, dz, action)
    for dz in FAR_FIRST:

        def action(dz=dz):
            far = spot.z + dz
            mine = merge(dz, 0, 0)
            arrive(from_y.at[far], recv.at[2, dz + 3])
            arrive(from_x.at[far], recv.at[3, dz + 3])
            add_into(mine, 16, from_y.at[far], from_x.at[far])
            line(dz, mine, 16, from_below, from_above, (recv.at[4], recv.at[5]), z_send)
            if dz == 0:
                out[...] = mine[...].astype(out.dtype)
                if with_kv:
                    kv_out[...] = kv_held[far].astype(kv_out.dtype)

        when_has(spot, dz, action)

    def await_view(rows, columns, sem):
        view = part.at[pl.ds(0, rows), columns]
        pltpu.make_async_copy(view, view, sem).wait()

    await_view(16 * count, whole, c_send)
    await_view(4 * count, whole, y_send)
    await_view(4 * count, whole, x_send)
    arrive(from_a, half_send.at[0])
    arrive(from_b, half_send.at[1])
    if with_kv:
        view = kv_part.at[pl.ds(0, 1024), :]
        pltpu.make_async_copy(view, view, kv_send).wait()
    for dz in FAR_FIRST[:-1]:

        def action(dz=dz):
            await_view(count, whole, z_send.at[dz + 3])
            if with_kv:
                view = kv_part.at[pl.ds(0, 256), :]
                pltpu.make_async_copy(view, view, kv_z_send.at[dz + 3]).wait()

        when_has(spot, dz, action)


def scatter_rows(partial_rows, ident, kv_partial=None):
    total, width = partial_rows.shape
    count = total // 32
    with_kv = kv_partial is not None
    dma, bf16 = pltpu.SemaphoreType.DMA, jnp.bfloat16
    split = 1536 if with_kv else 1024
    line = pltpu.VMEM((4, count, width), bf16)
    scratch = [
        pltpu.VMEM((4, 2, 2, count, width), bf16),
        pltpu.VMEM((4, count, split), bf16),
        pltpu.VMEM((4, count, width - split), bf16),
        line, line, line, line,
        dma((7, 2, 2)), dma((6, 7)), dma((7,)), dma((2,)), dma, dma, dma,
    ]
    vmem = pl.BlockSpec(memory_space=pltpu.VMEM)
    out_shape = jax.ShapeDtypeStruct((count, width), jnp.float32)
    if with_kv:
        kv_line = pltpu.VMEM((4, 256, kv_partial.shape[1]), bf16)
        scratch += [kv_line, kv_line, kv_line, kv_line, dma((3, 7)), dma((7,)), dma]
        out_shape = (out_shape, jax.ShapeDtypeStruct((256, kv_partial.shape[1]), bf16))
    return pl.pallas_call(
        partial(scatter_kernel, split, with_kv),
        out_shape=out_shape,
        in_specs=[vmem] * (2 if with_kv else 1),
        out_specs=(vmem, vmem) if with_kv else vmem,
        scratch_shapes=scratch,
        compiler_params=pltpu.CompilerParams(
            collective_id=ident, has_side_effects=True, vmem_limit_bytes=48 << 20
        ),
        name="scatter_rows_kv" if with_kv else "scatter_rows",
    )(*((partial_rows, kv_partial) if with_kv else (partial_rows,)))


def finish_kernel(
    query, kv, small, ends, query_out, kv_out, small_out, ends_out,
    z_recv, y_recv, x_recv, z_send, total_send, total_recv, local_sem,
):
    spot = Spot()
    dim = query.shape[1]
    few, many = small.shape[0], ends.shape[0]

    def query_at(dz, dy):
        group, _ = spot.device(dz, dy)
        return query_out.at[:, pl.ds(pl.multiple_of(group * dim, dim), dim)]

    def kv_at(dz, dy):
        group, _ = spot.device(dz, dy)
        return kv_out.at[pl.ds(pl.multiple_of(group * 256, 256), 256), :]

    def small_at(dz, dy, dx, dc):
        return small_out.at[spot.rows(dz, dy, dx, dc, few), :]

    def ends_at(dx, dc):
        _, part = spot.device(0, 0, dx, dc)
        return ends_out.at[pl.ds(pl.multiple_of(part * many, many), many), :]

    locals_ = [
        pltpu.make_async_copy(query, query_at(0, 0), local_sem.at[0]),
        pltpu.make_async_copy(kv, kv_at(0, 0), local_sem.at[1]),
        pltpu.make_async_copy(small, small_at(0, 0, 0, 0), local_sem.at[2]),
        pltpu.make_async_copy(ends, ends_at(0, 0), local_sem.at[3]),
    ]
    for copy in locals_:
        copy.start()
    spot.greet()
    to_y, to_x, to_c = spot.device(0, 1), spot.device(0, 0, 1), spot.device(0, 0, 0, 1)

    def spread(dz):
        own = dz == 0
        goods = (
            (small if own else small_at(dz, 0, 0, 0), small_at(dz, 0, 0, 0)),
            (kv if own else kv_at(dz, 0), kv_at(dz, 0)),
            (query if own else query_at(dz, 0), query_at(dz, 0)),
        )
        for kind, (src, dst) in enumerate(goods):
            if dz <= 0:

                @pl.when(spot.has(1))
                def _(kind=kind, src=src, dst=dst):
                    push(src, dst, z_send.at[kind, dz + 3, 0], z_recv.at[kind, dz + 2],
                         spot.device(1))

            if dz >= 0:

                @pl.when(spot.has(-1))
                def _(kind=kind, src=src, dst=dst):
                    push(src, dst, z_send.at[kind, dz + 3, 1], z_recv.at[kind, dz + 4],
                         spot.device(-1))

            push(src, dst, total_send.at[kind], y_recv.at[kind, dz + 3], to_y)
        src, dst = goods[0]
        push(src, dst, total_send.at[3], x_recv.at[dz + 3, 0], to_x)
        push(src, dst, total_send.at[4], total_recv.at[0], to_c)

    push(ends, ends_at(0, 0), total_send.at[5], total_recv.at[1], to_x)
    push(ends, ends_at(0, 0), total_send.at[6], total_recv.at[2], to_c)
    spread(0)
    for step in (1, 2, 3):
        for dz in (step, -step):

            def action(dz=dz):
                for kind, dst in enumerate((small_at(dz, 0, 0, 0), kv_at(dz, 0), query_at(dz, 0))):
                    arrive(dst, z_recv.at[kind, dz + 3])
                spread(dz)

            when_has(spot, dz, action)
    arrive(ends_at(1, 0), total_recv.at[1])
    push(ends_at(1, 0), ends_at(1, 0), total_send.at[6], total_recv.at[2], to_c)
    for dz in (0, 1, -1, 2, -2, 3, -3):

        def action(dz=dz):
            place = small_at(dz, 1, 0, 0)
            arrive(place, y_recv.at[0, dz + 3])
            push(place, place, total_send.at[3], x_recv.at[dz + 3, 1], to_x)
            push(place, place, total_send.at[4], total_recv.at[0], to_c)
            place = small_at(dz, 0, 1, 0)
            arrive(place, x_recv.at[dz + 3, 0])
            push(place, place, total_send.at[4], total_recv.at[0], to_c)

        when_has(spot, dz, action)
    for dz in (0, 1, -1, 2, -2, 3, -3):

        def action(dz=dz):
            place = small_at(dz, 1, 1, 0)
            arrive(place, x_recv.at[dz + 3, 1])
            push(place, place, total_send.at[4], total_recv.at[0], to_c)
            arrive(kv_at(dz, 1), y_recv.at[1, dz + 3])
            arrive(query_at(dz, 1), y_recv.at[2, dz + 3])

        when_has(spot, dz, action)

    def drain(ref, rows, sem):
        view = ref.at[pl.ds(0, rows), :]
        pltpu.make_async_copy(view, view, sem).wait()

    drain(small_out, 16 * few, total_recv.at[0])
    drain(ends_out, 2 * many, total_recv.at[2])
    drain(small_out, 4 * few, total_send.at[0])
    drain(kv_out, 4 * 256, total_send.at[1])
    half = query_out.at[:, pl.ds(0, 4 * dim)]
    pltpu.make_async_copy(half, half, total_send.at[2]).wait()
    drain(small_out, 8 * few, total_send.at[3])
    drain(small_out, 16 * few, total_send.at[4])
    drain(ends_out, many, total_send.at[5])
    drain(ends_out, 2 * many, total_send.at[6])
    for dz in range(-3, 4):
        for side, step in ((0, 1), (1, -1)):
            if dz * step <= 0:

                @pl.when(spot.has(dz) & spot.has(step))
                def _(dz=dz, side=side):
                    places = (small_at(dz, 0, 0, 0), kv_at(dz, 0), query_at(dz, 0))
                    for kind, place in enumerate(places):
                        arrive(place, z_send.at[kind, dz + 3, side])

    for copy in locals_:
        copy.wait()


def finish(query, kv, small, ends, ident):
    dma, shape = pltpu.SemaphoreType.DMA, jax.ShapeDtypeStruct
    hbm = pl.BlockSpec(memory_space=pl.ANY)
    return pl.pallas_call(
        finish_kernel,
        out_shape=(
            shape((query.shape[0], 8 * query.shape[1]), query.dtype),
            shape((8 * kv.shape[0], kv.shape[1]), kv.dtype),
            shape((32 * small.shape[0], small.shape[1]), small.dtype),
            shape((4 * ends.shape[0], ends.shape[1]), ends.dtype),
        ),
        in_specs=[hbm] * 4,
        out_specs=(hbm,) * 4,
        scratch_shapes=[
            dma((3, 7)), dma((3, 7)), dma((7, 2)), dma((3, 7, 2)), dma((7,)), dma((3,)), dma((4,)),
        ],
        compiler_params=pltpu.CompilerParams(collective_id=ident, has_side_effects=True),
        name="finish",
    )(query, kv, small, ends)


F32, BF16 = jnp.float32, jnp.bfloat16
VMEM_SPEC = pl.BlockSpec(memory_space=pltpu.VMEM)
HBM_SPEC = pl.BlockSpec(memory_space=pl.ANY)


def mxu(left, right, left_dim=1, right_dim=0):
    return lax.dot_general(
        left, right, (((left_dim,), (right_dim,)), ((), ())), preferred_element_type=F32
    )


def head_norm(lin):
    root = lax.rsqrt(jnp.mean(lin * lin, axis=-1, keepdims=True) + EPS)
    return lin * root, root


def project_kernel(
    which, hidden, gain, w_query, w_key, w_value, q_gain, k_gain, cosine, sine,
    normed, queries, keys, values, lin_out, weight,
):
    dim = w_query.shape[1]

    @pl.when(pl.program_id(0) == 0)
    def _():
        weight[:, :dim] = w_query[...]
        weight[:, dim : 2 * dim] = w_key[...]
        weight[:, 2 * dim :] = w_value[...]

    rows = hidden[...].astype(F32)
    scaled = rows * lax.rsqrt(jnp.mean(rows * rows, axis=-1, keepdims=True) + EPS) * gain[...]
    normed[...] = scaled.astype(BF16)
    lin = mxu(normed[...], weight[...])
    lin_out[...] = lin[:, : 2 * dim]
    values[...] = lin[:, 2 * dim :].astype(BF16)
    for at, head_gain, scale, out in ((0, q_gain, dim**-0.5, queries), (dim, k_gain, 1.0, keys)):
        plain, _ = head_norm(lin[:, at : at + dim])
        plain = plain * head_gain[...]
        turned = pltpu.roll(plain, dim // 2, 1)
        out[...] = ((plain * cosine[...] + turned * sine[...]) * scale).astype(BF16)


def project(group, hidden, gain, w_query, w_key, w_value, q_gain, k_gain, cosine, sine):
    total, width = hidden.shape
    dim = w_key.shape[1]
    rows = 256
    block = lambda columns: pl.BlockSpec((rows, columns), lambda i, _: (i, 0))
    fixed = lambda shape: pl.BlockSpec(shape, lambda i, _: (0, 0))
    shape = jax.ShapeDtypeStruct
    return pl.pallas_call(
        project_kernel,
        grid_spec=pltpu.PrefetchScalarGridSpec(
            num_scalar_prefetch=1,
            grid=(total // rows,),
            in_specs=[
                block(width), fixed((1, width)),
                pl.BlockSpec((width, dim), lambda i, which: (0, which[0])),
                fixed((width, dim)), fixed((width, dim)), fixed((1, dim)), fixed((1, dim)),
                block(dim), block(dim),
            ],
            out_specs=[block(width), block(dim), block(dim), block(dim), block(2 * dim)],
            scratch_shapes=[pltpu.VMEM((width, 3 * dim), BF16)],
        ),
        out_shape=[
            shape((total, width), BF16), shape((total, dim), BF16), shape((total, dim), BF16),
            shape((total, dim), BF16), shape((total, 2 * dim), F32),
        ],
        compiler_params=pltpu.CompilerParams(vmem_limit_bytes=40 << 20),
        name="project",
    )(group, hidden, gain, w_query, w_key, w_value, q_gain, k_gain, cosine, sine)


def attend_kernel(
    queries, keys, values, place_column, place_row, open_row,
    attended, log_total, att_rows, send_sem, recv_sem, local_sem,
):
    group, part = lax.axis_index("expert"), lax.axis_index("tensor")
    dim = queries.shape[1]
    rows = 256
    barrier = pltpu.get_barrier_semaphore()

    @pl.loop(1, 8)
    def _(step):
        pl.semaphore_signal(
            barrier, inc=1, device_id=((group + step) % 8, part), device_id_type=MESH
        )

    pl.semaphore_wait(barrier, 7)
    mine = att_rows.at[:, pl.ds(pl.multiple_of(group * dim, dim), dim)]

    def copy_of(step):
        target = (group + step) % 8
        block = attended.at[pl.ds(pl.multiple_of(target * rows, rows), rows), :]
        return pltpu.make_async_remote_copy(
            src_ref=block,
            dst_ref=mine,
            send_sem=send_sem.at[step],
            recv_sem=recv_sem.at[step],
            device_id=(target, part),
            device_id_type=MESH,
        )

    def block_of(step):
        at = pl.multiple_of((group + step) % 8 * rows, rows)
        here = pl.ds(at, rows)
        scores = mxu(keys[...], queries[here, :], 1, 1)
        seen = (place_column[...] <= place_row[:, here]) & (place_column[...] >= open_row[:, here])
        scores = jnp.where(seen, scores, NEG)
        highest = jnp.max(scores, axis=0, keepdims=True)
        weights = jnp.exp(scores - highest)
        totals = jnp.sum(weights, axis=0, keepdims=True)
        probability = (weights * (1.0 / totals)).astype(BF16)
        mixed = mxu(values[...], probability, 0, 0)
        attended[here, :] = mixed.T.astype(BF16)
        log_total[:, here] = highest + jnp.log(totals)

    @pl.loop(1, 8)
    def _(step):
        block_of(step)
        copy_of(step).start()

    block_of(0)
    own = attended.at[pl.ds(pl.multiple_of(group * rows, rows), rows), :]
    local = pltpu.make_async_copy(own, mine, local_sem)
    local.start()

    @pl.loop(1, 8)
    def _(step):
        copy_of(step).wait_send()
        source = (group + 8 - step) % 8
        there = att_rows.at[:, pl.ds(pl.multiple_of(source * dim, dim), dim)]
        pltpu.make_async_copy(there, there, recv_sem.at[step]).wait()

    local.wait()


def attend(queries, keys, values, place_column, place_row, open_row):
    total, dim = queries.shape
    shape = jax.ShapeDtypeStruct
    return pl.pallas_call(
        attend_kernel,
        out_shape=(
            shape((total, dim), BF16), shape((1, total), F32), shape((total // 8, 8 * dim), BF16),
        ),
        in_specs=[VMEM_SPEC] * 6,
        out_specs=(VMEM_SPEC, VMEM_SPEC, HBM_SPEC),
        scratch_shapes=dma_sems(((8,), (8,), None)),
        compiler_params=pltpu.CompilerParams(
            collective_id=6, has_side_effects=True, vmem_limit_bytes=40 << 20
        ),
        name="attend",
    )(queries, keys, values, place_column, place_row, open_row)


def branch_kernel(
    att_rows, w_out, hidden, gain, residual, normed,
    partial_sum, from_core, to_x_sum, from_x, tensor_sems,
):
    count, width = hidden.shape
    spot = Spot()

    @pl.loop(0, width // 256)
    def _(step):
        columns = pl.ds(pl.multiple_of(step * 256, 256), 256)
        partial_sum[:, columns] = mxu(att_rows[...], w_out[:, columns]).astype(BF16)

    spot.greet()

    def rows(dx, dc):
        _, part = spot.device(0, 0, dx, dc)
        return partial_sum.at[pl.ds(pl.multiple_of(part * count, count), count), :]

    to_x, to_c = spot.device(0, 0, 1), spot.device(0, 0, 0, 1)
    for dx in (1, 0):
        push(rows(dx, 1), from_core.at[dx], tensor_sems.at[dx], tensor_sems.at[2 + dx], to_c)
    arrive(from_core.at[1], tensor_sems.at[3])
    to_x_sum[...] = (rows(1, 0)[...].astype(F32) + from_core[1].astype(F32)).astype(BF16)
    push(to_x_sum, from_x, tensor_sems.at[4], tensor_sems.at[5], to_x)
    arrive(from_core.at[0], tensor_sems.at[2])
    arrive(from_x, tensor_sems.at[5])
    branch = rows(0, 0)[...].astype(F32) + from_core[0].astype(F32) + from_x[...].astype(F32)
    total = hidden[...].astype(F32) + branch
    residual[...] = total
    root = lax.rsqrt(jnp.mean(total * total, axis=-1, keepdims=True) + EPS)
    normed[...] = (total * root * gain[...]).astype(BF16)
    for at, view in ((0, from_core.at[0]), (1, from_core.at[1]), (4, from_x)):
        arrive(view, tensor_sems.at[at])


def branch_rows(att_rows, w_out, hidden, gain):
    count, width = hidden.shape
    shape = jax.ShapeDtypeStruct
    return pl.pallas_call(
        branch_kernel,
        out_shape=(
            shape((count, width), F32), shape((count, width), BF16),
        ),
        in_specs=[VMEM_SPEC] * 4,
        out_specs=(VMEM_SPEC, VMEM_SPEC),
        scratch_shapes=[
            pltpu.VMEM((4 * count, width), BF16), pltpu.VMEM((2, count, width), BF16),
            pltpu.VMEM((count, width), BF16), pltpu.VMEM((count, width), BF16),
        ]
        + dma_sems(((6,),)),
        compiler_params=pltpu.CompilerParams(
            collective_id=7, has_side_effects=True, vmem_limit_bytes=40 << 20
        ),
        name="branch",
    )(att_rows, w_out, hidden, gain)


def attend_back_kernel(
    which, grad_rows, w_out, queries, query_lin, cosine, sine, place_row, open_row, log_total,
    keys, values, place_column, lin, k_gain, q_gain, cosine_all, sine_all,
    grad_lin, grad_q_gain, grad_k_gain, grad_keys, grad_values,
):
    step = pl.program_id(0)
    rows, dim = queries.shape
    here = pl.ds(pl.multiple_of(step * rows, rows), rows)

    @pl.when(step == 0)
    def _():
        grad_keys[...] = jnp.zeros_like(grad_keys)
        grad_values[...] = jnp.zeros_like(grad_values)
        grad_q_gain[...] = jnp.zeros_like(grad_q_gain)

    def unshape(grad, plain, gain, cos, sin):
        grad = grad * cos + pltpu.roll(grad * sin, dim // 2, 1)
        normed, root = head_norm(plain)
        gain_part = jnp.sum(grad * normed, axis=0, keepdims=True)
        grad = grad * gain
        return root * (grad - normed * jnp.mean(grad * normed, axis=-1, keepdims=True)), gain_part

    grad_att = mxu(grad_rows[...], w_out[...], 1, 1).astype(BF16)
    scores = mxu(keys[...], queries[...], 1, 1)
    seen = (place_column[...] <= place_row[...]) & (place_column[...] >= open_row[...])
    probability = jnp.exp(jnp.where(seen, scores - log_total[...], NEG))
    grad_prob = mxu(values[...], grad_att, 1, 1)
    delta = jnp.sum(probability * grad_prob, axis=0, keepdims=True)
    grad_scores = (probability * (grad_prob - delta)).astype(BF16)
    grad_values[...] += mxu(probability.astype(BF16), grad_att)
    grad_keys[...] += mxu(grad_scores, queries[...])
    grad_query = mxu(grad_scores, keys[...], 0, 0) * dim**-0.5
    grad_query, gain_part = unshape(
        grad_query, query_lin[...], q_gain[...], cosine[...], sine[...]
    )
    grad_q_gain[...] += gain_part
    grad_lin[here, :dim] = grad_query.astype(BF16)

    @pl.when(step == pl.num_programs(0) - 1)
    def _():
        grad_key, key_part = unshape(
            grad_keys[...], lin[:, dim:], k_gain[...], cosine_all[...], sine_all[...]
        )
        grad_lin[:, dim : 2 * dim] = grad_key.astype(BF16)
        grad_lin[:, 2 * dim :] = grad_values[...].astype(BF16)
        grad_k_gain[...] = key_part


def attend_back(
    group, grad_rows, w_out, queries, lin, cosine, sine, place_row, open_row, log_total,
    keys, values, place_column, k_gain, q_gain,
):
    total, width = grad_rows.shape
    dim = keys.shape[1]
    rows = 256
    block = lambda columns: pl.BlockSpec((rows, columns), lambda i, _: (i, 0))
    across = pl.BlockSpec((1, rows), lambda i, _: (0, i))
    fixed = lambda shape: pl.BlockSpec(shape, lambda i, _: (0, 0))
    shape = jax.ShapeDtypeStruct
    return pl.pallas_call(
        attend_back_kernel,
        grid_spec=pltpu.PrefetchScalarGridSpec(
            num_scalar_prefetch=1,
            grid=(total // rows,),
            in_specs=[
                block(width), pl.BlockSpec((dim, width), lambda i, which: (which[0], 0)),
                block(dim), block(dim), block(dim), block(dim), across, across, across,
                fixed((total, dim)), fixed((total, dim)), fixed((total, 1)),
                fixed((total, 2 * dim)), fixed((1, dim)), fixed((1, dim)),
                fixed((total, dim)), fixed((total, dim)),
            ],
            out_specs=[fixed((total, 3 * dim)), fixed((1, dim)), fixed((1, dim))],
            scratch_shapes=[pltpu.VMEM((total, dim), F32), pltpu.VMEM((total, dim), F32)],
        ),
        out_shape=[shape((total, 3 * dim), BF16), shape((1, dim), F32), shape((1, dim), F32)],
        compiler_params=pltpu.CompilerParams(vmem_limit_bytes=48 << 20),
        name="attend_back",
    )(
        group, grad_rows, w_out, queries, lin, cosine, sine, place_row, open_row, log_total,
        keys, values, place_column, lin, k_gain, q_gain, cosine, sine,
    )


def near_first(step, z):
    high = z // 2
    folded = z + high * (3 - 2 * z)
    place = (step + folded * (1 - step // 2)) % 2 + 2 * (step // 2)
    return place + high * (3 - 2 * place)


class Gather:
    SEMS = ((5, 7), (7, 2), (4,), (7, 2, 2), None)

    def __init__(self, spot, src, out, recv, z_send, sends, c_recv, local_sem):
        self.spot, self.src, self.out = spot, src, out
        self.recv, self.z_send, self.sends, self.c_recv = recv, z_send, sends, c_recv
        self.count, self.width = src.shape
        half = self.width // 2
        self.first, self.second = pl.ds(0, half), pl.ds(half, half)
        self.whole = pl.ds(0, self.width)
        self.local = pltpu.make_async_copy(src, self.place(0, 0, 0), local_sem)

    def place(self, dz, dy, dx, dc=0, columns=None):
        rows = self.spot.rows(dz, dy, dx, dc, self.count)
        return self.out.at[rows, self.whole if columns is None else columns]

    def send(self, dz, dy, dx, columns, send_sem, recv_sem, device):
        here = self.place(dz, dy, dx, 0, columns)
        own = dz == 0 and dy == 0 and dx == 0
        push(self.src.at[:, columns] if own else here, here, send_sem, recv_sem, device)

    def to_core(self, dz, dy, dx):
        self.send(
            dz, dy, dx, self.whole, self.sends.at[0], self.c_recv.at[dz + 3, dy, dx],
            self.spot.device(0, 0, 0, 1),
        )

    def spread(self, dz):
        spot = self.spot
        for side, step in ((0, 1), (1, -1)):
            if dz * step <= 0:

                @pl.when(spot.has(step))
                def _(side=side, step=step):
                    self.send(
                        dz, 0, 0, self.whole, self.z_send.at[dz + 3, side],
                        self.recv.at[0, dz + 3 - step], spot.device(step),
                    )

        self.send(dz, 0, 0, self.whole, self.sends.at[1], self.recv.at[1, dz + 3], spot.device(0, 1))
        self.send(
            dz, 0, 0, self.whole, self.sends.at[2], self.recv.at[2, dz + 3], spot.device(0, 0, 1)
        )
        self.to_core(dz, 0, 0)

    def start(self):
        self.local.start()
        self.spread(0)

    def take_z(self, dz):
        def action():
            arrive(self.place(dz, 0, 0), self.recv.at[0, dz + 3])
            self.spread(dz)

        when_has(self.spot, dz, action)

    def take_yx(self, dz):
        spot = self.spot

        def action():
            arrive(self.place(dz, 1, 0), self.recv.at[1, dz + 3])
            self.send(
                dz, 1, 0, self.first, self.sends.at[3], self.recv.at[3, dz + 3],
                spot.device(0, 0, 1),
            )
            self.to_core(dz, 1, 0)
            arrive(self.place(dz, 0, 1), self.recv.at[2, dz + 3])
            self.send(
                dz, 0, 1, self.second, self.sends.at[3], self.recv.at[4, dz + 3],
                spot.device(0, 1),
            )
            self.to_core(dz, 0, 1)

        when_has(spot, dz, action)

    def take_diagonal(self, dz):
        def action():
            arrive(self.place(dz, 1, 1, 0, self.first), self.recv.at[3, dz + 3])
            arrive(self.place(dz, 1, 1, 0, self.second), self.recv.at[4, dz + 3])
            self.to_core(dz, 1, 1)

        when_has(self.spot, dz, action)

    def take_core(self, far, dy, dx):
        view = self.out.at[pl.ds(0, self.count), :]
        arrive(view, self.c_recv.at[far - self.spot.z + 3, dy, dx])

    def drain(self):
        count, spot = self.count, self.spot
        for at, pieces in ((0, 16), (1, 4), (2, 4), (3, 4)):
            arrive(self.out.at[pl.ds(0, pieces * count), :], self.sends.at[at])
        for dz in range(-3, 4):
            for side, step in ((0, 1), (1, -1)):
                if dz * step <= 0:

                    @pl.when(spot.has(dz) & spot.has(step))
                    def _(dz=dz, side=side):
                        arrive(self.place(0, 0, 0), self.z_send.at[dz + 3, side])


def experts_kernel(
    normed, grad_y, w_gate, w_up, w_down, router, chosen, kept,
    reduced, out_part, grad_gate, grad_up, grad_down,
    rows_all, weight, staged, grad_in, grad_in_down, y_block, out_block, back_block,
    mine, other, from_a, from_b, from_y, from_x, from_z,
    weight_sem, y_sem, out_sem, flush_sem, core_send, core_recv, half_send, yx_send, recv,
    line_send, line_recv, *gather_sems,
):
    spot = Spot()
    count, width = normed.shape
    wide = reduced.shape[1]
    local_count, _, ff = w_gate.shape
    both = local_count * ff
    block = 4 * count
    split = 1024
    first, second = pl.ds(0, split), pl.ds(split, wide - split)
    group = lax.axis_index("expert")
    to_y, to_x, to_c = spot.device(0, 1), spot.device(0, 0, 1), spot.device(0, 0, 0, 1)

    def dy_of(step):
        return (step + step // 4) % 2

    def place_of(step):
        return near_first(step // 2, spot.z), dy_of(step)

    def group_rows(step):
        far, dy = place_of(step)
        y = spot.y + dy * (1 - 2 * spot.y)
        return pl.ds(pl.multiple_of((far * 2 + y) * block, block), block)

    def y_copy(step):
        slot = step % 2
        return pltpu.make_async_copy(
            grad_y.at[group_rows(step), :], y_block.at[slot], y_sem.at[slot]
        )

    def out_copy(step):
        slot = step % 2
        return pltpu.make_async_copy(
            out_block.at[slot], out_part.at[group_rows(step), :], out_sem.at[slot]
        )

    sources = [ref.at[at] for ref in (w_gate, w_up) for at in range(local_count)]

    def weight_copy(at):
        return pltpu.make_async_copy(sources[at], staged.at[at % 2], weight_sem.at[at % 2])

    weight_copy(0).start()
    weight_copy(1).start()
    y_copy(0).start()
    gather = Gather(spot, normed, rows_all, *gather_sems)
    spot.greet()
    gather.start()
    for at in range(len(sources)):
        weight_copy(at).wait()
        weight[:, at * ff : (at + 1) * ff] = staged[at % 2]
        if at + 2 < len(sources):
            weight_copy(at + 2).start()
    grad_in[...] = jnp.zeros_like(grad_in)
    grad_in_down[...] = jnp.zeros_like(grad_in_down)
    gather.local.wait()

    def piece(dx, dc):
        _, part = spot.device(0, 0, dx, dc)
        return pl.ds(pl.multiple_of(part * count, count), count)

    def core_copy(step, dx):
        far, dy = place_of(step)
        slot = step % 2
        return pltpu.make_async_remote_copy(
            src_ref=back_block.at[slot, piece(dx, 1), :],
            dst_ref=other.at[far, dy, dx],
            send_sem=core_send.at[slot, dx],
            recv_sem=core_recv.at[far, dy, dx],
            device_id=to_c,
            device_id_type=MESH,
        )

    def merge(far, dy, dx):
        into = mine.at[far, dy, dx]
        arrive(other.at[far, dy, dx], core_recv.at[far, dy, dx])
        return into

    def merge_diagonal(k):
        far = near_first(k, spot.z)
        into = merge(far, 1, 1)
        add_into(into, 16, other.at[far, 1, 1])
        push(into.at[:, first], from_a.at[far], half_send.at[0], recv.at[0, far], to_x)
        push(into.at[:, second], from_b.at[far], half_send.at[1], recv.at[1, far], to_y)

    def merge_yx(k):
        far = near_first(k, spot.z)
        into = merge(far, 1, 0)
        add_into(into, 16, other.at[far, 1, 0])
        arrive(from_a.at[far], recv.at[0, far])
        add_into(into.at[:, first], 16, from_a.at[far])
        push(into, from_y.at[far], yx_send.at[0], recv.at[2, far], to_y)
        into = merge(far, 0, 1)
        add_into(into, 16, other.at[far, 0, 1])
        arrive(from_b.at[far], recv.at[1, far])
        add_into(into.at[:, second], 16, from_b.at[far])
        push(into, from_x.at[far], yx_send.at[1], recv.at[3, far], to_x)

    def merge_line(k):
        far = near_first(k, spot.z)
        into = merge(far, 0, 0)
        arrive(from_y.at[far], recv.at[2, far])
        arrive(from_x.at[far], recv.at[3, far])
        add_into(into, 16, other.at[far, 0, 0], from_y.at[far], from_x.at[far])
        if k > 0:
            push(
                into, from_z.at[spot.z], line_send.at[k], line_recv.at[spot.z],
                (far * 2 + spot.y, spot.x * 2 + spot.c),
            )

    def both_ways(take, distance):
        for dz in (distance, -distance) if distance else (0,):
            take(dz)

    columns = lax.broadcasted_iota(jnp.int32, (block, both), 1)
    lower = columns < ff
    lanes = lax.broadcasted_iota(jnp.int32, (block, 128), 1)
    names = lax.broadcasted_iota(jnp.int32, (router.shape[0], block), 0)

    def compute(step):
        slot = step % 2
        here = group_rows(step)
        rows = rows_all[here, :]
        lin = mxu(rows, weight[...])
        gate, up = lin[:, :both], lin[:, both:]
        logits = mxu(router[...], rows, 1, 1)
        picked = chosen[:, here] > 0.0
        top = jnp.max(jnp.where(picked, logits, NEG), axis=0, keepdims=True)
        exps = jnp.where(picked, jnp.exp(logits - top), 0.0)
        soft = exps / jnp.sum(exps, axis=0, keepdims=True)
        keep = kept[:, here]
        soft = jnp.where(keep > 0.0, soft, 0.0)
        lines = []
        for table in (soft, keep):
            for at in range(local_count):
                lines.append(
                    jnp.sum(
                        jnp.where(names == group * local_count + at, table, 0.0),
                        axis=0, keepdims=True,
                    )
                )
        stack = jnp.concatenate(lines + [jnp.zeros((8 - len(lines), block), F32)], axis=0).T
        spread = jnp.where(lower, stack[:, 0:1], stack[:, 1:2])
        sigmoid = 1.0 / (1.0 + jnp.exp(-gate))
        silu = gate * sigmoid
        act = (silu * up).astype(BF16).astype(F32)
        weighted = (act * spread).astype(BF16)
        y_copy(step).wait()

        @pl.when(step >= 2)
        def _():
            out_copy(step - 2).wait()
            for dx in (0, 1):
                core_copy(step - 2, dx).wait_send()

        out_block[slot] = mxu(weighted, w_down[...]).astype(BF16)
        out_copy(step).start()
        y_rows = y_block[slot]
        mid = mxu(y_rows, w_down[...], 1, 1)
        dots = act * mid
        low = jnp.sum(jnp.where(lower, dots, 0.0), axis=1, keepdims=True) * stack[:, 2:3]
        high = jnp.sum(jnp.where(lower, 0.0, dots), axis=1, keepdims=True) * stack[:, 3:4]
        mine_at = group * local_count
        tail = jnp.where(lanes == mine_at, low, jnp.where(lanes == mine_at + 1, high, 0.0))
        grad_act = mid * spread
        grad_up_lin = (grad_act * silu).astype(BF16)
        grad_gate_lin = (grad_act * up * sigmoid * (1.0 + gate * (1.0 - sigmoid))).astype(BF16)
        grad_lin = jnp.concatenate([grad_gate_lin, grad_up_lin], axis=1)
        back_block[slot, :, :width] = mxu(grad_lin, weight[...], 1, 1).astype(BF16)
        back_block[slot, :, width:] = tail.astype(BF16)
        far, dy = place_of(step)
        for dx in (1, 0):
            core_copy(step, dx).start()
            mine[far, dy, dx] = back_block[slot, piece(dx, 0), :]
        for at in range(2 * local_count):
            grad_in[at] += mxu(rows, grad_lin[:, at * ff : (at + 1) * ff], 0, 0)
        grad_in_down[...] += mxu(weighted, y_rows, 0, 0)

    plans = {
        0: lambda: (both_ways(gather.take_yx, 0), both_ways(gather.take_z, 1)),
        1: lambda: (both_ways(gather.take_z, 2), both_ways(gather.take_diagonal, 0)),
        2: lambda: (
            both_ways(gather.take_yx, 1), both_ways(gather.take_z, 3), merge_diagonal(0),
        ),
        3: lambda: (
            both_ways(gather.take_diagonal, 1), both_ways(gather.take_yx, 2), merge_yx(0),
        ),
        4: lambda: (
            both_ways(gather.take_diagonal, 2), both_ways(gather.take_yx, 3),
            merge_diagonal(1), merge_line(0),
        ),
        5: lambda: (both_ways(gather.take_diagonal, 3), merge_diagonal(2), merge_yx(1)),
        6: lambda: (merge_yx(2), merge_line(1)),
        7: lambda: (merge_diagonal(3), merge_line(2)),
    }

    @pl.loop(0, 8)
    def _(step):
        for at, plan in plans.items():

            @pl.when(step == at)
            def _(plan=plan):
                plan()

        @pl.when(step < 7)
        def _():
            y_copy(step + 1).start()

        far, dy = place_of(step)
        for dx in (0, 1):
            gather.take_core(far, dy, dx)
        compute(step)

    flush = [
        pltpu.make_async_copy(
            grad_in.at[at], (grad_gate, grad_up)[at // local_count].at[at % local_count],
            flush_sem.at[at],
        )
        for at in range(2 * local_count)
    ]
    flush.append(pltpu.make_async_copy(grad_in_down, grad_down, flush_sem.at[2 * local_count]))
    for copy in flush:
        copy.start()
    merge_yx(3)
    merge_line(3)
    total = mine[spot.z, 0, 0].astype(F32)
    for k in (1, 2, 3):
        source = near_first(k, spot.z)
        arrive(from_z.at[source], line_recv.at[source])
        total = total + from_z[source].astype(F32)
    reduced[...] = total
    gather.drain()
    for step in (6, 7):
        out_copy(step).wait()
        for dx in (0, 1):
            core_copy(step, dx).wait_send()
    arrive(from_a, half_send.at[0])
    arrive(from_b, half_send.at[1])
    arrive(from_y, yx_send.at[0])
    arrive(from_x, yx_send.at[1])
    for k in (1, 2, 3):
        arrive(from_z.at[0], line_send.at[k])
    for copy in flush:
        copy.wait()


def experts(normed, grad_y, w_gate, w_up, w_down, router, chosen, kept):
    count, width = normed.shape
    wide = width + 128
    total = grad_y.shape[0]
    local_count, _, ff = w_gate.shape
    both = local_count * ff
    shape, vmem, dma = jax.ShapeDtypeStruct, pltpu.VMEM, pltpu.SemaphoreType.DMA
    line = vmem((4, count, wide), BF16)
    return pl.pallas_call(
        experts_kernel,
        out_shape=(
            shape((count, wide), F32), shape((total, width), BF16),
            shape(w_gate.shape, F32), shape(w_up.shape, F32), shape((both, width), F32),
        ),
        in_specs=[VMEM_SPEC, HBM_SPEC, HBM_SPEC, HBM_SPEC] + [VMEM_SPEC] * 4,
        out_specs=(VMEM_SPEC,) + (HBM_SPEC,) * 4,
        scratch_shapes=[
            vmem((total, width), BF16),
            vmem((width, 2 * both), BF16),
            vmem((2, width, ff), BF16),
            vmem((2 * local_count, width, ff), F32),
            vmem((both, width), F32),
            vmem((2, 4 * count, width), BF16),
            vmem((2, 4 * count, width), BF16),
            vmem((2, 4 * count, wide), BF16),
            vmem((4, 2, 2, count, wide), BF16),
            vmem((4, 2, 2, count, wide), BF16),
            vmem((4, count, 1024), BF16),
            vmem((4, count, wide - 1024), BF16),
            line, line, line,
        ]
        + dma_sems(
            ((2,), (2,), (2,), (2 * local_count + 1,), (2, 2), (4, 2, 2), (2,), (2,), (4, 4),
             (4,), (4,))
            + Gather.SEMS
        ),
        compiler_params=pltpu.CompilerParams(
            collective_id=8, has_side_effects=True, vmem_limit_bytes=62 << 20
        ),
        name="experts",
    )(normed, grad_y, w_gate, w_up, w_down, router, chosen, kept)


def head_device(
    hidden_in,
    cotangent,
    layout,
    seq_lengths,
    expert_ids,
    drop_rank,
    norm1_gain,
    w_query,
    key_weight,
    value_weight,
    query_gain,
    key_gain,
    w_out,
    norm2_gain,
    w_router,
    w_gate,
    w_up,
    w_down,
):
    f32, bf16 = jnp.float32, jnp.bfloat16
    tok_rows, model_width = hidden_in.shape
    head_dim = query_gain.shape[0]
    expert_count = w_router.shape[1]
    local_count, _, ff_local = w_gate.shape
    groups = lax.axis_size("expert")
    tensor_size = lax.axis_size("tensor")
    total_rows = groups * tok_rows
    own_rows = tok_rows // tensor_size
    seq_count = seq_lengths.shape[0]
    group = lax.axis_index("expert")
    part = lax.axis_index("tensor")

    def own(rows):
        return lax.dynamic_slice_in_dim(rows, part * own_rows, own_rows, 0)

    which = jnp.reshape(group, (1,))
    tag = jnp.concatenate(
        [layout[None], drop_rank[None], expert_ids.T, jnp.zeros((6, tok_rows), jnp.int32)], axis=0
    )
    hidden_all, tags = gather_rows(own(hidden_in), tag)
    tags = jnp.transpose(tags, (1, 0, 2)).reshape(16, total_rows)
    place, rank, ids_t = tags[0], tags[1], tags[2:10]
    segment, position = token_tables(place, seq_lengths)
    valid = segment < seq_count
    cotangent_late, _ = lax.optimization_barrier((own(cotangent), tags))
    grad_y_all = lax.all_gather(cotangent_late, ("expert", "tensor"), axis=0, tiled=True)

    half_dim = head_dim // 2
    inverse = THETA ** (-(jnp.arange(half_dim, dtype=f32) * 2.0) / head_dim)
    angles = position.astype(f32)[:, None] * inverse[None, :]
    cosine, sine = jnp.cos(angles), jnp.sin(angles)
    cosine = jnp.concatenate([cosine, cosine], axis=1)
    sine = jnp.concatenate([-sine, sine], axis=1)
    q_gain, k_gain = query_gain[None], key_gain[None]
    normed1, queries, keys, values, lin = project(
        which, hidden_all, norm1_gain[None], w_query, key_weight, value_weight, q_gain, k_gain,
        cosine, sine,
    )
    place_row, open_row = place[None], (place - position)[None]
    place_column = place[:, None]
    attended, log_total, att_rows = attend(
        queries, keys, values, place_column, place_row, open_row
    )
    residual, normed2 = branch_rows(att_rows, w_out, own(hidden_in), norm2_gain[None])

    expert_range = jnp.arange(expert_count, dtype=jnp.int32)
    chosen = jnp.any(ids_t[:, None, :] == expert_range[:, None], axis=0)
    picks = (chosen & valid).astype(bf16)
    earlier = (rank[:, None] < rank[None, :]).astype(bf16)
    slot = jnp.dot(picks, earlier, preferred_element_type=f32)
    kept = chosen & valid & (slot < CAP)

    back, out_part, grad_gate, grad_up, grad_down = experts(
        normed2, grad_y_all, w_gate, w_up, w_down.reshape(-1, model_width), w_router.T,
        chosen.astype(f32), kept.astype(f32),
    )
    moe_branch = scatter_rows(out_part, 4)
    out_own = (residual + moe_branch).astype(bf16)

    start = group * tok_rows + part * own_rows
    chosen_own = lax.dynamic_slice_in_dim(chosen, start, own_rows, 1).T
    logits = jnp.dot(normed2, w_router, preferred_element_type=f32)
    soft_own = jax.nn.softmax(jnp.where(chosen_own, logits, -jnp.inf), axis=1)
    grad_soft = back[:, model_width : model_width + expert_count]
    grad_logits = (
        soft_own * (grad_soft - jnp.sum(soft_own * grad_soft, axis=1, keepdims=True))
    ).astype(bf16)
    grad_router = jnp.einsum("td,te->de", normed2, grad_logits, preferred_element_type=f32)
    grad_normed2 = back[:, :model_width] + jnp.einsum(
        "te,de->td", grad_logits, w_router, preferred_element_type=f32
    )
    norm2_pull = jax.vjp(norm_rows, residual, norm2_gain)[1]
    grad_resid_norm, grad_norm2 = norm2_pull(grad_normed2)
    grad_residual = own(cotangent).astype(f32) + grad_resid_norm
    grad_residual_all = gather_rows(grad_residual.astype(bf16))

    grad_out = jnp.einsum(
        "rc,rd->cd", attended, grad_residual_all, preferred_element_type=f32
    ).astype(bf16)
    grad_out_all = lax.all_gather(grad_out, "expert", axis=0, tiled=True)
    grad_residual_all, _ = lax.optimization_barrier((grad_residual_all, grad_out))
    grad_lin, grad_qgain, grad_kgain = attend_back(
        which, grad_residual_all, w_out, queries, lin, cosine, sine, place_row, open_row,
        log_total, keys, values, place_column, k_gain, q_gain,
    )
    head_query = lax.dynamic_slice_in_dim(w_query, group * head_dim, head_dim, 1)
    qkv_weight = jnp.concatenate([head_query, key_weight, value_weight], axis=1)
    grad_normed1_part = jnp.einsum(
        "tc,dc->td", grad_lin, qkv_weight, preferred_element_type=f32
    )
    grad_qkv = jnp.einsum(
        "td,tc->dc", normed1, grad_lin, preferred_element_type=f32
    ).astype(bf16)
    extra = jnp.zeros((model_width, head_dim), f32)
    router_rows = lax.dynamic_update_slice(extra, grad_router, (0, 0))
    extra = lax.dynamic_update_slice(router_rows, grad_norm2[:, None], (0, expert_count))
    extra = lax.dynamic_update_slice(extra, grad_qgain.T, (0, expert_count + 1))
    extra = lax.dynamic_update_slice(extra, grad_kgain.T, (0, expert_count + 2))
    reduced, kv_own = scatter_rows(
        jnp.concatenate([grad_normed1_part, extra], axis=1).astype(bf16),
        3,
        grad_qkv[:, head_dim:],
    )
    norm1_pull = jax.vjp(norm_rows, own(hidden_in).astype(f32), norm1_gain)[1]
    grad_hidden_norm, grad_norm1 = norm1_pull(reduced[:, :model_width])
    grad_hidden_own = (grad_residual + grad_hidden_norm).astype(bf16)
    extra_rows = own_rows * head_dim // model_width
    small = jnp.concatenate(
        [
            grad_norm1[None],
            reduced[:, model_width:].reshape(extra_rows, model_width),
            jnp.zeros((15 - extra_rows, model_width), f32),
        ],
        axis=0,
    ).astype(bf16)
    grad_query, grad_kv, small, ends = finish(
        grad_qkv[:, :head_dim], kv_own, small, jnp.concatenate([out_own, grad_hidden_own], axis=1), 5
    )
    grad_query, grad_kv, grad_out = (v.astype(f32) for v in (grad_query, grad_kv, grad_out_all))
    small = small.reshape(groups * tensor_size, 16, model_width).astype(f32)
    grad_norm1 = jnp.sum(small[:, 0], axis=0)
    extra = small[:, 1 : 1 + extra_rows].reshape(model_width, head_dim)
    grad_router = extra[:, :expert_count]
    grad_norm2 = extra[:, expert_count]
    grad_qgain, grad_kgain = extra[:head_dim, expert_count + 1], extra[:head_dim, expert_count + 2]
    grad_down = grad_down.reshape(local_count, ff_local, model_width)
    return (
        ends[:, :model_width],
        ends[:, model_width:],
        grad_norm1,
        grad_query,
        grad_kv[:, :head_dim],
        grad_kv[:, head_dim:],
        grad_qgain,
        grad_kgain,
        grad_out,
        grad_norm2,
        grad_router,
        grad_gate,
        grad_up,
        grad_down,
    )


def solution(mesh):
    groups = mesh.shape["expert"]

    def device_fn(*operands):
        heads = operands[7].shape[1] // operands[10].shape[0]
        one_head = heads == groups == 8 and operands[8].shape[1] == operands[10].shape[0]
        one_head = one_head and mesh.shape["tensor"] == 4
        return (head_device if one_head else per_device)(*operands)

    return jax.shard_map(
        device_fn,
        mesh=mesh,
        in_specs=(
            P("expert", None),
            P("expert", None),
            P("expert"),
            P(),
            P("expert", None),
            P("expert"),
            P(),
            P(None, "tensor"),
            P(None, "tensor"),
            P(None, "tensor"),
            P(),
            P(),
            P("tensor", None),
            P(),
            P(),
            P("expert", None, "tensor"),
            P("expert", None, "tensor"),
            P("expert", "tensor", None),
        ),
        out_specs=(
            P("expert", None),
            P("expert", None),
            P(),
            P(None, "tensor"),
            P(None, "tensor"),
            P(None, "tensor"),
            P(),
            P(),
            P("tensor", None),
            P(),
            P(),
            P("expert", None, "tensor"),
            P("expert", None, "tensor"),
            P("expert", "tensor", None),
        ),
        check_vma=False,
    )
```

```python
from functools import partial
import math

import jax
import jax.numpy as jnp
from jax import lax
from jax.experimental import pallas as pl
from jax.experimental.pallas import tpu as pltpu
from jax.sharding import PartitionSpec as P

TOPK = 8
CAP = 1280


EPS = 1e-06
THETA = 1000000.0
NEG = -1e30


def norm_rows(value_matrix, gain):
    return (
        value_matrix
        * lax.rsqrt(jnp.mean(value_matrix * value_matrix, axis=-1, keepdims=True) + EPS)
        * gain
    )


def rotary(value_matrix, position):
    half_dim = value_matrix.shape[-1] // 2
    inverse = THETA ** (-(jnp.arange(half_dim, dtype=jnp.float32) * 2.0) / value_matrix.shape[-1])
    angles = position.astype(jnp.float32)[:, None] * inverse[None, :]
    cosine_table = jnp.concatenate([jnp.cos(angles), jnp.cos(angles)], axis=-1)[:, None, :]
    sine_table = jnp.concatenate([jnp.sin(angles), jnp.sin(angles)], axis=-1)[:, None, :]
    turned = jnp.concatenate([-value_matrix[..., half_dim:], value_matrix[..., :half_dim]], axis=-1)
    return value_matrix * cosine_table + turned * sine_table


def shape_queries(linear, gain, position):
    head_dim = gain.shape[0]
    shaped = linear.reshape(linear.shape[0], linear.shape[1] // head_dim, head_dim)
    return rotary(norm_rows(shaped, gain), position) * head_dim ** (-0.5)


def shape_keys(linear, gain, position):
    head_dim = gain.shape[0]
    shaped = linear.reshape(linear.shape[0], linear.shape[1] // head_dim, head_dim)
    return rotary(norm_rows(shaped, gain), position)


def token_tables(token_position, seq_lengths):
    bounds = jnp.cumsum(seq_lengths)
    passed = token_position[:, None] >= bounds[None, :]
    segment_ids = jnp.sum(passed.astype(jnp.int32), axis=1)
    opening = jnp.max(jnp.where(passed, bounds[None, :], 0), axis=1)
    return (segment_ids, (token_position - opening).astype(jnp.int32))


def visible(query_segment, query_place, key_segment, key_place):
    return (query_segment[:, None] == key_segment[None, :]) & (
        key_place[None, :] <= query_place[:, None]
    )


def deliver(payload, slot_ids):
    return (
        lax.all_to_all(payload, "expert", split_axis=0, concat_axis=0, tiled=True),
        lax.all_to_all(slot_ids, "expert", split_axis=0, concat_axis=0, tiled=True),
    )


def bring_back(payload):
    return lax.all_to_all(payload, "expert", split_axis=0, concat_axis=0, tiled=True)


def expert_forward(entry_rows, w_gate, w_up, w_down):
    gate_lin = jnp.einsum("gesd,edf->gesf", entry_rows, w_gate, preferred_element_type=jnp.float32)
    up_lin = jnp.einsum("gesd,edf->gesf", entry_rows, w_up, preferred_element_type=jnp.float32)
    activation = (jax.nn.silu(gate_lin) * up_lin).astype(jnp.bfloat16)
    expert_out = jnp.einsum(
        "gesf,efd->gesd", activation, w_down, preferred_element_type=jnp.float32
    ).astype(jnp.bfloat16)
    return (gate_lin, up_lin, activation, expert_out)


def expert_backward(entry_rows, gate_lin, up_lin, activation, grad_in, w_gate, w_up, w_down):
    grad_down = jnp.einsum(
        "gesf,gesd->efd", activation, grad_in, preferred_element_type=jnp.float32
    )
    grad_act = jnp.einsum("gesd,efd->gesf", grad_in, w_down, preferred_element_type=jnp.float32)
    sigmoid = jax.nn.sigmoid(gate_lin)
    grad_gate_lin = (grad_act * up_lin * sigmoid * (1.0 + gate_lin * (1.0 - sigmoid))).astype(
        jnp.bfloat16
    )
    grad_up_lin = (grad_act * gate_lin * sigmoid).astype(jnp.bfloat16)
    grad_w_gate = jnp.einsum(
        "gesd,gesf->edf", entry_rows, grad_gate_lin, preferred_element_type=jnp.float32
    )
    grad_w_up = jnp.einsum(
        "gesd,gesf->edf", entry_rows, grad_up_lin, preferred_element_type=jnp.float32
    )
    grad_entry = jnp.einsum(
        "gesf,edf->gesd", grad_gate_lin, w_gate, preferred_element_type=jnp.float32
    )
    grad_entry = (
        grad_entry
        + jnp.einsum("gesf,edf->gesd", grad_up_lin, w_up, preferred_element_type=jnp.float32)
    ).astype(jnp.bfloat16)
    return (grad_entry, grad_w_gate, grad_w_up, grad_down)


def per_device(
    hidden_in,
    cotangent,
    layout,
    seq_lengths,
    expert_ids,
    drop_rank,
    norm1_gain,
    w_query,
    key_weight,
    value_weight,
    query_gain,
    key_gain,
    w_out,
    norm2_gain,
    w_router,
    w_gate,
    w_up,
    w_down,
):
    tok_rows = hidden_in.shape[0]
    model_width = hidden_in.shape[1]
    head_dim = query_gain.shape[0]
    local_heads = w_query.shape[1] // head_dim
    expert_count = w_router.shape[1]
    local_count = w_gate.shape[0]
    group_count = lax.axis_size("expert")
    slot_count = 2 * tok_rows * TOPK // expert_count
    seq_count = seq_lengths.shape[0]
    expert_range = jnp.arange(expert_count, dtype=jnp.int32)
    hidden = hidden_in.astype(jnp.float32)
    segment_ids, position = token_tables(layout, seq_lengths)
    valid = segment_ids < seq_count
    first_normalized = norm_rows(hidden, norm1_gain)
    normed1_low = first_normalized.astype(jnp.bfloat16)
    query_lin = jnp.dot(normed1_low, w_query, preferred_element_type=jnp.float32)
    key_lin = jnp.dot(normed1_low, key_weight, preferred_element_type=jnp.float32)
    value_lin = jnp.dot(normed1_low, value_weight, preferred_element_type=jnp.float32)
    query_shaped = shape_queries(query_lin, query_gain, position).astype(jnp.bfloat16)
    query_total = local_heads * tok_rows
    query_rows = jnp.transpose(query_shaped, (1, 0, 2)).reshape(query_total, head_dim)
    key_rows = (
        shape_keys(key_lin, key_gain, position).astype(jnp.bfloat16).reshape(tok_rows, head_dim)
    )
    value_rows = value_lin.astype(jnp.bfloat16)
    all_keys, all_values, all_place, all_ids, all_rank = (
        lax.all_gather(key_rows, "expert", axis=0, tiled=True),
        lax.all_gather(value_rows, "expert", axis=0, tiled=True),
        lax.all_gather(layout, "expert", axis=0, tiled=True),
        lax.all_gather(expert_ids, "expert", axis=0, tiled=True),
        lax.all_gather(drop_rank, "expert", axis=0, tiled=True),
    )
    all_segment = token_tables(all_place, seq_lengths)[0]
    rows_per_block = math.gcd(512, query_total)
    count_of_blocks = query_total // rows_per_block
    query_segment = jnp.tile(segment_ids, local_heads)
    query_place = jnp.tile(layout, local_heads)

    def attend_block(operands):
        query_block, segment_block, place_block = operands
        scores = jnp.einsum("qd,kd->qk", query_block, all_keys, preferred_element_type=jnp.float32)
        scores = jnp.where(visible(segment_block, place_block, all_segment, all_place), scores, NEG)
        highest = jnp.max(scores, axis=1, keepdims=True)
        weights = jnp.exp(scores - highest)
        totals = jnp.sum(weights, axis=1, keepdims=True)
        probability = (weights / totals).astype(jnp.bfloat16)
        mixed_out = jnp.dot(probability, all_values, preferred_element_type=jnp.float32)
        return (mixed_out, (highest + jnp.log(totals))[:, 0])

    attention_output, log_totals = lax.map(
        attend_block,
        (
            query_rows.reshape(count_of_blocks, rows_per_block, head_dim),
            query_segment.reshape(count_of_blocks, rows_per_block),
            query_place.reshape(count_of_blocks, rows_per_block),
        ),
    )
    attention_output = attention_output.reshape(local_heads, tok_rows, head_dim).astype(
        jnp.bfloat16
    )
    att_cat = jnp.transpose(attention_output, (1, 0, 2)).reshape(tok_rows, local_heads * head_dim)
    branch_part = jnp.dot(att_cat, w_out, preferred_element_type=jnp.float32)
    branch = lax.psum(branch_part, "tensor")
    residual = hidden + branch
    normed2 = norm_rows(residual, norm2_gain)
    normed2_low = normed2.astype(jnp.bfloat16)
    logits = jnp.dot(normed2_low, w_router, preferred_element_type=jnp.float32)
    soft_gate = jax.nn.softmax(jnp.take_along_axis(logits, expert_ids, axis=1), axis=1)
    picks = jnp.any(expert_ids[:, :, None] == expert_range, axis=1) & valid[:, None]
    all_valid = all_segment < seq_count
    all_picks = jnp.any(all_ids[:, :, None] == expert_range, axis=1) & all_valid[:, None]
    earlier = (all_rank[None, :] < drop_rank[:, None]).astype(jnp.bfloat16)
    before_counts = jnp.dot(
        earlier, all_picks.astype(jnp.bfloat16), preferred_element_type=jnp.float32
    )
    global_slot = jnp.take_along_axis(before_counts, expert_ids, axis=1).astype(jnp.int32)
    kept_mask = (global_slot < CAP) & valid[:, None]
    gate_weight = soft_gate * kept_mask.astype(jnp.float32)
    lower_rows = (jnp.arange(tok_rows)[None, :] < jnp.arange(tok_rows)[:, None]).astype(
        jnp.bfloat16
    )
    local_counts = jnp.dot(
        lower_rows, picks.astype(jnp.bfloat16), preferred_element_type=jnp.float32
    )
    local_slot = jnp.take_along_axis(local_counts, expert_ids, axis=1).astype(jnp.int32)
    pair_count = tok_rows * TOPK
    dump_index = expert_count * slot_count
    target = jnp.where(kept_mask, expert_ids * slot_count + local_slot, dump_index)
    pair_index = jnp.arange(pair_count, dtype=jnp.int32)
    slot_pair = (
        jnp.full((dump_index,), pair_count, jnp.int32)
        .at[target.reshape(-1)]
        .set(pair_index, mode="drop")
    )
    slot_token = jnp.where(slot_pair < pair_count, slot_pair // TOPK, tok_rows)
    slot_global = (
        jnp.full((dump_index,), -1, jnp.int32)
        .at[target.reshape(-1)]
        .set(global_slot.reshape(-1), mode="drop")
    )
    padded_rows = jnp.concatenate([normed2_low, jnp.zeros((1, model_width), jnp.bfloat16)], axis=0)
    send_rows = padded_rows[slot_token].reshape(group_count, local_count, slot_count, model_width)
    send_slot = slot_global.reshape(group_count, local_count, slot_count)
    received, received_slot = deliver(send_rows, send_slot)
    gate_lin, up_lin, activation, expert_out = expert_forward(received, w_gate, w_up, w_down)
    returned = bring_back(expert_out)
    returned_flat = jnp.concatenate(
        [returned.reshape(dump_index, model_width), jnp.zeros((1, model_width), returned.dtype)],
        axis=0,
    )
    pair_out = returned_flat[target]
    moe_part = jnp.sum(gate_weight[:, :, None] * pair_out, axis=1)
    moe_branch = lax.psum(moe_part.astype(jnp.bfloat16), "tensor").astype(jnp.float32)
    out_hidden = (residual + moe_branch).astype(jnp.bfloat16)
    grad_y = cotangent.astype(jnp.float32)
    gate_dot = jnp.sum(grad_y[:, None, :] * pair_out, axis=2)
    pair_grads = (
        (gate_weight[:, :, None] * grad_y[:, None, :])
        .astype(jnp.bfloat16)
        .reshape(pair_count, model_width)
    )
    pair_grads = jnp.concatenate([pair_grads, jnp.zeros((1, model_width), jnp.bfloat16)], axis=0)
    send_grad = pair_grads[slot_pair].reshape(group_count, local_count, slot_count, model_width)
    grad_received, grad_slot = deliver(send_grad, send_slot)
    grad_entry, grad_w_gate, grad_w_up, grad_w_down = expert_backward(
        received, gate_lin, up_lin, activation, grad_received, w_gate, w_up, w_down
    )
    grad_returned = bring_back(grad_entry)
    grad_flat = jnp.concatenate(
        [
            grad_returned.reshape(dump_index, model_width),
            jnp.zeros((1, model_width), grad_returned.dtype),
        ],
        axis=0,
    )
    grad_normed2_part = jnp.sum(grad_flat[target], axis=1, dtype=jnp.float32)
    grad_normed2_exp, gate_dot = lax.psum((grad_normed2_part, gate_dot), "tensor")
    grad_soft = gate_dot * kept_mask.astype(jnp.float32)
    grad_chosen = soft_gate * (grad_soft - jnp.sum(soft_gate * grad_soft, axis=1, keepdims=True))
    grad_logits = jnp.sum(
        grad_chosen[:, :, None] * (expert_ids[:, :, None] == expert_range).astype(jnp.float32),
        axis=1,
    ).astype(jnp.bfloat16)
    grad_w_router = jnp.einsum(
        "td,te->de", normed2_low, grad_logits, preferred_element_type=jnp.float32
    )
    grad_normed2 = grad_normed2_exp + jnp.einsum(
        "te,de->td", grad_logits, w_router, preferred_element_type=jnp.float32
    )
    norm2_pull = jax.vjp(norm_rows, residual, norm2_gain)[1]
    grad_resid_norm, grad_norm2 = norm2_pull(grad_normed2)
    grad_residual = grad_y + grad_resid_norm
    grad_residual_low = grad_residual.astype(jnp.bfloat16)
    grad_w_out = jnp.einsum(
        "tc,td->cd", att_cat, grad_residual_low, preferred_element_type=jnp.float32
    )
    grad_att_cat = jnp.einsum(
        "td,cd->tc", grad_residual_low, w_out, preferred_element_type=jnp.float32
    ).astype(jnp.bfloat16)
    grad_att_rows = jnp.transpose(
        grad_att_cat.reshape(tok_rows, local_heads, head_dim), (1, 0, 2)
    ).reshape(query_total, head_dim)

    def query_grad_block(operands):
        query_block, segment_block, place_block, grad_block, log_block = operands
        scores = jnp.einsum("qd,kd->qk", query_block, all_keys, preferred_element_type=jnp.float32)
        scores = jnp.where(visible(segment_block, place_block, all_segment, all_place), scores, NEG)
        probability = jnp.exp(scores - log_block[:, None])
        grad_prob = jnp.einsum(
            "qd,kd->qk", grad_block, all_values, preferred_element_type=jnp.float32
        )
        delta_row = jnp.sum(probability * grad_prob, axis=1)
        grad_scores = (probability * (grad_prob - delta_row[:, None])).astype(jnp.bfloat16)
        return (jnp.dot(grad_scores, all_keys, preferred_element_type=jnp.float32), delta_row)

    grad_query_rows, deltas = lax.map(
        query_grad_block,
        (
            query_rows.reshape(count_of_blocks, rows_per_block, head_dim),
            query_segment.reshape(count_of_blocks, rows_per_block),
            query_place.reshape(count_of_blocks, rows_per_block),
            grad_att_rows.reshape(count_of_blocks, rows_per_block, head_dim),
            log_totals,
        ),
    )
    log_flat = log_totals.reshape(query_total)
    delta_flat = deltas.reshape(query_total)
    key_block = math.gcd(lax.axis_size("expert") * tok_rows, 2048)

    def one_block(offset):
        key_part = lax.dynamic_slice_in_dim(all_keys, offset, key_block, 0)
        value_part = lax.dynamic_slice_in_dim(all_values, offset, key_block, 0)
        segment_part = lax.dynamic_slice_in_dim(all_segment, offset, key_block, 0)
        place_part = lax.dynamic_slice_in_dim(all_place, offset, key_block, 0)
        scores = jnp.einsum("qd,kd->qk", query_rows, key_part, preferred_element_type=jnp.float32)
        scores = jnp.where(
            visible(query_segment, query_place, segment_part, place_part), scores, NEG
        )
        probability = jnp.exp(scores - log_flat[:, None])
        grad_value = jnp.einsum(
            "qk,qd->kd",
            probability.astype(jnp.bfloat16),
            grad_att_rows,
            preferred_element_type=jnp.float32,
        )
        grad_prob = jnp.einsum(
            "qd,kd->qk", grad_att_rows, value_part, preferred_element_type=jnp.float32
        )
        grad_scores = (probability * (grad_prob - delta_flat[:, None])).astype(jnp.bfloat16)
        grad_key = jnp.einsum(
            "qk,qd->kd", grad_scores, query_rows, preferred_element_type=jnp.float32
        )
        return jnp.concatenate([grad_key, grad_value], axis=1)

    stacked = lax.map(
        one_block,
        jnp.arange(lax.axis_size("expert") * tok_rows // key_block, dtype=jnp.int32) * key_block,
    )
    key_value_grad = lax.psum_scatter(
        stacked.reshape(lax.axis_size("expert") * tok_rows, 2 * head_dim).astype(jnp.bfloat16),
        "expert",
        scatter_dimension=0,
        tiled=True,
    ).astype(jnp.float32)
    grad_key_post = key_value_grad[:, :head_dim].reshape(tok_rows, 1, head_dim)
    grad_values_low = key_value_grad[:, head_dim:].astype(jnp.bfloat16)
    grad_query_tok = jnp.transpose(
        grad_query_rows.reshape(local_heads, tok_rows, head_dim), (1, 0, 2)
    )
    query_pull = jax.vjp(partial(shape_queries, position=position), query_lin, query_gain)[1]
    grad_query_lin, grad_qgain_part = query_pull(grad_query_tok)
    key_pull = jax.vjp(partial(shape_keys, position=position), key_lin, key_gain)[1]
    grad_key_lin, grad_kgain_part = key_pull(grad_key_post)
    grad_query_low = grad_query_lin.astype(jnp.bfloat16)
    grad_key_low = grad_key_lin.astype(jnp.bfloat16)
    grad_w_query = jnp.einsum(
        "td,tc->dc", normed1_low, grad_query_low, preferred_element_type=jnp.float32
    )
    grad_w_key = jnp.einsum(
        "td,tc->dc", normed1_low, grad_key_low, preferred_element_type=jnp.float32
    )
    grad_w_value = jnp.einsum(
        "td,tc->dc", normed1_low, grad_values_low, preferred_element_type=jnp.float32
    )
    grad_normed1_part = jnp.einsum(
        "tc,dc->td", grad_query_low, w_query, preferred_element_type=jnp.float32
    )
    grad_normed1_part = grad_normed1_part + jnp.einsum(
        "tc,dc->td", grad_key_low, key_weight, preferred_element_type=jnp.float32
    )
    grad_normed1_part = grad_normed1_part + jnp.einsum(
        "tc,dc->td", grad_values_low, value_weight, preferred_element_type=jnp.float32
    )
    grad_normed1, grad_qgain_part, grad_kgain_part = (
        lax.psum(grad_normed1_part.astype(jnp.bfloat16), "tensor").astype(jnp.float32),
        lax.psum(grad_qgain_part.astype(jnp.bfloat16), "tensor").astype(jnp.float32),
        lax.psum(grad_kgain_part.astype(jnp.bfloat16), "tensor").astype(jnp.float32),
    )
    norm1_pull = jax.vjp(norm_rows, hidden, norm1_gain)[1]
    grad_hidden_norm, grad_norm1 = norm1_pull(grad_normed1)
    grad_hidden = (grad_residual + grad_hidden_norm).astype(jnp.bfloat16)
    summed = (
        lax.psum(grad_norm1.astype(jnp.bfloat16), "expert").astype(jnp.float32),
        lax.psum(grad_w_query.astype(jnp.bfloat16), "expert").astype(jnp.float32),
        lax.psum(grad_w_key.astype(jnp.bfloat16), "expert").astype(jnp.float32),
        lax.psum(grad_w_value.astype(jnp.bfloat16), "expert").astype(jnp.float32),
        lax.psum(grad_qgain_part.astype(jnp.bfloat16), "expert").astype(jnp.float32),
        lax.psum(grad_kgain_part.astype(jnp.bfloat16), "expert").astype(jnp.float32),
        lax.psum(grad_w_out.astype(jnp.bfloat16), "expert").astype(jnp.float32),
        lax.psum(grad_norm2.astype(jnp.bfloat16), "expert").astype(jnp.float32),
        lax.psum(grad_w_router.astype(jnp.bfloat16), "expert").astype(jnp.float32),
    )
    return (
        out_hidden,
        grad_hidden,
        summed[0],
        summed[1],
        summed[2],
        summed[3],
        summed[4],
        summed[5],
        summed[6],
        summed[7],
        summed[8],
        grad_w_gate,
        grad_w_up,
        grad_w_down,
    )


MESH = pl.DeviceIdType.MESH
FAR_FIRST = (3, -3, 2, -2, 1, -1, 0)


class Spot:
    def __init__(self):
        group, part = lax.axis_index("expert"), lax.axis_index("tensor")
        self.z, self.y = group // 2, group % 2
        self.x, self.c = part // 2, part % 2

    def has(self, dz):
        return (self.z + dz >= 0) & (self.z + dz <= 3)

    def device(self, dz=0, dy=0, dx=0, dc=0):
        y = 1 - self.y if dy else self.y
        x = 1 - self.x if dx else self.x
        c = 1 - self.c if dc else self.c
        return ((self.z + dz) * 2 + y, x * 2 + c)

    def rows(self, dz, dy, dx, dc, count):
        group, part = self.device(dz, dy, dx, dc)
        return pl.ds(pl.multiple_of((group * 4 + part) * count, count), count)

    def greet(self, line=False):
        barrier = pltpu.get_barrier_semaphore()
        for step in ((0, 1, 0, 0), (0, 0, 1, 0), (0, 0, 0, 1)):
            pl.semaphore_signal(barrier, inc=1, device_id=self.device(*step), device_id_type=MESH)
        for dz in (1, -1, 2, -2, 3, -3) if line else (1, -1):

            @pl.when(self.has(dz))
            def _(dz=dz):
                pl.semaphore_signal(
                    barrier, inc=1, device_id=self.device(dz), device_id_type=MESH
                )

        if line:
            pl.semaphore_wait(barrier, 6)
        else:
            inner = jnp.where((self.z > 0) & (self.z < 3), 1, 0)
            pl.semaphore_wait(barrier, 4 + inner)


def when_has(spot, dz, action):
    if dz == 0:
        action()
    else:
        pl.when(spot.has(dz))(action)


def dma_sems(shapes):
    return [pltpu.SemaphoreType.DMA(shape) if shape else pltpu.SemaphoreType.DMA for shape in shapes]


def add_into(into, chunk, *terms):
    @pl.loop(0, into.shape[0] // chunk)
    def _(step):
        rows = pl.ds(pl.multiple_of(step * chunk, chunk), chunk)
        for at in range(0, into.shape[1], 1024):
            columns = pl.ds(at, min(1024, into.shape[1] - at))
            total = into[rows, columns].astype(jnp.float32)
            for term in terms:
                total = total + term[rows, columns].astype(jnp.float32)
            into[rows, columns] = total.astype(into.dtype)


def push(src, dst, send_sem, recv_sem, device):
    pltpu.make_async_remote_copy(
        src_ref=src,
        dst_ref=dst,
        send_sem=send_sem,
        recv_sem=recv_sem,
        device_id=device,
        device_id_type=MESH,
    ).start()


def arrive(view, sem):
    pltpu.make_async_copy(view, view, sem).wait()


F32, BF16 = jnp.float32, jnp.bfloat16
VMEM_SPEC = pl.BlockSpec(memory_space=pltpu.VMEM)
HBM_SPEC = pl.BlockSpec(memory_space=pl.ANY)


def cost(flops, microseconds):
    return pl.CostEstimate(
        flops=flops, bytes_accessed=microseconds * 3_000_000, transcendentals=0
    )


def mxu(left, right, left_dim=1, right_dim=0):
    return lax.dot_general(
        left, right, (((left_dim,), (right_dim,)), ((), ())), preferred_element_type=F32
    )


def head_norm(lin):
    root = lax.rsqrt(jnp.mean(lin * lin, axis=-1, keepdims=True) + EPS)
    return lin * root, root


def near_first(step, z):
    high = z // 2
    folded = z + high * (3 - 2 * z)
    place = (step + folded * (1 - step // 2)) % 2 + 2 * (step // 2)
    return place + high * (3 - 2 * place)


class Gather:
    SEMS = ((5, 7), (7, 2), (6,), (7, 2, 2), None, (7, 2), (7, 2, 2))

    def __init__(
        self, spot, src, out, recv, z_send, sends, c_recv, local_sem, late_recv, late_send, full=None
    ):
        self.spot, self.src, self.out, self.full = spot, src, out, full
        self.recv, self.z_send, self.sends, self.c_recv = recv, z_send, sends, c_recv
        self.late_recv, self.late_send = late_recv, late_send
        self.count, self.width = src.shape
        width, late = self.width, self.width * 5 // 16
        half = width * 5 // 8 if full is not None else width // 2
        self.first, self.second = pl.ds(0, half), pl.ds(half, width - half)
        self.whole = pl.ds(0, width)
        self.early = (pl.ds(0, width - late), pl.ds(late, width - late))
        self.late = (pl.ds(width - late, late), pl.ds(0, late))
        if full is None:
            self.local = pltpu.make_async_copy(src, self.place(0, 0, 0), local_sem)
        else:
            group, _ = spot.device()
            rows = pl.ds(pl.multiple_of(group * 4 * self.count, 4 * self.count), 4 * self.count)
            self.local = pltpu.make_async_copy(full, out.at[rows, :], local_sem)

    def place(self, dz, dy, dx, dc=0, columns=None):
        rows = self.spot.rows(dz, dy, dx, dc, self.count)
        return self.out.at[rows, self.whole if columns is None else columns]

    def source(self, dz, dy, dx, columns):
        if dz == 0 and dy == 0 and dx == 0:
            return self.src.at[:, columns]
        if dz == 0 and dy == 0 and self.full is not None:
            _, part = self.spot.device(0, 0, 1)
            rows = pl.ds(pl.multiple_of(part * self.count, self.count), self.count)
            return self.full.at[rows, columns]
        return self.place(dz, dy, dx, 0, columns)

    def send(self, dz, dy, dx, columns, send_sem, recv_sem, device):
        push(
            self.source(dz, dy, dx, columns), self.place(dz, dy, dx, 0, columns), send_sem,
            recv_sem, device,
        )

    def to_core(self, dz, dy, dx):
        if dz == 0 and dy == 0 and self.full is not None:
            return
        self.send(
            dz, dy, dx, self.whole, self.sends.at[0], self.c_recv.at[dz + 3, dy, dx],
            self.spot.device(0, 0, 0, 1),
        )

    def along_z(self, dz, dy, dx, columns, send_sem, recv_sem):
        for side, step in ((0, 1), (1, -1)):
            if dz * step <= 0:

                @pl.when(self.spot.has(step))
                def _(side=side, step=step):
                    self.send(
                        dz, dy, dx, columns, send_sem(side), recv_sem(dz + 3 - step),
                        self.spot.device(step),
                    )

    def spread(self, dz):
        spot = self.spot
        self.along_z(
            dz, 0, 0, self.whole, lambda side: self.z_send.at[dz + 3, side],
            lambda at: self.recv.at[0, at],
        )
        if dz == 0:
            columns, at = (self.whole, self.whole), 0
        else:
            columns, at = self.early, 3
        self.send(
            dz, 0, 0, columns[0], self.sends.at[1 + at], self.recv.at[1, dz + 3], spot.device(0, 1)
        )
        if dz != 0 or self.full is None:
            self.send(
                dz, 0, 0, columns[1], self.sends.at[2 + at], self.recv.at[2, dz + 3],
                spot.device(0, 0, 1),
            )
        self.to_core(dz, 0, 0)

    def start(self):
        self.local.start()
        self.spread(0)

    def take_z(self, dz):
        def action():
            arrive(self.place(dz, 0, 0), self.recv.at[0, dz + 3])
            self.spread(dz)

        when_has(self.spot, dz, action)

    def take_yx(self, dz):
        spot = self.spot

        def action():
            columns = self.early if dz else (self.whole, self.whole)
            arrive(self.place(dz, 1, 0, 0, columns[0]), self.recv.at[1, dz + 3])
            self.send(
                dz, 1, 0, self.first, self.sends.at[3], self.recv.at[3, dz + 3],
                spot.device(0, 0, 1),
            )
            if dz != 0 or self.full is None:
                arrive(self.place(dz, 0, 1, 0, columns[1]), self.recv.at[2, dz + 3])
            self.send(
                dz, 0, 1, self.second, self.sends.at[3], self.recv.at[4, dz + 3],
                spot.device(0, 1),
            )

        when_has(spot, dz, action)

    def take_late(self, dz):
        def action():
            for dy, dx in ((1, 0), (0, 1)):
                columns = self.late[dx]
                if dz != 0:
                    arrive(self.place(dz, dy, dx, 0, columns), self.late_recv.at[dz + 3, dx])
                self.along_z(
                    dz, dy, dx, columns, lambda side: self.late_send.at[dz + 3, side, dx],
                    lambda at: self.late_recv.at[at, dx],
                )
                self.to_core(dz, dy, dx)

        when_has(self.spot, dz, action)

    def take_diagonal(self, dz):
        def action():
            arrive(self.place(dz, 1, 1, 0, self.first), self.recv.at[3, dz + 3])
            arrive(self.place(dz, 1, 1, 0, self.second), self.recv.at[4, dz + 3])
            self.to_core(dz, 1, 1)

        when_has(self.spot, dz, action)

    def take_core(self, far, dy, dx):
        view = self.out.at[pl.ds(0, self.count), :]
        arrive(view, self.c_recv.at[far - self.spot.z + 3, dy, dx])

    def drain(self):
        count, spot = self.count, self.spot
        replicated = self.full is not None
        for at, pieces, columns in (
            (0, 14 if replicated else 16, self.whole), (1, 1, self.whole), (2, 1, self.whole),
            (3, 4, self.whole), (4, 3, self.early[0]), (5, 3, self.early[1]),
        ):
            if at != 2 or not replicated:
                arrive(self.out.at[pl.ds(0, pieces * count), columns], self.sends.at[at])
        for dz in range(-3, 4):
            for side, step in ((0, 1), (1, -1)):
                if dz * step <= 0:

                    @pl.when(spot.has(dz) & spot.has(step))
                    def _(dz=dz, side=side):
                        arrive(self.place(0, 0, 0), self.z_send.at[dz + 3, side])
                        for at in (0, 1):
                            arrive(
                                self.place(0, 0, 0, 0, self.late[at]),
                                self.late_send.at[dz + 3, side, at],
                            )


def experts_kernel(
    normed, grad_y, w_gate, w_up, w_down, router, chosen, kept,
    reduced, grad_gate, grad_up, grad_down,
    rows_all, weight, grad_in, grad_in_down, y_block, back_block,
    mine, other, from_a, from_b, from_y, from_x, from_z,
    weight_sem, y_sem, flush_sem, core_send, core_recv, half_send, yx_send, recv,
    line_send, line_recv, *gather_sems,
):
    spot = Spot()
    count, width = normed.shape
    wide = reduced.shape[1]
    local_count, ff, _ = w_gate.shape
    both = local_count * ff
    block = 4 * count
    split = from_a.shape[2]
    first, second = pl.ds(0, split), pl.ds(split, wide - split)
    group = lax.axis_index("expert")
    to_y, to_x, to_c = spot.device(0, 1), spot.device(0, 0, 1), spot.device(0, 0, 0, 1)

    def place_of(step):
        return near_first((step // 2 + 1) % 4, spot.z), (step + (step + 6) // 8) % 2

    def group_rows(step):
        far, dy = place_of(step)
        y = spot.y + dy * (1 - 2 * spot.y)
        return pl.ds(pl.multiple_of((far * 2 + y) * block, block), block)

    def y_copy(step):
        slot = step % 2
        return pltpu.make_async_copy(
            grad_y.at[group_rows(step), :], y_block.at[slot], y_sem.at[slot]
        )

    sources = [ref.at[at] for ref in (w_gate, w_up) for at in range(local_count)]
    weights = [
        pltpu.make_async_copy(source, weight.at[pl.ds(at * ff, ff), :], weight_sem.at[at])
        for at, source in enumerate(sources)
    ]
    for copy in weights:
        copy.start()
    y_copy(0).start()
    gather = Gather(spot, normed, rows_all, *gather_sems)
    spot.greet()
    gather.start()
    grad_in[...] = jnp.zeros_like(grad_in)
    grad_in_down[...] = jnp.zeros_like(grad_in_down)
    gather.local.wait()
    for copy in weights:
        copy.wait()

    def piece(dx, dc):
        _, part = spot.device(0, 0, dx, dc)
        return pl.ds(pl.multiple_of(part * count, count), count)

    def core_copy(step, dx):
        far, dy = place_of(step)
        slot = step % 2
        return pltpu.make_async_remote_copy(
            src_ref=back_block.at[slot, piece(dx, 1), :],
            dst_ref=other.at[far, dy, dx],
            send_sem=core_send.at[slot, dx],
            recv_sem=core_recv.at[far, dy, dx],
            device_id=to_c,
            device_id_type=MESH,
        )

    def merge(far, dy, dx):
        into = mine.at[far, dy, dx]
        arrive(other.at[far, dy, dx], core_recv.at[far, dy, dx])
        return into

    def merge_diagonal(k):
        far = near_first(k, spot.z)
        into = merge(far, 1, 1)
        add_into(into, 16, other.at[far, 1, 1])
        push(into.at[:, first], from_a.at[far], half_send.at[0], recv.at[0, far], to_x)
        push(into.at[:, second], from_b.at[far], half_send.at[1], recv.at[1, far], to_y)

    def merge_yx(k):
        far = near_first(k, spot.z)
        into = merge(far, 1, 0)
        add_into(into, 16, other.at[far, 1, 0])
        arrive(from_a.at[far], recv.at[0, far])
        add_into(into.at[:, first], 16, from_a.at[far])
        push(into, from_y.at[far], yx_send.at[0], recv.at[2, far], to_y)
        into = merge(far, 0, 1)
        add_into(into, 16, other.at[far, 0, 1])
        arrive(from_b.at[far], recv.at[1, far])
        add_into(into.at[:, second], 16, from_b.at[far])
        push(into, from_x.at[far], yx_send.at[1], recv.at[3, far], to_x)

    def merge_line(k):
        far = near_first(k, spot.z)
        into = merge(far, 0, 0)
        arrive(from_y.at[far], recv.at[2, far])
        arrive(from_x.at[far], recv.at[3, far])
        add_into(into, 16, other.at[far, 0, 0], from_y.at[far], from_x.at[far])
        if k > 0:
            push(
                into, from_z.at[spot.z], line_send.at[k], line_recv.at[spot.z],
                (far * 2 + spot.y, spot.x * 2 + spot.c),
            )

    def both_ways(take, distance):
        for dz in (distance, -distance) if distance else (0,):
            take(dz)

    columns = lax.broadcasted_iota(jnp.int32, (block, both), 1)
    lower = columns < ff
    lanes = lax.broadcasted_iota(jnp.int32, (block, 128), 1)
    names = lax.broadcasted_iota(jnp.int32, (router.shape[0], block), 0)

    def compute(step):
        slot = step % 2
        here = group_rows(step)
        rows = rows_all[here, :]
        lin = mxu(rows, weight[...], 1, 1)
        gate, up = lin[:, :both], lin[:, both:]
        logits = mxu(router[...], rows, 1, 1)
        picked = chosen[:, here] > 0.0
        top = jnp.max(jnp.where(picked, logits, NEG), axis=0, keepdims=True)
        exps = jnp.where(picked, jnp.exp(logits - top), 0.0)
        soft = exps / jnp.sum(exps, axis=0, keepdims=True)
        keep = kept[:, here]
        soft = jnp.where(keep > 0.0, soft, 0.0)
        lines = []
        for table in (soft, keep):
            for at in range(local_count):
                lines.append(
                    jnp.sum(
                        jnp.where(names == group * local_count + at, table, 0.0),
                        axis=0, keepdims=True,
                    )
                )
        stack = jnp.concatenate(lines + [jnp.zeros((8 - len(lines), block), F32)], axis=0).T
        spread = jnp.where(lower, stack[:, 0:1], stack[:, 1:2])
        sigmoid = 1.0 / (1.0 + jnp.exp(-gate))
        silu = gate * sigmoid
        act = (silu * up).astype(BF16).astype(F32)
        weighted = (act * spread).astype(BF16)
        y_copy(step).wait()

        @pl.when(step >= 2)
        def _():
            for dx in (0, 1):
                core_copy(step - 2, dx).wait_send()

        back_block[slot, :, :width] = mxu(weighted, w_down[...]).astype(BF16)
        pass_on(step, 1)
        y_rows = y_block[slot]
        mid = mxu(y_rows, w_down[...], 1, 1)
        dots = act * mid
        low = jnp.sum(jnp.where(lower, dots, 0.0), axis=1, keepdims=True) * stack[:, 2:3]
        high = jnp.sum(jnp.where(lower, 0.0, dots), axis=1, keepdims=True) * stack[:, 3:4]
        mine_at = group * local_count
        tail = jnp.where(lanes == mine_at, low, jnp.where(lanes == mine_at + 1, high, 0.0))
        grad_act = mid * spread
        grad_up_lin = (grad_act * silu).astype(BF16)
        grad_gate_lin = (grad_act * up * sigmoid * (1.0 + gate * (1.0 - sigmoid))).astype(BF16)
        grad_lin = jnp.concatenate([grad_gate_lin, grad_up_lin], axis=1)
        back_block[slot, :, width : 2 * width] = mxu(grad_lin, weight[...]).astype(BF16)
        back_block[slot, :, 2 * width :] = tail.astype(BF16)
        far, dy = place_of(step)
        for dx in (1, 0):
            core_copy(step, dx).start()
            mine[far, dy, dx] = back_block[slot, piece(dx, 0), :]
        grad_in[...] += mxu(grad_lin, rows, 0, 0)
        grad_in_down[...] += mxu(weighted, y_rows, 0, 0)

    plans = {
        0: lambda: (
            both_ways(gather.take_yx, 0), both_ways(gather.take_z, 1),
            both_ways(gather.take_z, 2), both_ways(gather.take_diagonal, 0),
            both_ways(gather.take_late, 0), both_ways(gather.take_yx, 1),
            both_ways(gather.take_z, 3), both_ways(gather.take_late, 1),
        ),
        1: lambda: both_ways(gather.take_yx, 2),
        2: lambda: (both_ways(gather.take_diagonal, 1), both_ways(gather.take_late, 2)),
        3: lambda: both_ways(gather.take_yx, 3),
        4: lambda: (both_ways(gather.take_diagonal, 2), both_ways(gather.take_late, 3)),
        5: lambda: merge_diagonal(1),
        6: lambda: both_ways(gather.take_diagonal, 3),
        7: lambda: merge_diagonal(2),
        9: lambda: merge_yx(1),
        11: lambda: (merge_diagonal(3), merge_yx(2)),
        13: lambda: merge_line(1),
        15: lambda: (merge_diagonal(0), merge_yx(3)),
    }

    def pass_on(step, middle):
        for at, plan in plans.items():
            if at % 2 == middle:

                @pl.when(step == at // 2)
                def _(plan=plan):
                    plan()

    @pl.loop(0, 8)
    def _(step):
        pass_on(step, 0)

        @pl.when(step < 7)
        def _():
            y_copy(step + 1).start()

        far, dy = place_of(step)
        for dx in (0, 1):
            gather.take_core(far, dy, dx)
        compute(step)

    flush = [
        pltpu.make_async_copy(
            grad_in.at[pl.ds(at * ff, ff), :],
            (grad_gate, grad_up)[at // local_count].at[at % local_count],
            flush_sem.at[at],
        )
        for at in range(2 * local_count)
    ]
    flush.append(pltpu.make_async_copy(grad_in_down, grad_down, flush_sem.at[2 * local_count]))
    for copy in flush:
        copy.start()
    merge_line(2)
    merge_yx(0)
    merge_line(3)
    merge_line(0)
    total = mine[spot.z, 0, 0].astype(F32)
    for k in (1, 2, 3):
        source = near_first(k, spot.z)
        arrive(from_z.at[source], line_recv.at[source])
        total = total + from_z[source].astype(F32)
    reduced[...] = total
    gather.drain()
    for step in (6, 7):
        for dx in (0, 1):
            core_copy(step, dx).wait_send()
    arrive(from_a, half_send.at[0])
    arrive(from_b, half_send.at[1])
    arrive(from_y, yx_send.at[0])
    arrive(from_x, yx_send.at[1])
    for k in (1, 2, 3):
        arrive(from_z.at[0], line_send.at[k])
    for copy in flush:
        copy.wait()


def experts(normed, grad_y, w_gate, w_up, w_down, router, chosen, kept):
    count, width = normed.shape
    wide = 2 * width + 128
    total = grad_y.shape[0]
    local_count, ff, _ = w_gate.shape
    both = local_count * ff
    shape, vmem, dma = jax.ShapeDtypeStruct, pltpu.VMEM, pltpu.SemaphoreType.DMA
    line = vmem((4, count, wide), BF16)
    return pl.pallas_call(
        experts_kernel,
        out_shape=(
            shape((count, wide), F32),
            shape(w_gate.shape, F32), shape(w_up.shape, F32), shape((both, width), F32),
        ),
        in_specs=[VMEM_SPEC, HBM_SPEC, HBM_SPEC, HBM_SPEC] + [VMEM_SPEC] * 4,
        out_specs=(VMEM_SPEC,) + (HBM_SPEC,) * 3,
        scratch_shapes=[
            vmem((total, width), BF16),
            vmem((2 * both, width), BF16),
            vmem((2 * both, width), F32),
            vmem((both, width), F32),
            vmem((2, 4 * count, width), BF16),
            vmem((2, 4 * count, wide), BF16),
            vmem((4, 2, 2, count, wide), BF16),
            vmem((4, 2, 2, count, wide), BF16),
            vmem((4, count, width), BF16),
            vmem((4, count, wide - width), BF16),
            line, line, line,
        ]
        + dma_sems(
            ((2 * local_count,), (2,), (2 * local_count + 1,), (2, 2), (4, 2, 2), (2,), (2,), (4, 4),
             (4,), (4,))
            + Gather.SEMS
        ),
        compiler_params=pltpu.CompilerParams(
            collective_id=8, has_side_effects=True, vmem_limit_bytes=63 << 20
        ),
        name="experts",
        cost_estimate=cost(29_000_000_000, 120),
    )(normed, grad_y, w_gate, w_up, w_down, router, chosen, kept)


def attend_back_kernel(
    own_rows, w_out, queries, keys, values, attended, lin, cosine, sine, place_column,
    place_row, open_row, log_total, k_gain, q_gain,
    grad_lin, grad_out, grad_q_gain, grad_k_gain,
    rows_all, head_out, grad_keys, grad_values, out_sum, head_sem, *gather_sems,
):
    spot = Spot()
    count = own_rows.shape[0]
    block = 4 * count
    dim = queries.shape[1]
    group = lax.axis_index("expert")
    head_copy = pltpu.make_async_copy(
        w_out.at[pl.ds(pl.multiple_of(group * dim, dim), dim), :], head_out, head_sem
    )
    head_copy.start()
    gather = Gather(spot, own_rows, rows_all, *gather_sems)
    spot.greet()
    gather.start()
    grad_keys[...] = jnp.zeros_like(grad_keys)
    grad_values[...] = jnp.zeros_like(grad_values)
    out_sum[...] = jnp.zeros_like(out_sum)
    grad_q_gain[...] = jnp.zeros_like(grad_q_gain)
    gather.local.wait()
    head_copy.wait()

    def unshape(grad, plain, gain, cos, sin):
        grad = grad * cos + pltpu.roll(grad * sin, dim // 2, 1)
        normed, root = head_norm(plain)
        gain_part = jnp.sum(grad * normed, axis=0, keepdims=True)
        grad = grad * gain
        return root * (grad - normed * jnp.mean(grad * normed, axis=-1, keepdims=True)), gain_part

    def compute(far, dy):
        y = spot.y + dy * (1 - 2 * spot.y)
        here = pl.ds(pl.multiple_of((far * 2 + y) * block, block), block)
        rows = rows_all[here, :]
        query = queries[here, :]
        grad_att = mxu(rows, head_out[...], 1, 1).astype(BF16)
        scores = mxu(keys[...], query, 1, 1)
        seen = (place_column[...] <= place_row[:, here]) & (place_column[...] >= open_row[:, here])
        probability = jnp.exp(jnp.where(seen, scores - log_total[:, here], NEG))
        grad_prob = mxu(values[...], grad_att, 1, 1)
        delta = jnp.sum(probability * grad_prob, axis=0, keepdims=True)
        grad_scores = (probability * (grad_prob - delta)).astype(BF16)
        grad_values[...] += mxu(probability.astype(BF16), grad_att)
        grad_keys[...] += mxu(grad_scores, query)
        grad_query = mxu(grad_scores, keys[...], 0, 0) * dim**-0.5
        grad_query, gain_part = unshape(
            grad_query, lin[here, :dim], q_gain[...], cosine[here, :], sine[here, :]
        )
        grad_q_gain[...] += gain_part
        grad_lin[here, :dim] = grad_query.astype(BF16)
        out_sum[...] += mxu(attended[here, :], rows, 0, 0)

    def both_ways(take, distance):
        for dz in (distance, -distance) if distance else (0,):
            take(dz)

    plans = {
        0: lambda: (both_ways(gather.take_yx, 0), both_ways(gather.take_z, 1),
                    both_ways(gather.take_late, 0)),
        1: lambda: (both_ways(gather.take_diagonal, 0), both_ways(gather.take_z, 2)),
        2: lambda: (both_ways(gather.take_yx, 1), both_ways(gather.take_z, 3),
                    both_ways(gather.take_late, 1)),
        3: lambda: (both_ways(gather.take_yx, 2), both_ways(gather.take_diagonal, 1),
                    both_ways(gather.take_late, 2)),
        4: lambda: (both_ways(gather.take_yx, 3), both_ways(gather.take_late, 3)),
        5: lambda: both_ways(gather.take_diagonal, 2),
        7: lambda: both_ways(gather.take_diagonal, 3),
    }

    @pl.loop(0, 8)
    def _(step):
        for at, plan in plans.items():

            @pl.when(step == at)
            def _(plan=plan):
                plan()

        far, dy = near_first(step // 2, spot.z), step % 2
        for dx in (0, 1):
            gather.take_core(far, dy, dx)
        compute(far, dy)

    grad_out[...] = out_sum[...].astype(BF16)
    grad_key, key_part = unshape(grad_keys[...], lin[:, dim:], k_gain[...], cosine[...], sine[...])
    grad_lin[:, dim : 2 * dim] = grad_key.astype(BF16)
    grad_lin[:, 2 * dim :] = grad_values[...].astype(BF16)
    grad_k_gain[...] = key_part
    gather.drain()


def attend_back(
    own_rows, w_out, queries, keys, values, attended, lin, cosine, sine, place_column,
    place_row, open_row, log_total, k_gain, q_gain,
):
    count, width = own_rows.shape
    total, dim = keys.shape
    shape, vmem = jax.ShapeDtypeStruct, pltpu.VMEM
    return pl.pallas_call(
        attend_back_kernel,
        out_shape=[
            shape((total, 3 * dim), BF16), shape((dim, width), BF16),
            shape((1, dim), F32), shape((1, dim), F32),
        ],
        in_specs=[VMEM_SPEC, HBM_SPEC] + [VMEM_SPEC] * 13,
        out_specs=[VMEM_SPEC] * 4,
        scratch_shapes=[
            vmem((total, width), BF16), vmem((dim, width), BF16),
            vmem((total, dim), F32), vmem((total, dim), F32), vmem((dim, width), F32),
        ]
        + dma_sems((None,) + Gather.SEMS),
        compiler_params=pltpu.CompilerParams(
            collective_id=9, has_side_effects=True, vmem_limit_bytes=60 << 20
        ),
        name="attend_back",
        cost_estimate=cost(9_000_000_000, 50),
    )(
        own_rows, w_out, queries, keys, values, attended, lin, cosine, sine, place_column,
        place_row, open_row, log_total, k_gain, q_gain,
    )


class LineGather:
    SEMS = ((7,), (7,), (7, 2), None, None, (7, 2), (7, 2, 2), None)

    def __init__(self, spot, place, own, sems):
        self.spot, self.place, self.own = spot, place, own
        self.z_recv, self.y_recv, self.z_send, self.y_send = sems[:4]
        self.late_y_recv, self.late_z_recv, self.late_z_send, self.late_y_send = sems[4:]

    def source(self, dz, dy, part):
        return self.own(part) if dz == 0 and dy == 0 else self.place(dz, dy, part)

    def along_z(self, dz, dy, part):
        for side, step in ((0, 1), (1, -1)):
            if dz * step <= 0:

                @pl.when(self.spot.has(step))
                def _(side=side, step=step):
                    if part:
                        send = self.late_z_send.at[dz + 3, side, dy]
                        recv = self.late_z_recv.at[dz + 3 - step, dy]
                    else:
                        send = self.z_send.at[dz + 3, side]
                        recv = self.z_recv.at[dz + 3 - step]
                    push(
                        self.source(dz, dy, part), self.place(dz, dy, part), send, recv,
                        self.spot.device(step),
                    )

    def along_y(self, dz):
        push(
            self.source(dz, 0, 0), self.place(dz, 0, 0), self.y_send, self.y_recv.at[dz + 3],
            self.spot.device(0, 1),
        )

    def start(self):
        self.along_z(0, 0, 0)
        push(
            self.own(1), self.place(0, 0, 1), self.late_y_send, self.late_y_recv,
            self.spot.device(0, 1),
        )
        self.along_y(0)
        self.along_z(0, 0, 1)

    def take_z(self, distance):
        for dz in (distance, -distance):

            def action(dz=dz):
                arrive(self.place(dz, 0, 0), self.z_recv.at[dz + 3])
                self.along_z(dz, 0, 0)
                self.along_y(dz)

            when_has(self.spot, dz, action)

    def take_late_y(self):
        arrive(self.place(0, 1, 1), self.late_y_recv)
        self.along_z(0, 1, 1)

    def take_late_z(self, distance):
        for dz in (distance, -distance):

            def action(dz=dz):
                for dy in (0, 1):
                    arrive(self.place(dz, dy, 1), self.late_z_recv.at[dz + 3, dy])
                    self.along_z(dz, dy, 1)

            when_has(self.spot, dz, action)

    def drain(self, four):
        for dz in (0, 1, -1, 2, -2, 3, -3):

            def action(dz=dz):
                arrive(self.place(dz, 1, 0), self.y_recv.at[dz + 3])
                for side, step in ((0, 1), (1, -1)):
                    if dz * step <= 0:

                        @pl.when(self.spot.has(step))
                        def _(side=side):
                            arrive(self.place(dz, 0, 0), self.z_send.at[dz + 3, side])
                            for dy in (0, 1):
                                arrive(
                                    self.place(dz, dy, 1), self.late_z_send.at[dz + 3, side, dy]
                                )

            when_has(self.spot, dz, action)
        arrive(four, self.y_send)
        arrive(self.place(0, 0, 1), self.late_y_send)


def close_kernel(
    normed, grad_lin, w_query, w_key, w_value, head_out,
    reduced, kv_all, query_all, out_all,
    weight, rows, sums, query_own, kv_part, back, mine, other, from_x_diagonal, from_y, from_x,
    from_z, kv_mine, kv_y, kv_z, kv_own, row_sem, weight_sem, local_sem,
    core_send, core_recv, many_send, recv, line_send, line_recv,
    kv_send, kv_y_recv, kv_line_send, kv_line_recv, *gather_sems,
):
    spot = Spot()
    total, width = normed.shape
    count, wide = reduced.shape
    block = 4 * count
    dim = w_key.shape[1]
    group = lax.axis_index("expert")
    to_y, to_x, to_c = spot.device(0, 1), spot.device(0, 0, 1), spot.device(0, 0, 0, 1)
    cut = 1664

    def parts(part):
        return pl.ds(cut, total - cut) if part else pl.ds(0, cut)

    def lane_block(dz, dy):
        return pl.ds(pl.multiple_of(spot.device(dz, dy)[0] * dim, dim), dim)

    weights = [
        pltpu.make_async_copy(
            w_query.at[:, pl.ds(pl.multiple_of(group * dim, dim), dim)],
            weight.at[:, pl.ds(0, dim)], weight_sem.at[0],
        ),
        pltpu.make_async_copy(w_key, weight.at[:, pl.ds(dim, dim)], weight_sem.at[1]),
        pltpu.make_async_copy(w_value, weight.at[:, pl.ds(2 * dim, dim)], weight_sem.at[2]),
    ]

    def row_copy(step):
        return pltpu.make_async_copy(
            normed.at[pl.ds(pl.multiple_of(step * block, block), block), :],
            rows.at[step % 2], row_sem.at[step % 2],
        )

    for copy in weights:
        copy.start()
    row_copy(0).start()
    outs = LineGather(
        spot,
        lambda dz, dy, part: out_all.at[lane_block(dz, dy), parts(part)],
        lambda part: head_out.at[:, parts(part)],
        gather_sems[:8],
    )
    queries = LineGather(
        spot,
        lambda dz, dy, part: query_all.at[parts(part), lane_block(dz, dy)],
        lambda part: query_own.at[parts(part), :],
        gather_sems[8:16],
    )
    kv_rows = total // 8

    def kv_span(start, part):
        return pl.ds(pl.multiple_of(start + part * (kv_rows // 2), kv_rows // 2), kv_rows // 2)

    kvs = LineGather(
        spot,
        lambda dz, dy, part: kv_all.at[kv_span(spot.device(dz, dy)[0] * kv_rows, part), :],
        lambda part: kv_own.at[kv_span(0, part), :],
        gather_sems[16:],
    )
    out_copy = pltpu.make_async_copy(head_out, out_all.at[lane_block(0, 0), :], local_sem.at[0])
    out_copy.start()
    spot.greet(line=True)
    outs.start()

    sums[...] = jnp.zeros_like(sums)

    @pl.loop(0, total // block)
    def _(step):
        @pl.when(step < total // block - 1)
        def _():
            row_copy(step + 1).start()

        row_copy(step).wait()
        here = pl.ds(pl.multiple_of(step * block, block), block)
        sums[...] += mxu(grad_lin[here, :], rows[step % 2], 0, 0)

    query_own[...] = sums[:dim, :].T.astype(BF16)
    kv_part[...] = sums[dim:, :].T.astype(BF16)
    query_copy = pltpu.make_async_copy(query_own, query_all.at[:, lane_block(0, 0)], local_sem.at[1])
    query_copy.start()

    def group_rows(far, dy):
        y = spot.y + dy * (1 - 2 * spot.y)
        return pl.ds(pl.multiple_of((far * 2 + y) * block, block), block)

    for k in (3, 2, 1, 0):
        far = near_first(k, spot.z)
        push(
            kv_part.at[group_rows(far, 1), :], kv_y.at[far], kv_send, kv_y_recv.at[far], to_y
        )
    for copy in weights:
        copy.wait()

    def piece(dx, dc):
        _, part = spot.device(0, 0, dx, dc)
        return pl.ds(pl.multiple_of(part * count, count), count)

    def core_copy(step, far, dy, dx):
        return pltpu.make_async_remote_copy(
            src_ref=back.at[step % 2, piece(dx, 1), :],
            dst_ref=other.at[far, dy, dx],
            send_sem=core_send.at[step % 2, dx],
            recv_sem=core_recv.at[far, dy, dx],
            device_id=to_c,
            device_id_type=MESH,
        )

    def produce(k):
        far = near_first(k, spot.z)
        for dy in (1, 0):
            step = 2 * (3 - k) + 1 - dy
            if step >= 2:
                for dx in (1, 0):
                    core_copy(step, far, dy, dx).wait_send()
            here = group_rows(far, dy)
            back[step % 2] = mxu(grad_lin[here, :], weight[...], 1, 1).astype(BF16)
            for dx in (1, 0):
                core_copy(step, far, dy, dx).start()
                mine[far, dy, dx] = back[step % 2, piece(dx, 0), :]

    def merge(far, dy, dx, *terms):
        arrive(other.at[far, dy, dx], core_recv.at[far, dy, dx])
        add_into(mine.at[far, dy, dx], 16, other.at[far, dy, dx], *terms)
        return mine.at[far, dy, dx]

    def merge_diagonal(k):
        far = near_first(k, spot.z)
        push(
            merge(far, 1, 1), from_x_diagonal.at[far], many_send.at[0], recv.at[0, far], to_x
        )

    def merge_yx(k):
        far = near_first(k, spot.z)
        push(merge(far, 0, 1), from_x.at[far], many_send.at[1], recv.at[1, far], to_x)
        arrive(from_x_diagonal.at[far], recv.at[0, far])
        push(
            merge(far, 1, 0, from_x_diagonal.at[far]), from_y.at[far], many_send.at[2],
            recv.at[2, far], to_y,
        )

    def far_device(far):
        return (far * 2 + spot.y, spot.x * 2 + spot.c)

    def merge_kv(k):
        far = near_first(k, spot.z)
        kv_mine[far] = kv_part[group_rows(far, 0), :]
        arrive(kv_y.at[far], kv_y_recv.at[far])
        add_into(kv_mine.at[far], 64, kv_y.at[far])
        if k > 0:
            push(
                kv_mine.at[far], kv_z.at[spot.z], kv_line_send.at[k], kv_line_recv.at[spot.z],
                far_device(far),
            )

    def merge_line(k):
        far = near_first(k, spot.z)
        arrive(from_y.at[far], recv.at[2, far])
        arrive(from_x.at[far], recv.at[1, far])
        into = merge(far, 0, 0, from_y.at[far], from_x.at[far])
        if k > 0:
            push(
                into, from_z.at[spot.z], line_send.at[k], line_recv.at[spot.z], far_device(far)
            )

    def sum_kv():
        sums_kv = kv_mine[spot.z].astype(F32)
        for k in (1, 2, 3):
            source = near_first(k, spot.z)
            arrive(kv_z.at[source], kv_line_recv.at[source])
            sums_kv = sums_kv + kv_z[source].astype(F32)
        kv_own[...] = sums_kv.astype(BF16)

    produce(3)
    produce(2)
    outs.take_z(1)
    for k in (3, 2, 1, 0):
        merge_kv(k)
    queries.start()
    merge_diagonal(3)
    produce(1)
    merge_diagonal(2)
    outs.take_late_y()
    produce(0)
    merge_diagonal(1)
    sum_kv()
    kvs.start()
    kv_copy = pltpu.make_async_copy(
        kv_own, kv_all.at[pl.ds(pl.multiple_of(group * kv_rows, kv_rows), kv_rows), :],
        local_sem.at[2],
    )
    kv_copy.start()
    outs.take_z(2)
    queries.take_z(1)
    merge_diagonal(0)
    merge_yx(3)
    kvs.take_z(1)
    kvs.take_late_y()
    queries.take_late_y()
    outs.take_late_z(1)
    merge_yx(2)
    outs.take_z(3)
    queries.take_z(2)
    kvs.take_z(2)
    kvs.take_late_z(1)
    merge_line(3)
    merge_yx(1)
    queries.take_late_z(1)
    outs.take_late_z(2)
    kvs.take_z(3)
    kvs.take_late_z(2)
    merge_line(2)
    merge_yx(0)
    queries.take_z(3)
    queries.take_late_z(2)
    outs.take_late_z(3)
    merge_line(1)
    merge_line(0)
    kvs.take_late_z(3)
    queries.take_late_z(3)
    total_rows = mine[spot.z, 0, 0].astype(F32)
    for k in (1, 2, 3):
        source = near_first(k, spot.z)
        arrive(from_z.at[source], line_recv.at[source])
        total_rows = total_rows + from_z[source].astype(F32)
    reduced[...] = total_rows

    kvs.drain(kv_all.at[pl.ds(0, 2 * kv_rows), :])
    kv_copy.wait()
    outs.drain(out_all.at[pl.ds(0, 4 * dim), parts(0)])
    queries.drain(query_all.at[parts(0), pl.ds(0, 4 * dim)])
    out_copy.wait()
    query_copy.wait()
    for step in (6, 7):
        for dx in (0, 1):
            core_copy(step, near_first(0, spot.z), 0, dx).wait_send()
    arrive(from_x_diagonal, many_send.at[0])
    arrive(from_x, many_send.at[1])
    arrive(from_y, many_send.at[2])
    arrive(kv_y, kv_send)
    for k in (1, 2, 3):
        arrive(from_z.at[0], line_send.at[k])
        arrive(kv_z.at[0], kv_line_send.at[k])


def close(normed, grad_lin, w_query, w_key, w_value, head_out):
    total, width = normed.shape
    count, wide, dim = total // 32, width, w_key.shape[1]
    shape, vmem = jax.ShapeDtypeStruct, pltpu.VMEM
    line, kv_line = vmem((4, count, wide), BF16), vmem((4, 4 * count, 2 * dim), BF16)
    return pl.pallas_call(
        close_kernel,
        out_shape=(
            shape((count, wide), F32), shape((total, 2 * dim), BF16),
            shape((total, 8 * dim), BF16), shape((8 * dim, width), BF16),
        ),
        in_specs=[HBM_SPEC, VMEM_SPEC, HBM_SPEC, HBM_SPEC, HBM_SPEC, VMEM_SPEC],
        out_specs=(VMEM_SPEC, HBM_SPEC, HBM_SPEC, HBM_SPEC),
        scratch_shapes=[
            vmem((width, 3 * dim), BF16), vmem((2, 4 * count, width), BF16),
            vmem((3 * dim, width), F32), vmem((width, dim), BF16), vmem((width, 2 * dim), BF16),
            vmem((2, 4 * count, wide), BF16),
            vmem((4, 2, 2, count, wide), BF16), vmem((4, 2, 2, count, wide), BF16),
            line, line, line, line, kv_line, kv_line, kv_line,
            vmem((4 * count, 2 * dim), BF16),
        ]
        + dma_sems(
            ((2,), (3,), (3,), (2, 2), (4, 2, 2), (3,), (3, 4), (4,), (4,),
             None, (4,), (4,), (4,)) + LineGather.SEMS * 3
        ),
        compiler_params=pltpu.CompilerParams(
            collective_id=10, has_side_effects=True, vmem_limit_bytes=60 << 20
        ),
        name="close",
        cost_estimate=cost(7_000_000_000, 110),
    )(normed, grad_lin, w_query, w_key, w_value, head_out)


def cosine_sine(angles):
    lanes = lax.broadcasted_iota(jnp.int32, angles.shape, 1)
    turns = jnp.floor(angles * (2.0 / math.pi) + 0.5)
    rest = angles - turns * 1.5703125
    rest = rest - turns * 4.837512969970703125e-4
    rest = rest - turns * 7.54978995489188216e-8
    square = rest * rest
    sine = square * (8.3321608736e-3 + square * -1.9515295891e-4) - 1.6666654611e-1
    sine = rest + rest * square * sine
    cosine = -1.388731625493765e-3 + square * 2.443315711809948e-5
    cosine = 1.0 - 0.5 * square + square * square * (4.166664568298827e-2 + square * cosine)
    turns = jnp.where(lanes < angles.shape[1] // 2, turns, turns - 1.0)
    turns = turns - 4.0 * jnp.floor(turns * 0.25)
    odd = (turns == 1.0) | (turns == 3.0)
    value = jnp.where(odd, sine, cosine)
    return jnp.where((turns == 1.0) | (turns == 2.0), -value, value)


def front_kernel(
    hidden, cotangent, tag, lengths, gain, w_query, w_key, w_value, q_gain, k_gain, inverse,
    w_out, second_gain,
    normed_all, queries, keys, values, lin_out, cosine, sine, attended, log_total,
    place_row, open_row, place_column, residual, normed, chosen, kept, grad_y_all,
    rows_all, weight, out_weight, staged, tags, ranks, picks, att_rows,
    partial_sum, from_core, to_x_sum, from_x,
    weight_sem, stage_sem, tag_z, tag_y, tag_z_send, tag_y_send, tag_local,
    send_sem, recv_sem, own_sem, tensor_sems, *gather_sems,
):
    spot = Spot()
    group, part = lax.axis_index("expert"), lax.axis_index("tensor")
    count, width = residual.shape
    block = 4 * count
    total = 32 * count
    dim = w_key.shape[1]
    own = pl.ds(pl.multiple_of(part * count, count), count)

    weights = [
        pltpu.make_async_copy(
            w_query.at[:, pl.ds(pl.multiple_of(group * dim, dim), dim)],
            weight.at[:, pl.ds(0, dim)], weight_sem.at[0],
        ),
        pltpu.make_async_copy(w_key, weight.at[:, pl.ds(dim, dim)], weight_sem.at[1]),
        pltpu.make_async_copy(w_value, weight.at[:, pl.ds(2 * dim, dim)], weight_sem.at[2]),
        pltpu.make_async_copy(w_out, out_weight, weight_sem.at[3]),
    ]
    for copy in weights:
        copy.start()
    barrier = pltpu.get_barrier_semaphore()

    @pl.loop(1, 8)
    def _(step):
        pl.semaphore_signal(
            barrier, inc=1, device_id=((group + step) % 8, part), device_id_type=MESH
        )

    for device in (spot.device(0, 0, 1), spot.device(0, 0, 0, 1)):
        pl.semaphore_signal(barrier, inc=1, device_id=device, device_id_type=MESH)

    def tag_place(dz, dy):
        return tags.at[spot.device(dz, dy)[0]]

    tag_copy = pltpu.make_async_copy(tag, tag_place(0, 0), tag_local)
    tag_copy.start()
    pl.semaphore_wait(barrier, 9)

    def spread_tag(dz):
        here = tag_place(dz, 0)
        source = tag if dz == 0 else here
        for side, step in ((0, 1), (1, -1)):
            if dz * step <= 0:

                @pl.when(spot.has(step))
                def _(side=side, step=step):
                    push(
                        source, here, tag_z_send.at[dz + 3, side], tag_z.at[dz + 3 - step],
                        spot.device(step),
                    )

        push(source, here, tag_y_send.at[dz + 3], tag_y.at[dz + 3], spot.device(0, 1))

    def take_tag(dz):
        def action():
            arrive(tag_place(dz, 0), tag_z.at[dz + 3])
            spread_tag(dz)

        when_has(spot, dz, action)

    def take_tag_y(dz):
        when_has(spot, dz, lambda: arrive(tag_place(dz, 1), tag_y.at[dz + 3]))

    spread_tag(0)
    gather = Gather(spot, hidden.at[own, :], rows_all, *gather_sems[:7], full=hidden)
    gather.start()
    late = Gather(spot, cotangent.at[own, :], grad_y_all, *gather_sems[7:], full=cotangent)
    tag_copy.wait()
    gather.local.wait()
    for copy in weights:
        copy.wait()

    def group_of(step):
        far, dy = near_first(step // 2, spot.z), step % 2
        return far, dy, far * 2 + spot.y + dy * (1 - 2 * spot.y)

    def stage_copy(step):
        _, _, index = group_of(step)
        return pltpu.make_async_copy(
            staged.at[step % 2],
            normed_all.at[pl.ds(pl.multiple_of(index * block, block), block), :],
            stage_sem.at[step % 2],
        )

    experts_count = chosen.shape[0]
    names = lax.broadcasted_iota(jnp.int32, (experts_count, block), 0)
    lanes = lax.broadcasted_iota(jnp.int32, (block, dim), 1)

    def project_group(step):
        _, _, index = group_of(step)
        here = pl.ds(pl.multiple_of(index * block, block), block)
        entries = tags[index]
        place = entries[0:1, :]
        segment, opening, bound = jnp.zeros_like(place), jnp.zeros_like(place), 0
        for at in range(lengths.shape[0]):
            bound = bound + lengths[at]
            segment = segment + jnp.where(place >= bound, 1, 0)
            opening = jnp.where(place >= bound, bound, opening)
        place_row[:, here] = place.astype(F32)
        open_row[:, here] = opening.astype(F32)
        lines = jnp.concatenate(
            [place.astype(F32), (place - opening).astype(F32), entries[1:2, :].astype(F32),
             jnp.zeros((5, block), F32)],
            axis=0,
        ).T
        place_column[here, :] = lines[:, 0:1]
        ranks[here, :] = lines[:, 2:3]
        named = jnp.zeros((experts_count, block), F32)
        for at in range(2, 2 + TOPK):
            named = jnp.where(entries[at : at + 1, :] == names, 1.0, named)
        chosen[:, here] = named
        valid = segment < lengths.shape[0]
        picks[:, here] = jnp.where(valid, named, 0.0).astype(BF16)
        table = cosine_sine(lines[:, 1:2] * inverse[...])
        turned_table = pltpu.roll(table, dim // 2, 1)
        cos = jnp.where(lanes < dim // 2, table, turned_table)
        sin = jnp.where(lanes < dim // 2, -turned_table, table)
        cosine[here, :] = cos
        sine[here, :] = sin
        rows = rows_all[here, :].astype(F32)
        root = lax.rsqrt(jnp.mean(rows * rows, axis=-1, keepdims=True) + EPS)

        @pl.when(step >= 2)
        def _():
            stage_copy(step - 2).wait()

        staged[step % 2] = (rows * root * gain[...]).astype(BF16)
        stage_copy(step).start()
        lin = mxu(staged[step % 2], weight[...])
        lin_out[here, :] = lin[:, : 2 * dim]
        values[here, :] = lin[:, 2 * dim :].astype(BF16)
        for at, head_gain, scale, out in (
            (0, q_gain, dim**-0.5, queries), (dim, k_gain, 1.0, keys),
        ):
            plain, _ = head_norm(lin[:, at : at + dim])
            plain = plain * head_gain[...]
            out[here, :] = ((plain * cos + pltpu.roll(plain, dim // 2, 1) * sin) * scale).astype(
                BF16
            )

    def both_ways(take, distance):
        for dz in (distance, -distance) if distance else (0,):
            take(dz)

    def run(plans, step):
        for at, plan in plans.items():

            @pl.when(step == at)
            def _(plan=plan):
                plan()

    plans = {
        0: lambda: (both_ways(gather.take_yx, 0), both_ways(take_tag, 1),
                    both_ways(gather.take_z, 1)),
        1: lambda: (both_ways(take_tag_y, 0), both_ways(gather.take_diagonal, 0),
                    both_ways(take_tag, 2), both_ways(gather.take_z, 2),
                    both_ways(gather.take_late, 0)),
        2: lambda: (both_ways(gather.take_yx, 1), both_ways(take_tag, 3),
                    both_ways(gather.take_z, 3), both_ways(gather.take_late, 1)),
        3: lambda: (both_ways(take_tag_y, 1), both_ways(gather.take_yx, 2),
                    both_ways(gather.take_diagonal, 1), both_ways(gather.take_late, 2)),
        4: lambda: (both_ways(gather.take_yx, 3), late.start()),
        5: lambda: (both_ways(take_tag_y, 2), both_ways(gather.take_diagonal, 2),
                    both_ways(gather.take_late, 3)),
        7: lambda: (both_ways(take_tag_y, 3), both_ways(gather.take_diagonal, 3)),
    }

    @pl.loop(0, 8)
    def _(step):
        run(plans, step)
        far, dy, _ = group_of(step)

        @pl.when(step > 0)
        def _():
            for dx in (0, 1):
                gather.take_core(far, dy, dx)

        project_group(step)

    mine = att_rows.at[:, pl.ds(pl.multiple_of(group * dim, dim), dim)]

    def block_copy(step):
        target = (group + step) % 8
        return pltpu.make_async_remote_copy(
            src_ref=attended.at[pl.ds(pl.multiple_of(target * block, block), block), :],
            dst_ref=mine,
            send_sem=send_sem.at[step],
            recv_sem=recv_sem.at[step],
            device_id=(target, part),
            device_id_type=MESH,
        )

    def attend_block(step):
        here = pl.ds(pl.multiple_of((group + step) % 8 * block, block), block)
        scores = mxu(keys[...], queries[here, :], 1, 1)
        seen = (place_column[...] <= place_row[:, here]) & (place_column[...] >= open_row[:, here])
        scores = jnp.where(seen, scores, NEG)
        highest = jnp.max(scores, axis=0, keepdims=True)
        exps = jnp.exp(scores - highest)
        totals = jnp.sum(exps, axis=0, keepdims=True)
        probability = (exps * (1.0 / totals)).astype(BF16)
        attended[here, :] = mxu(values[...], probability, 0, 0).T.astype(BF16)
        log_total[:, here] = highest + jnp.log(totals)

    late_plans = {
        1: lambda: (both_ways(late.take_yx, 0), both_ways(late.take_z, 1)),
        3: lambda: (both_ways(late.take_z, 2), both_ways(late.take_diagonal, 0),
                    both_ways(late.take_late, 0)),
        5: lambda: (both_ways(late.take_yx, 1), both_ways(late.take_z, 3)),
        7: lambda: (both_ways(late.take_late, 1), both_ways(late.take_yx, 2),
                    both_ways(late.take_diagonal, 1)),
    }

    @pl.loop(1, 8)
    def _(step):
        run(late_plans, step)
        attend_block(step)
        block_copy(step).start()

    attend_block(0)
    own_copy = pltpu.make_async_copy(
        attended.at[pl.ds(pl.multiple_of(group * block, block), block), :], mine, own_sem
    )
    own_copy.start()
    both_ways(late.take_yx, 3)
    both_ways(late.take_late, 2)

    kept[...] = jnp.zeros_like(kept)

    @pl.loop(0, total // block)
    def _(step):
        here = pl.ds(pl.multiple_of(step * block, block), block)
        for at in range(0, total // block):
            columns = pl.ds(at * block, block)
            lower = jnp.where(
                ranks[here, :] < tags[at, 1:2, :].astype(F32), 1.0, 0.0
            ).astype(BF16)
            kept[:, columns] += mxu(picks[:, here], lower)

    kept[...] = jnp.where((picks[...].astype(F32) > 0.0) & (kept[...] < CAP), 1.0, 0.0)

    both_ways(late.take_diagonal, 2)
    both_ways(late.take_late, 3)

    @pl.loop(1, 8)
    def _(step):
        block_copy(step).wait_send()
        source = (group + 8 - step) % 8
        there = att_rows.at[:, pl.ds(pl.multiple_of(source * dim, dim), dim)]
        arrive(there, recv_sem.at[step])

    own_copy.wait()

    @pl.loop(0, width // 256)
    def _(step):
        columns = pl.ds(pl.multiple_of(step * 256, 256), 256)
        partial_sum[:, columns] = mxu(att_rows[...], out_weight[:, columns]).astype(BF16)

    def rows_of(dx, dc):
        _, there = spot.device(0, 0, dx, dc)
        return partial_sum.at[pl.ds(pl.multiple_of(there * count, count), count), :]

    to_x, to_c = spot.device(0, 0, 1), spot.device(0, 0, 0, 1)
    for dx in (1, 0):
        push(rows_of(dx, 1), from_core.at[dx], tensor_sems.at[dx], tensor_sems.at[2 + dx], to_c)
    arrive(from_core.at[1], tensor_sems.at[3])
    to_x_sum[...] = (rows_of(1, 0)[...].astype(F32) + from_core[1].astype(F32)).astype(BF16)
    push(to_x_sum, from_x, tensor_sems.at[4], tensor_sems.at[5], to_x)
    both_ways(late.take_diagonal, 3)
    arrive(from_core.at[0], tensor_sems.at[2])
    arrive(from_x, tensor_sems.at[5])
    branch = rows_of(0, 0)[...].astype(F32) + from_core[0].astype(F32) + from_x[...].astype(F32)
    sum_rows = hidden[own, :].astype(F32) + branch
    residual[...] = sum_rows
    root = lax.rsqrt(jnp.mean(sum_rows * sum_rows, axis=-1, keepdims=True) + EPS)
    normed[...] = (sum_rows * root * second_gain[...]).astype(BF16)
    for at, view in ((0, from_core.at[0]), (1, from_core.at[1]), (4, from_x)):
        arrive(view, tensor_sems.at[at])
    for step in (6, 7):
        stage_copy(step).wait()
    gather.drain()
    late.local.wait()
    for far in range(4):
        for dx in (0, 1):
            late.take_core(far, 1, dx)

            @pl.when(spot.z != far)
            def _(far=far, dx=dx):
                late.take_core(far, 0, dx)

    late.drain()
    for dz in range(-3, 4):

        def action(dz=dz):
            arrive(tag_place(dz, 0), tag_y_send.at[dz + 3])
            for side, step in ((0, 1), (1, -1)):
                if dz * step <= 0:

                    @pl.when(spot.has(step))
                    def _(side=side):
                        arrive(tag_place(dz, 0), tag_z_send.at[dz + 3, side])

        when_has(spot, dz, action)


def front(
    hidden, cotangent, tag, lengths, gain, w_query, w_key, w_value, q_gain, k_gain, inverse,
    w_out, second_gain, expert_count,
):
    block, width = hidden.shape
    total, count, dim = 8 * block, block // 4, w_key.shape[1]
    shape, vmem = jax.ShapeDtypeStruct, pltpu.VMEM
    smem = pl.BlockSpec(memory_space=pltpu.SMEM)
    small = (total, dim)
    return pl.pallas_call(
        front_kernel,
        out_shape=(
            shape((total, width), BF16), shape(small, BF16), shape(small, BF16),
            shape(small, BF16), shape((total, 2 * dim), F32), shape(small, F32),
            shape(small, F32), shape(small, BF16), shape((1, total), F32),
            shape((1, total), F32), shape((1, total), F32), shape((total, 1), F32),
            shape((count, width), F32), shape((count, width), BF16),
            shape((expert_count, total), F32), shape((expert_count, total), F32),
            shape((total, width), BF16),
        ),
        in_specs=[VMEM_SPEC, VMEM_SPEC, VMEM_SPEC, smem, VMEM_SPEC, HBM_SPEC, HBM_SPEC, HBM_SPEC,
                  VMEM_SPEC, VMEM_SPEC, VMEM_SPEC, HBM_SPEC, VMEM_SPEC],
        out_specs=(HBM_SPEC,) + (VMEM_SPEC,) * 15 + (HBM_SPEC,),
        scratch_shapes=[
            vmem((total, width), BF16), vmem((width, 3 * dim), BF16), vmem((8 * dim, width), BF16),
            vmem((2, block, width), BF16), vmem((8, 16, block), jnp.int32), vmem((total, 1), F32),
            vmem((expert_count, total), BF16), vmem((block, 8 * dim), BF16),
            vmem((block, width), BF16), vmem((2, count, width), BF16), vmem((count, width), BF16),
            vmem((count, width), BF16),
        ]
        + dma_sems(
            ((4,), (2,), (7,), (7,), (7, 2), (7,), None, (8,), (8,), None, (6,)) + Gather.SEMS * 2
        ),
        compiler_params=pltpu.CompilerParams(
            collective_id=1, has_side_effects=True, vmem_limit_bytes=62 << 20
        ),
        name="front",
        cost_estimate=cost(8_000_000_000, 90),
    )(
        hidden, cotangent, tag, lengths, gain, w_query, w_key, w_value, q_gain, k_gain, inverse,
        w_out, second_gain,
    )


def swap(value, bits):
    return lax.ppermute(
        value, ("expert", "tensor"), [(device, device ^ bits) for device in range(32)]
    )


def tensor_rows(rows):
    by_core = swap(rows, 1)
    by_x = swap(rows, 2)
    by_both = swap(by_x, 1)

    return in_order(rows, by_core, by_x, by_both)


def in_order(rows, by_core, by_x, by_both):
    part = lax.axis_index("tensor")

    def ordered(first, second, bit):
        swapped = part // bit % 2 == 1
        return jnp.concatenate(
            [jnp.where(swapped, second, first), jnp.where(swapped, first, second)], axis=0
        )

    return ordered(ordered(rows, by_core, 1), ordered(by_x, by_both, 1), 2)


def head_device(
    hidden_in,
    cotangent,
    layout,
    seq_lengths,
    expert_ids,
    drop_rank,
    norm1_gain,
    w_query,
    key_weight,
    value_weight,
    query_gain,
    key_gain,
    w_out,
    norm2_gain,
    w_router,
    w_gate,
    w_up,
    w_down,
):
    f32, bf16 = jnp.float32, jnp.bfloat16
    tok_rows, model_width = hidden_in.shape
    head_dim = query_gain.shape[0]
    expert_count = w_router.shape[1]
    local_count, _, ff_local = w_gate.shape
    groups = lax.axis_size("expert")
    tensor_size = lax.axis_size("tensor")
    total_rows = groups * tok_rows
    own_rows = tok_rows // tensor_size
    group = lax.axis_index("expert")
    part = lax.axis_index("tensor")

    def own(rows):
        return lax.dynamic_slice_in_dim(rows, part * own_rows, own_rows, 0)

    tag = jnp.concatenate(
        [layout[None], drop_rank[None], expert_ids.T, jnp.zeros((6, tok_rows), jnp.int32)], axis=0
    )
    half_dim = head_dim // 2
    inverse = THETA ** (-(jnp.arange(half_dim, dtype=f32) * 2.0) / head_dim)
    q_gain, k_gain = query_gain[None], key_gain[None]
    (
        normed1, queries, keys, values, lin, cosine, sine, attended, log_total,
        place_row, open_row, place_column, residual, normed2, chosen, kept, grad_y_all,
    ) = front(
        hidden_in, cotangent, tag, seq_lengths, norm1_gain[None], w_query, key_weight,
        value_weight, q_gain, k_gain, jnp.concatenate([inverse, inverse])[None], w_out,
        norm2_gain[None], expert_count,
    )
    turn = lambda v: jnp.transpose(v, (0, 2, 1))
    back, grad_gate, grad_up, grad_down = experts(
        normed2, grad_y_all, turn(w_gate), turn(w_up), w_down.reshape(-1, model_width),
        w_router.T, chosen, kept,
    )
    out_hidden = tensor_rows((residual + back[:, :model_width]).astype(bf16))
    back = back[:, model_width:]

    start = group * tok_rows + part * own_rows
    chosen_own = lax.dynamic_slice_in_dim(chosen, start, own_rows, 1).T
    logits = jnp.dot(normed2, w_router, preferred_element_type=f32)
    soft_own = jax.nn.softmax(jnp.where(chosen_own > 0.0, logits, -jnp.inf), axis=1)
    grad_soft = back[:, model_width : model_width + expert_count]
    grad_logits = (
        soft_own * (grad_soft - jnp.sum(soft_own * grad_soft, axis=1, keepdims=True))
    ).astype(bf16)
    grad_router = jnp.einsum("td,te->de", normed2, grad_logits, preferred_element_type=f32)
    grad_normed2 = back[:, :model_width] + jnp.einsum(
        "te,de->td", grad_logits, w_router, preferred_element_type=f32
    )
    norm2_pull = jax.vjp(norm_rows, residual, norm2_gain)[1]
    grad_resid_norm, grad_norm2 = norm2_pull(grad_normed2)
    grad_residual = own(cotangent).astype(f32) + grad_resid_norm
    small = jnp.concatenate([grad_router.T, grad_norm2[None]], axis=0)
    small = small + swap(small, 16)

    grad_lin, grad_out, grad_qgain, grad_kgain = attend_back(
        grad_residual.astype(bf16), w_out, queries, keys, values, attended, lin, cosine, sine,
        place_column, place_row, open_row, log_total, k_gain, q_gain,
    )
    grad_lin, small = lax.optimization_barrier((grad_lin, small))
    small_moved = swap(small, 8)
    gains = jnp.concatenate(
        [grad_qgain, grad_kgain, jnp.zeros((1, model_width - 2 * head_dim), f32)], axis=1
    )
    reduced, grad_kv, grad_query, grad_out = close(
        normed1, grad_lin, w_query, key_weight, value_weight, grad_out
    )
    reduced, out_hidden, small_moved = lax.optimization_barrier(
        (reduced, out_hidden, small_moved)
    )
    small = small + small_moved
    norm1_pull = jax.vjp(norm_rows, own(hidden_in).astype(f32), norm1_gain)[1]
    grad_hidden_norm, grad_norm1 = norm1_pull(reduced)
    late_sums = jnp.concatenate([grad_norm1[None], gains], axis=0)
    hidden_rows = (grad_residual + grad_hidden_norm).astype(bf16)
    grad_query, hidden_rows, late_sums = lax.optimization_barrier(
        (grad_query, hidden_rows, late_sums)
    )
    moved, by_x, by_core = swap(late_sums, 16), swap(hidden_rows, 2), swap(hidden_rows, 1)
    grad_query = grad_query.astype(f32)
    grad_query, grad_out, moved = lax.optimization_barrier((grad_query, grad_out, moved))
    late_sums = late_sums + moved
    moved = swap(late_sums, 8)
    grad_out = grad_out.astype(f32)
    grad_out, grad_kv, moved = lax.optimization_barrier((grad_out, grad_kv, moved))
    small = jnp.concatenate([small, late_sums + moved], axis=0)
    moved = swap(small, 4)
    by_x, moved = lax.optimization_barrier((by_x, moved))
    by_both = swap(by_x, 1)
    grad_hidden = in_order(hidden_rows, by_core, by_x, by_both)
    small = small + moved
    grad_kv = grad_kv.astype(f32)
    for bit in (1, 0):
        small = small + swap(small, 1 << bit)
    grad_norm1 = small[expert_count + 1]
    grad_router, grad_norm2 = small[:expert_count].T, small[expert_count]
    grad_qgain, grad_kgain = jnp.split(small[expert_count + 2, : 2 * head_dim], 2)
    grad_down = grad_down.reshape(local_count, ff_local, model_width)
    return (
        out_hidden,
        grad_hidden,
        grad_norm1,
        grad_query,
        grad_kv[:, :head_dim],
        grad_kv[:, head_dim:],
        grad_qgain,
        grad_kgain,
        grad_out,
        grad_norm2,
        grad_router,
        turn(grad_gate),
        turn(grad_up),
        grad_down,
    )


def solution(mesh):
    groups = mesh.shape["expert"]

    def device_fn(*operands):
        heads = operands[7].shape[1] // operands[10].shape[0]
        one_head = heads == groups == 8 and operands[8].shape[1] == operands[10].shape[0]
        one_head = one_head and mesh.shape["tensor"] == 4
        return (head_device if one_head else per_device)(*operands)

    return jax.shard_map(
        device_fn,
        mesh=mesh,
        in_specs=(
            P("expert", None),
            P("expert", None),
            P("expert"),
            P(),
            P("expert", None),
            P("expert"),
            P(),
            P(None, "tensor"),
            P(None, "tensor"),
            P(None, "tensor"),
            P(),
            P(),
            P("tensor", None),
            P(),
            P(),
            P("expert", None, "tensor"),
            P("expert", None, "tensor"),
            P("expert", "tensor", None),
        ),
        out_specs=(
            P("expert", None),
            P("expert", None),
            P(),
            P(None, "tensor"),
            P(None, "tensor"),
            P(None, "tensor"),
            P(),
            P(),
            P("tensor", None),
            P(),
            P(),
            P("expert", None, "tensor"),
            P("expert", None, "tensor"),
            P("expert", "tensor", None),
        ),
        check_vma=False,
    )
```

```python
from functools import partial
import math

import jax
import jax.numpy as jnp
from jax import lax
from jax.experimental import pallas as pl
from jax.experimental.pallas import tpu as pltpu
from jax.sharding import PartitionSpec as P

TOPK = 8
CAP = 1280


EPS = 1e-06
THETA = 1000000.0
NEG = -1e30


def norm_rows(value_matrix, gain):
    return (
        value_matrix
        * lax.rsqrt(jnp.mean(value_matrix * value_matrix, axis=-1, keepdims=True) + EPS)
        * gain
    )


def rotary(value_matrix, position):
    half_dim = value_matrix.shape[-1] // 2
    inverse = THETA ** (-(jnp.arange(half_dim, dtype=jnp.float32) * 2.0) / value_matrix.shape[-1])
    angles = position.astype(jnp.float32)[:, None] * inverse[None, :]
    cosine_table = jnp.concatenate([jnp.cos(angles), jnp.cos(angles)], axis=-1)[:, None, :]
    sine_table = jnp.concatenate([jnp.sin(angles), jnp.sin(angles)], axis=-1)[:, None, :]
    turned = jnp.concatenate([-value_matrix[..., half_dim:], value_matrix[..., :half_dim]], axis=-1)
    return value_matrix * cosine_table + turned * sine_table


def shape_queries(linear, gain, position):
    head_dim = gain.shape[0]
    shaped = linear.reshape(linear.shape[0], linear.shape[1] // head_dim, head_dim)
    return rotary(norm_rows(shaped, gain), position) * head_dim ** (-0.5)


def shape_keys(linear, gain, position):
    head_dim = gain.shape[0]
    shaped = linear.reshape(linear.shape[0], linear.shape[1] // head_dim, head_dim)
    return rotary(norm_rows(shaped, gain), position)


def token_tables(token_position, seq_lengths):
    bounds = jnp.cumsum(seq_lengths)
    passed = token_position[:, None] >= bounds[None, :]
    segment_ids = jnp.sum(passed.astype(jnp.int32), axis=1)
    opening = jnp.max(jnp.where(passed, bounds[None, :], 0), axis=1)
    return (segment_ids, (token_position - opening).astype(jnp.int32))


def visible(query_segment, query_place, key_segment, key_place):
    return (query_segment[:, None] == key_segment[None, :]) & (
        key_place[None, :] <= query_place[:, None]
    )


def deliver(payload, slot_ids):
    return (
        lax.all_to_all(payload, "expert", split_axis=0, concat_axis=0, tiled=True),
        lax.all_to_all(slot_ids, "expert", split_axis=0, concat_axis=0, tiled=True),
    )


def bring_back(payload):
    return lax.all_to_all(payload, "expert", split_axis=0, concat_axis=0, tiled=True)


def expert_forward(entry_rows, w_gate, w_up, w_down):
    gate_lin = jnp.einsum("gesd,edf->gesf", entry_rows, w_gate, preferred_element_type=jnp.float32)
    up_lin = jnp.einsum("gesd,edf->gesf", entry_rows, w_up, preferred_element_type=jnp.float32)
    activation = (jax.nn.silu(gate_lin) * up_lin).astype(jnp.bfloat16)
    expert_out = jnp.einsum(
        "gesf,efd->gesd", activation, w_down, preferred_element_type=jnp.float32
    ).astype(jnp.bfloat16)
    return (gate_lin, up_lin, activation, expert_out)


def expert_backward(entry_rows, gate_lin, up_lin, activation, grad_in, w_gate, w_up, w_down):
    grad_down = jnp.einsum(
        "gesf,gesd->efd", activation, grad_in, preferred_element_type=jnp.float32
    )
    grad_act = jnp.einsum("gesd,efd->gesf", grad_in, w_down, preferred_element_type=jnp.float32)
    sigmoid = jax.nn.sigmoid(gate_lin)
    grad_gate_lin = (grad_act * up_lin * sigmoid * (1.0 + gate_lin * (1.0 - sigmoid))).astype(
        jnp.bfloat16
    )
    grad_up_lin = (grad_act * gate_lin * sigmoid).astype(jnp.bfloat16)
    grad_w_gate = jnp.einsum(
        "gesd,gesf->edf", entry_rows, grad_gate_lin, preferred_element_type=jnp.float32
    )
    grad_w_up = jnp.einsum(
        "gesd,gesf->edf", entry_rows, grad_up_lin, preferred_element_type=jnp.float32
    )
    grad_entry = jnp.einsum(
        "gesf,edf->gesd", grad_gate_lin, w_gate, preferred_element_type=jnp.float32
    )
    grad_entry = (
        grad_entry
        + jnp.einsum("gesf,edf->gesd", grad_up_lin, w_up, preferred_element_type=jnp.float32)
    ).astype(jnp.bfloat16)
    return (grad_entry, grad_w_gate, grad_w_up, grad_down)


def per_device(
    hidden_in,
    cotangent,
    layout,
    seq_lengths,
    expert_ids,
    drop_rank,
    norm1_gain,
    w_query,
    key_weight,
    value_weight,
    query_gain,
    key_gain,
    w_out,
    norm2_gain,
    w_router,
    w_gate,
    w_up,
    w_down,
):
    tok_rows = hidden_in.shape[0]
    model_width = hidden_in.shape[1]
    head_dim = query_gain.shape[0]
    local_heads = w_query.shape[1] // head_dim
    expert_count = w_router.shape[1]
    local_count = w_gate.shape[0]
    group_count = lax.axis_size("expert")
    slot_count = 2 * tok_rows * TOPK // expert_count
    seq_count = seq_lengths.shape[0]
    expert_range = jnp.arange(expert_count, dtype=jnp.int32)
    hidden = hidden_in.astype(jnp.float32)
    segment_ids, position = token_tables(layout, seq_lengths)
    valid = segment_ids < seq_count
    first_normalized = norm_rows(hidden, norm1_gain)
    normed1_low = first_normalized.astype(jnp.bfloat16)
    query_lin = jnp.dot(normed1_low, w_query, preferred_element_type=jnp.float32)
    key_lin = jnp.dot(normed1_low, key_weight, preferred_element_type=jnp.float32)
    value_lin = jnp.dot(normed1_low, value_weight, preferred_element_type=jnp.float32)
    query_shaped = shape_queries(query_lin, query_gain, position).astype(jnp.bfloat16)
    query_total = local_heads * tok_rows
    query_rows = jnp.transpose(query_shaped, (1, 0, 2)).reshape(query_total, head_dim)
    key_rows = (
        shape_keys(key_lin, key_gain, position).astype(jnp.bfloat16).reshape(tok_rows, head_dim)
    )
    value_rows = value_lin.astype(jnp.bfloat16)
    all_keys, all_values, all_place, all_ids, all_rank = (
        lax.all_gather(key_rows, "expert", axis=0, tiled=True),
        lax.all_gather(value_rows, "expert", axis=0, tiled=True),
        lax.all_gather(layout, "expert", axis=0, tiled=True),
        lax.all_gather(expert_ids, "expert", axis=0, tiled=True),
        lax.all_gather(drop_rank, "expert", axis=0, tiled=True),
    )
    all_segment = token_tables(all_place, seq_lengths)[0]
    rows_per_block = math.gcd(512, query_total)
    count_of_blocks = query_total // rows_per_block
    query_segment = jnp.tile(segment_ids, local_heads)
    query_place = jnp.tile(layout, local_heads)

    def attend_block(operands):
        query_block, segment_block, place_block = operands
        scores = jnp.einsum("qd,kd->qk", query_block, all_keys, preferred_element_type=jnp.float32)
        scores = jnp.where(visible(segment_block, place_block, all_segment, all_place), scores, NEG)
        highest = jnp.max(scores, axis=1, keepdims=True)
        weights = jnp.exp(scores - highest)
        totals = jnp.sum(weights, axis=1, keepdims=True)
        probability = (weights / totals).astype(jnp.bfloat16)
        mixed_out = jnp.dot(probability, all_values, preferred_element_type=jnp.float32)
        return (mixed_out, (highest + jnp.log(totals))[:, 0])

    attention_output, log_totals = lax.map(
        attend_block,
        (
            query_rows.reshape(count_of_blocks, rows_per_block, head_dim),
            query_segment.reshape(count_of_blocks, rows_per_block),
            query_place.reshape(count_of_blocks, rows_per_block),
        ),
    )
    attention_output = attention_output.reshape(local_heads, tok_rows, head_dim).astype(
        jnp.bfloat16
    )
    att_cat = jnp.transpose(attention_output, (1, 0, 2)).reshape(tok_rows, local_heads * head_dim)
    branch_part = jnp.dot(att_cat, w_out, preferred_element_type=jnp.float32)
    branch = lax.psum(branch_part, "tensor")
    residual = hidden + branch
    normed2 = norm_rows(residual, norm2_gain)
    normed2_low = normed2.astype(jnp.bfloat16)
    logits = jnp.dot(normed2_low, w_router, preferred_element_type=jnp.float32)
    soft_gate = jax.nn.softmax(jnp.take_along_axis(logits, expert_ids, axis=1), axis=1)
    picks = jnp.any(expert_ids[:, :, None] == expert_range, axis=1) & valid[:, None]
    all_valid = all_segment < seq_count
    all_picks = jnp.any(all_ids[:, :, None] == expert_range, axis=1) & all_valid[:, None]
    earlier = (all_rank[None, :] < drop_rank[:, None]).astype(jnp.bfloat16)
    before_counts = jnp.dot(
        earlier, all_picks.astype(jnp.bfloat16), preferred_element_type=jnp.float32
    )
    global_slot = jnp.take_along_axis(before_counts, expert_ids, axis=1).astype(jnp.int32)
    kept_mask = (global_slot < CAP) & valid[:, None]
    gate_weight = soft_gate * kept_mask.astype(jnp.float32)
    lower_rows = (jnp.arange(tok_rows)[None, :] < jnp.arange(tok_rows)[:, None]).astype(
        jnp.bfloat16
    )
    local_counts = jnp.dot(
        lower_rows, picks.astype(jnp.bfloat16), preferred_element_type=jnp.float32
    )
    local_slot = jnp.take_along_axis(local_counts, expert_ids, axis=1).astype(jnp.int32)
    pair_count = tok_rows * TOPK
    dump_index = expert_count * slot_count
    target = jnp.where(kept_mask, expert_ids * slot_count + local_slot, dump_index)
    pair_index = jnp.arange(pair_count, dtype=jnp.int32)
    slot_pair = (
        jnp.full((dump_index,), pair_count, jnp.int32)
        .at[target.reshape(-1)]
        .set(pair_index, mode="drop")
    )
    slot_token = jnp.where(slot_pair < pair_count, slot_pair // TOPK, tok_rows)
    slot_global = (
        jnp.full((dump_index,), -1, jnp.int32)
        .at[target.reshape(-1)]
        .set(global_slot.reshape(-1), mode="drop")
    )
    padded_rows = jnp.concatenate([normed2_low, jnp.zeros((1, model_width), jnp.bfloat16)], axis=0)
    send_rows = padded_rows[slot_token].reshape(group_count, local_count, slot_count, model_width)
    send_slot = slot_global.reshape(group_count, local_count, slot_count)
    received, received_slot = deliver(send_rows, send_slot)
    gate_lin, up_lin, activation, expert_out = expert_forward(received, w_gate, w_up, w_down)
    returned = bring_back(expert_out)
    returned_flat = jnp.concatenate(
        [returned.reshape(dump_index, model_width), jnp.zeros((1, model_width), returned.dtype)],
        axis=0,
    )
    pair_out = returned_flat[target]
    moe_part = jnp.sum(gate_weight[:, :, None] * pair_out, axis=1)
    moe_branch = lax.psum(moe_part.astype(jnp.bfloat16), "tensor").astype(jnp.float32)
    out_hidden = (residual + moe_branch).astype(jnp.bfloat16)
    grad_y = cotangent.astype(jnp.float32)
    gate_dot = jnp.sum(grad_y[:, None, :] * pair_out, axis=2)
    pair_grads = (
        (gate_weight[:, :, None] * grad_y[:, None, :])
        .astype(jnp.bfloat16)
        .reshape(pair_count, model_width)
    )
    pair_grads = jnp.concatenate([pair_grads, jnp.zeros((1, model_width), jnp.bfloat16)], axis=0)
    send_grad = pair_grads[slot_pair].reshape(group_count, local_count, slot_count, model_width)
    grad_received, grad_slot = deliver(send_grad, send_slot)
    grad_entry, grad_w_gate, grad_w_up, grad_w_down = expert_backward(
        received, gate_lin, up_lin, activation, grad_received, w_gate, w_up, w_down
    )
    grad_returned = bring_back(grad_entry)
    grad_flat = jnp.concatenate(
        [
            grad_returned.reshape(dump_index, model_width),
            jnp.zeros((1, model_width), grad_returned.dtype),
        ],
        axis=0,
    )
    grad_normed2_part = jnp.sum(grad_flat[target], axis=1, dtype=jnp.float32)
    grad_normed2_exp, gate_dot = lax.psum((grad_normed2_part, gate_dot), "tensor")
    grad_soft = gate_dot * kept_mask.astype(jnp.float32)
    grad_chosen = soft_gate * (grad_soft - jnp.sum(soft_gate * grad_soft, axis=1, keepdims=True))
    grad_logits = jnp.sum(
        grad_chosen[:, :, None] * (expert_ids[:, :, None] == expert_range).astype(jnp.float32),
        axis=1,
    ).astype(jnp.bfloat16)
    grad_w_router = jnp.einsum(
        "td,te->de", normed2_low, grad_logits, preferred_element_type=jnp.float32
    )
    grad_normed2 = grad_normed2_exp + jnp.einsum(
        "te,de->td", grad_logits, w_router, preferred_element_type=jnp.float32
    )
    norm2_pull = jax.vjp(norm_rows, residual, norm2_gain)[1]
    grad_resid_norm, grad_norm2 = norm2_pull(grad_normed2)
    grad_residual = grad_y + grad_resid_norm
    grad_residual_low = grad_residual.astype(jnp.bfloat16)
    grad_w_out = jnp.einsum(
        "tc,td->cd", att_cat, grad_residual_low, preferred_element_type=jnp.float32
    )
    grad_att_cat = jnp.einsum(
        "td,cd->tc", grad_residual_low, w_out, preferred_element_type=jnp.float32
    ).astype(jnp.bfloat16)
    grad_att_rows = jnp.transpose(
        grad_att_cat.reshape(tok_rows, local_heads, head_dim), (1, 0, 2)
    ).reshape(query_total, head_dim)

    def query_grad_block(operands):
        query_block, segment_block, place_block, grad_block, log_block = operands
        scores = jnp.einsum("qd,kd->qk", query_block, all_keys, preferred_element_type=jnp.float32)
        scores = jnp.where(visible(segment_block, place_block, all_segment, all_place), scores, NEG)
        probability = jnp.exp(scores - log_block[:, None])
        grad_prob = jnp.einsum(
            "qd,kd->qk", grad_block, all_values, preferred_element_type=jnp.float32
        )
        delta_row = jnp.sum(probability * grad_prob, axis=1)
        grad_scores = (probability * (grad_prob - delta_row[:, None])).astype(jnp.bfloat16)
        return (jnp.dot(grad_scores, all_keys, preferred_element_type=jnp.float32), delta_row)

    grad_query_rows, deltas = lax.map(
        query_grad_block,
        (
            query_rows.reshape(count_of_blocks, rows_per_block, head_dim),
            query_segment.reshape(count_of_blocks, rows_per_block),
            query_place.reshape(count_of_blocks, rows_per_block),
            grad_att_rows.reshape(count_of_blocks, rows_per_block, head_dim),
            log_totals,
        ),
    )
    log_flat = log_totals.reshape(query_total)
    delta_flat = deltas.reshape(query_total)
    key_block = math.gcd(lax.axis_size("expert") * tok_rows, 2048)

    def one_block(offset):
        key_part = lax.dynamic_slice_in_dim(all_keys, offset, key_block, 0)
        value_part = lax.dynamic_slice_in_dim(all_values, offset, key_block, 0)
        segment_part = lax.dynamic_slice_in_dim(all_segment, offset, key_block, 0)
        place_part = lax.dynamic_slice_in_dim(all_place, offset, key_block, 0)
        scores = jnp.einsum("qd,kd->qk", query_rows, key_part, preferred_element_type=jnp.float32)
        scores = jnp.where(
            visible(query_segment, query_place, segment_part, place_part), scores, NEG
        )
        probability = jnp.exp(scores - log_flat[:, None])
        grad_value = jnp.einsum(
            "qk,qd->kd",
            probability.astype(jnp.bfloat16),
            grad_att_rows,
            preferred_element_type=jnp.float32,
        )
        grad_prob = jnp.einsum(
            "qd,kd->qk", grad_att_rows, value_part, preferred_element_type=jnp.float32
        )
        grad_scores = (probability * (grad_prob - delta_flat[:, None])).astype(jnp.bfloat16)
        grad_key = jnp.einsum(
            "qk,qd->kd", grad_scores, query_rows, preferred_element_type=jnp.float32
        )
        return jnp.concatenate([grad_key, grad_value], axis=1)

    stacked = lax.map(
        one_block,
        jnp.arange(lax.axis_size("expert") * tok_rows // key_block, dtype=jnp.int32) * key_block,
    )
    key_value_grad = lax.psum_scatter(
        stacked.reshape(lax.axis_size("expert") * tok_rows, 2 * head_dim).astype(jnp.bfloat16),
        "expert",
        scatter_dimension=0,
        tiled=True,
    ).astype(jnp.float32)
    grad_key_post = key_value_grad[:, :head_dim].reshape(tok_rows, 1, head_dim)
    grad_values_low = key_value_grad[:, head_dim:].astype(jnp.bfloat16)
    grad_query_tok = jnp.transpose(
        grad_query_rows.reshape(local_heads, tok_rows, head_dim), (1, 0, 2)
    )
    query_pull = jax.vjp(partial(shape_queries, position=position), query_lin, query_gain)[1]
    grad_query_lin, grad_qgain_part = query_pull(grad_query_tok)
    key_pull = jax.vjp(partial(shape_keys, position=position), key_lin, key_gain)[1]
    grad_key_lin, grad_kgain_part = key_pull(grad_key_post)
    grad_query_low = grad_query_lin.astype(jnp.bfloat16)
    grad_key_low = grad_key_lin.astype(jnp.bfloat16)
    grad_w_query = jnp.einsum(
        "td,tc->dc", normed1_low, grad_query_low, preferred_element_type=jnp.float32
    )
    grad_w_key = jnp.einsum(
        "td,tc->dc", normed1_low, grad_key_low, preferred_element_type=jnp.float32
    )
    grad_w_value = jnp.einsum(
        "td,tc->dc", normed1_low, grad_values_low, preferred_element_type=jnp.float32
    )
    grad_normed1_part = jnp.einsum(
        "tc,dc->td", grad_query_low, w_query, preferred_element_type=jnp.float32
    )
    grad_normed1_part = grad_normed1_part + jnp.einsum(
        "tc,dc->td", grad_key_low, key_weight, preferred_element_type=jnp.float32
    )
    grad_normed1_part = grad_normed1_part + jnp.einsum(
        "tc,dc->td", grad_values_low, value_weight, preferred_element_type=jnp.float32
    )
    grad_normed1, grad_qgain_part, grad_kgain_part = (
        lax.psum(grad_normed1_part.astype(jnp.bfloat16), "tensor").astype(jnp.float32),
        lax.psum(grad_qgain_part.astype(jnp.bfloat16), "tensor").astype(jnp.float32),
        lax.psum(grad_kgain_part.astype(jnp.bfloat16), "tensor").astype(jnp.float32),
    )
    norm1_pull = jax.vjp(norm_rows, hidden, norm1_gain)[1]
    grad_hidden_norm, grad_norm1 = norm1_pull(grad_normed1)
    grad_hidden = (grad_residual + grad_hidden_norm).astype(jnp.bfloat16)
    summed = (
        lax.psum(grad_norm1.astype(jnp.bfloat16), "expert").astype(jnp.float32),
        lax.psum(grad_w_query.astype(jnp.bfloat16), "expert").astype(jnp.float32),
        lax.psum(grad_w_key.astype(jnp.bfloat16), "expert").astype(jnp.float32),
        lax.psum(grad_w_value.astype(jnp.bfloat16), "expert").astype(jnp.float32),
        lax.psum(grad_qgain_part.astype(jnp.bfloat16), "expert").astype(jnp.float32),
        lax.psum(grad_kgain_part.astype(jnp.bfloat16), "expert").astype(jnp.float32),
        lax.psum(grad_w_out.astype(jnp.bfloat16), "expert").astype(jnp.float32),
        lax.psum(grad_norm2.astype(jnp.bfloat16), "expert").astype(jnp.float32),
        lax.psum(grad_w_router.astype(jnp.bfloat16), "expert").astype(jnp.float32),
    )
    return (
        out_hidden,
        grad_hidden,
        summed[0],
        summed[1],
        summed[2],
        summed[3],
        summed[4],
        summed[5],
        summed[6],
        summed[7],
        summed[8],
        grad_w_gate,
        grad_w_up,
        grad_w_down,
    )


MESH = pl.DeviceIdType.MESH
FAR_FIRST = (3, -3, 2, -2, 1, -1, 0)


class Spot:
    def __init__(self):
        group, part = lax.axis_index("expert"), lax.axis_index("tensor")
        self.z, self.y = group // 2, group % 2
        self.x, self.c = part // 2, part % 2

    def has(self, dz):
        return (self.z + dz >= 0) & (self.z + dz <= 3)

    def device(self, dz=0, dy=0, dx=0, dc=0):
        y = 1 - self.y if dy else self.y
        x = 1 - self.x if dx else self.x
        c = 1 - self.c if dc else self.c
        return ((self.z + dz) * 2 + y, x * 2 + c)

    def rows(self, dz, dy, dx, dc, count):
        group, part = self.device(dz, dy, dx, dc)
        return pl.ds(pl.multiple_of((group * 4 + part) * count, count), count)

    def greet(self, line=False):
        barrier = pltpu.get_barrier_semaphore()
        for step in ((0, 1, 0, 0), (0, 0, 1, 0), (0, 0, 0, 1)):
            pl.semaphore_signal(barrier, inc=1, device_id=self.device(*step), device_id_type=MESH)
        for dz in (1, -1, 2, -2, 3, -3) if line else (1, -1):

            @pl.when(self.has(dz))
            def _(dz=dz):
                pl.semaphore_signal(
                    barrier, inc=1, device_id=self.device(dz), device_id_type=MESH
                )

        if line:
            pl.semaphore_wait(barrier, 6)
        else:
            inner = jnp.where((self.z > 0) & (self.z < 3), 1, 0)
            pl.semaphore_wait(barrier, 4 + inner)


def when_has(spot, dz, action):
    if dz == 0:
        action()
    else:
        pl.when(spot.has(dz))(action)


def dma_sems(shapes):
    return [pltpu.SemaphoreType.DMA(shape) if shape else pltpu.SemaphoreType.DMA for shape in shapes]


def add_into(into, chunk, *terms):
    @pl.loop(0, into.shape[0] // chunk)
    def _(step):
        rows = pl.ds(pl.multiple_of(step * chunk, chunk), chunk)
        for at in range(0, into.shape[1], 1024):
            columns = pl.ds(at, min(1024, into.shape[1] - at))
            total = into[rows, columns].astype(jnp.float32)
            for term in terms:
                total = total + term[rows, columns].astype(jnp.float32)
            into[rows, columns] = total.astype(into.dtype)


def push(src, dst, send_sem, recv_sem, device):
    pltpu.make_async_remote_copy(
        src_ref=src,
        dst_ref=dst,
        send_sem=send_sem,
        recv_sem=recv_sem,
        device_id=device,
        device_id_type=MESH,
    ).start()


def arrive(view, sem):
    pltpu.make_async_copy(view, view, sem).wait()


F32, BF16 = jnp.float32, jnp.bfloat16
VMEM_SPEC = pl.BlockSpec(memory_space=pltpu.VMEM)
HBM_SPEC = pl.BlockSpec(memory_space=pl.ANY)


def cost(flops, microseconds):
    return pl.CostEstimate(
        flops=flops, bytes_accessed=microseconds * 3_000_000, transcendentals=0
    )


def mxu(left, right, left_dim=1, right_dim=0):
    return lax.dot_general(
        left, right, (((left_dim,), (right_dim,)), ((), ())), preferred_element_type=F32
    )


def head_norm(lin):
    root = lax.rsqrt(jnp.mean(lin * lin, axis=-1, keepdims=True) + EPS)
    return lin * root, root


def near_first(step, z):
    high = z // 2
    folded = z + high * (3 - 2 * z)
    place = (step + folded * (1 - step // 2)) % 2 + 2 * (step // 2)
    return place + high * (3 - 2 * place)


class Gather:
    SEMS = ((5, 7), (7, 2), (6,), (7, 2, 2), None, (7, 2), (7, 2, 2))

    def __init__(
        self, spot, src, out, recv, z_send, sends, c_recv, local_sem, late_recv, late_send, full=None
    ):
        self.spot, self.src, self.out, self.full = spot, src, out, full
        self.recv, self.z_send, self.sends, self.c_recv = recv, z_send, sends, c_recv
        self.late_recv, self.late_send = late_recv, late_send
        self.count, self.width = src.shape
        width, late = self.width, self.width * 5 // 16
        half = width * 5 // 8 if full is not None else width // 2
        self.first, self.second = pl.ds(0, half), pl.ds(half, width - half)
        self.whole = pl.ds(0, width)
        self.early = (pl.ds(0, width - late), pl.ds(late, width - late))
        self.late = (pl.ds(width - late, late), pl.ds(0, late))
        if full is None:
            self.local = pltpu.make_async_copy(src, self.place(0, 0, 0), local_sem)
        else:
            group, _ = spot.device()
            rows = pl.ds(pl.multiple_of(group * 4 * self.count, 4 * self.count), 4 * self.count)
            self.local = pltpu.make_async_copy(full, out.at[rows, :], local_sem)

    def place(self, dz, dy, dx, dc=0, columns=None):
        rows = self.spot.rows(dz, dy, dx, dc, self.count)
        return self.out.at[rows, self.whole if columns is None else columns]

    def source(self, dz, dy, dx, columns):
        if dz == 0 and dy == 0 and dx == 0:
            return self.src.at[:, columns]
        if dz == 0 and dy == 0 and self.full is not None:
            _, part = self.spot.device(0, 0, 1)
            rows = pl.ds(pl.multiple_of(part * self.count, self.count), self.count)
            return self.full.at[rows, columns]
        return self.place(dz, dy, dx, 0, columns)

    def send(self, dz, dy, dx, columns, send_sem, recv_sem, device):
        push(
            self.source(dz, dy, dx, columns), self.place(dz, dy, dx, 0, columns), send_sem,
            recv_sem, device,
        )

    def to_core(self, dz, dy, dx):
        if dz == 0 and dy == 0 and self.full is not None:
            return
        self.send(
            dz, dy, dx, self.whole, self.sends.at[0], self.c_recv.at[dz + 3, dy, dx],
            self.spot.device(0, 0, 0, 1),
        )

    def along_z(self, dz, dy, dx, columns, send_sem, recv_sem):
        for side, step in ((0, 1), (1, -1)):
            if dz * step <= 0:

                @pl.when(self.spot.has(step))
                def _(side=side, step=step):
                    self.send(
                        dz, dy, dx, columns, send_sem(side), recv_sem(dz + 3 - step),
                        self.spot.device(step),
                    )

    def spread(self, dz):
        spot = self.spot
        self.along_z(
            dz, 0, 0, self.whole, lambda side: self.z_send.at[dz + 3, side],
            lambda at: self.recv.at[0, at],
        )
        if dz == 0:
            columns, at = (self.whole, self.whole), 0
        else:
            columns, at = self.early, 3
        self.send(
            dz, 0, 0, columns[0], self.sends.at[1 + at], self.recv.at[1, dz + 3], spot.device(0, 1)
        )
        if dz != 0 or self.full is None:
            self.send(
                dz, 0, 0, columns[1], self.sends.at[2 + at], self.recv.at[2, dz + 3],
                spot.device(0, 0, 1),
            )
        self.to_core(dz, 0, 0)

    def start(self):
        self.local.start()
        self.spread(0)

    def take_z(self, dz):
        def action():
            arrive(self.place(dz, 0, 0), self.recv.at[0, dz + 3])
            self.spread(dz)

        when_has(self.spot, dz, action)

    def take_yx(self, dz):
        spot = self.spot

        def action():
            columns = self.early if dz else (self.whole, self.whole)
            arrive(self.place(dz, 1, 0, 0, columns[0]), self.recv.at[1, dz + 3])
            self.send(
                dz, 1, 0, self.first, self.sends.at[3], self.recv.at[3, dz + 3],
                spot.device(0, 0, 1),
            )
            if dz != 0 or self.full is None:
                arrive(self.place(dz, 0, 1, 0, columns[1]), self.recv.at[2, dz + 3])
            self.send(
                dz, 0, 1, self.second, self.sends.at[3], self.recv.at[4, dz + 3],
                spot.device(0, 1),
            )

        when_has(spot, dz, action)

    def take_late(self, dz):
        def action():
            for dy, dx in ((1, 0), (0, 1)):
                columns = self.late[dx]
                if dz != 0:
                    arrive(self.place(dz, dy, dx, 0, columns), self.late_recv.at[dz + 3, dx])
                self.along_z(
                    dz, dy, dx, columns, lambda side: self.late_send.at[dz + 3, side, dx],
                    lambda at: self.late_recv.at[at, dx],
                )
                self.to_core(dz, dy, dx)

        when_has(self.spot, dz, action)

    def take_diagonal(self, dz):
        def action():
            arrive(self.place(dz, 1, 1, 0, self.first), self.recv.at[3, dz + 3])
            arrive(self.place(dz, 1, 1, 0, self.second), self.recv.at[4, dz + 3])
            self.to_core(dz, 1, 1)

        when_has(self.spot, dz, action)

    def take_core(self, far, dy, dx):
        view = self.out.at[pl.ds(0, self.count), :]
        arrive(view, self.c_recv.at[far - self.spot.z + 3, dy, dx])

    def drain(self):
        count, spot = self.count, self.spot
        replicated = self.full is not None
        for at, pieces, columns in (
            (0, 14 if replicated else 16, self.whole), (1, 1, self.whole), (2, 1, self.whole),
            (3, 4, self.whole), (4, 3, self.early[0]), (5, 3, self.early[1]),
        ):
            if at != 2 or not replicated:
                arrive(self.out.at[pl.ds(0, pieces * count), columns], self.sends.at[at])
        for dz in range(-3, 4):
            for side, step in ((0, 1), (1, -1)):
                if dz * step <= 0:

                    @pl.when(spot.has(dz) & spot.has(step))
                    def _(dz=dz, side=side):
                        arrive(self.place(0, 0, 0), self.z_send.at[dz + 3, side])
                        for at in (0, 1):
                            arrive(
                                self.place(0, 0, 0, 0, self.late[at]),
                                self.late_send.at[dz + 3, side, at],
                            )


def experts_kernel(
    normed, grad_y, w_gate, w_up, w_down, router, chosen, kept,
    reduced, grad_gate, grad_up, grad_down,
    rows_all, weight, grad_in, grad_in_down, y_block, back_block,
    mine, other, from_a, from_b, from_y, from_x, from_z,
    weight_sem, y_sem, flush_sem, core_send, core_recv, half_send, yx_send, recv,
    line_send, line_recv, *gather_sems,
):
    spot = Spot()
    count, width = normed.shape
    wide = reduced.shape[1]
    local_count, ff, _ = w_gate.shape
    both = local_count * ff
    block = 4 * count
    split = from_a.shape[2]
    first, second = pl.ds(0, split), pl.ds(split, wide - split)
    group = lax.axis_index("expert")
    to_y, to_x, to_c = spot.device(0, 1), spot.device(0, 0, 1), spot.device(0, 0, 0, 1)

    def place_of(step):
        return near_first((step // 2 + 1) % 4, spot.z), (step + (step + 6) // 8) % 2

    def group_rows(step):
        far, dy = place_of(step)
        y = spot.y + dy * (1 - 2 * spot.y)
        return pl.ds(pl.multiple_of((far * 2 + y) * block, block), block)

    def y_copy(step):
        slot = step % 2
        return pltpu.make_async_copy(
            grad_y.at[group_rows(step), :], y_block.at[slot], y_sem.at[slot]
        )

    sources = [ref.at[at] for ref in (w_gate, w_up) for at in range(local_count)]
    weights = [
        pltpu.make_async_copy(source, weight.at[pl.ds(at * ff, ff), :], weight_sem.at[at])
        for at, source in enumerate(sources)
    ]
    for copy in weights:
        copy.start()
    y_copy(0).start()
    gather = Gather(spot, normed, rows_all, *gather_sems)
    spot.greet()
    gather.start()
    grad_in[...] = jnp.zeros_like(grad_in)
    grad_in_down[...] = jnp.zeros_like(grad_in_down)
    gather.local.wait()
    for copy in weights:
        copy.wait()

    def piece(dx, dc):
        _, part = spot.device(0, 0, dx, dc)
        return pl.ds(pl.multiple_of(part * count, count), count)

    def core_copy(step, dx):
        far, dy = place_of(step)
        slot = step % 2
        return pltpu.make_async_remote_copy(
            src_ref=back_block.at[slot, piece(dx, 1), :],
            dst_ref=other.at[far, dy, dx],
            send_sem=core_send.at[slot, dx],
            recv_sem=core_recv.at[far, dy, dx],
            device_id=to_c,
            device_id_type=MESH,
        )

    def merge(far, dy, dx):
        into = mine.at[far, dy, dx]
        arrive(other.at[far, dy, dx], core_recv.at[far, dy, dx])
        return into

    def merge_diagonal(k):
        far = near_first(k, spot.z)
        into = merge(far, 1, 1)
        add_into(into, 16, other.at[far, 1, 1])
        push(into.at[:, first], from_a.at[far], half_send.at[0], recv.at[0, far], to_x)
        push(into.at[:, second], from_b.at[far], half_send.at[1], recv.at[1, far], to_y)

    def merge_yx(k):
        far = near_first(k, spot.z)
        into = merge(far, 1, 0)
        add_into(into, 16, other.at[far, 1, 0])
        arrive(from_a.at[far], recv.at[0, far])
        add_into(into.at[:, first], 16, from_a.at[far])
        push(into, from_y.at[far], yx_send.at[0], recv.at[2, far], to_y)
        into = merge(far, 0, 1)
        add_into(into, 16, other.at[far, 0, 1])
        arrive(from_b.at[far], recv.at[1, far])
        add_into(into.at[:, second], 16, from_b.at[far])
        push(into, from_x.at[far], yx_send.at[1], recv.at[3, far], to_x)

    def merge_line(k):
        far = near_first(k, spot.z)
        into = merge(far, 0, 0)
        arrive(from_y.at[far], recv.at[2, far])
        arrive(from_x.at[far], recv.at[3, far])
        add_into(into, 16, other.at[far, 0, 0], from_y.at[far], from_x.at[far])
        if k > 0:
            push(
                into, from_z.at[spot.z], line_send.at[k], line_recv.at[spot.z],
                (far * 2 + spot.y, spot.x * 2 + spot.c),
            )

    def both_ways(take, distance):
        for dz in (distance, -distance) if distance else (0,):
            take(dz)

    columns = lax.broadcasted_iota(jnp.int32, (block, both), 1)
    lower = columns < ff
    lanes = lax.broadcasted_iota(jnp.int32, (block, 128), 1)
    names = lax.broadcasted_iota(jnp.int32, (router.shape[0], block), 0)

    def compute(step):
        slot = step % 2
        here = group_rows(step)
        rows = rows_all[here, :]
        lin = mxu(rows, weight[...], 1, 1)
        gate, up = lin[:, :both], lin[:, both:]
        logits = mxu(router[...], rows, 1, 1)
        picked = chosen[:, here] > 0.0
        top = jnp.max(jnp.where(picked, logits, NEG), axis=0, keepdims=True)
        exps = jnp.where(picked, jnp.exp(logits - top), 0.0)
        soft = exps / jnp.sum(exps, axis=0, keepdims=True)
        keep = kept[:, here]
        soft = jnp.where(keep > 0.0, soft, 0.0)
        lines = []
        for table in (soft, keep):
            for at in range(local_count):
                lines.append(
                    jnp.sum(
                        jnp.where(names == group * local_count + at, table, 0.0),
                        axis=0, keepdims=True,
                    )
                )
        stack = jnp.concatenate(lines + [jnp.zeros((8 - len(lines), block), F32)], axis=0).T
        spread = jnp.where(lower, stack[:, 0:1], stack[:, 1:2])
        sigmoid = 1.0 / (1.0 + jnp.exp(-gate))
        silu = gate * sigmoid
        act = (silu * up).astype(BF16).astype(F32)
        weighted = (act * spread).astype(BF16)
        y_copy(step).wait()

        @pl.when(step >= 2)
        def _():
            for dx in (0, 1):
                core_copy(step - 2, dx).wait_send()

        back_block[slot, :, :width] = mxu(weighted, w_down[...]).astype(BF16)
        pass_on(step, 1)
        y_rows = y_block[slot]
        mid = mxu(y_rows, w_down[...], 1, 1)
        dots = act * mid
        low = jnp.sum(jnp.where(lower, dots, 0.0), axis=1, keepdims=True) * stack[:, 2:3]
        high = jnp.sum(jnp.where(lower, 0.0, dots), axis=1, keepdims=True) * stack[:, 3:4]
        mine_at = group * local_count
        tail = jnp.where(lanes == mine_at, low, jnp.where(lanes == mine_at + 1, high, 0.0))
        grad_act = mid * spread
        grad_up_lin = (grad_act * silu).astype(BF16)
        grad_gate_lin = (grad_act * up * sigmoid * (1.0 + gate * (1.0 - sigmoid))).astype(BF16)
        grad_lin = jnp.concatenate([grad_gate_lin, grad_up_lin], axis=1)
        back_block[slot, :, width : 2 * width] = mxu(grad_lin, weight[...]).astype(BF16)
        back_block[slot, :, 2 * width :] = tail.astype(BF16)
        far, dy = place_of(step)
        for dx in (1, 0):
            core_copy(step, dx).start()
            mine[far, dy, dx] = back_block[slot, piece(dx, 0), :]
        grad_in[...] += mxu(grad_lin, rows, 0, 0)
        grad_in_down[...] += mxu(weighted, y_rows, 0, 0)

    plans = {
        0: lambda: (
            both_ways(gather.take_yx, 0), both_ways(gather.take_z, 1),
            both_ways(gather.take_z, 2), both_ways(gather.take_diagonal, 0),
            both_ways(gather.take_late, 0), both_ways(gather.take_yx, 1),
            both_ways(gather.take_z, 3), both_ways(gather.take_late, 1),
        ),
        1: lambda: both_ways(gather.take_yx, 2),
        2: lambda: (both_ways(gather.take_diagonal, 1), both_ways(gather.take_late, 2)),
        3: lambda: both_ways(gather.take_yx, 3),
        4: lambda: (both_ways(gather.take_diagonal, 2), both_ways(gather.take_late, 3)),
        5: lambda: merge_diagonal(1),
        6: lambda: both_ways(gather.take_diagonal, 3),
        7: lambda: merge_diagonal(2),
        9: lambda: merge_yx(1),
        11: lambda: (merge_diagonal(3), merge_yx(2)),
        13: lambda: merge_line(1),
        15: lambda: (merge_diagonal(0), merge_yx(3)),
    }

    def pass_on(step, middle):
        for at, plan in plans.items():
            if at % 2 == middle:

                @pl.when(step == at // 2)
                def _(plan=plan):
                    plan()

    @pl.loop(0, 8)
    def _(step):
        pass_on(step, 0)

        @pl.when(step < 7)
        def _():
            y_copy(step + 1).start()

        far, dy = place_of(step)
        for dx in (0, 1):
            gather.take_core(far, dy, dx)
        compute(step)

    flush = [
        pltpu.make_async_copy(
            grad_in.at[pl.ds(at * ff, ff), :],
            (grad_gate, grad_up)[at // local_count].at[at % local_count],
            flush_sem.at[at],
        )
        for at in range(2 * local_count)
    ]
    flush.append(pltpu.make_async_copy(grad_in_down, grad_down, flush_sem.at[2 * local_count]))
    for copy in flush:
        copy.start()
    merge_line(2)
    merge_yx(0)
    merge_line(3)
    merge_line(0)
    total = mine[spot.z, 0, 0].astype(F32)
    for k in (1, 2, 3):
        source = near_first(k, spot.z)
        arrive(from_z.at[source], line_recv.at[source])
        total = total + from_z[source].astype(F32)
    reduced[...] = total
    gather.drain()
    for step in (6, 7):
        for dx in (0, 1):
            core_copy(step, dx).wait_send()
    arrive(from_a, half_send.at[0])
    arrive(from_b, half_send.at[1])
    arrive(from_y, yx_send.at[0])
    arrive(from_x, yx_send.at[1])
    for k in (1, 2, 3):
        arrive(from_z.at[0], line_send.at[k])
    for copy in flush:
        copy.wait()


def experts(normed, grad_y, w_gate, w_up, w_down, router, chosen, kept):
    count, width = normed.shape
    wide = 2 * width + 128
    total = grad_y.shape[0]
    local_count, ff, _ = w_gate.shape
    both = local_count * ff
    shape, vmem, dma = jax.ShapeDtypeStruct, pltpu.VMEM, pltpu.SemaphoreType.DMA
    line = vmem((4, count, wide), BF16)
    return pl.pallas_call(
        experts_kernel,
        out_shape=(
            shape((count, wide), F32),
            shape(w_gate.shape, F32), shape(w_up.shape, F32), shape((both, width), F32),
        ),
        in_specs=[VMEM_SPEC, HBM_SPEC, HBM_SPEC, HBM_SPEC] + [VMEM_SPEC] * 4,
        out_specs=(VMEM_SPEC,) + (HBM_SPEC,) * 3,
        scratch_shapes=[
            vmem((total, width), BF16),
            vmem((2 * both, width), BF16),
            vmem((2 * both, width), F32),
            vmem((both, width), F32),
            vmem((2, 4 * count, width), BF16),
            vmem((2, 4 * count, wide), BF16),
            vmem((4, 2, 2, count, wide), BF16),
            vmem((4, 2, 2, count, wide), BF16),
            vmem((4, count, width), BF16),
            vmem((4, count, wide - width), BF16),
            line, line, line,
        ]
        + dma_sems(
            ((2 * local_count,), (2,), (2 * local_count + 1,), (2, 2), (4, 2, 2), (2,), (2,), (4, 4),
             (4,), (4,))
            + Gather.SEMS
        ),
        compiler_params=pltpu.CompilerParams(
            collective_id=8, has_side_effects=True, vmem_limit_bytes=63 << 20
        ),
        name="experts",
        cost_estimate=cost(29_000_000_000, 120),
    )(normed, grad_y, w_gate, w_up, w_down, router, chosen, kept)


def attend_back_kernel(
    own_rows, w_out, queries, keys, values, attended, lin, cosine, sine, place_column,
    place_row, open_row, log_total, k_gain, q_gain,
    grad_lin, grad_out, grad_q_gain, grad_k_gain,
    rows_all, head_out, grad_keys, grad_values, out_sum, head_sem, *gather_sems,
):
    spot = Spot()
    count = own_rows.shape[0]
    block = 4 * count
    dim = queries.shape[1]
    group = lax.axis_index("expert")
    head_copy = pltpu.make_async_copy(
        w_out.at[pl.ds(pl.multiple_of(group * dim, dim), dim), :], head_out, head_sem
    )
    head_copy.start()
    gather = Gather(spot, own_rows, rows_all, *gather_sems)
    spot.greet()
    gather.start()
    grad_keys[...] = jnp.zeros_like(grad_keys)
    grad_values[...] = jnp.zeros_like(grad_values)
    out_sum[...] = jnp.zeros_like(out_sum)
    grad_q_gain[...] = jnp.zeros_like(grad_q_gain)
    gather.local.wait()
    head_copy.wait()

    def unshape(grad, plain, gain, cos, sin):
        grad = grad * cos + pltpu.roll(grad * sin, dim // 2, 1)
        normed, root = head_norm(plain)
        gain_part = jnp.sum(grad * normed, axis=0, keepdims=True)
        grad = grad * gain
        return root * (grad - normed * jnp.mean(grad * normed, axis=-1, keepdims=True)), gain_part

    def compute(far, dy):
        y = spot.y + dy * (1 - 2 * spot.y)
        here = pl.ds(pl.multiple_of((far * 2 + y) * block, block), block)
        rows = rows_all[here, :]
        query = queries[here, :]
        grad_att = mxu(rows, head_out[...], 1, 1).astype(BF16)
        scores = mxu(keys[...], query, 1, 1)
        seen = (place_column[...] <= place_row[:, here]) & (place_column[...] >= open_row[:, here])
        probability = jnp.exp(jnp.where(seen, scores - log_total[:, here], NEG))
        grad_prob = mxu(values[...], grad_att, 1, 1)
        delta = jnp.sum(probability * grad_prob, axis=0, keepdims=True)
        grad_scores = (probability * (grad_prob - delta)).astype(BF16)
        grad_values[...] += mxu(probability.astype(BF16), grad_att)
        grad_keys[...] += mxu(grad_scores, query)
        grad_query = mxu(grad_scores, keys[...], 0, 0) * dim**-0.5
        grad_query, gain_part = unshape(
            grad_query, lin[here, :dim], q_gain[...], cosine[here, :], sine[here, :]
        )
        grad_q_gain[...] += gain_part
        grad_lin[here, :dim] = grad_query.astype(BF16)
        out_sum[...] += mxu(attended[here, :], rows, 0, 0)

    def both_ways(take, distance):
        for dz in (distance, -distance) if distance else (0,):
            take(dz)

    plans = {
        0: lambda: (both_ways(gather.take_yx, 0), both_ways(gather.take_z, 1),
                    both_ways(gather.take_late, 0)),
        1: lambda: (both_ways(gather.take_diagonal, 0), both_ways(gather.take_z, 2)),
        2: lambda: (both_ways(gather.take_yx, 1), both_ways(gather.take_z, 3),
                    both_ways(gather.take_late, 1)),
        3: lambda: (both_ways(gather.take_yx, 2), both_ways(gather.take_diagonal, 1),
                    both_ways(gather.take_late, 2)),
        4: lambda: (both_ways(gather.take_yx, 3), both_ways(gather.take_late, 3)),
        5: lambda: both_ways(gather.take_diagonal, 2),
        7: lambda: both_ways(gather.take_diagonal, 3),
    }

    @pl.loop(0, 8)
    def _(step):
        for at, plan in plans.items():

            @pl.when(step == at)
            def _(plan=plan):
                plan()

        far, dy = near_first(step // 2, spot.z), step % 2
        for dx in (0, 1):
            gather.take_core(far, dy, dx)
        compute(far, dy)

    grad_out[...] = out_sum[...].astype(BF16)
    grad_key, key_part = unshape(grad_keys[...], lin[:, dim:], k_gain[...], cosine[...], sine[...])
    grad_lin[:, dim : 2 * dim] = grad_key.astype(BF16)
    grad_lin[:, 2 * dim :] = grad_values[...].astype(BF16)
    grad_k_gain[...] = key_part
    gather.drain()


def attend_back(
    own_rows, w_out, queries, keys, values, attended, lin, cosine, sine, place_column,
    place_row, open_row, log_total, k_gain, q_gain,
):
    count, width = own_rows.shape
    total, dim = keys.shape
    shape, vmem = jax.ShapeDtypeStruct, pltpu.VMEM
    return pl.pallas_call(
        attend_back_kernel,
        out_shape=[
            shape((total, 3 * dim), BF16), shape((dim, width), BF16),
            shape((1, dim), F32), shape((1, dim), F32),
        ],
        in_specs=[VMEM_SPEC, HBM_SPEC] + [VMEM_SPEC] * 13,
        out_specs=[VMEM_SPEC] * 4,
        scratch_shapes=[
            vmem((total, width), BF16), vmem((dim, width), BF16),
            vmem((total, dim), F32), vmem((total, dim), F32), vmem((dim, width), F32),
        ]
        + dma_sems((None,) + Gather.SEMS),
        compiler_params=pltpu.CompilerParams(
            collective_id=9, has_side_effects=True, vmem_limit_bytes=60 << 20
        ),
        name="attend_back",
        cost_estimate=cost(9_000_000_000, 50),
    )(
        own_rows, w_out, queries, keys, values, attended, lin, cosine, sine, place_column,
        place_row, open_row, log_total, k_gain, q_gain,
    )


class LineGather:
    SEMS = ((7,), (7,), (7, 2), None, None, (7, 2), (7, 2, 2), None)

    def __init__(self, spot, place, own, sems):
        self.spot, self.place, self.own = spot, place, own
        self.z_recv, self.y_recv, self.z_send, self.y_send = sems[:4]
        self.late_y_recv, self.late_z_recv, self.late_z_send, self.late_y_send = sems[4:]

    def source(self, dz, dy, part):
        return self.own(part) if dz == 0 and dy == 0 else self.place(dz, dy, part)

    def along_z(self, dz, dy, part):
        for side, step in ((0, 1), (1, -1)):
            if dz * step <= 0:

                @pl.when(self.spot.has(step))
                def _(side=side, step=step):
                    if part:
                        send = self.late_z_send.at[dz + 3, side, dy]
                        recv = self.late_z_recv.at[dz + 3 - step, dy]
                    else:
                        send = self.z_send.at[dz + 3, side]
                        recv = self.z_recv.at[dz + 3 - step]
                    push(
                        self.source(dz, dy, part), self.place(dz, dy, part), send, recv,
                        self.spot.device(step),
                    )

    def along_y(self, dz):
        push(
            self.source(dz, 0, 0), self.place(dz, 0, 0), self.y_send, self.y_recv.at[dz + 3],
            self.spot.device(0, 1),
        )

    def start(self):
        self.along_z(0, 0, 0)
        push(
            self.own(1), self.place(0, 0, 1), self.late_y_send, self.late_y_recv,
            self.spot.device(0, 1),
        )
        self.along_y(0)
        self.along_z(0, 0, 1)

    def take_z(self, distance):
        for dz in (distance, -distance):

            def action(dz=dz):
                arrive(self.place(dz, 0, 0), self.z_recv.at[dz + 3])
                self.along_z(dz, 0, 0)
                self.along_y(dz)

            when_has(self.spot, dz, action)

    def take_late_y(self):
        arrive(self.place(0, 1, 1), self.late_y_recv)
        self.along_z(0, 1, 1)

    def take_late_z(self, distance):
        for dz in (distance, -distance):

            def action(dz=dz):
                for dy in (0, 1):
                    arrive(self.place(dz, dy, 1), self.late_z_recv.at[dz + 3, dy])
                    self.along_z(dz, dy, 1)

            when_has(self.spot, dz, action)

    def drain(self, four):
        for dz in (0, 1, -1, 2, -2, 3, -3):

            def action(dz=dz):
                arrive(self.place(dz, 1, 0), self.y_recv.at[dz + 3])
                for side, step in ((0, 1), (1, -1)):
                    if dz * step <= 0:

                        @pl.when(self.spot.has(step))
                        def _(side=side):
                            arrive(self.place(dz, 0, 0), self.z_send.at[dz + 3, side])
                            for dy in (0, 1):
                                arrive(
                                    self.place(dz, dy, 1), self.late_z_send.at[dz + 3, side, dy]
                                )

            when_has(self.spot, dz, action)
        arrive(four, self.y_send)
        arrive(self.place(0, 0, 1), self.late_y_send)


def close_kernel(
    normed, grad_lin, w_query, w_key, w_value, head_out,
    reduced, kv_all, query_all, out_all,
    weight, rows, sums, query_own, kv_part, back, mine, other, from_x_diagonal, from_y, from_x,
    from_z, kv_mine, kv_y, kv_z, kv_own, row_sem, weight_sem, local_sem,
    core_send, core_recv, many_send, recv, line_send, line_recv,
    kv_send, kv_y_recv, kv_line_send, kv_line_recv, *gather_sems,
):
    spot = Spot()
    total, width = normed.shape
    count, wide = reduced.shape
    block = 4 * count
    dim = w_key.shape[1]
    group = lax.axis_index("expert")
    to_y, to_x, to_c = spot.device(0, 1), spot.device(0, 0, 1), spot.device(0, 0, 0, 1)
    cut = 1664

    def parts(part):
        return pl.ds(cut, total - cut) if part else pl.ds(0, cut)

    def lane_block(dz, dy):
        return pl.ds(pl.multiple_of(spot.device(dz, dy)[0] * dim, dim), dim)

    weights = [
        pltpu.make_async_copy(
            w_query.at[:, pl.ds(pl.multiple_of(group * dim, dim), dim)],
            weight.at[:, pl.ds(0, dim)], weight_sem.at[0],
        ),
        pltpu.make_async_copy(w_key, weight.at[:, pl.ds(dim, dim)], weight_sem.at[1]),
        pltpu.make_async_copy(w_value, weight.at[:, pl.ds(2 * dim, dim)], weight_sem.at[2]),
    ]

    def row_copy(step):
        return pltpu.make_async_copy(
            normed.at[pl.ds(pl.multiple_of(step * block, block), block), :],
            rows.at[step % 2], row_sem.at[step % 2],
        )

    for copy in weights:
        copy.start()
    row_copy(0).start()
    outs = LineGather(
        spot,
        lambda dz, dy, part: out_all.at[lane_block(dz, dy), parts(part)],
        lambda part: head_out.at[:, parts(part)],
        gather_sems[:8],
    )
    queries = LineGather(
        spot,
        lambda dz, dy, part: query_all.at[parts(part), lane_block(dz, dy)],
        lambda part: query_own.at[parts(part), :],
        gather_sems[8:16],
    )
    kv_rows = total // 8

    def kv_span(start, part):
        return pl.ds(pl.multiple_of(start + part * (kv_rows // 2), kv_rows // 2), kv_rows // 2)

    kvs = LineGather(
        spot,
        lambda dz, dy, part: kv_all.at[kv_span(spot.device(dz, dy)[0] * kv_rows, part), :],
        lambda part: kv_own.at[kv_span(0, part), :],
        gather_sems[16:],
    )
    out_copy = pltpu.make_async_copy(head_out, out_all.at[lane_block(0, 0), :], local_sem.at[0])
    out_copy.start()
    spot.greet(line=True)
    outs.start()

    sums[...] = jnp.zeros_like(sums)

    @pl.loop(0, total // block)
    def _(step):
        @pl.when(step < total // block - 1)
        def _():
            row_copy(step + 1).start()

        row_copy(step).wait()
        here = pl.ds(pl.multiple_of(step * block, block), block)
        sums[...] += mxu(grad_lin[here, :], rows[step % 2], 0, 0)

    query_own[...] = sums[:dim, :].T.astype(BF16)
    kv_part[...] = sums[dim:, :].T.astype(BF16)
    query_copy = pltpu.make_async_copy(query_own, query_all.at[:, lane_block(0, 0)], local_sem.at[1])
    query_copy.start()

    def group_rows(far, dy):
        y = spot.y + dy * (1 - 2 * spot.y)
        return pl.ds(pl.multiple_of((far * 2 + y) * block, block), block)

    for k in (3, 2, 1, 0):
        far = near_first(k, spot.z)
        push(
            kv_part.at[group_rows(far, 1), :], kv_y.at[far], kv_send, kv_y_recv.at[far], to_y
        )
    for copy in weights:
        copy.wait()

    def piece(dx, dc):
        _, part = spot.device(0, 0, dx, dc)
        return pl.ds(pl.multiple_of(part * count, count), count)

    def core_copy(step, far, dy, dx):
        return pltpu.make_async_remote_copy(
            src_ref=back.at[step % 2, piece(dx, 1), :],
            dst_ref=other.at[far, dy, dx],
            send_sem=core_send.at[step % 2, dx],
            recv_sem=core_recv.at[far, dy, dx],
            device_id=to_c,
            device_id_type=MESH,
        )

    def produce(k):
        far = near_first(k, spot.z)
        for dy in (1, 0):
            step = 2 * (3 - k) + 1 - dy
            if step >= 2:
                for dx in (1, 0):
                    core_copy(step, far, dy, dx).wait_send()
            here = group_rows(far, dy)
            back[step % 2] = mxu(grad_lin[here, :], weight[...], 1, 1).astype(BF16)
            for dx in (1, 0):
                core_copy(step, far, dy, dx).start()
                mine[far, dy, dx] = back[step % 2, piece(dx, 0), :]

    def merge(far, dy, dx, *terms):
        arrive(other.at[far, dy, dx], core_recv.at[far, dy, dx])
        add_into(mine.at[far, dy, dx], 16, other.at[far, dy, dx], *terms)
        return mine.at[far, dy, dx]

    def merge_diagonal(k):
        far = near_first(k, spot.z)
        push(
            merge(far, 1, 1), from_x_diagonal.at[far], many_send.at[0], recv.at[0, far], to_x
        )

    def merge_yx(k):
        far = near_first(k, spot.z)
        push(merge(far, 0, 1), from_x.at[far], many_send.at[1], recv.at[1, far], to_x)
        arrive(from_x_diagonal.at[far], recv.at[0, far])
        push(
            merge(far, 1, 0, from_x_diagonal.at[far]), from_y.at[far], many_send.at[2],
            recv.at[2, far], to_y,
        )

    def far_device(far):
        return (far * 2 + spot.y, spot.x * 2 + spot.c)

    def merge_kv(k):
        far = near_first(k, spot.z)
        kv_mine[far] = kv_part[group_rows(far, 0), :]
        arrive(kv_y.at[far], kv_y_recv.at[far])
        add_into(kv_mine.at[far], 64, kv_y.at[far])
        if k > 0:
            push(
                kv_mine.at[far], kv_z.at[spot.z], kv_line_send.at[k], kv_line_recv.at[spot.z],
                far_device(far),
            )

    def merge_line(k):
        far = near_first(k, spot.z)
        arrive(from_y.at[far], recv.at[2, far])
        arrive(from_x.at[far], recv.at[1, far])
        into = merge(far, 0, 0, from_y.at[far], from_x.at[far])
        if k > 0:
            push(
                into, from_z.at[spot.z], line_send.at[k], line_recv.at[spot.z], far_device(far)
            )

    def sum_kv():
        sums_kv = kv_mine[spot.z].astype(F32)
        for k in (1, 2, 3):
            source = near_first(k, spot.z)
            arrive(kv_z.at[source], kv_line_recv.at[source])
            sums_kv = sums_kv + kv_z[source].astype(F32)
        kv_own[...] = sums_kv.astype(BF16)

    produce(3)
    produce(2)
    outs.take_z(1)
    for k in (3, 2, 1, 0):
        merge_kv(k)
    queries.start()
    merge_diagonal(3)
    produce(1)
    merge_diagonal(2)
    outs.take_late_y()
    produce(0)
    merge_diagonal(1)
    sum_kv()
    kvs.start()
    kv_copy = pltpu.make_async_copy(
        kv_own, kv_all.at[pl.ds(pl.multiple_of(group * kv_rows, kv_rows), kv_rows), :],
        local_sem.at[2],
    )
    kv_copy.start()
    outs.take_z(2)
    queries.take_z(1)
    merge_diagonal(0)
    merge_yx(3)
    kvs.take_z(1)
    kvs.take_late_y()
    queries.take_late_y()
    outs.take_late_z(1)
    merge_yx(2)
    outs.take_z(3)
    queries.take_z(2)
    kvs.take_z(2)
    kvs.take_late_z(1)
    merge_line(3)
    merge_yx(1)
    queries.take_late_z(1)
    outs.take_late_z(2)
    kvs.take_z(3)
    kvs.take_late_z(2)
    merge_line(2)
    merge_yx(0)
    queries.take_z(3)
    queries.take_late_z(2)
    outs.take_late_z(3)
    merge_line(1)
    merge_line(0)
    kvs.take_late_z(3)
    queries.take_late_z(3)
    total_rows = mine[spot.z, 0, 0].astype(F32)
    for k in (1, 2, 3):
        source = near_first(k, spot.z)
        arrive(from_z.at[source], line_recv.at[source])
        total_rows = total_rows + from_z[source].astype(F32)
    reduced[...] = total_rows

    kvs.drain(kv_all.at[pl.ds(0, 2 * kv_rows), :])
    kv_copy.wait()
    outs.drain(out_all.at[pl.ds(0, 4 * dim), parts(0)])
    queries.drain(query_all.at[parts(0), pl.ds(0, 4 * dim)])
    out_copy.wait()
    query_copy.wait()
    for step in (6, 7):
        for dx in (0, 1):
            core_copy(step, near_first(0, spot.z), 0, dx).wait_send()
    arrive(from_x_diagonal, many_send.at[0])
    arrive(from_x, many_send.at[1])
    arrive(from_y, many_send.at[2])
    arrive(kv_y, kv_send)
    for k in (1, 2, 3):
        arrive(from_z.at[0], line_send.at[k])
        arrive(kv_z.at[0], kv_line_send.at[k])


def close(normed, grad_lin, w_query, w_key, w_value, head_out):
    total, width = normed.shape
    count, wide, dim = total // 32, width, w_key.shape[1]
    shape, vmem = jax.ShapeDtypeStruct, pltpu.VMEM
    line, kv_line = vmem((4, count, wide), BF16), vmem((4, 4 * count, 2 * dim), BF16)
    return pl.pallas_call(
        close_kernel,
        out_shape=(
            shape((count, wide), F32), shape((total, 2 * dim), BF16),
            shape((total, 8 * dim), BF16), shape((8 * dim, width), BF16),
        ),
        in_specs=[HBM_SPEC, VMEM_SPEC, HBM_SPEC, HBM_SPEC, HBM_SPEC, VMEM_SPEC],
        out_specs=(VMEM_SPEC, HBM_SPEC, HBM_SPEC, HBM_SPEC),
        scratch_shapes=[
            vmem((width, 3 * dim), BF16), vmem((2, 4 * count, width), BF16),
            vmem((3 * dim, width), F32), vmem((width, dim), BF16), vmem((width, 2 * dim), BF16),
            vmem((2, 4 * count, wide), BF16),
            vmem((4, 2, 2, count, wide), BF16), vmem((4, 2, 2, count, wide), BF16),
            line, line, line, line, kv_line, kv_line, kv_line,
            vmem((4 * count, 2 * dim), BF16),
        ]
        + dma_sems(
            ((2,), (3,), (3,), (2, 2), (4, 2, 2), (3,), (3, 4), (4,), (4,),
             None, (4,), (4,), (4,)) + LineGather.SEMS * 3
        ),
        compiler_params=pltpu.CompilerParams(
            collective_id=10, has_side_effects=True, vmem_limit_bytes=60 << 20
        ),
        name="close",
        cost_estimate=cost(7_000_000_000, 110),
    )(normed, grad_lin, w_query, w_key, w_value, head_out)


def cosine_sine(angles):
    lanes = lax.broadcasted_iota(jnp.int32, angles.shape, 1)
    turns = jnp.floor(angles * (2.0 / math.pi) + 0.5)
    rest = angles - turns * 1.5703125
    rest = rest - turns * 4.837512969970703125e-4
    rest = rest - turns * 7.54978995489188216e-8
    square = rest * rest
    sine = square * (8.3321608736e-3 + square * -1.9515295891e-4) - 1.6666654611e-1
    sine = rest + rest * square * sine
    cosine = -1.388731625493765e-3 + square * 2.443315711809948e-5
    cosine = 1.0 - 0.5 * square + square * square * (4.166664568298827e-2 + square * cosine)
    turns = jnp.where(lanes < angles.shape[1] // 2, turns, turns - 1.0)
    turns = turns - 4.0 * jnp.floor(turns * 0.25)
    odd = (turns == 1.0) | (turns == 3.0)
    value = jnp.where(odd, sine, cosine)
    return jnp.where((turns == 1.0) | (turns == 2.0), -value, value)


def front_kernel(
    hidden, cotangent, tag, lengths, gain, w_query, w_key, w_value, q_gain, k_gain, inverse,
    w_out, second_gain,
    normed_all, queries, keys, values, lin_out, cosine, sine, attended, log_total,
    place_row, open_row, place_column, residual, normed, chosen, kept, grad_y_all,
    rows_all, weight, out_weight, staged, tags, ranks, picks, att_rows,
    partial_sum, from_core, to_x_sum, from_x,
    weight_sem, stage_sem, tag_z, tag_y, tag_z_send, tag_y_send, tag_local,
    send_sem, recv_sem, own_sem, tensor_sems, *gather_sems,
):
    spot = Spot()
    group, part = lax.axis_index("expert"), lax.axis_index("tensor")
    count, width = residual.shape
    block = 4 * count
    total = 32 * count
    dim = w_key.shape[1]
    own = pl.ds(pl.multiple_of(part * count, count), count)

    weights = [
        pltpu.make_async_copy(
            w_query.at[:, pl.ds(pl.multiple_of(group * dim, dim), dim)],
            weight.at[:, pl.ds(0, dim)], weight_sem.at[0],
        ),
        pltpu.make_async_copy(w_key, weight.at[:, pl.ds(dim, dim)], weight_sem.at[1]),
        pltpu.make_async_copy(w_value, weight.at[:, pl.ds(2 * dim, dim)], weight_sem.at[2]),
        pltpu.make_async_copy(w_out, out_weight, weight_sem.at[3]),
    ]
    for copy in weights:
        copy.start()
    barrier = pltpu.get_barrier_semaphore()

    @pl.loop(1, 8)
    def _(step):
        pl.semaphore_signal(
            barrier, inc=1, device_id=((group + step) % 8, part), device_id_type=MESH
        )

    for device in (spot.device(0, 0, 1), spot.device(0, 0, 0, 1)):
        pl.semaphore_signal(barrier, inc=1, device_id=device, device_id_type=MESH)

    def tag_place(dz, dy):
        return tags.at[spot.device(dz, dy)[0]]

    tag_copy = pltpu.make_async_copy(tag, tag_place(0, 0), tag_local)
    tag_copy.start()
    pl.semaphore_wait(barrier, 9)

    def spread_tag(dz):
        here = tag_place(dz, 0)
        source = tag if dz == 0 else here
        for side, step in ((0, 1), (1, -1)):
            if dz * step <= 0:

                @pl.when(spot.has(step))
                def _(side=side, step=step):
                    push(
                        source, here, tag_z_send.at[dz + 3, side], tag_z.at[dz + 3 - step],
                        spot.device(step),
                    )

        push(source, here, tag_y_send.at[dz + 3], tag_y.at[dz + 3], spot.device(0, 1))

    def take_tag(dz):
        def action():
            arrive(tag_place(dz, 0), tag_z.at[dz + 3])
            spread_tag(dz)

        when_has(spot, dz, action)

    def take_tag_y(dz):
        when_has(spot, dz, lambda: arrive(tag_place(dz, 1), tag_y.at[dz + 3]))

    spread_tag(0)
    gather = Gather(spot, hidden.at[own, :], rows_all, *gather_sems[:7], full=hidden)
    gather.start()
    late = Gather(spot, cotangent.at[own, :], grad_y_all, *gather_sems[7:], full=cotangent)
    tag_copy.wait()
    gather.local.wait()
    for copy in weights:
        copy.wait()

    def group_of(step):
        far, dy = near_first(step // 2, spot.z), step % 2
        return far, dy, far * 2 + spot.y + dy * (1 - 2 * spot.y)

    def stage_copy(step):
        _, _, index = group_of(step)
        return pltpu.make_async_copy(
            staged.at[step % 2],
            normed_all.at[pl.ds(pl.multiple_of(index * block, block), block), :],
            stage_sem.at[step % 2],
        )

    experts_count = chosen.shape[0]
    names = lax.broadcasted_iota(jnp.int32, (experts_count, block), 0)
    lanes = lax.broadcasted_iota(jnp.int32, (block, dim), 1)

    def project_group(step):
        _, _, index = group_of(step)
        here = pl.ds(pl.multiple_of(index * block, block), block)
        entries = tags[index]
        place = entries[0:1, :]
        segment, opening, bound = jnp.zeros_like(place), jnp.zeros_like(place), 0
        for at in range(lengths.shape[0]):
            bound = bound + lengths[at]
            segment = segment + jnp.where(place >= bound, 1, 0)
            opening = jnp.where(place >= bound, bound, opening)
        place_row[:, here] = place.astype(F32)
        open_row[:, here] = opening.astype(F32)
        lines = jnp.concatenate(
            [place.astype(F32), (place - opening).astype(F32), entries[1:2, :].astype(F32),
             jnp.zeros((5, block), F32)],
            axis=0,
        ).T
        place_column[here, :] = lines[:, 0:1]
        ranks[here, :] = lines[:, 2:3]
        named = jnp.zeros((experts_count, block), F32)
        for at in range(2, 2 + TOPK):
            named = jnp.where(entries[at : at + 1, :] == names, 1.0, named)
        chosen[:, here] = named
        valid = segment < lengths.shape[0]
        picks[:, here] = jnp.where(valid, named, 0.0).astype(BF16)
        table = cosine_sine(lines[:, 1:2] * inverse[...])
        turned_table = pltpu.roll(table, dim // 2, 1)
        cos = jnp.where(lanes < dim // 2, table, turned_table)
        sin = jnp.where(lanes < dim // 2, -turned_table, table)
        cosine[here, :] = cos
        sine[here, :] = sin
        rows = rows_all[here, :].astype(F32)
        root = lax.rsqrt(jnp.mean(rows * rows, axis=-1, keepdims=True) + EPS)

        @pl.when(step >= 2)
        def _():
            stage_copy(step - 2).wait()

        staged[step % 2] = (rows * root * gain[...]).astype(BF16)
        stage_copy(step).start()
        lin = mxu(staged[step % 2], weight[...])
        lin_out[here, :] = lin[:, : 2 * dim]
        values[here, :] = lin[:, 2 * dim :].astype(BF16)
        for at, head_gain, scale, out in (
            (0, q_gain, dim**-0.5, queries), (dim, k_gain, 1.0, keys),
        ):
            plain, _ = head_norm(lin[:, at : at + dim])
            plain = plain * head_gain[...]
            out[here, :] = ((plain * cos + pltpu.roll(plain, dim // 2, 1) * sin) * scale).astype(
                BF16
            )

    def both_ways(take, distance):
        for dz in (distance, -distance) if distance else (0,):
            take(dz)

    def run(plans, step):
        for at, plan in plans.items():

            @pl.when(step == at)
            def _(plan=plan):
                plan()

    plans = {
        0: lambda: (both_ways(gather.take_yx, 0), both_ways(take_tag, 1),
                    both_ways(gather.take_z, 1)),
        1: lambda: (both_ways(take_tag_y, 0), both_ways(gather.take_diagonal, 0),
                    both_ways(take_tag, 2), both_ways(gather.take_z, 2),
                    both_ways(gather.take_late, 0)),
        2: lambda: (both_ways(gather.take_yx, 1), both_ways(take_tag, 3),
                    both_ways(gather.take_z, 3), both_ways(gather.take_late, 1)),
        3: lambda: (both_ways(take_tag_y, 1), both_ways(gather.take_yx, 2),
                    both_ways(gather.take_diagonal, 1), both_ways(gather.take_late, 2)),
        4: lambda: (both_ways(gather.take_yx, 3), late.start()),
        5: lambda: (both_ways(take_tag_y, 2), both_ways(gather.take_diagonal, 2),
                    both_ways(gather.take_late, 3)),
        7: lambda: (both_ways(take_tag_y, 3), both_ways(gather.take_diagonal, 3)),
    }

    @pl.loop(0, 8)
    def _(step):
        run(plans, step)
        far, dy, _ = group_of(step)

        @pl.when(step > 0)
        def _():
            for dx in (0, 1):
                gather.take_core(far, dy, dx)

        project_group(step)

    mine = att_rows.at[:, pl.ds(pl.multiple_of(group * dim, dim), dim)]

    def block_copy(step):
        target = (group + step) % 8
        return pltpu.make_async_remote_copy(
            src_ref=attended.at[pl.ds(pl.multiple_of(target * block, block), block), :],
            dst_ref=mine,
            send_sem=send_sem.at[step],
            recv_sem=recv_sem.at[step],
            device_id=(target, part),
            device_id_type=MESH,
        )

    def attend_block(step):
        here = pl.ds(pl.multiple_of((group + step) % 8 * block, block), block)
        scores = mxu(keys[...], queries[here, :], 1, 1)
        seen = (place_column[...] <= place_row[:, here]) & (place_column[...] >= open_row[:, here])
        scores = jnp.where(seen, scores, NEG)
        highest = jnp.max(scores, axis=0, keepdims=True)
        exps = jnp.exp(scores - highest)
        totals = jnp.sum(exps, axis=0, keepdims=True)
        probability = (exps * (1.0 / totals)).astype(BF16)
        attended[here, :] = mxu(values[...], probability, 0, 0).T.astype(BF16)
        log_total[:, here] = highest + jnp.log(totals)

    late_plans = {
        1: lambda: (both_ways(late.take_yx, 0), both_ways(late.take_z, 1)),
        3: lambda: (both_ways(late.take_z, 2), both_ways(late.take_diagonal, 0),
                    both_ways(late.take_late, 0)),
        5: lambda: (both_ways(late.take_yx, 1), both_ways(late.take_z, 3)),
        7: lambda: (both_ways(late.take_late, 1), both_ways(late.take_yx, 2),
                    both_ways(late.take_diagonal, 1)),
    }

    @pl.loop(1, 8)
    def _(step):
        run(late_plans, step)
        attend_block(step)
        block_copy(step).start()

    attend_block(0)
    own_copy = pltpu.make_async_copy(
        attended.at[pl.ds(pl.multiple_of(group * block, block), block), :], mine, own_sem
    )
    own_copy.start()
    both_ways(late.take_yx, 3)
    both_ways(late.take_late, 2)

    kept[...] = jnp.zeros_like(kept)

    @pl.loop(0, total // block)
    def _(step):
        here = pl.ds(pl.multiple_of(step * block, block), block)
        for at in range(0, total // block):
            columns = pl.ds(at * block, block)
            lower = jnp.where(
                ranks[here, :] < tags[at, 1:2, :].astype(F32), 1.0, 0.0
            ).astype(BF16)
            kept[:, columns] += mxu(picks[:, here], lower)

    kept[...] = jnp.where((picks[...].astype(F32) > 0.0) & (kept[...] < CAP), 1.0, 0.0)

    both_ways(late.take_diagonal, 2)
    both_ways(late.take_late, 3)

    @pl.loop(1, 8)
    def _(step):
        block_copy(step).wait_send()
        source = (group + 8 - step) % 8
        there = att_rows.at[:, pl.ds(pl.multiple_of(source * dim, dim), dim)]
        arrive(there, recv_sem.at[step])

    own_copy.wait()

    @pl.loop(0, width // 256)
    def _(step):
        columns = pl.ds(pl.multiple_of(step * 256, 256), 256)
        partial_sum[:, columns] = mxu(att_rows[...], out_weight[:, columns]).astype(BF16)

    def rows_of(dx, dc):
        _, there = spot.device(0, 0, dx, dc)
        return partial_sum.at[pl.ds(pl.multiple_of(there * count, count), count), :]

    to_x, to_c = spot.device(0, 0, 1), spot.device(0, 0, 0, 1)
    for dx in (1, 0):
        push(rows_of(dx, 1), from_core.at[dx], tensor_sems.at[dx], tensor_sems.at[2 + dx], to_c)
    arrive(from_core.at[1], tensor_sems.at[3])
    to_x_sum[...] = (rows_of(1, 0)[...].astype(F32) + from_core[1].astype(F32)).astype(BF16)
    push(to_x_sum, from_x, tensor_sems.at[4], tensor_sems.at[5], to_x)
    both_ways(late.take_diagonal, 3)
    arrive(from_core.at[0], tensor_sems.at[2])
    arrive(from_x, tensor_sems.at[5])
    branch = rows_of(0, 0)[...].astype(F32) + from_core[0].astype(F32) + from_x[...].astype(F32)
    sum_rows = hidden[own, :].astype(F32) + branch
    residual[...] = sum_rows
    root = lax.rsqrt(jnp.mean(sum_rows * sum_rows, axis=-1, keepdims=True) + EPS)
    normed[...] = (sum_rows * root * second_gain[...]).astype(BF16)
    for at, view in ((0, from_core.at[0]), (1, from_core.at[1]), (4, from_x)):
        arrive(view, tensor_sems.at[at])
    for step in (6, 7):
        stage_copy(step).wait()
    gather.drain()
    late.local.wait()
    for far in range(4):
        for dx in (0, 1):
            late.take_core(far, 1, dx)

            @pl.when(spot.z != far)
            def _(far=far, dx=dx):
                late.take_core(far, 0, dx)

    late.drain()
    for dz in range(-3, 4):

        def action(dz=dz):
            arrive(tag_place(dz, 0), tag_y_send.at[dz + 3])
            for side, step in ((0, 1), (1, -1)):
                if dz * step <= 0:

                    @pl.when(spot.has(step))
                    def _(side=side):
                        arrive(tag_place(dz, 0), tag_z_send.at[dz + 3, side])

        when_has(spot, dz, action)


def front(
    hidden, cotangent, tag, lengths, gain, w_query, w_key, w_value, q_gain, k_gain, inverse,
    w_out, second_gain, expert_count,
):
    block, width = hidden.shape
    total, count, dim = 8 * block, block // 4, w_key.shape[1]
    shape, vmem = jax.ShapeDtypeStruct, pltpu.VMEM
    smem = pl.BlockSpec(memory_space=pltpu.SMEM)
    small = (total, dim)
    return pl.pallas_call(
        front_kernel,
        out_shape=(
            shape((total, width), BF16), shape(small, BF16), shape(small, BF16),
            shape(small, BF16), shape((total, 2 * dim), F32), shape(small, F32),
            shape(small, F32), shape(small, BF16), shape((1, total), F32),
            shape((1, total), F32), shape((1, total), F32), shape((total, 1), F32),
            shape((count, width), F32), shape((count, width), BF16),
            shape((expert_count, total), F32), shape((expert_count, total), F32),
            shape((total, width), BF16),
        ),
        in_specs=[VMEM_SPEC, VMEM_SPEC, VMEM_SPEC, smem, VMEM_SPEC, HBM_SPEC, HBM_SPEC, HBM_SPEC,
                  VMEM_SPEC, VMEM_SPEC, VMEM_SPEC, HBM_SPEC, VMEM_SPEC],
        out_specs=(HBM_SPEC,) + (VMEM_SPEC,) * 15 + (HBM_SPEC,),
        scratch_shapes=[
            vmem((total, width), BF16), vmem((width, 3 * dim), BF16), vmem((8 * dim, width), BF16),
            vmem((2, block, width), BF16), vmem((8, 16, block), jnp.int32), vmem((total, 1), F32),
            vmem((expert_count, total), BF16), vmem((block, 8 * dim), BF16),
            vmem((block, width), BF16), vmem((2, count, width), BF16), vmem((count, width), BF16),
            vmem((count, width), BF16),
        ]
        + dma_sems(
            ((4,), (2,), (7,), (7,), (7, 2), (7,), None, (8,), (8,), None, (6,)) + Gather.SEMS * 2
        ),
        compiler_params=pltpu.CompilerParams(
            collective_id=1, has_side_effects=True, vmem_limit_bytes=62 << 20
        ),
        name="front",
        cost_estimate=cost(8_000_000_000, 90),
    )(
        hidden, cotangent, tag, lengths, gain, w_query, w_key, w_value, q_gain, k_gain, inverse,
        w_out, second_gain,
    )


def settle_kernel(*refs):
    half = len(refs) // 2
    sems = refs[-1]
    copies = [
        pltpu.make_async_copy(refs[at], refs[half + at], sems.at[at]) for at in range(half)
    ]
    for copy in copies:
        copy.start()
    for copy in copies:
        copy.wait()


def settle(*arrays):
    return pl.pallas_call(
        settle_kernel,
        out_shape=tuple(jax.ShapeDtypeStruct(v.shape, v.dtype) for v in arrays),
        in_specs=[HBM_SPEC] * len(arrays),
        out_specs=(HBM_SPEC,) * len(arrays),
        scratch_shapes=dma_sems(((len(arrays),),)),
        cost_estimate=cost(0, 6),
        name="settle",
    )(*arrays)


def swap(value, bits):
    return lax.ppermute(
        value, ("expert", "tensor"), [(device, device ^ bits) for device in range(32)]
    )


def pair_sums(own, first, second, third):
    own, first, second, third = (v.astype(jnp.float32) for v in (own, first, second, third))
    return (own + first) + (second + third)


def in_order(rows, by_core, by_x, by_both):
    part = lax.axis_index("tensor")

    def ordered(first, second, bit):
        swapped = part // bit % 2 == 1
        return jnp.concatenate(
            [jnp.where(swapped, second, first), jnp.where(swapped, first, second)], axis=0
        )

    return ordered(ordered(rows, by_core, 1), ordered(by_x, by_both, 1), 2)


def head_device(
    hidden_in,
    cotangent,
    layout,
    seq_lengths,
    expert_ids,
    drop_rank,
    norm1_gain,
    w_query,
    key_weight,
    value_weight,
    query_gain,
    key_gain,
    w_out,
    norm2_gain,
    w_router,
    w_gate,
    w_up,
    w_down,
):
    f32, bf16 = jnp.float32, jnp.bfloat16
    tok_rows, model_width = hidden_in.shape
    head_dim = query_gain.shape[0]
    expert_count = w_router.shape[1]
    local_count, _, ff_local = w_gate.shape
    groups = lax.axis_size("expert")
    tensor_size = lax.axis_size("tensor")
    total_rows = groups * tok_rows
    own_rows = tok_rows // tensor_size
    group = lax.axis_index("expert")
    part = lax.axis_index("tensor")

    def own(rows):
        return lax.dynamic_slice_in_dim(rows, part * own_rows, own_rows, 0)

    tag = jnp.concatenate(
        [layout[None], drop_rank[None], expert_ids.T, jnp.zeros((6, tok_rows), jnp.int32)], axis=0
    )
    half_dim = head_dim // 2
    inverse = THETA ** (-(jnp.arange(half_dim, dtype=f32) * 2.0) / head_dim)
    q_gain, k_gain = query_gain[None], key_gain[None]
    (
        normed1, queries, keys, values, lin, cosine, sine, attended, log_total,
        place_row, open_row, place_column, residual, normed2, chosen, kept, grad_y_all,
    ) = front(
        hidden_in, cotangent, tag, seq_lengths, norm1_gain[None], w_query, key_weight,
        value_weight, q_gain, k_gain, jnp.concatenate([inverse, inverse])[None], w_out,
        norm2_gain[None], expert_count,
    )
    turn = lambda v: jnp.transpose(v, (0, 2, 1))
    back, grad_gate, grad_up, grad_down = experts(
        normed2, grad_y_all, turn(w_gate), turn(w_up), w_down.reshape(-1, model_width),
        w_router.T, chosen, kept,
    )
    out_own = (residual + back[:, :model_width]).astype(bf16)
    back = back[:, model_width:]

    start = group * tok_rows + part * own_rows
    chosen_own = lax.dynamic_slice_in_dim(chosen, start, own_rows, 1).T
    logits = jnp.dot(normed2, w_router, preferred_element_type=f32)
    soft_own = jax.nn.softmax(jnp.where(chosen_own > 0.0, logits, -jnp.inf), axis=1)
    grad_soft = back[:, model_width : model_width + expert_count]
    grad_logits = (
        soft_own * (grad_soft - jnp.sum(soft_own * grad_soft, axis=1, keepdims=True))
    ).astype(bf16)
    grad_router = jnp.einsum("td,te->de", normed2, grad_logits, preferred_element_type=f32)
    grad_normed2 = back[:, :model_width] + jnp.einsum(
        "te,de->td", grad_logits, w_router, preferred_element_type=f32
    )
    norm2_pull = jax.vjp(norm_rows, residual, norm2_gain)[1]
    grad_resid_norm, grad_norm2 = norm2_pull(grad_normed2)
    grad_residual = own(cotangent).astype(f32) + grad_resid_norm
    small = jnp.concatenate([grad_router.T, grad_norm2[None]], axis=0).astype(bf16)
    z_parts = [swap(small, 8 * step) for step in (1, 2, 3)]

    grad_lin, grad_out, grad_qgain, grad_kgain = attend_back(
        grad_residual.astype(bf16), w_out, queries, keys, values, attended, lin, cosine, sine,
        place_column, place_row, open_row, log_total, k_gain, q_gain,
    )
    small = pair_sums(small, *z_parts).astype(bf16)
    grad_lin, small, out_own = lax.optimization_barrier((grad_lin, small, out_own))
    yx_parts = [swap(small, 2 * step) for step in (1, 2, 3)]
    out_by_x, out_by_core = swap(out_own, 2), swap(out_own, 1)
    gains = jnp.concatenate(
        [grad_qgain, grad_kgain, jnp.zeros((1, model_width - 2 * head_dim), f32)], axis=1
    )
    reduced, grad_kv, grad_query, grad_out = close(
        normed1, grad_lin, w_query, key_weight, value_weight, grad_out
    )
    reduced, yx_parts, out_by_x = lax.optimization_barrier((reduced, yx_parts, out_by_x))
    small = pair_sums(small, *yx_parts)
    norm1_pull = jax.vjp(norm_rows, own(hidden_in).astype(f32), norm1_gain)[1]
    grad_hidden_norm, grad_norm1 = norm1_pull(reduced)
    late_sums = jnp.concatenate([grad_norm1[None], gains], axis=0)
    hidden_rows = (grad_residual + grad_hidden_norm).astype(bf16)
    grad_query, hidden_rows, late_sums = lax.optimization_barrier(
        (grad_query, hidden_rows, late_sums)
    )
    by_x, by_core = swap(hidden_rows, 2), swap(hidden_rows, 1)
    moved = [swap(late_sums, 8 * step) for step in (1, 2, 3)]
    out_by_both = swap(out_by_x, 1)
    grad_query = grad_query.astype(f32)
    grad_query, grad_out, moved = lax.optimization_barrier((grad_query, grad_out, moved))
    late_sums = pair_sums(late_sums, *moved)
    moved = [swap(late_sums, 2 * step) for step in (1, 2, 3)]
    grad_out, grad_kv = grad_out.astype(f32), grad_kv.astype(f32)
    out_hidden = in_order(out_own, out_by_core, out_by_x, out_by_both)
    grads = (grad_gate, grad_up, grad_down)
    grad_out, grad_kv, out_hidden, by_x, moved, grads = lax.optimization_barrier(
        (grad_out, grad_kv, out_hidden, by_x, moved, grads)
    )
    small = jnp.concatenate([small, pair_sums(late_sums, *moved)], axis=0)
    moved, by_both = swap(small, 1), swap(by_x, 1)
    grads = settle(*grads)
    grads, moved, by_both = lax.optimization_barrier((grads, moved, by_both))
    grad_gate, grad_up, grad_down = grads
    small = small + moved
    grad_hidden = in_order(hidden_rows, by_core, by_x, by_both)
    grad_norm1 = small[expert_count + 1]
    grad_router, grad_norm2 = small[:expert_count].T, small[expert_count]
    grad_qgain, grad_kgain = jnp.split(small[expert_count + 2, : 2 * head_dim], 2)
    grad_down = grad_down.reshape(local_count, ff_local, model_width)
    return (
        out_hidden,
        grad_hidden,
        grad_norm1,
        grad_query,
        grad_kv[:, :head_dim],
        grad_kv[:, head_dim:],
        grad_qgain,
        grad_kgain,
        grad_out,
        grad_norm2,
        grad_router,
        turn(grad_gate),
        turn(grad_up),
        grad_down,
    )


def solution(mesh):
    groups = mesh.shape["expert"]

    def device_fn(*operands):
        heads = operands[7].shape[1] // operands[10].shape[0]
        one_head = heads == groups == 8 and operands[8].shape[1] == operands[10].shape[0]
        one_head = one_head and mesh.shape["tensor"] == 4
        return (head_device if one_head else per_device)(*operands)

    return jax.shard_map(
        device_fn,
        mesh=mesh,
        in_specs=(
            P("expert", None),
            P("expert", None),
            P("expert"),
            P(),
            P("expert", None),
            P("expert"),
            P(),
            P(None, "tensor"),
            P(None, "tensor"),
            P(None, "tensor"),
            P(),
            P(),
            P("tensor", None),
            P(),
            P(),
            P("expert", None, "tensor"),
            P("expert", None, "tensor"),
            P("expert", "tensor", None),
        ),
        out_specs=(
            P("expert", None),
            P("expert", None),
            P(),
            P(None, "tensor"),
            P(None, "tensor"),
            P(None, "tensor"),
            P(),
            P(),
            P("tensor", None),
            P(),
            P(),
            P("expert", None, "tensor"),
            P("expert", None, "tensor"),
            P("expert", "tensor", None),
        ),
        check_vma=False,
    )
```

```python
from functools import partial
import math

import jax
import jax.numpy as jnp
from jax import lax
from jax.experimental import pallas as pl
from jax.experimental.pallas import tpu as pltpu
from jax.sharding import PartitionSpec as P

TOPK = 8
CAP = 1280


EPS = 1e-06
THETA = 1000000.0
NEG = -1e30


def norm_rows(value_matrix, gain):
    return (
        value_matrix
        * lax.rsqrt(jnp.mean(value_matrix * value_matrix, axis=-1, keepdims=True) + EPS)
        * gain
    )


def rotary(value_matrix, position):
    half_dim = value_matrix.shape[-1] // 2
    inverse = THETA ** (-(jnp.arange(half_dim, dtype=jnp.float32) * 2.0) / value_matrix.shape[-1])
    angles = position.astype(jnp.float32)[:, None] * inverse[None, :]
    cosine_table = jnp.concatenate([jnp.cos(angles), jnp.cos(angles)], axis=-1)[:, None, :]
    sine_table = jnp.concatenate([jnp.sin(angles), jnp.sin(angles)], axis=-1)[:, None, :]
    turned = jnp.concatenate([-value_matrix[..., half_dim:], value_matrix[..., :half_dim]], axis=-1)
    return value_matrix * cosine_table + turned * sine_table


def shape_queries(linear, gain, position):
    head_dim = gain.shape[0]
    shaped = linear.reshape(linear.shape[0], linear.shape[1] // head_dim, head_dim)
    return rotary(norm_rows(shaped, gain), position) * head_dim ** (-0.5)


def shape_keys(linear, gain, position):
    head_dim = gain.shape[0]
    shaped = linear.reshape(linear.shape[0], linear.shape[1] // head_dim, head_dim)
    return rotary(norm_rows(shaped, gain), position)


def token_tables(token_position, seq_lengths):
    bounds = jnp.cumsum(seq_lengths)
    passed = token_position[:, None] >= bounds[None, :]
    segment_ids = jnp.sum(passed.astype(jnp.int32), axis=1)
    opening = jnp.max(jnp.where(passed, bounds[None, :], 0), axis=1)
    return (segment_ids, (token_position - opening).astype(jnp.int32))


def visible(query_segment, query_place, key_segment, key_place):
    return (query_segment[:, None] == key_segment[None, :]) & (
        key_place[None, :] <= query_place[:, None]
    )


def deliver(payload, slot_ids):
    return (
        lax.all_to_all(payload, "expert", split_axis=0, concat_axis=0, tiled=True),
        lax.all_to_all(slot_ids, "expert", split_axis=0, concat_axis=0, tiled=True),
    )


def bring_back(payload):
    return lax.all_to_all(payload, "expert", split_axis=0, concat_axis=0, tiled=True)


def expert_forward(entry_rows, w_gate, w_up, w_down):
    gate_lin = jnp.einsum("gesd,edf->gesf", entry_rows, w_gate, preferred_element_type=jnp.float32)
    up_lin = jnp.einsum("gesd,edf->gesf", entry_rows, w_up, preferred_element_type=jnp.float32)
    activation = (jax.nn.silu(gate_lin) * up_lin).astype(jnp.bfloat16)
    expert_out = jnp.einsum(
        "gesf,efd->gesd", activation, w_down, preferred_element_type=jnp.float32
    ).astype(jnp.bfloat16)
    return (gate_lin, up_lin, activation, expert_out)


def expert_backward(entry_rows, gate_lin, up_lin, activation, grad_in, w_gate, w_up, w_down):
    grad_down = jnp.einsum(
        "gesf,gesd->efd", activation, grad_in, preferred_element_type=jnp.float32
    )
    grad_act = jnp.einsum("gesd,efd->gesf", grad_in, w_down, preferred_element_type=jnp.float32)
    sigmoid = jax.nn.sigmoid(gate_lin)
    grad_gate_lin = (grad_act * up_lin * sigmoid * (1.0 + gate_lin * (1.0 - sigmoid))).astype(
        jnp.bfloat16
    )
    grad_up_lin = (grad_act * gate_lin * sigmoid).astype(jnp.bfloat16)
    grad_w_gate = jnp.einsum(
        "gesd,gesf->edf", entry_rows, grad_gate_lin, preferred_element_type=jnp.float32
    )
    grad_w_up = jnp.einsum(
        "gesd,gesf->edf", entry_rows, grad_up_lin, preferred_element_type=jnp.float32
    )
    grad_entry = jnp.einsum(
        "gesf,edf->gesd", grad_gate_lin, w_gate, preferred_element_type=jnp.float32
    )
    grad_entry = (
        grad_entry
        + jnp.einsum("gesf,edf->gesd", grad_up_lin, w_up, preferred_element_type=jnp.float32)
    ).astype(jnp.bfloat16)
    return (grad_entry, grad_w_gate, grad_w_up, grad_down)


def per_device(
    hidden_in,
    cotangent,
    layout,
    seq_lengths,
    expert_ids,
    drop_rank,
    norm1_gain,
    w_query,
    key_weight,
    value_weight,
    query_gain,
    key_gain,
    w_out,
    norm2_gain,
    w_router,
    w_gate,
    w_up,
    w_down,
):
    tok_rows = hidden_in.shape[0]
    model_width = hidden_in.shape[1]
    head_dim = query_gain.shape[0]
    local_heads = w_query.shape[1] // head_dim
    expert_count = w_router.shape[1]
    local_count = w_gate.shape[0]
    group_count = lax.axis_size("expert")
    slot_count = 2 * tok_rows * TOPK // expert_count
    seq_count = seq_lengths.shape[0]
    expert_range = jnp.arange(expert_count, dtype=jnp.int32)
    hidden = hidden_in.astype(jnp.float32)
    segment_ids, position = token_tables(layout, seq_lengths)
    valid = segment_ids < seq_count
    first_normalized = norm_rows(hidden, norm1_gain)
    normed1_low = first_normalized.astype(jnp.bfloat16)
    query_lin = jnp.dot(normed1_low, w_query, preferred_element_type=jnp.float32)
    key_lin = jnp.dot(normed1_low, key_weight, preferred_element_type=jnp.float32)
    value_lin = jnp.dot(normed1_low, value_weight, preferred_element_type=jnp.float32)
    query_shaped = shape_queries(query_lin, query_gain, position).astype(jnp.bfloat16)
    query_total = local_heads * tok_rows
    query_rows = jnp.transpose(query_shaped, (1, 0, 2)).reshape(query_total, head_dim)
    key_rows = (
        shape_keys(key_lin, key_gain, position).astype(jnp.bfloat16).reshape(tok_rows, head_dim)
    )
    value_rows = value_lin.astype(jnp.bfloat16)
    all_keys, all_values, all_place, all_ids, all_rank = (
        lax.all_gather(key_rows, "expert", axis=0, tiled=True),
        lax.all_gather(value_rows, "expert", axis=0, tiled=True),
        lax.all_gather(layout, "expert", axis=0, tiled=True),
        lax.all_gather(expert_ids, "expert", axis=0, tiled=True),
        lax.all_gather(drop_rank, "expert", axis=0, tiled=True),
    )
    all_segment = token_tables(all_place, seq_lengths)[0]
    rows_per_block = math.gcd(512, query_total)
    count_of_blocks = query_total // rows_per_block
    query_segment = jnp.tile(segment_ids, local_heads)
    query_place = jnp.tile(layout, local_heads)

    def attend_block(operands):
        query_block, segment_block, place_block = operands
        scores = jnp.einsum("qd,kd->qk", query_block, all_keys, preferred_element_type=jnp.float32)
        scores = jnp.where(visible(segment_block, place_block, all_segment, all_place), scores, NEG)
        highest = jnp.max(scores, axis=1, keepdims=True)
        weights = jnp.exp(scores - highest)
        totals = jnp.sum(weights, axis=1, keepdims=True)
        probability = (weights / totals).astype(jnp.bfloat16)
        mixed_out = jnp.dot(probability, all_values, preferred_element_type=jnp.float32)
        return (mixed_out, (highest + jnp.log(totals))[:, 0])

    attention_output, log_totals = lax.map(
        attend_block,
        (
            query_rows.reshape(count_of_blocks, rows_per_block, head_dim),
            query_segment.reshape(count_of_blocks, rows_per_block),
            query_place.reshape(count_of_blocks, rows_per_block),
        ),
    )
    attention_output = attention_output.reshape(local_heads, tok_rows, head_dim).astype(
        jnp.bfloat16
    )
    att_cat = jnp.transpose(attention_output, (1, 0, 2)).reshape(tok_rows, local_heads * head_dim)
    branch_part = jnp.dot(att_cat, w_out, preferred_element_type=jnp.float32)
    branch = lax.psum(branch_part, "tensor")
    residual = hidden + branch
    normed2 = norm_rows(residual, norm2_gain)
    normed2_low = normed2.astype(jnp.bfloat16)
    logits = jnp.dot(normed2_low, w_router, preferred_element_type=jnp.float32)
    soft_gate = jax.nn.softmax(jnp.take_along_axis(logits, expert_ids, axis=1), axis=1)
    picks = jnp.any(expert_ids[:, :, None] == expert_range, axis=1) & valid[:, None]
    all_valid = all_segment < seq_count
    all_picks = jnp.any(all_ids[:, :, None] == expert_range, axis=1) & all_valid[:, None]
    earlier = (all_rank[None, :] < drop_rank[:, None]).astype(jnp.bfloat16)
    before_counts = jnp.dot(
        earlier, all_picks.astype(jnp.bfloat16), preferred_element_type=jnp.float32
    )
    global_slot = jnp.take_along_axis(before_counts, expert_ids, axis=1).astype(jnp.int32)
    kept_mask = (global_slot < CAP) & valid[:, None]
    gate_weight = soft_gate * kept_mask.astype(jnp.float32)
    lower_rows = (jnp.arange(tok_rows)[None, :] < jnp.arange(tok_rows)[:, None]).astype(
        jnp.bfloat16
    )
    local_counts = jnp.dot(
        lower_rows, picks.astype(jnp.bfloat16), preferred_element_type=jnp.float32
    )
    local_slot = jnp.take_along_axis(local_counts, expert_ids, axis=1).astype(jnp.int32)
    pair_count = tok_rows * TOPK
    dump_index = expert_count * slot_count
    target = jnp.where(kept_mask, expert_ids * slot_count + local_slot, dump_index)
    pair_index = jnp.arange(pair_count, dtype=jnp.int32)
    slot_pair = (
        jnp.full((dump_index,), pair_count, jnp.int32)
        .at[target.reshape(-1)]
        .set(pair_index, mode="drop")
    )
    slot_token = jnp.where(slot_pair < pair_count, slot_pair // TOPK, tok_rows)
    slot_global = (
        jnp.full((dump_index,), -1, jnp.int32)
        .at[target.reshape(-1)]
        .set(global_slot.reshape(-1), mode="drop")
    )
    padded_rows = jnp.concatenate([normed2_low, jnp.zeros((1, model_width), jnp.bfloat16)], axis=0)
    send_rows = padded_rows[slot_token].reshape(group_count, local_count, slot_count, model_width)
    send_slot = slot_global.reshape(group_count, local_count, slot_count)
    received, received_slot = deliver(send_rows, send_slot)
    gate_lin, up_lin, activation, expert_out = expert_forward(received, w_gate, w_up, w_down)
    returned = bring_back(expert_out)
    returned_flat = jnp.concatenate(
        [returned.reshape(dump_index, model_width), jnp.zeros((1, model_width), returned.dtype)],
        axis=0,
    )
    pair_out = returned_flat[target]
    moe_part = jnp.sum(gate_weight[:, :, None] * pair_out, axis=1)
    moe_branch = lax.psum(moe_part.astype(jnp.bfloat16), "tensor").astype(jnp.float32)
    out_hidden = (residual + moe_branch).astype(jnp.bfloat16)
    grad_y = cotangent.astype(jnp.float32)
    gate_dot = jnp.sum(grad_y[:, None, :] * pair_out, axis=2)
    pair_grads = (
        (gate_weight[:, :, None] * grad_y[:, None, :])
        .astype(jnp.bfloat16)
        .reshape(pair_count, model_width)
    )
    pair_grads = jnp.concatenate([pair_grads, jnp.zeros((1, model_width), jnp.bfloat16)], axis=0)
    send_grad = pair_grads[slot_pair].reshape(group_count, local_count, slot_count, model_width)
    grad_received, grad_slot = deliver(send_grad, send_slot)
    grad_entry, grad_w_gate, grad_w_up, grad_w_down = expert_backward(
        received, gate_lin, up_lin, activation, grad_received, w_gate, w_up, w_down
    )
    grad_returned = bring_back(grad_entry)
    grad_flat = jnp.concatenate(
        [
            grad_returned.reshape(dump_index, model_width),
            jnp.zeros((1, model_width), grad_returned.dtype),
        ],
        axis=0,
    )
    grad_normed2_part = jnp.sum(grad_flat[target], axis=1, dtype=jnp.float32)
    grad_normed2_exp, gate_dot = lax.psum((grad_normed2_part, gate_dot), "tensor")
    grad_soft = gate_dot * kept_mask.astype(jnp.float32)
    grad_chosen = soft_gate * (grad_soft - jnp.sum(soft_gate * grad_soft, axis=1, keepdims=True))
    grad_logits = jnp.sum(
        grad_chosen[:, :, None] * (expert_ids[:, :, None] == expert_range).astype(jnp.float32),
        axis=1,
    ).astype(jnp.bfloat16)
    grad_w_router = jnp.einsum(
        "td,te->de", normed2_low, grad_logits, preferred_element_type=jnp.float32
    )
    grad_normed2 = grad_normed2_exp + jnp.einsum(
        "te,de->td", grad_logits, w_router, preferred_element_type=jnp.float32
    )
    norm2_pull = jax.vjp(norm_rows, residual, norm2_gain)[1]
    grad_resid_norm, grad_norm2 = norm2_pull(grad_normed2)
    grad_residual = grad_y + grad_resid_norm
    grad_residual_low = grad_residual.astype(jnp.bfloat16)
    grad_w_out = jnp.einsum(
        "tc,td->cd", att_cat, grad_residual_low, preferred_element_type=jnp.float32
    )
    grad_att_cat = jnp.einsum(
        "td,cd->tc", grad_residual_low, w_out, preferred_element_type=jnp.float32
    ).astype(jnp.bfloat16)
    grad_att_rows = jnp.transpose(
        grad_att_cat.reshape(tok_rows, local_heads, head_dim), (1, 0, 2)
    ).reshape(query_total, head_dim)

    def query_grad_block(operands):
        query_block, segment_block, place_block, grad_block, log_block = operands
        scores = jnp.einsum("qd,kd->qk", query_block, all_keys, preferred_element_type=jnp.float32)
        scores = jnp.where(visible(segment_block, place_block, all_segment, all_place), scores, NEG)
        probability = jnp.exp(scores - log_block[:, None])
        grad_prob = jnp.einsum(
            "qd,kd->qk", grad_block, all_values, preferred_element_type=jnp.float32
        )
        delta_row = jnp.sum(probability * grad_prob, axis=1)
        grad_scores = (probability * (grad_prob - delta_row[:, None])).astype(jnp.bfloat16)
        return (jnp.dot(grad_scores, all_keys, preferred_element_type=jnp.float32), delta_row)

    grad_query_rows, deltas = lax.map(
        query_grad_block,
        (
            query_rows.reshape(count_of_blocks, rows_per_block, head_dim),
            query_segment.reshape(count_of_blocks, rows_per_block),
            query_place.reshape(count_of_blocks, rows_per_block),
            grad_att_rows.reshape(count_of_blocks, rows_per_block, head_dim),
            log_totals,
        ),
    )
    log_flat = log_totals.reshape(query_total)
    delta_flat = deltas.reshape(query_total)
    key_block = math.gcd(lax.axis_size("expert") * tok_rows, 2048)

    def one_block(offset):
        key_part = lax.dynamic_slice_in_dim(all_keys, offset, key_block, 0)
        value_part = lax.dynamic_slice_in_dim(all_values, offset, key_block, 0)
        segment_part = lax.dynamic_slice_in_dim(all_segment, offset, key_block, 0)
        place_part = lax.dynamic_slice_in_dim(all_place, offset, key_block, 0)
        scores = jnp.einsum("qd,kd->qk", query_rows, key_part, preferred_element_type=jnp.float32)
        scores = jnp.where(
            visible(query_segment, query_place, segment_part, place_part), scores, NEG
        )
        probability = jnp.exp(scores - log_flat[:, None])
        grad_value = jnp.einsum(
            "qk,qd->kd",
            probability.astype(jnp.bfloat16),
            grad_att_rows,
            preferred_element_type=jnp.float32,
        )
        grad_prob = jnp.einsum(
            "qd,kd->qk", grad_att_rows, value_part, preferred_element_type=jnp.float32
        )
        grad_scores = (probability * (grad_prob - delta_flat[:, None])).astype(jnp.bfloat16)
        grad_key = jnp.einsum(
            "qk,qd->kd", grad_scores, query_rows, preferred_element_type=jnp.float32
        )
        return jnp.concatenate([grad_key, grad_value], axis=1)

    stacked = lax.map(
        one_block,
        jnp.arange(lax.axis_size("expert") * tok_rows // key_block, dtype=jnp.int32) * key_block,
    )
    key_value_grad = lax.psum_scatter(
        stacked.reshape(lax.axis_size("expert") * tok_rows, 2 * head_dim).astype(jnp.bfloat16),
        "expert",
        scatter_dimension=0,
        tiled=True,
    ).astype(jnp.float32)
    grad_key_post = key_value_grad[:, :head_dim].reshape(tok_rows, 1, head_dim)
    grad_values_low = key_value_grad[:, head_dim:].astype(jnp.bfloat16)
    grad_query_tok = jnp.transpose(
        grad_query_rows.reshape(local_heads, tok_rows, head_dim), (1, 0, 2)
    )
    query_pull = jax.vjp(partial(shape_queries, position=position), query_lin, query_gain)[1]
    grad_query_lin, grad_qgain_part = query_pull(grad_query_tok)
    key_pull = jax.vjp(partial(shape_keys, position=position), key_lin, key_gain)[1]
    grad_key_lin, grad_kgain_part = key_pull(grad_key_post)
    grad_query_low = grad_query_lin.astype(jnp.bfloat16)
    grad_key_low = grad_key_lin.astype(jnp.bfloat16)
    grad_w_query = jnp.einsum(
        "td,tc->dc", normed1_low, grad_query_low, preferred_element_type=jnp.float32
    )
    grad_w_key = jnp.einsum(
        "td,tc->dc", normed1_low, grad_key_low, preferred_element_type=jnp.float32
    )
    grad_w_value = jnp.einsum(
        "td,tc->dc", normed1_low, grad_values_low, preferred_element_type=jnp.float32
    )
    grad_normed1_part = jnp.einsum(
        "tc,dc->td", grad_query_low, w_query, preferred_element_type=jnp.float32
    )
    grad_normed1_part = grad_normed1_part + jnp.einsum(
        "tc,dc->td", grad_key_low, key_weight, preferred_element_type=jnp.float32
    )
    grad_normed1_part = grad_normed1_part + jnp.einsum(
        "tc,dc->td", grad_values_low, value_weight, preferred_element_type=jnp.float32
    )
    grad_normed1, grad_qgain_part, grad_kgain_part = (
        lax.psum(grad_normed1_part.astype(jnp.bfloat16), "tensor").astype(jnp.float32),
        lax.psum(grad_qgain_part.astype(jnp.bfloat16), "tensor").astype(jnp.float32),
        lax.psum(grad_kgain_part.astype(jnp.bfloat16), "tensor").astype(jnp.float32),
    )
    norm1_pull = jax.vjp(norm_rows, hidden, norm1_gain)[1]
    grad_hidden_norm, grad_norm1 = norm1_pull(grad_normed1)
    grad_hidden = (grad_residual + grad_hidden_norm).astype(jnp.bfloat16)
    summed = (
        lax.psum(grad_norm1.astype(jnp.bfloat16), "expert").astype(jnp.float32),
        lax.psum(grad_w_query.astype(jnp.bfloat16), "expert").astype(jnp.float32),
        lax.psum(grad_w_key.astype(jnp.bfloat16), "expert").astype(jnp.float32),
        lax.psum(grad_w_value.astype(jnp.bfloat16), "expert").astype(jnp.float32),
        lax.psum(grad_qgain_part.astype(jnp.bfloat16), "expert").astype(jnp.float32),
        lax.psum(grad_kgain_part.astype(jnp.bfloat16), "expert").astype(jnp.float32),
        lax.psum(grad_w_out.astype(jnp.bfloat16), "expert").astype(jnp.float32),
        lax.psum(grad_norm2.astype(jnp.bfloat16), "expert").astype(jnp.float32),
        lax.psum(grad_w_router.astype(jnp.bfloat16), "expert").astype(jnp.float32),
    )
    return (
        out_hidden,
        grad_hidden,
        summed[0],
        summed[1],
        summed[2],
        summed[3],
        summed[4],
        summed[5],
        summed[6],
        summed[7],
        summed[8],
        grad_w_gate,
        grad_w_up,
        grad_w_down,
    )


MESH = pl.DeviceIdType.MESH
FAR_FIRST = (3, -3, 2, -2, 1, -1, 0)


class Spot:
    def __init__(self):
        group, part = lax.axis_index("expert"), lax.axis_index("tensor")
        self.z, self.y = group // 2, group % 2
        self.x, self.c = part // 2, part % 2

    def has(self, dz):
        return (self.z + dz >= 0) & (self.z + dz <= 3)

    def device(self, dz=0, dy=0, dx=0, dc=0):
        y = 1 - self.y if dy else self.y
        x = 1 - self.x if dx else self.x
        c = 1 - self.c if dc else self.c
        return ((self.z + dz) * 2 + y, x * 2 + c)

    def rows(self, dz, dy, dx, dc, count):
        group, part = self.device(dz, dy, dx, dc)
        return pl.ds(pl.multiple_of((group * 4 + part) * count, count), count)

    def greet(self, line=False):
        barrier = pltpu.get_barrier_semaphore()
        for step in ((0, 1, 0, 0), (0, 0, 1, 0), (0, 0, 0, 1)):
            pl.semaphore_signal(barrier, inc=1, device_id=self.device(*step), device_id_type=MESH)
        for dz in (1, -1, 2, -2, 3, -3) if line else (1, -1):

            @pl.when(self.has(dz))
            def _(dz=dz):
                pl.semaphore_signal(
                    barrier, inc=1, device_id=self.device(dz), device_id_type=MESH
                )

        if line:
            pl.semaphore_wait(barrier, 6)
        else:
            inner = jnp.where((self.z > 0) & (self.z < 3), 1, 0)
            pl.semaphore_wait(barrier, 4 + inner)


def when_has(spot, dz, action):
    if dz == 0:
        action()
    else:
        pl.when(spot.has(dz))(action)


def dma_sems(shapes):
    return [pltpu.SemaphoreType.DMA(shape) if shape else pltpu.SemaphoreType.DMA for shape in shapes]


def add_into(into, chunk, *terms):
    @pl.loop(0, into.shape[0] // chunk)
    def _(step):
        rows = pl.ds(pl.multiple_of(step * chunk, chunk), chunk)
        for at in range(0, into.shape[1], 1024):
            columns = pl.ds(at, min(1024, into.shape[1] - at))
            total = into[rows, columns].astype(jnp.float32)
            for term in terms:
                total = total + term[rows, columns].astype(jnp.float32)
            into[rows, columns] = total.astype(into.dtype)


def push(src, dst, send_sem, recv_sem, device):
    pltpu.make_async_remote_copy(
        src_ref=src,
        dst_ref=dst,
        send_sem=send_sem,
        recv_sem=recv_sem,
        device_id=device,
        device_id_type=MESH,
    ).start()


def arrive(view, sem):
    pltpu.make_async_copy(view, view, sem).wait()


F32, BF16 = jnp.float32, jnp.bfloat16
VMEM_SPEC = pl.BlockSpec(memory_space=pltpu.VMEM)
HBM_SPEC = pl.BlockSpec(memory_space=pl.ANY)


def cost(flops, microseconds):
    return pl.CostEstimate(
        flops=flops, bytes_accessed=microseconds * 3_000_000, transcendentals=0
    )


def mxu(left, right, left_dim=1, right_dim=0):
    return lax.dot_general(
        left, right, (((left_dim,), (right_dim,)), ((), ())), preferred_element_type=F32
    )


def head_norm(lin):
    root = lax.rsqrt(jnp.mean(lin * lin, axis=-1, keepdims=True) + EPS)
    return lin * root, root


def near_first(step, z):
    high = z // 2
    folded = z + high * (3 - 2 * z)
    place = (step + folded * (1 - step // 2)) % 2 + 2 * (step // 2)
    return place + high * (3 - 2 * place)


class Gather:
    SEMS = ((5, 7), (7, 2), (6,), (7, 2, 2), None, (7, 2), (7, 2, 2))

    def __init__(
        self, spot, src, out, recv, z_send, sends, c_recv, local_sem, late_recv, late_send, full=None
    ):
        self.spot, self.src, self.out, self.full = spot, src, out, full
        self.recv, self.z_send, self.sends, self.c_recv = recv, z_send, sends, c_recv
        self.late_recv, self.late_send = late_recv, late_send
        self.count, self.width = src.shape
        width, late = self.width, self.width * 5 // 16
        half = width * 5 // 8 if full is not None else width // 2
        self.first, self.second = pl.ds(0, half), pl.ds(half, width - half)
        self.whole = pl.ds(0, width)
        self.early = (pl.ds(0, width - late), pl.ds(late, width - late))
        self.late = (pl.ds(width - late, late), pl.ds(0, late))
        if full is None:
            self.local = pltpu.make_async_copy(src, self.place(0, 0, 0), local_sem)
        else:
            group, _ = spot.device()
            rows = pl.ds(pl.multiple_of(group * 4 * self.count, 4 * self.count), 4 * self.count)
            self.local = pltpu.make_async_copy(full, out.at[rows, :], local_sem)

    def place(self, dz, dy, dx, dc=0, columns=None):
        rows = self.spot.rows(dz, dy, dx, dc, self.count)
        return self.out.at[rows, self.whole if columns is None else columns]

    def source(self, dz, dy, dx, columns):
        if dz == 0 and dy == 0 and dx == 0:
            return self.src.at[:, columns]
        if dz == 0 and dy == 0 and self.full is not None:
            _, part = self.spot.device(0, 0, 1)
            rows = pl.ds(pl.multiple_of(part * self.count, self.count), self.count)
            return self.full.at[rows, columns]
        return self.place(dz, dy, dx, 0, columns)

    def send(self, dz, dy, dx, columns, send_sem, recv_sem, device):
        push(
            self.source(dz, dy, dx, columns), self.place(dz, dy, dx, 0, columns), send_sem,
            recv_sem, device,
        )

    def to_core(self, dz, dy, dx):
        if dz == 0 and dy == 0 and self.full is not None:
            return
        self.send(
            dz, dy, dx, self.whole, self.sends.at[0], self.c_recv.at[dz + 3, dy, dx],
            self.spot.device(0, 0, 0, 1),
        )

    def along_z(self, dz, dy, dx, columns, send_sem, recv_sem):
        for side, step in ((0, 1), (1, -1)):
            if dz * step <= 0:

                @pl.when(self.spot.has(step))
                def _(side=side, step=step):
                    self.send(
                        dz, dy, dx, columns, send_sem(side), recv_sem(dz + 3 - step),
                        self.spot.device(step),
                    )

    def spread(self, dz):
        spot = self.spot
        self.along_z(
            dz, 0, 0, self.whole, lambda side: self.z_send.at[dz + 3, side],
            lambda at: self.recv.at[0, at],
        )
        if dz == 0:
            columns, at = (self.whole, self.whole), 0
        else:
            columns, at = self.early, 3
        self.send(
            dz, 0, 0, columns[0], self.sends.at[1 + at], self.recv.at[1, dz + 3], spot.device(0, 1)
        )
        if dz != 0 or self.full is None:
            self.send(
                dz, 0, 0, columns[1], self.sends.at[2 + at], self.recv.at[2, dz + 3],
                spot.device(0, 0, 1),
            )
        self.to_core(dz, 0, 0)

    def start(self):
        self.local.start()
        self.spread(0)

    def take_z(self, dz):
        def action():
            arrive(self.place(dz, 0, 0), self.recv.at[0, dz + 3])
            self.spread(dz)

        when_has(self.spot, dz, action)

    def take_yx(self, dz):
        spot = self.spot

        def action():
            columns = self.early if dz else (self.whole, self.whole)
            arrive(self.place(dz, 1, 0, 0, columns[0]), self.recv.at[1, dz + 3])
            self.send(
                dz, 1, 0, self.first, self.sends.at[3], self.recv.at[3, dz + 3],
                spot.device(0, 0, 1),
            )
            if dz != 0 or self.full is None:
                arrive(self.place(dz, 0, 1, 0, columns[1]), self.recv.at[2, dz + 3])
            self.send(
                dz, 0, 1, self.second, self.sends.at[3], self.recv.at[4, dz + 3],
                spot.device(0, 1),
            )

        when_has(spot, dz, action)

    def take_late(self, dz):
        def action():
            for dy, dx in ((1, 0), (0, 1)):
                columns = self.late[dx]
                if dz != 0:
                    arrive(self.place(dz, dy, dx, 0, columns), self.late_recv.at[dz + 3, dx])
                self.along_z(
                    dz, dy, dx, columns, lambda side: self.late_send.at[dz + 3, side, dx],
                    lambda at: self.late_recv.at[at, dx],
                )
                self.to_core(dz, dy, dx)

        when_has(self.spot, dz, action)

    def take_diagonal(self, dz):
        def action():
            arrive(self.place(dz, 1, 1, 0, self.first), self.recv.at[3, dz + 3])
            arrive(self.place(dz, 1, 1, 0, self.second), self.recv.at[4, dz + 3])
            self.to_core(dz, 1, 1)

        when_has(self.spot, dz, action)

    def take_core(self, far, dy, dx):
        view = self.out.at[pl.ds(0, self.count), :]
        arrive(view, self.c_recv.at[far - self.spot.z + 3, dy, dx])

    def drain(self):
        count, spot = self.count, self.spot
        replicated = self.full is not None
        for at, pieces, columns in (
            (0, 14 if replicated else 16, self.whole), (1, 1, self.whole), (2, 1, self.whole),
            (3, 4, self.whole), (4, 3, self.early[0]), (5, 3, self.early[1]),
        ):
            if at != 2 or not replicated:
                arrive(self.out.at[pl.ds(0, pieces * count), columns], self.sends.at[at])
        for dz in range(-3, 4):
            for side, step in ((0, 1), (1, -1)):
                if dz * step <= 0:

                    @pl.when(spot.has(dz) & spot.has(step))
                    def _(dz=dz, side=side):
                        arrive(self.place(0, 0, 0), self.z_send.at[dz + 3, side])
                        for at in (0, 1):
                            arrive(
                                self.place(0, 0, 0, 0, self.late[at]),
                                self.late_send.at[dz + 3, side, at],
                            )


def experts_kernel(
    normed, grad_y, w_gate, w_up, w_down, router, chosen, kept,
    reduced, grad_gate, grad_up, grad_down,
    rows_all, weight, grad_in, grad_in_down, y_block, back_block,
    mine, other, from_a, from_b, from_y, from_x, from_z,
    weight_sem, y_sem, flush_sem, core_send, core_recv, half_send, yx_send, recv,
    line_send, line_recv, *gather_sems,
):
    spot = Spot()
    count, width = normed.shape
    wide = reduced.shape[1]
    local_count, ff, _ = w_gate.shape
    both = local_count * ff
    block = 4 * count
    split = from_a.shape[2]
    first, second = pl.ds(0, split), pl.ds(split, wide - split)
    group = lax.axis_index("expert")
    to_y, to_x, to_c = spot.device(0, 1), spot.device(0, 0, 1), spot.device(0, 0, 0, 1)

    def place_of(step):
        return near_first((step // 2 + 1) % 4, spot.z), (step + (step + 6) // 8) % 2

    def group_rows(step):
        far, dy = place_of(step)
        y = spot.y + dy * (1 - 2 * spot.y)
        return pl.ds(pl.multiple_of((far * 2 + y) * block, block), block)

    def y_copy(step):
        slot = step % 2
        return pltpu.make_async_copy(
            grad_y.at[group_rows(step), :], y_block.at[slot], y_sem.at[slot]
        )

    sources = [ref.at[at] for ref in (w_gate, w_up) for at in range(local_count)]
    weights = [
        pltpu.make_async_copy(source, weight.at[pl.ds(at * ff, ff), :], weight_sem.at[at])
        for at, source in enumerate(sources)
    ]
    for copy in weights:
        copy.start()
    y_copy(0).start()
    gather = Gather(spot, normed, rows_all, *gather_sems)
    spot.greet()
    gather.start()
    grad_in[...] = jnp.zeros_like(grad_in)
    grad_in_down[...] = jnp.zeros_like(grad_in_down)
    gather.local.wait()
    for copy in weights:
        copy.wait()

    def piece(dx, dc):
        _, part = spot.device(0, 0, dx, dc)
        return pl.ds(pl.multiple_of(part * count, count), count)

    def core_copy(step, dx):
        far, dy = place_of(step)
        slot = step % 2
        return pltpu.make_async_remote_copy(
            src_ref=back_block.at[slot, piece(dx, 1), :],
            dst_ref=other.at[far, dy, dx],
            send_sem=core_send.at[slot, dx],
            recv_sem=core_recv.at[far, dy, dx],
            device_id=to_c,
            device_id_type=MESH,
        )

    def merge(far, dy, dx):
        into = mine.at[far, dy, dx]
        arrive(other.at[far, dy, dx], core_recv.at[far, dy, dx])
        return into

    def merge_diagonal(k):
        far = near_first(k, spot.z)
        into = merge(far, 1, 1)
        add_into(into, 16, other.at[far, 1, 1])
        push(into.at[:, first], from_a.at[far], half_send.at[0], recv.at[0, far], to_x)
        push(into.at[:, second], from_b.at[far], half_send.at[1], recv.at[1, far], to_y)

    def merge_yx(k):
        far = near_first(k, spot.z)
        into = merge(far, 1, 0)
        add_into(into, 16, other.at[far, 1, 0])
        arrive(from_a.at[far], recv.at[0, far])
        add_into(into.at[:, first], 16, from_a.at[far])
        push(into, from_y.at[far], yx_send.at[0], recv.at[2, far], to_y)
        into = merge(far, 0, 1)
        add_into(into, 16, other.at[far, 0, 1])
        arrive(from_b.at[far], recv.at[1, far])
        add_into(into.at[:, second], 16, from_b.at[far])
        push(into, from_x.at[far], yx_send.at[1], recv.at[3, far], to_x)

    def merge_line(k):
        far = near_first(k, spot.z)
        into = merge(far, 0, 0)
        arrive(from_y.at[far], recv.at[2, far])
        arrive(from_x.at[far], recv.at[3, far])
        add_into(into, 16, other.at[far, 0, 0], from_y.at[far], from_x.at[far])
        if k > 0:
            push(
                into, from_z.at[spot.z], line_send.at[k], line_recv.at[spot.z],
                (far * 2 + spot.y, spot.x * 2 + spot.c),
            )

    def both_ways(take, distance):
        for dz in (distance, -distance) if distance else (0,):
            take(dz)

    columns = lax.broadcasted_iota(jnp.int32, (block, both), 1)
    lower = columns < ff
    lanes = lax.broadcasted_iota(jnp.int32, (block, 128), 1)
    names = lax.broadcasted_iota(jnp.int32, (router.shape[0], block), 0)

    def compute(step):
        slot = step % 2
        here = group_rows(step)
        rows = rows_all[here, :]
        lin = mxu(rows, weight[...], 1, 1)
        gate, up = lin[:, :both], lin[:, both:]
        logits = mxu(router[...], rows, 1, 1)
        picked = chosen[:, here] > 0.0
        top = jnp.max(jnp.where(picked, logits, NEG), axis=0, keepdims=True)
        exps = jnp.where(picked, jnp.exp(logits - top), 0.0)
        soft = exps / jnp.sum(exps, axis=0, keepdims=True)
        keep = kept[:, here]
        soft = jnp.where(keep > 0.0, soft, 0.0)
        lines = []
        for table in (soft, keep):
            for at in range(local_count):
                lines.append(
                    jnp.sum(
                        jnp.where(names == group * local_count + at, table, 0.0),
                        axis=0, keepdims=True,
                    )
                )
        stack = jnp.concatenate(lines + [jnp.zeros((8 - len(lines), block), F32)], axis=0).T
        spread = jnp.where(lower, stack[:, 0:1], stack[:, 1:2])
        sigmoid = 1.0 / (1.0 + jnp.exp(-gate))
        silu = gate * sigmoid
        act = (silu * up).astype(BF16).astype(F32)
        weighted = (act * spread).astype(BF16)
        y_copy(step).wait()

        @pl.when(step >= 2)
        def _():
            for dx in (0, 1):
                core_copy(step - 2, dx).wait_send()

        back_block[slot, :, :width] = mxu(weighted, w_down[...]).astype(BF16)
        pass_on(step, 1)
        y_rows = y_block[slot]
        mid = mxu(y_rows, w_down[...], 1, 1)
        dots = act * mid
        low = jnp.sum(jnp.where(lower, dots, 0.0), axis=1, keepdims=True) * stack[:, 2:3]
        high = jnp.sum(jnp.where(lower, 0.0, dots), axis=1, keepdims=True) * stack[:, 3:4]
        mine_at = group * local_count
        tail = jnp.where(lanes == mine_at, low, jnp.where(lanes == mine_at + 1, high, 0.0))
        grad_act = mid * spread
        grad_up_lin = (grad_act * silu).astype(BF16)
        grad_gate_lin = (grad_act * up * sigmoid * (1.0 + gate * (1.0 - sigmoid))).astype(BF16)
        grad_lin = jnp.concatenate([grad_gate_lin, grad_up_lin], axis=1)
        back_block[slot, :, width : 2 * width] = mxu(grad_lin, weight[...]).astype(BF16)
        back_block[slot, :, 2 * width :] = tail.astype(BF16)
        far, dy = place_of(step)
        for dx in (1, 0):
            core_copy(step, dx).start()
            mine[far, dy, dx] = back_block[slot, piece(dx, 0), :]
        grad_in[...] += mxu(grad_lin, rows, 0, 0)
        grad_in_down[...] += mxu(weighted, y_rows, 0, 0)

    plans = {
        0: lambda: (
            both_ways(gather.take_yx, 0), both_ways(gather.take_z, 1),
            both_ways(gather.take_z, 2), both_ways(gather.take_diagonal, 0),
            both_ways(gather.take_late, 0), both_ways(gather.take_yx, 1),
            both_ways(gather.take_z, 3), both_ways(gather.take_late, 1),
        ),
        1: lambda: both_ways(gather.take_yx, 2),
        2: lambda: (both_ways(gather.take_diagonal, 1), both_ways(gather.take_late, 2)),
        3: lambda: both_ways(gather.take_yx, 3),
        4: lambda: (both_ways(gather.take_diagonal, 2), both_ways(gather.take_late, 3)),
        5: lambda: merge_diagonal(1),
        6: lambda: both_ways(gather.take_diagonal, 3),
        7: lambda: merge_diagonal(2),
        9: lambda: merge_yx(1),
        11: lambda: (merge_diagonal(3), merge_yx(2)),
        13: lambda: merge_line(1),
        15: lambda: (merge_diagonal(0), merge_yx(3)),
    }

    def pass_on(step, middle):
        for at, plan in plans.items():
            if at % 2 == middle:

                @pl.when(step == at // 2)
                def _(plan=plan):
                    plan()

    @pl.loop(0, 8)
    def _(step):
        pass_on(step, 0)

        @pl.when(step < 7)
        def _():
            y_copy(step + 1).start()

        far, dy = place_of(step)
        for dx in (0, 1):
            gather.take_core(far, dy, dx)
        compute(step)

    flush = [
        pltpu.make_async_copy(
            grad_in.at[pl.ds(at * ff, ff), :],
            (grad_gate, grad_up)[at // local_count].at[at % local_count],
            flush_sem.at[at],
        )
        for at in range(2 * local_count)
    ]
    flush.append(pltpu.make_async_copy(grad_in_down, grad_down, flush_sem.at[2 * local_count]))
    for copy in flush:
        copy.start()
    merge_line(2)
    merge_yx(0)
    merge_line(3)
    merge_line(0)
    total = mine[spot.z, 0, 0].astype(F32)
    for k in (1, 2, 3):
        source = near_first(k, spot.z)
        arrive(from_z.at[source], line_recv.at[source])
        total = total + from_z[source].astype(F32)
    reduced[...] = total
    gather.drain()
    for step in (6, 7):
        for dx in (0, 1):
            core_copy(step, dx).wait_send()
    arrive(from_a, half_send.at[0])
    arrive(from_b, half_send.at[1])
    arrive(from_y, yx_send.at[0])
    arrive(from_x, yx_send.at[1])
    for k in (1, 2, 3):
        arrive(from_z.at[0], line_send.at[k])
    for copy in flush:
        copy.wait()


def experts(normed, grad_y, w_gate, w_up, w_down, router, chosen, kept):
    count, width = normed.shape
    wide = 2 * width + 128
    total = grad_y.shape[0]
    local_count, ff, _ = w_gate.shape
    both = local_count * ff
    shape, vmem, dma = jax.ShapeDtypeStruct, pltpu.VMEM, pltpu.SemaphoreType.DMA
    line = vmem((4, count, wide), BF16)
    return pl.pallas_call(
        experts_kernel,
        out_shape=(
            shape((count, wide), F32),
            shape(w_gate.shape, F32), shape(w_up.shape, F32), shape((both, width), F32),
        ),
        in_specs=[VMEM_SPEC, HBM_SPEC, HBM_SPEC, HBM_SPEC] + [VMEM_SPEC] * 4,
        out_specs=(VMEM_SPEC,) + (HBM_SPEC,) * 3,
        scratch_shapes=[
            vmem((total, width), BF16),
            vmem((2 * both, width), BF16),
            vmem((2 * both, width), F32),
            vmem((both, width), F32),
            vmem((2, 4 * count, width), BF16),
            vmem((2, 4 * count, wide), BF16),
            vmem((4, 2, 2, count, wide), BF16),
            vmem((4, 2, 2, count, wide), BF16),
            vmem((4, count, width), BF16),
            vmem((4, count, wide - width), BF16),
            line, line, line,
        ]
        + dma_sems(
            ((2 * local_count,), (2,), (2 * local_count + 1,), (2, 2), (4, 2, 2), (2,), (2,), (4, 4),
             (4,), (4,))
            + Gather.SEMS
        ),
        compiler_params=pltpu.CompilerParams(
            collective_id=8, has_side_effects=True, vmem_limit_bytes=63 << 20
        ),
        name="experts",
        cost_estimate=cost(29_000_000_000, 120),
    )(normed, grad_y, w_gate, w_up, w_down, router, chosen, kept)


def attend_back_kernel(
    own_rows, w_out, queries, keys, values, attended, lin, cosine, sine, place_column,
    place_row, open_row, log_total, k_gain, q_gain,
    grad_lin, grad_out, grad_q_gain, grad_k_gain,
    rows_all, head_out, grad_keys, grad_values, out_sum, head_sem, *gather_sems,
):
    spot = Spot()
    count = own_rows.shape[0]
    block = 4 * count
    dim = queries.shape[1]
    group = lax.axis_index("expert")
    head_copy = pltpu.make_async_copy(
        w_out.at[pl.ds(pl.multiple_of(group * dim, dim), dim), :], head_out, head_sem
    )
    head_copy.start()
    gather = Gather(spot, own_rows, rows_all, *gather_sems)
    spot.greet()
    gather.start()
    grad_keys[...] = jnp.zeros_like(grad_keys)
    grad_values[...] = jnp.zeros_like(grad_values)
    out_sum[...] = jnp.zeros_like(out_sum)
    grad_q_gain[...] = jnp.zeros_like(grad_q_gain)
    gather.local.wait()
    head_copy.wait()

    def unshape(grad, plain, gain, cos, sin):
        grad = grad * cos + pltpu.roll(grad * sin, dim // 2, 1)
        normed, root = head_norm(plain)
        gain_part = jnp.sum(grad * normed, axis=0, keepdims=True)
        grad = grad * gain
        return root * (grad - normed * jnp.mean(grad * normed, axis=-1, keepdims=True)), gain_part

    def compute(far, dy):
        y = spot.y + dy * (1 - 2 * spot.y)
        here = pl.ds(pl.multiple_of((far * 2 + y) * block, block), block)
        rows = rows_all[here, :]
        query = queries[here, :]
        grad_att = mxu(rows, head_out[...], 1, 1).astype(BF16)
        scores = mxu(keys[...], query, 1, 1)
        seen = (place_column[...] <= place_row[:, here]) & (place_column[...] >= open_row[:, here])
        probability = jnp.exp(jnp.where(seen, scores - log_total[:, here], NEG))
        grad_prob = mxu(values[...], grad_att, 1, 1)
        delta = jnp.sum(probability * grad_prob, axis=0, keepdims=True)
        grad_scores = (probability * (grad_prob - delta)).astype(BF16)
        grad_values[...] += mxu(probability.astype(BF16), grad_att)
        grad_keys[...] += mxu(grad_scores, query)
        grad_query = mxu(grad_scores, keys[...], 0, 0) * dim**-0.5
        grad_query, gain_part = unshape(
            grad_query, lin[here, :dim], q_gain[...], cosine[here, :], sine[here, :]
        )
        grad_q_gain[...] += gain_part
        grad_lin[here, :dim] = grad_query.astype(BF16)
        out_sum[...] += mxu(attended[here, :], rows, 0, 0)

    def both_ways(take, distance):
        for dz in (distance, -distance) if distance else (0,):
            take(dz)

    plans = {
        0: lambda: (both_ways(gather.take_yx, 0), both_ways(gather.take_z, 1),
                    both_ways(gather.take_late, 0)),
        1: lambda: (both_ways(gather.take_diagonal, 0), both_ways(gather.take_z, 2)),
        2: lambda: (both_ways(gather.take_yx, 1), both_ways(gather.take_z, 3),
                    both_ways(gather.take_late, 1)),
        3: lambda: (both_ways(gather.take_yx, 2), both_ways(gather.take_diagonal, 1),
                    both_ways(gather.take_late, 2)),
        4: lambda: (both_ways(gather.take_yx, 3), both_ways(gather.take_late, 3)),
        5: lambda: both_ways(gather.take_diagonal, 2),
        7: lambda: both_ways(gather.take_diagonal, 3),
    }

    @pl.loop(0, 8)
    def _(step):
        for at, plan in plans.items():

            @pl.when(step == at)
            def _(plan=plan):
                plan()

        far, dy = near_first(step // 2, spot.z), step % 2
        for dx in (0, 1):
            gather.take_core(far, dy, dx)
        compute(far, dy)

    grad_out[...] = out_sum[...].astype(BF16)
    grad_key, key_part = unshape(grad_keys[...], lin[:, dim:], k_gain[...], cosine[...], sine[...])
    grad_lin[:, dim : 2 * dim] = grad_key.astype(BF16)
    grad_lin[:, 2 * dim :] = grad_values[...].astype(BF16)
    grad_k_gain[...] = key_part
    gather.drain()


def attend_back(
    own_rows, w_out, queries, keys, values, attended, lin, cosine, sine, place_column,
    place_row, open_row, log_total, k_gain, q_gain,
):
    count, width = own_rows.shape
    total, dim = keys.shape
    shape, vmem = jax.ShapeDtypeStruct, pltpu.VMEM
    return pl.pallas_call(
        attend_back_kernel,
        out_shape=[
            shape((total, 3 * dim), BF16), shape((dim, width), BF16),
            shape((1, dim), F32), shape((1, dim), F32),
        ],
        in_specs=[VMEM_SPEC, HBM_SPEC] + [VMEM_SPEC] * 13,
        out_specs=[VMEM_SPEC] * 4,
        scratch_shapes=[
            vmem((total, width), BF16), vmem((dim, width), BF16),
            vmem((total, dim), F32), vmem((total, dim), F32), vmem((dim, width), F32),
        ]
        + dma_sems((None,) + Gather.SEMS),
        compiler_params=pltpu.CompilerParams(
            collective_id=9, has_side_effects=True, vmem_limit_bytes=60 << 20
        ),
        name="attend_back",
        cost_estimate=cost(9_000_000_000, 50),
    )(
        own_rows, w_out, queries, keys, values, attended, lin, cosine, sine, place_column,
        place_row, open_row, log_total, k_gain, q_gain,
    )


class LineGather:
    SEMS = ((7,), (7,), (7, 2), None, None, (7, 2), (7, 2, 2), None)

    def __init__(self, spot, place, own, sems):
        self.spot, self.place, self.own = spot, place, own
        self.z_recv, self.y_recv, self.z_send, self.y_send = sems[:4]
        self.late_y_recv, self.late_z_recv, self.late_z_send, self.late_y_send = sems[4:]

    def source(self, dz, dy, part):
        return self.own(part) if dz == 0 and dy == 0 else self.place(dz, dy, part)

    def along_z(self, dz, dy, part):
        for side, step in ((0, 1), (1, -1)):
            if dz * step <= 0:

                @pl.when(self.spot.has(step))
                def _(side=side, step=step):
                    if part:
                        send = self.late_z_send.at[dz + 3, side, dy]
                        recv = self.late_z_recv.at[dz + 3 - step, dy]
                    else:
                        send = self.z_send.at[dz + 3, side]
                        recv = self.z_recv.at[dz + 3 - step]
                    push(
                        self.source(dz, dy, part), self.place(dz, dy, part), send, recv,
                        self.spot.device(step),
                    )

    def along_y(self, dz):
        push(
            self.source(dz, 0, 0), self.place(dz, 0, 0), self.y_send, self.y_recv.at[dz + 3],
            self.spot.device(0, 1),
        )

    def start(self):
        self.along_z(0, 0, 0)
        push(
            self.own(1), self.place(0, 0, 1), self.late_y_send, self.late_y_recv,
            self.spot.device(0, 1),
        )
        self.along_y(0)
        self.along_z(0, 0, 1)

    def take_z(self, distance):
        for dz in (distance, -distance):

            def action(dz=dz):
                arrive(self.place(dz, 0, 0), self.z_recv.at[dz + 3])
                self.along_z(dz, 0, 0)
                self.along_y(dz)

            when_has(self.spot, dz, action)

    def take_late_y(self):
        arrive(self.place(0, 1, 1), self.late_y_recv)
        self.along_z(0, 1, 1)

    def take_late_z(self, distance):
        for dz in (distance, -distance):

            def action(dz=dz):
                for dy in (0, 1):
                    arrive(self.place(dz, dy, 1), self.late_z_recv.at[dz + 3, dy])
                    self.along_z(dz, dy, 1)

            when_has(self.spot, dz, action)

    def drain(self, four):
        for dz in (0, 1, -1, 2, -2, 3, -3):

            def action(dz=dz):
                arrive(self.place(dz, 1, 0), self.y_recv.at[dz + 3])
                for side, step in ((0, 1), (1, -1)):
                    if dz * step <= 0:

                        @pl.when(self.spot.has(step))
                        def _(side=side):
                            arrive(self.place(dz, 0, 0), self.z_send.at[dz + 3, side])
                            for dy in (0, 1):
                                arrive(
                                    self.place(dz, dy, 1), self.late_z_send.at[dz + 3, side, dy]
                                )

            when_has(self.spot, dz, action)
        arrive(four, self.y_send)
        arrive(self.place(0, 0, 1), self.late_y_send)


def close_kernel(
    normed, grad_lin, w_query, w_key, w_value, head_out,
    reduced, kv_all, query_all, out_all,
    weight, rows, sums, query_own, kv_part, back, mine, other, from_x_diagonal, from_y, from_x,
    from_z, kv_mine, kv_y, kv_z, kv_own, row_sem, weight_sem, local_sem,
    core_send, core_recv, many_send, recv, line_send, line_recv,
    kv_send, kv_y_recv, kv_line_send, kv_line_recv, *gather_sems,
):
    spot = Spot()
    total, width = normed.shape
    count, wide = reduced.shape
    block = 4 * count
    dim = w_key.shape[1]
    group = lax.axis_index("expert")
    to_y, to_x, to_c = spot.device(0, 1), spot.device(0, 0, 1), spot.device(0, 0, 0, 1)
    cut = 1664

    def parts(part):
        return pl.ds(cut, total - cut) if part else pl.ds(0, cut)

    def lane_block(dz, dy):
        return pl.ds(pl.multiple_of(spot.device(dz, dy)[0] * dim, dim), dim)

    weights = [
        pltpu.make_async_copy(
            w_query.at[:, pl.ds(pl.multiple_of(group * dim, dim), dim)],
            weight.at[:, pl.ds(0, dim)], weight_sem.at[0],
        ),
        pltpu.make_async_copy(w_key, weight.at[:, pl.ds(dim, dim)], weight_sem.at[1]),
        pltpu.make_async_copy(w_value, weight.at[:, pl.ds(2 * dim, dim)], weight_sem.at[2]),
    ]

    def row_copy(step):
        return pltpu.make_async_copy(
            normed.at[pl.ds(pl.multiple_of(step * block, block), block), :],
            rows.at[step % 2], row_sem.at[step % 2],
        )

    for copy in weights:
        copy.start()
    row_copy(0).start()
    outs = LineGather(
        spot,
        lambda dz, dy, part: out_all.at[lane_block(dz, dy), parts(part)],
        lambda part: head_out.at[:, parts(part)],
        gather_sems[:8],
    )
    queries = LineGather(
        spot,
        lambda dz, dy, part: query_all.at[parts(part), lane_block(dz, dy)],
        lambda part: query_own.at[parts(part), :],
        gather_sems[8:16],
    )
    kv_rows = total // 8

    def kv_span(start, part):
        return pl.ds(pl.multiple_of(start + part * (kv_rows // 2), kv_rows // 2), kv_rows // 2)

    kvs = LineGather(
        spot,
        lambda dz, dy, part: kv_all.at[kv_span(spot.device(dz, dy)[0] * kv_rows, part), :],
        lambda part: kv_own.at[kv_span(0, part), :],
        gather_sems[16:],
    )
    out_copy = pltpu.make_async_copy(head_out, out_all.at[lane_block(0, 0), :], local_sem.at[0])
    out_copy.start()
    spot.greet(line=True)
    outs.start()

    sums[...] = jnp.zeros_like(sums)

    @pl.loop(0, total // block)
    def _(step):
        @pl.when(step < total // block - 1)
        def _():
            row_copy(step + 1).start()

        row_copy(step).wait()
        here = pl.ds(pl.multiple_of(step * block, block), block)
        sums[...] += mxu(grad_lin[here, :], rows[step % 2], 0, 0)

    query_own[...] = sums[:dim, :].T.astype(BF16)
    kv_part[...] = sums[dim:, :].T.astype(BF16)
    query_copy = pltpu.make_async_copy(query_own, query_all.at[:, lane_block(0, 0)], local_sem.at[1])
    query_copy.start()

    def group_rows(far, dy):
        y = spot.y + dy * (1 - 2 * spot.y)
        return pl.ds(pl.multiple_of((far * 2 + y) * block, block), block)

    for k in (3, 2, 1, 0):
        far = near_first(k, spot.z)
        push(
            kv_part.at[group_rows(far, 1), :], kv_y.at[far], kv_send, kv_y_recv.at[far], to_y
        )
    for copy in weights:
        copy.wait()

    def piece(dx, dc):
        _, part = spot.device(0, 0, dx, dc)
        return pl.ds(pl.multiple_of(part * count, count), count)

    def core_copy(step, far, dy, dx):
        return pltpu.make_async_remote_copy(
            src_ref=back.at[step % 2, piece(dx, 1), :],
            dst_ref=other.at[far, dy, dx],
            send_sem=core_send.at[step % 2, dx],
            recv_sem=core_recv.at[far, dy, dx],
            device_id=to_c,
            device_id_type=MESH,
        )

    def produce(k):
        far = near_first(k, spot.z)
        for dy in (1, 0):
            step = 2 * (3 - k) + 1 - dy
            if step >= 2:
                for dx in (1, 0):
                    core_copy(step, far, dy, dx).wait_send()
            here = group_rows(far, dy)
            back[step % 2] = mxu(grad_lin[here, :], weight[...], 1, 1).astype(BF16)
            for dx in (1, 0):
                core_copy(step, far, dy, dx).start()
                mine[far, dy, dx] = back[step % 2, piece(dx, 0), :]

    def merge(far, dy, dx, *terms):
        arrive(other.at[far, dy, dx], core_recv.at[far, dy, dx])
        add_into(mine.at[far, dy, dx], 16, other.at[far, dy, dx], *terms)
        return mine.at[far, dy, dx]

    def merge_diagonal(k):
        far = near_first(k, spot.z)
        push(
            merge(far, 1, 1), from_x_diagonal.at[far], many_send.at[0], recv.at[0, far], to_x
        )

    def merge_yx(k):
        far = near_first(k, spot.z)
        push(merge(far, 0, 1), from_x.at[far], many_send.at[1], recv.at[1, far], to_x)
        arrive(from_x_diagonal.at[far], recv.at[0, far])
        push(
            merge(far, 1, 0, from_x_diagonal.at[far]), from_y.at[far], many_send.at[2],
            recv.at[2, far], to_y,
        )

    def far_device(far):
        return (far * 2 + spot.y, spot.x * 2 + spot.c)

    def merge_kv(k):
        far = near_first(k, spot.z)
        kv_mine[far] = kv_part[group_rows(far, 0), :]
        arrive(kv_y.at[far], kv_y_recv.at[far])
        add_into(kv_mine.at[far], 64, kv_y.at[far])
        if k > 0:
            push(
                kv_mine.at[far], kv_z.at[spot.z], kv_line_send.at[k], kv_line_recv.at[spot.z],
                far_device(far),
            )

    def merge_line(k):
        far = near_first(k, spot.z)
        arrive(from_y.at[far], recv.at[2, far])
        arrive(from_x.at[far], recv.at[1, far])
        into = merge(far, 0, 0, from_y.at[far], from_x.at[far])
        if k > 0:
            push(
                into, from_z.at[spot.z], line_send.at[k], line_recv.at[spot.z], far_device(far)
            )

    def sum_kv():
        sums_kv = kv_mine[spot.z].astype(F32)
        for k in (1, 2, 3):
            source = near_first(k, spot.z)
            arrive(kv_z.at[source], kv_line_recv.at[source])
            sums_kv = sums_kv + kv_z[source].astype(F32)
        kv_own[...] = sums_kv.astype(BF16)

    produce(3)
    produce(2)
    outs.take_z(1)
    for k in (3, 2, 1, 0):
        merge_kv(k)
    queries.start()
    merge_diagonal(3)
    produce(1)
    merge_diagonal(2)
    outs.take_late_y()
    produce(0)
    merge_diagonal(1)
    sum_kv()
    kvs.start()
    kv_copy = pltpu.make_async_copy(
        kv_own, kv_all.at[pl.ds(pl.multiple_of(group * kv_rows, kv_rows), kv_rows), :],
        local_sem.at[2],
    )
    kv_copy.start()
    outs.take_z(2)
    queries.take_z(1)
    merge_diagonal(0)
    merge_yx(3)
    kvs.take_z(1)
    kvs.take_late_y()
    queries.take_late_y()
    outs.take_late_z(1)
    merge_yx(2)
    outs.take_z(3)
    queries.take_z(2)
    kvs.take_z(2)
    kvs.take_late_z(1)
    merge_line(3)
    merge_yx(1)
    queries.take_late_z(1)
    outs.take_late_z(2)
    kvs.take_z(3)
    kvs.take_late_z(2)
    merge_line(2)
    merge_yx(0)
    queries.take_z(3)
    queries.take_late_z(2)
    outs.take_late_z(3)
    merge_line(1)
    merge_line(0)
    kvs.take_late_z(3)
    queries.take_late_z(3)
    total_rows = mine[spot.z, 0, 0].astype(F32)
    for k in (1, 2, 3):
        source = near_first(k, spot.z)
        arrive(from_z.at[source], line_recv.at[source])
        total_rows = total_rows + from_z[source].astype(F32)
    reduced[...] = total_rows

    kvs.drain(kv_all.at[pl.ds(0, 2 * kv_rows), :])
    kv_copy.wait()
    outs.drain(out_all.at[pl.ds(0, 4 * dim), parts(0)])
    queries.drain(query_all.at[parts(0), pl.ds(0, 4 * dim)])
    out_copy.wait()
    query_copy.wait()
    for step in (6, 7):
        for dx in (0, 1):
            core_copy(step, near_first(0, spot.z), 0, dx).wait_send()
    arrive(from_x_diagonal, many_send.at[0])
    arrive(from_x, many_send.at[1])
    arrive(from_y, many_send.at[2])
    arrive(kv_y, kv_send)
    for k in (1, 2, 3):
        arrive(from_z.at[0], line_send.at[k])
        arrive(kv_z.at[0], kv_line_send.at[k])


def close(normed, grad_lin, w_query, w_key, w_value, head_out):
    total, width = normed.shape
    count, wide, dim = total // 32, width, w_key.shape[1]
    shape, vmem = jax.ShapeDtypeStruct, pltpu.VMEM
    line, kv_line = vmem((4, count, wide), BF16), vmem((4, 4 * count, 2 * dim), BF16)
    return pl.pallas_call(
        close_kernel,
        out_shape=(
            shape((count, wide), F32), shape((total, 2 * dim), BF16),
            shape((total, 8 * dim), BF16), shape((8 * dim, width), BF16),
        ),
        in_specs=[HBM_SPEC, VMEM_SPEC, HBM_SPEC, HBM_SPEC, HBM_SPEC, VMEM_SPEC],
        out_specs=(VMEM_SPEC, HBM_SPEC, HBM_SPEC, HBM_SPEC),
        scratch_shapes=[
            vmem((width, 3 * dim), BF16), vmem((2, 4 * count, width), BF16),
            vmem((3 * dim, width), F32), vmem((width, dim), BF16), vmem((width, 2 * dim), BF16),
            vmem((2, 4 * count, wide), BF16),
            vmem((4, 2, 2, count, wide), BF16), vmem((4, 2, 2, count, wide), BF16),
            line, line, line, line, kv_line, kv_line, kv_line,
            vmem((4 * count, 2 * dim), BF16),
        ]
        + dma_sems(
            ((2,), (3,), (3,), (2, 2), (4, 2, 2), (3,), (3, 4), (4,), (4,),
             None, (4,), (4,), (4,)) + LineGather.SEMS * 3
        ),
        compiler_params=pltpu.CompilerParams(
            collective_id=10, has_side_effects=True, vmem_limit_bytes=60 << 20
        ),
        name="close",
        cost_estimate=cost(7_000_000_000, 110),
    )(normed, grad_lin, w_query, w_key, w_value, head_out)


def cosine_sine(angles):
    lanes = lax.broadcasted_iota(jnp.int32, angles.shape, 1)
    turns = jnp.floor(angles * (2.0 / math.pi) + 0.5)
    rest = angles - turns * 1.5703125
    rest = rest - turns * 4.837512969970703125e-4
    rest = rest - turns * 7.54978995489188216e-8
    square = rest * rest
    sine = square * (8.3321608736e-3 + square * -1.9515295891e-4) - 1.6666654611e-1
    sine = rest + rest * square * sine
    cosine = -1.388731625493765e-3 + square * 2.443315711809948e-5
    cosine = 1.0 - 0.5 * square + square * square * (4.166664568298827e-2 + square * cosine)
    turns = jnp.where(lanes < angles.shape[1] // 2, turns, turns - 1.0)
    turns = turns - 4.0 * jnp.floor(turns * 0.25)
    odd = (turns == 1.0) | (turns == 3.0)
    value = jnp.where(odd, sine, cosine)
    return jnp.where((turns == 1.0) | (turns == 2.0), -value, value)


def front_kernel(
    hidden, cotangent, tag, lengths, gain, w_query, w_key, w_value, q_gain, k_gain, inverse,
    w_out, second_gain,
    normed_all, queries, keys, values, lin_out, cosine, sine, attended, log_total,
    place_row, open_row, place_column, residual, normed, chosen, kept, grad_y_all,
    rows_all, weight, out_weight, staged, tags, ranks, picks, att_rows,
    partial_sum, from_core, to_x_sum, from_x,
    weight_sem, stage_sem, tag_z, tag_y, tag_z_send, tag_y_send, tag_local,
    send_sem, recv_sem, own_sem, tensor_sems, *gather_sems,
):
    spot = Spot()
    group, part = lax.axis_index("expert"), lax.axis_index("tensor")
    count, width = residual.shape
    block = 4 * count
    total = 32 * count
    dim = w_key.shape[1]
    own = pl.ds(pl.multiple_of(part * count, count), count)

    weights = [
        pltpu.make_async_copy(
            w_query.at[:, pl.ds(pl.multiple_of(group * dim, dim), dim)],
            weight.at[:, pl.ds(0, dim)], weight_sem.at[0],
        ),
        pltpu.make_async_copy(w_key, weight.at[:, pl.ds(dim, dim)], weight_sem.at[1]),
        pltpu.make_async_copy(w_value, weight.at[:, pl.ds(2 * dim, dim)], weight_sem.at[2]),
        pltpu.make_async_copy(w_out, out_weight, weight_sem.at[3]),
    ]
    for copy in weights:
        copy.start()
    barrier = pltpu.get_barrier_semaphore()

    @pl.loop(1, 8)
    def _(step):
        pl.semaphore_signal(
            barrier, inc=1, device_id=((group + step) % 8, part), device_id_type=MESH
        )

    for device in (spot.device(0, 0, 1), spot.device(0, 0, 0, 1)):
        pl.semaphore_signal(barrier, inc=1, device_id=device, device_id_type=MESH)

    def tag_place(dz, dy):
        return tags.at[spot.device(dz, dy)[0]]

    tag_copy = pltpu.make_async_copy(tag, tag_place(0, 0), tag_local)
    tag_copy.start()
    pl.semaphore_wait(barrier, 9)

    def spread_tag(dz):
        here = tag_place(dz, 0)
        source = tag if dz == 0 else here
        for side, step in ((0, 1), (1, -1)):
            if dz * step <= 0:

                @pl.when(spot.has(step))
                def _(side=side, step=step):
                    push(
                        source, here, tag_z_send.at[dz + 3, side], tag_z.at[dz + 3 - step],
                        spot.device(step),
                    )

        push(source, here, tag_y_send.at[dz + 3], tag_y.at[dz + 3], spot.device(0, 1))

    def take_tag(dz):
        def action():
            arrive(tag_place(dz, 0), tag_z.at[dz + 3])
            spread_tag(dz)

        when_has(spot, dz, action)

    def take_tag_y(dz):
        when_has(spot, dz, lambda: arrive(tag_place(dz, 1), tag_y.at[dz + 3]))

    spread_tag(0)
    gather = Gather(spot, hidden.at[own, :], rows_all, *gather_sems[:7], full=hidden)
    gather.start()
    late = Gather(spot, cotangent.at[own, :], grad_y_all, *gather_sems[7:], full=cotangent)
    tag_copy.wait()
    gather.local.wait()
    for copy in weights:
        copy.wait()

    def group_of(step):
        far, dy = near_first(step // 2, spot.z), step % 2
        return far, dy, far * 2 + spot.y + dy * (1 - 2 * spot.y)

    def stage_copy(step):
        _, _, index = group_of(step)
        return pltpu.make_async_copy(
            staged.at[step % 2],
            normed_all.at[pl.ds(pl.multiple_of(index * block, block), block), :],
            stage_sem.at[step % 2],
        )

    experts_count = chosen.shape[0]
    names = lax.broadcasted_iota(jnp.int32, (experts_count, block), 0)
    lanes = lax.broadcasted_iota(jnp.int32, (block, dim), 1)

    def project_group(step):
        _, _, index = group_of(step)
        here = pl.ds(pl.multiple_of(index * block, block), block)
        entries = tags[index]
        place = entries[0:1, :]
        segment, opening, bound = jnp.zeros_like(place), jnp.zeros_like(place), 0
        for at in range(lengths.shape[0]):
            bound = bound + lengths[at]
            segment = segment + jnp.where(place >= bound, 1, 0)
            opening = jnp.where(place >= bound, bound, opening)
        place_row[:, here] = place.astype(F32)
        open_row[:, here] = opening.astype(F32)
        lines = jnp.concatenate(
            [place.astype(F32), (place - opening).astype(F32), entries[1:2, :].astype(F32),
             jnp.zeros((5, block), F32)],
            axis=0,
        ).T
        place_column[here, :] = lines[:, 0:1]
        ranks[here, :] = lines[:, 2:3]
        named = jnp.zeros((experts_count, block), F32)
        for at in range(2, 2 + TOPK):
            named = jnp.where(entries[at : at + 1, :] == names, 1.0, named)
        chosen[:, here] = named
        valid = segment < lengths.shape[0]
        picks[:, here] = jnp.where(valid, named, 0.0).astype(BF16)
        table = cosine_sine(lines[:, 1:2] * inverse[...])
        turned_table = pltpu.roll(table, dim // 2, 1)
        cos = jnp.where(lanes < dim // 2, table, turned_table)
        sin = jnp.where(lanes < dim // 2, -turned_table, table)
        cosine[here, :] = cos
        sine[here, :] = sin
        rows = rows_all[here, :].astype(F32)
        root = lax.rsqrt(jnp.mean(rows * rows, axis=-1, keepdims=True) + EPS)

        @pl.when(step >= 2)
        def _():
            stage_copy(step - 2).wait()

        staged[step % 2] = (rows * root * gain[...]).astype(BF16)
        stage_copy(step).start()
        lin = mxu(staged[step % 2], weight[...])
        lin_out[here, :] = lin[:, : 2 * dim]
        values[here, :] = lin[:, 2 * dim :].astype(BF16)
        for at, head_gain, scale, out in (
            (0, q_gain, dim**-0.5, queries), (dim, k_gain, 1.0, keys),
        ):
            plain, _ = head_norm(lin[:, at : at + dim])
            plain = plain * head_gain[...]
            out[here, :] = ((plain * cos + pltpu.roll(plain, dim // 2, 1) * sin) * scale).astype(
                BF16
            )

    def both_ways(take, distance):
        for dz in (distance, -distance) if distance else (0,):
            take(dz)

    def run(plans, step):
        for at, plan in plans.items():

            @pl.when(step == at)
            def _(plan=plan):
                plan()

    plans = {
        0: lambda: (both_ways(gather.take_yx, 0), both_ways(take_tag, 1),
                    both_ways(gather.take_z, 1)),
        1: lambda: (both_ways(take_tag_y, 0), both_ways(gather.take_diagonal, 0),
                    both_ways(take_tag, 2), both_ways(gather.take_z, 2),
                    both_ways(gather.take_late, 0)),
        2: lambda: (both_ways(gather.take_yx, 1), both_ways(take_tag, 3),
                    both_ways(gather.take_z, 3), both_ways(gather.take_late, 1)),
        3: lambda: (both_ways(take_tag_y, 1), both_ways(gather.take_yx, 2),
                    both_ways(gather.take_diagonal, 1), both_ways(gather.take_late, 2)),
        4: lambda: (both_ways(gather.take_yx, 3), late.start()),
        5: lambda: (both_ways(take_tag_y, 2), both_ways(gather.take_diagonal, 2),
                    both_ways(gather.take_late, 3)),
        7: lambda: (both_ways(take_tag_y, 3), both_ways(gather.take_diagonal, 3)),
    }

    @pl.loop(0, 8)
    def _(step):
        run(plans, step)
        far, dy, _ = group_of(step)

        @pl.when(step > 0)
        def _():
            for dx in (0, 1):
                gather.take_core(far, dy, dx)

        project_group(step)

    mine = att_rows.at[:, pl.ds(pl.multiple_of(group * dim, dim), dim)]

    def block_copy(step):
        target = (group + step) % 8
        return pltpu.make_async_remote_copy(
            src_ref=attended.at[pl.ds(pl.multiple_of(target * block, block), block), :],
            dst_ref=mine,
            send_sem=send_sem.at[step],
            recv_sem=recv_sem.at[step],
            device_id=(target, part),
            device_id_type=MESH,
        )

    def attend_block(step):
        here = pl.ds(pl.multiple_of((group + step) % 8 * block, block), block)
        scores = mxu(keys[...], queries[here, :], 1, 1)
        seen = (place_column[...] <= place_row[:, here]) & (place_column[...] >= open_row[:, here])
        scores = jnp.where(seen, scores, NEG)
        highest = jnp.max(scores, axis=0, keepdims=True)
        exps = jnp.exp(scores - highest)
        totals = jnp.sum(exps, axis=0, keepdims=True)
        probability = (exps * (1.0 / totals)).astype(BF16)
        attended[here, :] = mxu(values[...], probability, 0, 0).T.astype(BF16)
        log_total[:, here] = highest + jnp.log(totals)

    late_plans = {
        1: lambda: (both_ways(late.take_yx, 0), both_ways(late.take_z, 1)),
        3: lambda: (both_ways(late.take_z, 2), both_ways(late.take_diagonal, 0),
                    both_ways(late.take_late, 0)),
        5: lambda: (both_ways(late.take_yx, 1), both_ways(late.take_z, 3)),
        7: lambda: (both_ways(late.take_late, 1), both_ways(late.take_yx, 2),
                    both_ways(late.take_diagonal, 1)),
    }

    @pl.loop(1, 8)
    def _(step):
        run(late_plans, step)
        attend_block(step)
        block_copy(step).start()

    attend_block(0)
    own_copy = pltpu.make_async_copy(
        attended.at[pl.ds(pl.multiple_of(group * block, block), block), :], mine, own_sem
    )
    own_copy.start()
    both_ways(late.take_yx, 3)
    both_ways(late.take_late, 2)

    kept[...] = jnp.zeros_like(kept)

    @pl.loop(0, total // block)
    def _(step):
        here = pl.ds(pl.multiple_of(step * block, block), block)
        for at in range(0, total // block):
            columns = pl.ds(at * block, block)
            lower = jnp.where(
                ranks[here, :] < tags[at, 1:2, :].astype(F32), 1.0, 0.0
            ).astype(BF16)
            kept[:, columns] += mxu(picks[:, here], lower)

    kept[...] = jnp.where((picks[...].astype(F32) > 0.0) & (kept[...] < CAP), 1.0, 0.0)

    both_ways(late.take_diagonal, 2)
    both_ways(late.take_late, 3)

    @pl.loop(1, 8)
    def _(step):
        block_copy(step).wait_send()
        source = (group + 8 - step) % 8
        there = att_rows.at[:, pl.ds(pl.multiple_of(source * dim, dim), dim)]
        arrive(there, recv_sem.at[step])

    own_copy.wait()

    @pl.loop(0, width // 256)
    def _(step):
        columns = pl.ds(pl.multiple_of(step * 256, 256), 256)
        partial_sum[:, columns] = mxu(att_rows[...], out_weight[:, columns]).astype(BF16)

    def rows_of(dx, dc):
        _, there = spot.device(0, 0, dx, dc)
        return partial_sum.at[pl.ds(pl.multiple_of(there * count, count), count), :]

    to_x, to_c = spot.device(0, 0, 1), spot.device(0, 0, 0, 1)
    for dx in (1, 0):
        push(rows_of(dx, 1), from_core.at[dx], tensor_sems.at[dx], tensor_sems.at[2 + dx], to_c)
    arrive(from_core.at[1], tensor_sems.at[3])
    to_x_sum[...] = (rows_of(1, 0)[...].astype(F32) + from_core[1].astype(F32)).astype(BF16)
    push(to_x_sum, from_x, tensor_sems.at[4], tensor_sems.at[5], to_x)
    both_ways(late.take_diagonal, 3)
    arrive(from_core.at[0], tensor_sems.at[2])
    arrive(from_x, tensor_sems.at[5])
    branch = rows_of(0, 0)[...].astype(F32) + from_core[0].astype(F32) + from_x[...].astype(F32)
    sum_rows = hidden[own, :].astype(F32) + branch
    residual[...] = sum_rows
    root = lax.rsqrt(jnp.mean(sum_rows * sum_rows, axis=-1, keepdims=True) + EPS)
    normed[...] = (sum_rows * root * second_gain[...]).astype(BF16)
    for at, view in ((0, from_core.at[0]), (1, from_core.at[1]), (4, from_x)):
        arrive(view, tensor_sems.at[at])
    for step in (6, 7):
        stage_copy(step).wait()
    gather.drain()
    late.local.wait()
    for far in range(4):
        for dx in (0, 1):
            late.take_core(far, 1, dx)

            @pl.when(spot.z != far)
            def _(far=far, dx=dx):
                late.take_core(far, 0, dx)

    late.drain()
    for dz in range(-3, 4):

        def action(dz=dz):
            arrive(tag_place(dz, 0), tag_y_send.at[dz + 3])
            for side, step in ((0, 1), (1, -1)):
                if dz * step <= 0:

                    @pl.when(spot.has(step))
                    def _(side=side):
                        arrive(tag_place(dz, 0), tag_z_send.at[dz + 3, side])

        when_has(spot, dz, action)


def front(
    hidden, cotangent, tag, lengths, gain, w_query, w_key, w_value, q_gain, k_gain, inverse,
    w_out, second_gain, expert_count,
):
    block, width = hidden.shape
    total, count, dim = 8 * block, block // 4, w_key.shape[1]
    shape, vmem = jax.ShapeDtypeStruct, pltpu.VMEM
    smem = pl.BlockSpec(memory_space=pltpu.SMEM)
    small = (total, dim)
    return pl.pallas_call(
        front_kernel,
        out_shape=(
            shape((total, width), BF16), shape(small, BF16), shape(small, BF16),
            shape(small, BF16), shape((total, 2 * dim), F32), shape(small, F32),
            shape(small, F32), shape(small, BF16), shape((1, total), F32),
            shape((1, total), F32), shape((1, total), F32), shape((total, 1), F32),
            shape((count, width), F32), shape((count, width), BF16),
            shape((expert_count, total), F32), shape((expert_count, total), F32),
            shape((total, width), BF16),
        ),
        in_specs=[VMEM_SPEC, VMEM_SPEC, VMEM_SPEC, smem, VMEM_SPEC, HBM_SPEC, HBM_SPEC, HBM_SPEC,
                  VMEM_SPEC, VMEM_SPEC, VMEM_SPEC, HBM_SPEC, VMEM_SPEC],
        out_specs=(HBM_SPEC,) + (VMEM_SPEC,) * 15 + (HBM_SPEC,),
        scratch_shapes=[
            vmem((total, width), BF16), vmem((width, 3 * dim), BF16), vmem((8 * dim, width), BF16),
            vmem((2, block, width), BF16), vmem((8, 16, block), jnp.int32), vmem((total, 1), F32),
            vmem((expert_count, total), BF16), vmem((block, 8 * dim), BF16),
            vmem((block, width), BF16), vmem((2, count, width), BF16), vmem((count, width), BF16),
            vmem((count, width), BF16),
        ]
        + dma_sems(
            ((4,), (2,), (7,), (7,), (7, 2), (7,), None, (8,), (8,), None, (6,)) + Gather.SEMS * 2
        ),
        compiler_params=pltpu.CompilerParams(
            collective_id=1, has_side_effects=True, vmem_limit_bytes=62 << 20
        ),
        name="front",
        cost_estimate=cost(8_000_000_000, 90),
    )(
        hidden, cotangent, tag, lengths, gain, w_query, w_key, w_value, q_gain, k_gain, inverse,
        w_out, second_gain,
    )


def settle_kernel(*refs):
    half = len(refs) // 2
    for source, target in zip(refs[:half], refs[half:]):
        target[...] = source[...]


def settle(*arrays):
    width = arrays[0].shape[-1]
    flat = [v.reshape(-1, width) for v in arrays]
    steps = 6
    blocks = [pl.BlockSpec((v.shape[0] // steps, width), lambda i: (i, 0)) for v in flat]
    out = pl.pallas_call(
        settle_kernel,
        grid=(steps,),
        out_shape=tuple(jax.ShapeDtypeStruct(v.shape, v.dtype) for v in flat),
        in_specs=blocks,
        out_specs=tuple(blocks),
        cost_estimate=cost(0, 6),
        compiler_params=pltpu.CompilerParams(vmem_limit_bytes=32 << 20),
        name="settle",
    )(*flat)
    return tuple(v.reshape(w.shape) for v, w in zip(out, arrays))


def swap(value, bits):
    return lax.ppermute(
        value, ("expert", "tensor"), [(device, device ^ bits) for device in range(32)]
    )


def pair_sums(own, first, second, third):
    own, first, second, third = (v.astype(jnp.float32) for v in (own, first, second, third))
    return (own + first) + (second + third)


def in_order(rows, by_core, by_x, by_both):
    part = lax.axis_index("tensor")

    def ordered(first, second, bit):
        swapped = part // bit % 2 == 1
        return jnp.concatenate(
            [jnp.where(swapped, second, first), jnp.where(swapped, first, second)], axis=0
        )

    return ordered(ordered(rows, by_core, 1), ordered(by_x, by_both, 1), 2)


def head_device(
    hidden_in,
    cotangent,
    layout,
    seq_lengths,
    expert_ids,
    drop_rank,
    norm1_gain,
    w_query,
    key_weight,
    value_weight,
    query_gain,
    key_gain,
    w_out,
    norm2_gain,
    w_router,
    w_gate,
    w_up,
    w_down,
):
    f32, bf16 = jnp.float32, jnp.bfloat16
    tok_rows, model_width = hidden_in.shape
    head_dim = query_gain.shape[0]
    expert_count = w_router.shape[1]
    local_count, _, ff_local = w_gate.shape
    groups = lax.axis_size("expert")
    tensor_size = lax.axis_size("tensor")
    total_rows = groups * tok_rows
    own_rows = tok_rows // tensor_size
    group = lax.axis_index("expert")
    part = lax.axis_index("tensor")

    def own(rows):
        return lax.dynamic_slice_in_dim(rows, part * own_rows, own_rows, 0)

    tag = jnp.concatenate(
        [layout[None], drop_rank[None], expert_ids.T, jnp.zeros((6, tok_rows), jnp.int32)], axis=0
    )
    half_dim = head_dim // 2
    inverse = THETA ** (-(jnp.arange(half_dim, dtype=f32) * 2.0) / head_dim)
    q_gain, k_gain = query_gain[None], key_gain[None]
    (
        normed1, queries, keys, values, lin, cosine, sine, attended, log_total,
        place_row, open_row, place_column, residual, normed2, chosen, kept, grad_y_all,
    ) = front(
        hidden_in, cotangent, tag, seq_lengths, norm1_gain[None], w_query, key_weight,
        value_weight, q_gain, k_gain, jnp.concatenate([inverse, inverse])[None], w_out,
        norm2_gain[None], expert_count,
    )
    turn = lambda v: jnp.transpose(v, (0, 2, 1))
    back, grad_gate, grad_up, grad_down = experts(
        normed2, grad_y_all, turn(w_gate), turn(w_up), w_down.reshape(-1, model_width),
        w_router.T, chosen, kept,
    )
    out_own = (residual + back[:, :model_width]).astype(bf16)
    back = back[:, model_width:]

    start = group * tok_rows + part * own_rows
    chosen_own = lax.dynamic_slice_in_dim(chosen, start, own_rows, 1).T
    logits = jnp.dot(normed2, w_router, preferred_element_type=f32)
    soft_own = jax.nn.softmax(jnp.where(chosen_own > 0.0, logits, -jnp.inf), axis=1)
    grad_soft = back[:, model_width : model_width + expert_count]
    grad_logits = (
        soft_own * (grad_soft - jnp.sum(soft_own * grad_soft, axis=1, keepdims=True))
    ).astype(bf16)
    grad_router = jnp.einsum("td,te->de", normed2, grad_logits, preferred_element_type=f32)
    grad_normed2 = back[:, :model_width] + jnp.einsum(
        "te,de->td", grad_logits, w_router, preferred_element_type=f32
    )
    norm2_pull = jax.vjp(norm_rows, residual, norm2_gain)[1]
    grad_resid_norm, grad_norm2 = norm2_pull(grad_normed2)
    grad_residual = own(cotangent).astype(f32) + grad_resid_norm
    small = jnp.concatenate([grad_router.T, grad_norm2[None]], axis=0).astype(bf16)
    small = lax.optimization_barrier(small)
    far_part = swap(small, 16)

    grad_lin, grad_out, grad_qgain, grad_kgain = attend_back(
        grad_residual.astype(bf16), w_out, queries, keys, values, attended, lin, cosine, sine,
        place_column, place_row, open_row, log_total, k_gain, q_gain,
    )
    small = (small.astype(f32) + far_part.astype(f32)).astype(bf16)
    grad_lin, small, out_own = lax.optimization_barrier((grad_lin, small, out_own))
    near_part = swap(small, 8)
    out_by_x, out_by_core = swap(out_own, 2), swap(out_own, 1)
    gains = jnp.concatenate(
        [grad_qgain, grad_kgain, jnp.zeros((1, model_width - 2 * head_dim), f32)], axis=1
    )
    reduced, grad_kv, grad_query, grad_out = close(
        normed1, grad_lin, w_query, key_weight, value_weight, grad_out
    )
    reduced, near_part, out_by_x = lax.optimization_barrier((reduced, near_part, out_by_x))
    small = small.astype(f32) + near_part.astype(f32)
    norm1_pull = jax.vjp(norm_rows, own(hidden_in).astype(f32), norm1_gain)[1]
    grad_hidden_norm, grad_norm1 = norm1_pull(reduced)
    late_sums = jnp.concatenate([grad_norm1[None], gains], axis=0)
    hidden_rows = (grad_residual + grad_hidden_norm).astype(bf16)
    grad_query, hidden_rows, late_sums = lax.optimization_barrier(
        (grad_query, hidden_rows, late_sums)
    )
    by_x, by_core = swap(hidden_rows, 2), swap(hidden_rows, 1)
    moved = [swap(late_sums, 8 * step) for step in (1, 2, 3)]
    out_by_both = swap(out_by_x, 1)
    grad_query = grad_query.astype(f32)
    grad_query, grad_out, moved = lax.optimization_barrier((grad_query, grad_out, moved))
    small = jnp.concatenate([small, pair_sums(late_sums, *moved)], axis=0).astype(bf16)
    small = lax.optimization_barrier(small)
    moved = [swap(small, 2 * step) for step in (1, 2, 3)]
    grad_out, grad_kv = grad_out.astype(f32), grad_kv.astype(f32)
    out_hidden = in_order(out_own, out_by_core, out_by_x, out_by_both)
    grads = (grad_gate, grad_up, grad_down)
    grad_out, grad_kv, out_hidden, by_x, moved, grads = lax.optimization_barrier(
        (grad_out, grad_kv, out_hidden, by_x, moved, grads)
    )
    small = pair_sums(small, *moved)
    moved, by_both = swap(small, 1), swap(by_x, 1)
    grads = settle(*grads)
    grads, moved, by_both = lax.optimization_barrier((grads, moved, by_both))
    grad_gate, grad_up, grad_down = grads
    small = small + moved
    grad_hidden = in_order(hidden_rows, by_core, by_x, by_both)
    grad_norm1 = small[expert_count + 1]
    grad_router, grad_norm2 = small[:expert_count].T, small[expert_count]
    grad_qgain, grad_kgain = jnp.split(small[expert_count + 2, : 2 * head_dim], 2)
    grad_down = grad_down.reshape(local_count, ff_local, model_width)
    return (
        out_hidden,
        grad_hidden,
        grad_norm1,
        grad_query,
        grad_kv[:, :head_dim],
        grad_kv[:, head_dim:],
        grad_qgain,
        grad_kgain,
        grad_out,
        grad_norm2,
        grad_router,
        turn(grad_gate),
        turn(grad_up),
        grad_down,
    )


def solution(mesh):
    groups = mesh.shape["expert"]

    def device_fn(*operands):
        heads = operands[7].shape[1] // operands[10].shape[0]
        one_head = heads == groups == 8 and operands[8].shape[1] == operands[10].shape[0]
        one_head = one_head and mesh.shape["tensor"] == 4
        return (head_device if one_head else per_device)(*operands)

    return jax.shard_map(
        device_fn,
        mesh=mesh,
        in_specs=(
            P("expert", None),
            P("expert", None),
            P("expert"),
            P(),
            P("expert", None),
            P("expert"),
            P(),
            P(None, "tensor"),
            P(None, "tensor"),
            P(None, "tensor"),
            P(),
            P(),
            P("tensor", None),
            P(),
            P(),
            P("expert", None, "tensor"),
            P("expert", None, "tensor"),
            P("expert", "tensor", None),
        ),
        out_specs=(
            P("expert", None),
            P("expert", None),
            P(),
            P(None, "tensor"),
            P(None, "tensor"),
            P(None, "tensor"),
            P(),
            P(),
            P("tensor", None),
            P(),
            P(),
            P("expert", None, "tensor"),
            P("expert", None, "tensor"),
            P("expert", "tensor", None),
        ),
        check_vma=False,
    )
```

```python
from functools import partial
import math

import jax
import jax.numpy as jnp
from jax import lax
from jax.experimental import pallas as pl
from jax.experimental.pallas import tpu as pltpu
from jax.sharding import PartitionSpec as P

TOPK = 8
CAP = 1280


EPS = 1e-06
THETA = 1000000.0
NEG = -1e30


def norm_rows(value_matrix, gain):
    return (
        value_matrix
        * lax.rsqrt(jnp.mean(value_matrix * value_matrix, axis=-1, keepdims=True) + EPS)
        * gain
    )


def rotary(value_matrix, position):
    half_dim = value_matrix.shape[-1] // 2
    inverse = THETA ** (-(jnp.arange(half_dim, dtype=jnp.float32) * 2.0) / value_matrix.shape[-1])
    angles = position.astype(jnp.float32)[:, None] * inverse[None, :]
    cosine_table = jnp.concatenate([jnp.cos(angles), jnp.cos(angles)], axis=-1)[:, None, :]
    sine_table = jnp.concatenate([jnp.sin(angles), jnp.sin(angles)], axis=-1)[:, None, :]
    turned = jnp.concatenate([-value_matrix[..., half_dim:], value_matrix[..., :half_dim]], axis=-1)
    return value_matrix * cosine_table + turned * sine_table


def shape_queries(linear, gain, position):
    head_dim = gain.shape[0]
    shaped = linear.reshape(linear.shape[0], linear.shape[1] // head_dim, head_dim)
    return rotary(norm_rows(shaped, gain), position) * head_dim ** (-0.5)


def shape_keys(linear, gain, position):
    head_dim = gain.shape[0]
    shaped = linear.reshape(linear.shape[0], linear.shape[1] // head_dim, head_dim)
    return rotary(norm_rows(shaped, gain), position)


def token_tables(token_position, seq_lengths):
    bounds = jnp.cumsum(seq_lengths)
    passed = token_position[:, None] >= bounds[None, :]
    segment_ids = jnp.sum(passed.astype(jnp.int32), axis=1)
    opening = jnp.max(jnp.where(passed, bounds[None, :], 0), axis=1)
    return (segment_ids, (token_position - opening).astype(jnp.int32))


def visible(query_segment, query_place, key_segment, key_place):
    return (query_segment[:, None] == key_segment[None, :]) & (
        key_place[None, :] <= query_place[:, None]
    )


def deliver(payload, slot_ids):
    return (
        lax.all_to_all(payload, "expert", split_axis=0, concat_axis=0, tiled=True),
        lax.all_to_all(slot_ids, "expert", split_axis=0, concat_axis=0, tiled=True),
    )


def bring_back(payload):
    return lax.all_to_all(payload, "expert", split_axis=0, concat_axis=0, tiled=True)


def expert_forward(entry_rows, w_gate, w_up, w_down):
    gate_lin = jnp.einsum("gesd,edf->gesf", entry_rows, w_gate, preferred_element_type=jnp.float32)
    up_lin = jnp.einsum("gesd,edf->gesf", entry_rows, w_up, preferred_element_type=jnp.float32)
    activation = (jax.nn.silu(gate_lin) * up_lin).astype(jnp.bfloat16)
    expert_out = jnp.einsum(
        "gesf,efd->gesd", activation, w_down, preferred_element_type=jnp.float32
    ).astype(jnp.bfloat16)
    return (gate_lin, up_lin, activation, expert_out)


def expert_backward(entry_rows, gate_lin, up_lin, activation, grad_in, w_gate, w_up, w_down):
    grad_down = jnp.einsum(
        "gesf,gesd->efd", activation, grad_in, preferred_element_type=jnp.float32
    )
    grad_act = jnp.einsum("gesd,efd->gesf", grad_in, w_down, preferred_element_type=jnp.float32)
    sigmoid = jax.nn.sigmoid(gate_lin)
    grad_gate_lin = (grad_act * up_lin * sigmoid * (1.0 + gate_lin * (1.0 - sigmoid))).astype(
        jnp.bfloat16
    )
    grad_up_lin = (grad_act * gate_lin * sigmoid).astype(jnp.bfloat16)
    grad_w_gate = jnp.einsum(
        "gesd,gesf->edf", entry_rows, grad_gate_lin, preferred_element_type=jnp.float32
    )
    grad_w_up = jnp.einsum(
        "gesd,gesf->edf", entry_rows, grad_up_lin, preferred_element_type=jnp.float32
    )
    grad_entry = jnp.einsum(
        "gesf,edf->gesd", grad_gate_lin, w_gate, preferred_element_type=jnp.float32
    )
    grad_entry = (
        grad_entry
        + jnp.einsum("gesf,edf->gesd", grad_up_lin, w_up, preferred_element_type=jnp.float32)
    ).astype(jnp.bfloat16)
    return (grad_entry, grad_w_gate, grad_w_up, grad_down)


def per_device(
    hidden_in,
    cotangent,
    layout,
    seq_lengths,
    expert_ids,
    drop_rank,
    norm1_gain,
    w_query,
    key_weight,
    value_weight,
    query_gain,
    key_gain,
    w_out,
    norm2_gain,
    w_router,
    w_gate,
    w_up,
    w_down,
):
    tok_rows = hidden_in.shape[0]
    model_width = hidden_in.shape[1]
    head_dim = query_gain.shape[0]
    local_heads = w_query.shape[1] // head_dim
    expert_count = w_router.shape[1]
    local_count = w_gate.shape[0]
    group_count = lax.axis_size("expert")
    slot_count = 2 * tok_rows * TOPK // expert_count
    seq_count = seq_lengths.shape[0]
    expert_range = jnp.arange(expert_count, dtype=jnp.int32)
    hidden = hidden_in.astype(jnp.float32)
    segment_ids, position = token_tables(layout, seq_lengths)
    valid = segment_ids < seq_count
    first_normalized = norm_rows(hidden, norm1_gain)
    normed1_low = first_normalized.astype(jnp.bfloat16)
    query_lin = jnp.dot(normed1_low, w_query, preferred_element_type=jnp.float32)
    key_lin = jnp.dot(normed1_low, key_weight, preferred_element_type=jnp.float32)
    value_lin = jnp.dot(normed1_low, value_weight, preferred_element_type=jnp.float32)
    query_shaped = shape_queries(query_lin, query_gain, position).astype(jnp.bfloat16)
    query_total = local_heads * tok_rows
    query_rows = jnp.transpose(query_shaped, (1, 0, 2)).reshape(query_total, head_dim)
    key_rows = (
        shape_keys(key_lin, key_gain, position).astype(jnp.bfloat16).reshape(tok_rows, head_dim)
    )
    value_rows = value_lin.astype(jnp.bfloat16)
    all_keys, all_values, all_place, all_ids, all_rank = (
        lax.all_gather(key_rows, "expert", axis=0, tiled=True),
        lax.all_gather(value_rows, "expert", axis=0, tiled=True),
        lax.all_gather(layout, "expert", axis=0, tiled=True),
        lax.all_gather(expert_ids, "expert", axis=0, tiled=True),
        lax.all_gather(drop_rank, "expert", axis=0, tiled=True),
    )
    all_segment = token_tables(all_place, seq_lengths)[0]
    rows_per_block = math.gcd(512, query_total)
    count_of_blocks = query_total // rows_per_block
    query_segment = jnp.tile(segment_ids, local_heads)
    query_place = jnp.tile(layout, local_heads)

    def attend_block(operands):
        query_block, segment_block, place_block = operands
        scores = jnp.einsum("qd,kd->qk", query_block, all_keys, preferred_element_type=jnp.float32)
        scores = jnp.where(visible(segment_block, place_block, all_segment, all_place), scores, NEG)
        highest = jnp.max(scores, axis=1, keepdims=True)
        weights = jnp.exp(scores - highest)
        totals = jnp.sum(weights, axis=1, keepdims=True)
        probability = (weights / totals).astype(jnp.bfloat16)
        mixed_out = jnp.dot(probability, all_values, preferred_element_type=jnp.float32)
        return (mixed_out, (highest + jnp.log(totals))[:, 0])

    attention_output, log_totals = lax.map(
        attend_block,
        (
            query_rows.reshape(count_of_blocks, rows_per_block, head_dim),
            query_segment.reshape(count_of_blocks, rows_per_block),
            query_place.reshape(count_of_blocks, rows_per_block),
        ),
    )
    attention_output = attention_output.reshape(local_heads, tok_rows, head_dim).astype(
        jnp.bfloat16
    )
    att_cat = jnp.transpose(attention_output, (1, 0, 2)).reshape(tok_rows, local_heads * head_dim)
    branch_part = jnp.dot(att_cat, w_out, preferred_element_type=jnp.float32)
    branch = lax.psum(branch_part, "tensor")
    residual = hidden + branch
    normed2 = norm_rows(residual, norm2_gain)
    normed2_low = normed2.astype(jnp.bfloat16)
    logits = jnp.dot(normed2_low, w_router, preferred_element_type=jnp.float32)
    soft_gate = jax.nn.softmax(jnp.take_along_axis(logits, expert_ids, axis=1), axis=1)
    picks = jnp.any(expert_ids[:, :, None] == expert_range, axis=1) & valid[:, None]
    all_valid = all_segment < seq_count
    all_picks = jnp.any(all_ids[:, :, None] == expert_range, axis=1) & all_valid[:, None]
    earlier = (all_rank[None, :] < drop_rank[:, None]).astype(jnp.bfloat16)
    before_counts = jnp.dot(
        earlier, all_picks.astype(jnp.bfloat16), preferred_element_type=jnp.float32
    )
    global_slot = jnp.take_along_axis(before_counts, expert_ids, axis=1).astype(jnp.int32)
    kept_mask = (global_slot < CAP) & valid[:, None]
    gate_weight = soft_gate * kept_mask.astype(jnp.float32)
    lower_rows = (jnp.arange(tok_rows)[None, :] < jnp.arange(tok_rows)[:, None]).astype(
        jnp.bfloat16
    )
    local_counts = jnp.dot(
        lower_rows, picks.astype(jnp.bfloat16), preferred_element_type=jnp.float32
    )
    local_slot = jnp.take_along_axis(local_counts, expert_ids, axis=1).astype(jnp.int32)
    pair_count = tok_rows * TOPK
    dump_index = expert_count * slot_count
    target = jnp.where(kept_mask, expert_ids * slot_count + local_slot, dump_index)
    pair_index = jnp.arange(pair_count, dtype=jnp.int32)
    slot_pair = (
        jnp.full((dump_index,), pair_count, jnp.int32)
        .at[target.reshape(-1)]
        .set(pair_index, mode="drop")
    )
    slot_token = jnp.where(slot_pair < pair_count, slot_pair // TOPK, tok_rows)
    slot_global = (
        jnp.full((dump_index,), -1, jnp.int32)
        .at[target.reshape(-1)]
        .set(global_slot.reshape(-1), mode="drop")
    )
    padded_rows = jnp.concatenate([normed2_low, jnp.zeros((1, model_width), jnp.bfloat16)], axis=0)
    send_rows = padded_rows[slot_token].reshape(group_count, local_count, slot_count, model_width)
    send_slot = slot_global.reshape(group_count, local_count, slot_count)
    received, received_slot = deliver(send_rows, send_slot)
    gate_lin, up_lin, activation, expert_out = expert_forward(received, w_gate, w_up, w_down)
    returned = bring_back(expert_out)
    returned_flat = jnp.concatenate(
        [returned.reshape(dump_index, model_width), jnp.zeros((1, model_width), returned.dtype)],
        axis=0,
    )
    pair_out = returned_flat[target]
    moe_part = jnp.sum(gate_weight[:, :, None] * pair_out, axis=1)
    moe_branch = lax.psum(moe_part.astype(jnp.bfloat16), "tensor").astype(jnp.float32)
    out_hidden = (residual + moe_branch).astype(jnp.bfloat16)
    grad_y = cotangent.astype(jnp.float32)
    gate_dot = jnp.sum(grad_y[:, None, :] * pair_out, axis=2)
    pair_grads = (
        (gate_weight[:, :, None] * grad_y[:, None, :])
        .astype(jnp.bfloat16)
        .reshape(pair_count, model_width)
    )
    pair_grads = jnp.concatenate([pair_grads, jnp.zeros((1, model_width), jnp.bfloat16)], axis=0)
    send_grad = pair_grads[slot_pair].reshape(group_count, local_count, slot_count, model_width)
    grad_received, grad_slot = deliver(send_grad, send_slot)
    grad_entry, grad_w_gate, grad_w_up, grad_w_down = expert_backward(
        received, gate_lin, up_lin, activation, grad_received, w_gate, w_up, w_down
    )
    grad_returned = bring_back(grad_entry)
    grad_flat = jnp.concatenate(
        [
            grad_returned.reshape(dump_index, model_width),
            jnp.zeros((1, model_width), grad_returned.dtype),
        ],
        axis=0,
    )
    grad_normed2_part = jnp.sum(grad_flat[target], axis=1, dtype=jnp.float32)
    grad_normed2_exp, gate_dot = lax.psum((grad_normed2_part, gate_dot), "tensor")
    grad_soft = gate_dot * kept_mask.astype(jnp.float32)
    grad_chosen = soft_gate * (grad_soft - jnp.sum(soft_gate * grad_soft, axis=1, keepdims=True))
    grad_logits = jnp.sum(
        grad_chosen[:, :, None] * (expert_ids[:, :, None] == expert_range).astype(jnp.float32),
        axis=1,
    ).astype(jnp.bfloat16)
    grad_w_router = jnp.einsum(
        "td,te->de", normed2_low, grad_logits, preferred_element_type=jnp.float32
    )
    grad_normed2 = grad_normed2_exp + jnp.einsum(
        "te,de->td", grad_logits, w_router, preferred_element_type=jnp.float32
    )
    norm2_pull = jax.vjp(norm_rows, residual, norm2_gain)[1]
    grad_resid_norm, grad_norm2 = norm2_pull(grad_normed2)
    grad_residual = grad_y + grad_resid_norm
    grad_residual_low = grad_residual.astype(jnp.bfloat16)
    grad_w_out = jnp.einsum(
        "tc,td->cd", att_cat, grad_residual_low, preferred_element_type=jnp.float32
    )
    grad_att_cat = jnp.einsum(
        "td,cd->tc", grad_residual_low, w_out, preferred_element_type=jnp.float32
    ).astype(jnp.bfloat16)
    grad_att_rows = jnp.transpose(
        grad_att_cat.reshape(tok_rows, local_heads, head_dim), (1, 0, 2)
    ).reshape(query_total, head_dim)

    def query_grad_block(operands):
        query_block, segment_block, place_block, grad_block, log_block = operands
        scores = jnp.einsum("qd,kd->qk", query_block, all_keys, preferred_element_type=jnp.float32)
        scores = jnp.where(visible(segment_block, place_block, all_segment, all_place), scores, NEG)
        probability = jnp.exp(scores - log_block[:, None])
        grad_prob = jnp.einsum(
            "qd,kd->qk", grad_block, all_values, preferred_element_type=jnp.float32
        )
        delta_row = jnp.sum(probability * grad_prob, axis=1)
        grad_scores = (probability * (grad_prob - delta_row[:, None])).astype(jnp.bfloat16)
        return (jnp.dot(grad_scores, all_keys, preferred_element_type=jnp.float32), delta_row)

    grad_query_rows, deltas = lax.map(
        query_grad_block,
        (
            query_rows.reshape(count_of_blocks, rows_per_block, head_dim),
            query_segment.reshape(count_of_blocks, rows_per_block),
            query_place.reshape(count_of_blocks, rows_per_block),
            grad_att_rows.reshape(count_of_blocks, rows_per_block, head_dim),
            log_totals,
        ),
    )
    log_flat = log_totals.reshape(query_total)
    delta_flat = deltas.reshape(query_total)
    key_block = math.gcd(lax.axis_size("expert") * tok_rows, 2048)

    def one_block(offset):
        key_part = lax.dynamic_slice_in_dim(all_keys, offset, key_block, 0)
        value_part = lax.dynamic_slice_in_dim(all_values, offset, key_block, 0)
        segment_part = lax.dynamic_slice_in_dim(all_segment, offset, key_block, 0)
        place_part = lax.dynamic_slice_in_dim(all_place, offset, key_block, 0)
        scores = jnp.einsum("qd,kd->qk", query_rows, key_part, preferred_element_type=jnp.float32)
        scores = jnp.where(
            visible(query_segment, query_place, segment_part, place_part), scores, NEG
        )
        probability = jnp.exp(scores - log_flat[:, None])
        grad_value = jnp.einsum(
            "qk,qd->kd",
            probability.astype(jnp.bfloat16),
            grad_att_rows,
            preferred_element_type=jnp.float32,
        )
        grad_prob = jnp.einsum(
            "qd,kd->qk", grad_att_rows, value_part, preferred_element_type=jnp.float32
        )
        grad_scores = (probability * (grad_prob - delta_flat[:, None])).astype(jnp.bfloat16)
        grad_key = jnp.einsum(
            "qk,qd->kd", grad_scores, query_rows, preferred_element_type=jnp.float32
        )
        return jnp.concatenate([grad_key, grad_value], axis=1)

    stacked = lax.map(
        one_block,
        jnp.arange(lax.axis_size("expert") * tok_rows // key_block, dtype=jnp.int32) * key_block,
    )
    key_value_grad = lax.psum_scatter(
        stacked.reshape(lax.axis_size("expert") * tok_rows, 2 * head_dim).astype(jnp.bfloat16),
        "expert",
        scatter_dimension=0,
        tiled=True,
    ).astype(jnp.float32)
    grad_key_post = key_value_grad[:, :head_dim].reshape(tok_rows, 1, head_dim)
    grad_values_low = key_value_grad[:, head_dim:].astype(jnp.bfloat16)
    grad_query_tok = jnp.transpose(
        grad_query_rows.reshape(local_heads, tok_rows, head_dim), (1, 0, 2)
    )
    query_pull = jax.vjp(partial(shape_queries, position=position), query_lin, query_gain)[1]
    grad_query_lin, grad_qgain_part = query_pull(grad_query_tok)
    key_pull = jax.vjp(partial(shape_keys, position=position), key_lin, key_gain)[1]
    grad_key_lin, grad_kgain_part = key_pull(grad_key_post)
    grad_query_low = grad_query_lin.astype(jnp.bfloat16)
    grad_key_low = grad_key_lin.astype(jnp.bfloat16)
    grad_w_query = jnp.einsum(
        "td,tc->dc", normed1_low, grad_query_low, preferred_element_type=jnp.float32
    )
    grad_w_key = jnp.einsum(
        "td,tc->dc", normed1_low, grad_key_low, preferred_element_type=jnp.float32
    )
    grad_w_value = jnp.einsum(
        "td,tc->dc", normed1_low, grad_values_low, preferred_element_type=jnp.float32
    )
    grad_normed1_part = jnp.einsum(
        "tc,dc->td", grad_query_low, w_query, preferred_element_type=jnp.float32
    )
    grad_normed1_part = grad_normed1_part + jnp.einsum(
        "tc,dc->td", grad_key_low, key_weight, preferred_element_type=jnp.float32
    )
    grad_normed1_part = grad_normed1_part + jnp.einsum(
        "tc,dc->td", grad_values_low, value_weight, preferred_element_type=jnp.float32
    )
    grad_normed1, grad_qgain_part, grad_kgain_part = (
        lax.psum(grad_normed1_part.astype(jnp.bfloat16), "tensor").astype(jnp.float32),
        lax.psum(grad_qgain_part.astype(jnp.bfloat16), "tensor").astype(jnp.float32),
        lax.psum(grad_kgain_part.astype(jnp.bfloat16), "tensor").astype(jnp.float32),
    )
    norm1_pull = jax.vjp(norm_rows, hidden, norm1_gain)[1]
    grad_hidden_norm, grad_norm1 = norm1_pull(grad_normed1)
    grad_hidden = (grad_residual + grad_hidden_norm).astype(jnp.bfloat16)
    summed = (
        lax.psum(grad_norm1.astype(jnp.bfloat16), "expert").astype(jnp.float32),
        lax.psum(grad_w_query.astype(jnp.bfloat16), "expert").astype(jnp.float32),
        lax.psum(grad_w_key.astype(jnp.bfloat16), "expert").astype(jnp.float32),
        lax.psum(grad_w_value.astype(jnp.bfloat16), "expert").astype(jnp.float32),
        lax.psum(grad_qgain_part.astype(jnp.bfloat16), "expert").astype(jnp.float32),
        lax.psum(grad_kgain_part.astype(jnp.bfloat16), "expert").astype(jnp.float32),
        lax.psum(grad_w_out.astype(jnp.bfloat16), "expert").astype(jnp.float32),
        lax.psum(grad_norm2.astype(jnp.bfloat16), "expert").astype(jnp.float32),
        lax.psum(grad_w_router.astype(jnp.bfloat16), "expert").astype(jnp.float32),
    )
    return (
        out_hidden,
        grad_hidden,
        summed[0],
        summed[1],
        summed[2],
        summed[3],
        summed[4],
        summed[5],
        summed[6],
        summed[7],
        summed[8],
        grad_w_gate,
        grad_w_up,
        grad_w_down,
    )


MESH = pl.DeviceIdType.MESH
FAR_FIRST = (3, -3, 2, -2, 1, -1, 0)


class Spot:
    def __init__(self):
        group, part = lax.axis_index("expert"), lax.axis_index("tensor")
        self.z, self.y = group // 2, group % 2
        self.x, self.c = part // 2, part % 2

    def has(self, dz):
        return (self.z + dz >= 0) & (self.z + dz <= 3)

    def device(self, dz=0, dy=0, dx=0, dc=0):
        y = 1 - self.y if dy else self.y
        x = 1 - self.x if dx else self.x
        c = 1 - self.c if dc else self.c
        return ((self.z + dz) * 2 + y, x * 2 + c)

    def rows(self, dz, dy, dx, dc, count):
        group, part = self.device(dz, dy, dx, dc)
        return pl.ds(pl.multiple_of((group * 4 + part) * count, count), count)

    def greet(self, line=False):
        barrier = pltpu.get_barrier_semaphore()
        for step in ((0, 1, 0, 0), (0, 0, 1, 0), (0, 0, 0, 1)):
            pl.semaphore_signal(barrier, inc=1, device_id=self.device(*step), device_id_type=MESH)
        for dz in (1, -1, 2, -2, 3, -3) if line else (1, -1):

            @pl.when(self.has(dz))
            def _(dz=dz):
                pl.semaphore_signal(
                    barrier, inc=1, device_id=self.device(dz), device_id_type=MESH
                )

        if line:
            pl.semaphore_wait(barrier, 6)
        else:
            inner = jnp.where((self.z > 0) & (self.z < 3), 1, 0)
            pl.semaphore_wait(barrier, 4 + inner)


def when_has(spot, dz, action):
    if dz == 0:
        action()
    else:
        pl.when(spot.has(dz))(action)


def dma_sems(shapes):
    return [pltpu.SemaphoreType.DMA(shape) if shape else pltpu.SemaphoreType.DMA for shape in shapes]


def add_into(into, chunk, *terms):
    @pl.loop(0, into.shape[0] // chunk)
    def _(step):
        rows = pl.ds(pl.multiple_of(step * chunk, chunk), chunk)
        for at in range(0, into.shape[1], 1024):
            columns = pl.ds(at, min(1024, into.shape[1] - at))
            total = into[rows, columns].astype(jnp.float32)
            for term in terms:
                total = total + term[rows, columns].astype(jnp.float32)
            into[rows, columns] = total.astype(into.dtype)


def push(src, dst, send_sem, recv_sem, device):
    pltpu.make_async_remote_copy(
        src_ref=src,
        dst_ref=dst,
        send_sem=send_sem,
        recv_sem=recv_sem,
        device_id=device,
        device_id_type=MESH,
    ).start()


def arrive(view, sem):
    pltpu.make_async_copy(view, view, sem).wait()


F32, BF16 = jnp.float32, jnp.bfloat16
VMEM_SPEC = pl.BlockSpec(memory_space=pltpu.VMEM)
HBM_SPEC = pl.BlockSpec(memory_space=pl.ANY)


def cost(flops, microseconds):
    return pl.CostEstimate(
        flops=flops, bytes_accessed=microseconds * 3_000_000, transcendentals=0
    )


def mxu(left, right, left_dim=1, right_dim=0):
    return lax.dot_general(
        left, right, (((left_dim,), (right_dim,)), ((), ())), preferred_element_type=F32
    )


def head_norm(lin):
    root = lax.rsqrt(jnp.mean(lin * lin, axis=-1, keepdims=True) + EPS)
    return lin * root, root


def near_first(step, z):
    high = z // 2
    folded = z + high * (3 - 2 * z)
    place = (step + folded * (1 - step // 2)) % 2 + 2 * (step // 2)
    return place + high * (3 - 2 * place)


class Gather:
    SEMS = ((5, 7), (7, 2), (6,), (7, 2, 2), None, (7, 2), (7, 2, 2))

    def __init__(
        self, spot, src, out, recv, z_send, sends, c_recv, local_sem, late_recv, late_send, full=None, share=5
    ):
        self.spot, self.src, self.out, self.full = spot, src, out, full
        self.recv, self.z_send, self.sends, self.c_recv = recv, z_send, sends, c_recv
        self.late_recv, self.late_send = late_recv, late_send
        self.count, self.width = src.shape
        width, late = self.width, self.width * share // 16
        self.share = share
        half = width * 5 // 8 if full is not None else width // 2
        self.first, self.second = pl.ds(0, half), pl.ds(half, width - half)
        self.whole = pl.ds(0, width)
        self.early = (pl.ds(0, width - late), pl.ds(late, width - late))
        self.late = (pl.ds(width - late, late), pl.ds(0, late))
        if full is None:
            self.local = pltpu.make_async_copy(src, self.place(0, 0, 0), local_sem)
        else:
            group, _ = spot.device()
            rows = pl.ds(pl.multiple_of(group * 4 * self.count, 4 * self.count), 4 * self.count)
            self.local = pltpu.make_async_copy(full, out.at[rows, :], local_sem)

    def place(self, dz, dy, dx, dc=0, columns=None):
        rows = self.spot.rows(dz, dy, dx, dc, self.count)
        return self.out.at[rows, self.whole if columns is None else columns]

    def source(self, dz, dy, dx, columns):
        if dz == 0 and dy == 0 and dx == 0:
            return self.src.at[:, columns]
        if dz == 0 and dy == 0 and self.full is not None:
            _, part = self.spot.device(0, 0, 1)
            rows = pl.ds(pl.multiple_of(part * self.count, self.count), self.count)
            return self.full.at[rows, columns]
        return self.place(dz, dy, dx, 0, columns)

    def send(self, dz, dy, dx, columns, send_sem, recv_sem, device):
        push(
            self.source(dz, dy, dx, columns), self.place(dz, dy, dx, 0, columns), send_sem,
            recv_sem, device,
        )

    def to_core(self, dz, dy, dx):
        if dz == 0 and dy == 0 and self.full is not None:
            return
        self.send(
            dz, dy, dx, self.whole, self.sends.at[0], self.c_recv.at[dz + 3, dy, dx],
            self.spot.device(0, 0, 0, 1),
        )

    def along_z(self, dz, dy, dx, columns, send_sem, recv_sem):
        for side, step in ((0, 1), (1, -1)):
            if dz * step <= 0:

                @pl.when(self.spot.has(step))
                def _(side=side, step=step):
                    self.send(
                        dz, dy, dx, columns, send_sem(side), recv_sem(dz + 3 - step),
                        self.spot.device(step),
                    )

    def spread(self, dz):
        spot = self.spot
        self.along_z(
            dz, 0, 0, self.whole, lambda side: self.z_send.at[dz + 3, side],
            lambda at: self.recv.at[0, at],
        )
        if dz == 0:
            columns, at = (self.whole, self.whole), 0
        else:
            columns, at = self.early, 3
        self.send(
            dz, 0, 0, columns[0], self.sends.at[1 + at], self.recv.at[1, dz + 3], spot.device(0, 1)
        )
        if dz != 0 or self.full is None:
            self.send(
                dz, 0, 0, columns[1], self.sends.at[2 + at], self.recv.at[2, dz + 3],
                spot.device(0, 0, 1),
            )
        self.to_core(dz, 0, 0)

    def start(self):
        self.local.start()
        self.spread(0)

    def take_z(self, dz):
        def action():
            arrive(self.place(dz, 0, 0), self.recv.at[0, dz + 3])
            self.spread(dz)

        when_has(self.spot, dz, action)

    def take_yx(self, dz):
        spot = self.spot

        def action():
            columns = self.early if dz else (self.whole, self.whole)
            arrive(self.place(dz, 1, 0, 0, columns[0]), self.recv.at[1, dz + 3])
            self.send(
                dz, 1, 0, self.first, self.sends.at[3], self.recv.at[3, dz + 3],
                spot.device(0, 0, 1),
            )
            if dz != 0 or self.full is None:
                arrive(self.place(dz, 0, 1, 0, columns[1]), self.recv.at[2, dz + 3])
            self.send(
                dz, 0, 1, self.second, self.sends.at[3], self.recv.at[4, dz + 3],
                spot.device(0, 1),
            )

        when_has(spot, dz, action)

    def take_late(self, dz):
        def action():
            for dy, dx in ((1, 0), (0, 1)):
                columns = self.late[dx]
                if self.share and dz != 0:
                    arrive(self.place(dz, dy, dx, 0, columns), self.late_recv.at[dz + 3, dx])
                if self.share:
                    self.along_z(
                        dz, dy, dx, columns, lambda side: self.late_send.at[dz + 3, side, dx],
                        lambda at: self.late_recv.at[at, dx],
                    )
                self.to_core(dz, dy, dx)

        when_has(self.spot, dz, action)

    def take_diagonal(self, dz):
        def action():
            arrive(self.place(dz, 1, 1, 0, self.first), self.recv.at[3, dz + 3])
            arrive(self.place(dz, 1, 1, 0, self.second), self.recv.at[4, dz + 3])
            self.to_core(dz, 1, 1)

        when_has(self.spot, dz, action)

    def take_core(self, far, dy, dx):
        view = self.out.at[pl.ds(0, self.count), :]
        arrive(view, self.c_recv.at[far - self.spot.z + 3, dy, dx])

    def drain(self):
        count, spot = self.count, self.spot
        replicated = self.full is not None
        for at, pieces, columns in (
            (0, 14 if replicated else 16, self.whole), (1, 1, self.whole), (2, 1, self.whole),
            (3, 4, self.whole), (4, 3, self.early[0]), (5, 3, self.early[1]),
        ):
            if at != 2 or not replicated:
                arrive(self.out.at[pl.ds(0, pieces * count), columns], self.sends.at[at])
        for dz in range(-3, 4):
            for side, step in ((0, 1), (1, -1)):
                if dz * step <= 0:

                    @pl.when(spot.has(dz) & spot.has(step))
                    def _(dz=dz, side=side):
                        arrive(self.place(0, 0, 0), self.z_send.at[dz + 3, side])
                        for at in (0, 1) if self.share else ():
                            arrive(
                                self.place(0, 0, 0, 0, self.late[at]),
                                self.late_send.at[dz + 3, side, at],
                            )


def experts_kernel(
    normed, grad_y, w_gate, w_up, w_down, router, chosen, kept,
    reduced, grad_gate, grad_up, grad_down,
    rows_all, weight, grad_in, grad_in_down, y_block, back_block,
    mine, other, from_a, from_b, from_y, from_x, from_z,
    weight_sem, y_sem, flush_sem, core_send, core_recv, half_send, yx_send, recv,
    line_send, line_recv, *gather_sems,
):
    spot = Spot()
    count, width = normed.shape
    wide = reduced.shape[1]
    local_count, ff, _ = w_gate.shape
    both = local_count * ff
    block = 4 * count
    split = from_a.shape[2]
    first, second = pl.ds(0, split), pl.ds(split, wide - split)
    group = lax.axis_index("expert")
    to_y, to_x, to_c = spot.device(0, 1), spot.device(0, 0, 1), spot.device(0, 0, 0, 1)

    def place_of(step):
        return near_first((step // 2 + 1) % 4, spot.z), (step + (step + 6) // 8) % 2

    def group_rows(step):
        far, dy = place_of(step)
        y = spot.y + dy * (1 - 2 * spot.y)
        return pl.ds(pl.multiple_of((far * 2 + y) * block, block), block)

    def y_copy(step):
        slot = step % 2
        return pltpu.make_async_copy(
            grad_y.at[group_rows(step), :], y_block.at[slot], y_sem.at[slot]
        )

    sources = [ref.at[at] for ref in (w_gate, w_up) for at in range(local_count)]
    weights = [
        pltpu.make_async_copy(source, weight.at[pl.ds(at * ff, ff), :], weight_sem.at[at])
        for at, source in enumerate(sources)
    ]
    for copy in weights:
        copy.start()
    y_copy(0).start()
    gather = Gather(spot, normed, rows_all, *gather_sems, share=7)
    spot.greet()
    gather.start()
    grad_in[...] = jnp.zeros_like(grad_in)
    grad_in_down[...] = jnp.zeros_like(grad_in_down)
    gather.local.wait()
    for copy in weights:
        copy.wait()

    def piece(dx, dc):
        _, part = spot.device(0, 0, dx, dc)
        return pl.ds(pl.multiple_of(part * count, count), count)

    def core_copy(step, dx):
        far, dy = place_of(step)
        slot = step % 2
        return pltpu.make_async_remote_copy(
            src_ref=back_block.at[slot, piece(dx, 1), :],
            dst_ref=other.at[far, dy, dx],
            send_sem=core_send.at[slot, dx],
            recv_sem=core_recv.at[far, dy, dx],
            device_id=to_c,
            device_id_type=MESH,
        )

    def merge(far, dy, dx):
        into = mine.at[far, dy, dx]
        arrive(other.at[far, dy, dx], core_recv.at[far, dy, dx])
        return into

    def merge_diagonal(k):
        far = near_first(k, spot.z)
        into = merge(far, 1, 1)
        add_into(into, 16, other.at[far, 1, 1])
        push(into.at[:, first], from_a.at[far], half_send.at[0], recv.at[0, far], to_x)
        push(into.at[:, second], from_b.at[far], half_send.at[1], recv.at[1, far], to_y)

    def merge_yx(k):
        far = near_first(k, spot.z)
        into = merge(far, 1, 0)
        add_into(into, 16, other.at[far, 1, 0])
        arrive(from_a.at[far], recv.at[0, far])
        add_into(into.at[:, first], 16, from_a.at[far])
        push(into, from_y.at[far], yx_send.at[0], recv.at[2, far], to_y)
        into = merge(far, 0, 1)
        add_into(into, 16, other.at[far, 0, 1])
        arrive(from_b.at[far], recv.at[1, far])
        add_into(into.at[:, second], 16, from_b.at[far])
        push(into, from_x.at[far], yx_send.at[1], recv.at[3, far], to_x)

    def merge_line(k):
        far = near_first(k, spot.z)
        into = merge(far, 0, 0)
        arrive(from_y.at[far], recv.at[2, far])
        arrive(from_x.at[far], recv.at[3, far])
        add_into(into, 16, other.at[far, 0, 0], from_y.at[far], from_x.at[far])
        if k > 0:
            push(
                into, from_z.at[spot.z], line_send.at[k], line_recv.at[spot.z],
                (far * 2 + spot.y, spot.x * 2 + spot.c),
            )

    def both_ways(take, distance):
        for dz in (distance, -distance) if distance else (0,):
            take(dz)

    columns = lax.broadcasted_iota(jnp.int32, (block, both), 1)
    lower = columns < ff
    lanes = lax.broadcasted_iota(jnp.int32, (block, 128), 1)
    names = lax.broadcasted_iota(jnp.int32, (router.shape[0], block), 0)

    def compute(step):
        slot = step % 2
        here = group_rows(step)
        rows = rows_all[here, :]
        lin = mxu(rows, weight[...], 1, 1)
        gate, up = lin[:, :both], lin[:, both:]
        logits = mxu(router[...], rows, 1, 1)
        picked = chosen[:, here] > 0.0
        top = jnp.max(jnp.where(picked, logits, NEG), axis=0, keepdims=True)
        exps = jnp.where(picked, jnp.exp(logits - top), 0.0)
        soft = exps / jnp.sum(exps, axis=0, keepdims=True)
        keep = kept[:, here]
        soft = jnp.where(keep > 0.0, soft, 0.0)
        lines = []
        for table in (soft, keep):
            for at in range(local_count):
                lines.append(
                    jnp.sum(
                        jnp.where(names == group * local_count + at, table, 0.0),
                        axis=0, keepdims=True,
                    )
                )
        stack = jnp.concatenate(lines + [jnp.zeros((8 - len(lines), block), F32)], axis=0).T
        spread = jnp.where(lower, stack[:, 0:1], stack[:, 1:2])
        sigmoid = 1.0 / (1.0 + jnp.exp(-gate))
        silu = gate * sigmoid
        act = (silu * up).astype(BF16).astype(F32)
        weighted = (act * spread).astype(BF16)
        y_copy(step).wait()

        @pl.when(step >= 2)
        def _():
            for dx in (0, 1):
                core_copy(step - 2, dx).wait_send()

        back_block[slot, :, :width] = mxu(weighted, w_down[...]).astype(BF16)
        pass_on(step, 1)
        y_rows = y_block[slot]
        mid = mxu(y_rows, w_down[...], 1, 1)
        dots = act * mid
        low = jnp.sum(jnp.where(lower, dots, 0.0), axis=1, keepdims=True) * stack[:, 2:3]
        high = jnp.sum(jnp.where(lower, 0.0, dots), axis=1, keepdims=True) * stack[:, 3:4]
        mine_at = group * local_count
        tail = jnp.where(lanes == mine_at, low, jnp.where(lanes == mine_at + 1, high, 0.0))
        grad_act = mid * spread
        grad_up_lin = (grad_act * silu).astype(BF16)
        grad_gate_lin = (grad_act * up * sigmoid * (1.0 + gate * (1.0 - sigmoid))).astype(BF16)
        grad_lin = jnp.concatenate([grad_gate_lin, grad_up_lin], axis=1)
        back_block[slot, :, width : 2 * width] = mxu(grad_lin, weight[...]).astype(BF16)
        back_block[slot, :, 2 * width :] = tail.astype(BF16)
        far, dy = place_of(step)
        for dx in (1, 0):
            core_copy(step, dx).start()
            mine[far, dy, dx] = back_block[slot, piece(dx, 0), :]
        grad_in[...] += mxu(grad_lin, rows, 0, 0)
        grad_in_down[...] += mxu(weighted, y_rows, 0, 0)

    plans = {
        0: lambda: (
            both_ways(gather.take_yx, 0), both_ways(gather.take_z, 1),
            both_ways(gather.take_z, 2), both_ways(gather.take_diagonal, 0),
            both_ways(gather.take_late, 0), both_ways(gather.take_yx, 1),
            both_ways(gather.take_z, 3), both_ways(gather.take_late, 1),
        ),
        1: lambda: both_ways(gather.take_yx, 2),
        2: lambda: (both_ways(gather.take_diagonal, 1), both_ways(gather.take_late, 2)),
        3: lambda: both_ways(gather.take_yx, 3),
        4: lambda: (both_ways(gather.take_diagonal, 2), both_ways(gather.take_late, 3)),
        5: lambda: merge_diagonal(1),
        6: lambda: both_ways(gather.take_diagonal, 3),
        7: lambda: merge_diagonal(2),
        9: lambda: merge_yx(1),
        11: lambda: (merge_diagonal(3), merge_yx(2)),
        13: lambda: merge_line(1),
        15: lambda: (merge_diagonal(0), merge_yx(3)),
    }

    def pass_on(step, middle):
        for at, plan in plans.items():
            if at % 2 == middle:

                @pl.when(step == at // 2)
                def _(plan=plan):
                    plan()

    @pl.loop(0, 8)
    def _(step):
        pass_on(step, 0)

        @pl.when(step < 7)
        def _():
            y_copy(step + 1).start()

        far, dy = place_of(step)
        for dx in (0, 1):
            gather.take_core(far, dy, dx)
        compute(step)

    flush = [
        pltpu.make_async_copy(
            grad_in.at[pl.ds(at * ff, ff), :],
            (grad_gate, grad_up)[at // local_count].at[at % local_count],
            flush_sem.at[at],
        )
        for at in range(2 * local_count)
    ]
    flush.append(pltpu.make_async_copy(grad_in_down, grad_down, flush_sem.at[2 * local_count]))
    for copy in flush:
        copy.start()
    merge_line(2)
    merge_yx(0)
    merge_line(3)
    merge_line(0)
    total = mine[spot.z, 0, 0].astype(F32)
    for k in (1, 2, 3):
        source = near_first(k, spot.z)
        arrive(from_z.at[source], line_recv.at[source])
        total = total + from_z[source].astype(F32)
    reduced[...] = total
    gather.drain()
    for step in (6, 7):
        for dx in (0, 1):
            core_copy(step, dx).wait_send()
    arrive(from_a, half_send.at[0])
    arrive(from_b, half_send.at[1])
    arrive(from_y, yx_send.at[0])
    arrive(from_x, yx_send.at[1])
    for k in (1, 2, 3):
        arrive(from_z.at[0], line_send.at[k])
    for copy in flush:
        copy.wait()


def experts(normed, grad_y, w_gate, w_up, w_down, router, chosen, kept):
    count, width = normed.shape
    wide = 2 * width + 128
    total = grad_y.shape[0]
    local_count, ff, _ = w_gate.shape
    both = local_count * ff
    shape, vmem, dma = jax.ShapeDtypeStruct, pltpu.VMEM, pltpu.SemaphoreType.DMA
    line = vmem((4, count, wide), BF16)
    return pl.pallas_call(
        experts_kernel,
        out_shape=(
            shape((count, wide), F32),
            shape(w_gate.shape, F32), shape(w_up.shape, F32), shape((both, width), F32),
        ),
        in_specs=[VMEM_SPEC, HBM_SPEC, HBM_SPEC, HBM_SPEC] + [VMEM_SPEC] * 4,
        out_specs=(VMEM_SPEC,) + (HBM_SPEC,) * 3,
        scratch_shapes=[
            vmem((total, width), BF16),
            vmem((2 * both, width), BF16),
            vmem((2 * both, width), F32),
            vmem((both, width), F32),
            vmem((2, 4 * count, width), BF16),
            vmem((2, 4 * count, wide), BF16),
            vmem((4, 2, 2, count, wide), BF16),
            vmem((4, 2, 2, count, wide), BF16),
            vmem((4, count, width), BF16),
            vmem((4, count, wide - width), BF16),
            line, line, line,
        ]
        + dma_sems(
            ((2 * local_count,), (2,), (2 * local_count + 1,), (2, 2), (4, 2, 2), (2,), (2,), (4, 4),
             (4,), (4,))
            + Gather.SEMS
        ),
        compiler_params=pltpu.CompilerParams(
            collective_id=8, has_side_effects=True, vmem_limit_bytes=63 << 20
        ),
        name="experts",
        cost_estimate=cost(29_000_000_000, 120),
    )(normed, grad_y, w_gate, w_up, w_down, router, chosen, kept)


def attend_back_kernel(
    own_rows, w_out, queries, keys, values, attended, lin, cosine, sine, place_column,
    place_row, open_row, log_total, k_gain, q_gain,
    grad_lin, grad_out, grad_q_gain, grad_k_gain,
    rows_all, head_out, grad_keys, grad_values, out_sum, head_sem, *gather_sems,
):
    spot = Spot()
    count = own_rows.shape[0]
    block = 4 * count
    dim = queries.shape[1]
    group = lax.axis_index("expert")
    head_copy = pltpu.make_async_copy(
        w_out.at[pl.ds(pl.multiple_of(group * dim, dim), dim), :], head_out, head_sem
    )
    head_copy.start()
    gather = Gather(spot, own_rows, rows_all, *gather_sems, share=3)
    spot.greet()
    gather.start()
    grad_keys[...] = jnp.zeros_like(grad_keys)
    grad_values[...] = jnp.zeros_like(grad_values)
    out_sum[...] = jnp.zeros_like(out_sum)
    grad_q_gain[...] = jnp.zeros_like(grad_q_gain)
    gather.local.wait()
    head_copy.wait()

    def unshape(grad, plain, gain, cos, sin):
        grad = grad * cos + pltpu.roll(grad * sin, dim // 2, 1)
        normed, root = head_norm(plain)
        gain_part = jnp.sum(grad * normed, axis=0, keepdims=True)
        grad = grad * gain
        return root * (grad - normed * jnp.mean(grad * normed, axis=-1, keepdims=True)), gain_part

    def compute(far, dy):
        y = spot.y + dy * (1 - 2 * spot.y)
        here = pl.ds(pl.multiple_of((far * 2 + y) * block, block), block)
        rows = rows_all[here, :]
        query = queries[here, :]
        grad_att = mxu(rows, head_out[...], 1, 1).astype(BF16)
        scores = mxu(keys[...], query, 1, 1)
        seen = (place_column[...] <= place_row[:, here]) & (place_column[...] >= open_row[:, here])
        probability = jnp.exp(jnp.where(seen, scores - log_total[:, here], NEG))
        grad_prob = mxu(values[...], grad_att, 1, 1)
        delta = jnp.sum(probability * grad_prob, axis=0, keepdims=True)
        grad_scores = (probability * (grad_prob - delta)).astype(BF16)
        grad_values[...] += mxu(probability.astype(BF16), grad_att)
        grad_keys[...] += mxu(grad_scores, query)
        grad_query = mxu(grad_scores, keys[...], 0, 0) * dim**-0.5
        grad_query, gain_part = unshape(
            grad_query, lin[here, :dim], q_gain[...], cosine[here, :], sine[here, :]
        )
        grad_q_gain[...] += gain_part
        grad_lin[here, :dim] = grad_query.astype(BF16)
        out_sum[...] += mxu(attended[here, :], rows, 0, 0)

    def both_ways(take, distance):
        for dz in (distance, -distance) if distance else (0,):
            take(dz)

    plans = {
        0: lambda: (both_ways(gather.take_yx, 0), both_ways(gather.take_late, 0),
                    both_ways(gather.take_z, 1)),
        1: lambda: (both_ways(gather.take_diagonal, 0), both_ways(gather.take_z, 2)),
        2: lambda: (both_ways(gather.take_yx, 1), both_ways(gather.take_late, 1),
                    both_ways(gather.take_z, 3)),
        3: lambda: (both_ways(gather.take_yx, 2), both_ways(gather.take_late, 2),
                    both_ways(gather.take_diagonal, 1)),
        4: lambda: (both_ways(gather.take_yx, 3), both_ways(gather.take_late, 3)),
        5: lambda: both_ways(gather.take_diagonal, 2),
        7: lambda: both_ways(gather.take_diagonal, 3),
    }

    @pl.loop(0, 8)
    def _(step):
        for at, plan in plans.items():

            @pl.when(step == at)
            def _(plan=plan):
                plan()

        far, dy = near_first(step // 2, spot.z), step % 2
        for dx in (0, 1):
            gather.take_core(far, dy, dx)
        compute(far, dy)

    grad_out[...] = out_sum[...].astype(BF16)
    grad_key, key_part = unshape(grad_keys[...], lin[:, dim:], k_gain[...], cosine[...], sine[...])
    grad_lin[:, dim : 2 * dim] = grad_key.astype(BF16)
    grad_lin[:, 2 * dim :] = grad_values[...].astype(BF16)
    grad_k_gain[...] = key_part
    gather.drain()


def attend_back(
    own_rows, w_out, queries, keys, values, attended, lin, cosine, sine, place_column,
    place_row, open_row, log_total, k_gain, q_gain,
):
    count, width = own_rows.shape
    total, dim = keys.shape
    shape, vmem = jax.ShapeDtypeStruct, pltpu.VMEM
    return pl.pallas_call(
        attend_back_kernel,
        out_shape=[
            shape((total, 3 * dim), BF16), shape((dim, width), BF16),
            shape((1, dim), F32), shape((1, dim), F32),
        ],
        in_specs=[VMEM_SPEC, HBM_SPEC] + [VMEM_SPEC] * 13,
        out_specs=[VMEM_SPEC] * 4,
        scratch_shapes=[
            vmem((total, width), BF16), vmem((dim, width), BF16),
            vmem((total, dim), F32), vmem((total, dim), F32), vmem((dim, width), F32),
        ]
        + dma_sems((None,) + Gather.SEMS),
        compiler_params=pltpu.CompilerParams(
            collective_id=9, has_side_effects=True, vmem_limit_bytes=60 << 20
        ),
        name="attend_back",
        cost_estimate=cost(9_000_000_000, 50),
    )(
        own_rows, w_out, queries, keys, values, attended, lin, cosine, sine, place_column,
        place_row, open_row, log_total, k_gain, q_gain,
    )


class LineGather:
    SEMS = ((7,), (7,), (7, 2), None, None, (7, 2), (7, 2, 2), None)

    def __init__(self, spot, place, own, sems):
        self.spot, self.place, self.own = spot, place, own
        self.z_recv, self.y_recv, self.z_send, self.y_send = sems[:4]
        self.late_y_recv, self.late_z_recv, self.late_z_send, self.late_y_send = sems[4:]

    def source(self, dz, dy, part):
        return self.own(part) if dz == 0 and dy == 0 else self.place(dz, dy, part)

    def along_z(self, dz, dy, part):
        for side, step in ((0, 1), (1, -1)):
            if dz * step <= 0:

                @pl.when(self.spot.has(step))
                def _(side=side, step=step):
                    if part:
                        send = self.late_z_send.at[dz + 3, side, dy]
                        recv = self.late_z_recv.at[dz + 3 - step, dy]
                    else:
                        send = self.z_send.at[dz + 3, side]
                        recv = self.z_recv.at[dz + 3 - step]
                    push(
                        self.source(dz, dy, part), self.place(dz, dy, part), send, recv,
                        self.spot.device(step),
                    )

    def along_y(self, dz):
        push(
            self.source(dz, 0, 0), self.place(dz, 0, 0), self.y_send, self.y_recv.at[dz + 3],
            self.spot.device(0, 1),
        )

    def start(self):
        self.along_z(0, 0, 0)
        push(
            self.own(1), self.place(0, 0, 1), self.late_y_send, self.late_y_recv,
            self.spot.device(0, 1),
        )
        self.along_y(0)
        self.along_z(0, 0, 1)

    def take_z(self, distance):
        for dz in (distance, -distance):

            def action(dz=dz):
                arrive(self.place(dz, 0, 0), self.z_recv.at[dz + 3])
                self.along_z(dz, 0, 0)
                self.along_y(dz)

            when_has(self.spot, dz, action)

    def take_late_y(self):
        arrive(self.place(0, 1, 1), self.late_y_recv)
        self.along_z(0, 1, 1)

    def take_late_z(self, distance):
        for dz in (distance, -distance):

            def action(dz=dz):
                for dy in (0, 1):
                    arrive(self.place(dz, dy, 1), self.late_z_recv.at[dz + 3, dy])
                    self.along_z(dz, dy, 1)

            when_has(self.spot, dz, action)

    def drain(self, four):
        for dz in (0, 1, -1, 2, -2, 3, -3):

            def action(dz=dz):
                arrive(self.place(dz, 1, 0), self.y_recv.at[dz + 3])
                for side, step in ((0, 1), (1, -1)):
                    if dz * step <= 0:

                        @pl.when(self.spot.has(step))
                        def _(side=side):
                            arrive(self.place(dz, 0, 0), self.z_send.at[dz + 3, side])
                            for dy in (0, 1):
                                arrive(
                                    self.place(dz, dy, 1), self.late_z_send.at[dz + 3, side, dy]
                                )

            when_has(self.spot, dz, action)
        arrive(four, self.y_send)
        arrive(self.place(0, 0, 1), self.late_y_send)


def close_kernel(
    normed, grad_lin, w_query, w_key, w_value, head_out,
    reduced, kv_all, query_all, out_all,
    weight, rows, sums, query_own, kv_part, back, mine, other, from_x_diagonal, from_y, from_x,
    from_z, kv_mine, kv_y, kv_z, kv_own, row_sem, weight_sem, local_sem,
    core_send, core_recv, many_send, recv, line_send, line_recv,
    kv_send, kv_y_recv, kv_line_send, kv_line_recv, *gather_sems,
):
    spot = Spot()
    total, width = normed.shape
    count, wide = reduced.shape
    block = 4 * count
    dim = w_key.shape[1]
    group = lax.axis_index("expert")
    to_y, to_x, to_c = spot.device(0, 1), spot.device(0, 0, 1), spot.device(0, 0, 0, 1)
    cut = 1664

    def parts(part):
        return pl.ds(cut, total - cut) if part else pl.ds(0, cut)

    def lane_block(dz, dy):
        return pl.ds(pl.multiple_of(spot.device(dz, dy)[0] * dim, dim), dim)

    weights = [
        pltpu.make_async_copy(
            w_query.at[:, pl.ds(pl.multiple_of(group * dim, dim), dim)],
            weight.at[:, pl.ds(0, dim)], weight_sem.at[0],
        ),
        pltpu.make_async_copy(w_key, weight.at[:, pl.ds(dim, dim)], weight_sem.at[1]),
        pltpu.make_async_copy(w_value, weight.at[:, pl.ds(2 * dim, dim)], weight_sem.at[2]),
    ]

    def row_copy(step):
        return pltpu.make_async_copy(
            normed.at[pl.ds(pl.multiple_of(step * block, block), block), :],
            rows.at[step % 2], row_sem.at[step % 2],
        )

    for copy in weights:
        copy.start()
    row_copy(0).start()
    outs = LineGather(
        spot,
        lambda dz, dy, part: out_all.at[lane_block(dz, dy), parts(part)],
        lambda part: head_out.at[:, parts(part)],
        gather_sems[:8],
    )
    queries = LineGather(
        spot,
        lambda dz, dy, part: query_all.at[parts(part), lane_block(dz, dy)],
        lambda part: query_own.at[parts(part), :],
        gather_sems[8:16],
    )
    kv_rows = total // 8

    def kv_span(start, part):
        return pl.ds(pl.multiple_of(start + part * (kv_rows // 2), kv_rows // 2), kv_rows // 2)

    kvs = LineGather(
        spot,
        lambda dz, dy, part: kv_all.at[kv_span(spot.device(dz, dy)[0] * kv_rows, part), :],
        lambda part: kv_own.at[kv_span(0, part), :],
        gather_sems[16:],
    )
    out_copy = pltpu.make_async_copy(head_out, out_all.at[lane_block(0, 0), :], local_sem.at[0])
    out_copy.start()
    spot.greet(line=True)
    outs.start()

    sums[...] = jnp.zeros_like(sums)

    @pl.loop(0, total // block)
    def _(step):
        @pl.when(step < total // block - 1)
        def _():
            row_copy(step + 1).start()

        row_copy(step).wait()
        here = pl.ds(pl.multiple_of(step * block, block), block)
        sums[...] += mxu(grad_lin[here, :], rows[step % 2], 0, 0)

    query_own[...] = sums[:dim, :].T.astype(BF16)
    kv_part[...] = sums[dim:, :].T.astype(BF16)
    query_copy = pltpu.make_async_copy(query_own, query_all.at[:, lane_block(0, 0)], local_sem.at[1])
    query_copy.start()

    def group_rows(far, dy):
        y = spot.y + dy * (1 - 2 * spot.y)
        return pl.ds(pl.multiple_of((far * 2 + y) * block, block), block)

    for k in (3, 2, 1, 0):
        far = near_first(k, spot.z)
        push(
            kv_part.at[group_rows(far, 1), :], kv_y.at[far], kv_send, kv_y_recv.at[far], to_y
        )
    for copy in weights:
        copy.wait()

    def piece(dx, dc):
        _, part = spot.device(0, 0, dx, dc)
        return pl.ds(pl.multiple_of(part * count, count), count)

    def core_copy(step, far, dy, dx):
        return pltpu.make_async_remote_copy(
            src_ref=back.at[step % 2, piece(dx, 1), :],
            dst_ref=other.at[far, dy, dx],
            send_sem=core_send.at[step % 2, dx],
            recv_sem=core_recv.at[far, dy, dx],
            device_id=to_c,
            device_id_type=MESH,
        )

    def produce(k):
        far = near_first(k, spot.z)
        for dy in (1, 0):
            step = 2 * (3 - k) + 1 - dy
            if step >= 2:
                for dx in (1, 0):
                    core_copy(step, far, dy, dx).wait_send()
            here = group_rows(far, dy)
            back[step % 2] = mxu(grad_lin[here, :], weight[...], 1, 1).astype(BF16)
            for dx in (1, 0):
                core_copy(step, far, dy, dx).start()
                mine[far, dy, dx] = back[step % 2, piece(dx, 0), :]

    def merge(far, dy, dx, *terms):
        arrive(other.at[far, dy, dx], core_recv.at[far, dy, dx])
        add_into(mine.at[far, dy, dx], 16, other.at[far, dy, dx], *terms)
        return mine.at[far, dy, dx]

    def merge_diagonal(k):
        far = near_first(k, spot.z)
        push(
            merge(far, 1, 1), from_x_diagonal.at[far], many_send.at[0], recv.at[0, far], to_x
        )

    def merge_yx(k):
        far = near_first(k, spot.z)
        push(merge(far, 0, 1), from_x.at[far], many_send.at[1], recv.at[1, far], to_x)
        arrive(from_x_diagonal.at[far], recv.at[0, far])
        push(
            merge(far, 1, 0, from_x_diagonal.at[far]), from_y.at[far], many_send.at[2],
            recv.at[2, far], to_y,
        )

    def far_device(far):
        return (far * 2 + spot.y, spot.x * 2 + spot.c)

    def merge_kv(k):
        far = near_first(k, spot.z)
        kv_mine[far] = kv_part[group_rows(far, 0), :]
        arrive(kv_y.at[far], kv_y_recv.at[far])
        add_into(kv_mine.at[far], 64, kv_y.at[far])
        if k > 0:
            push(
                kv_mine.at[far], kv_z.at[spot.z], kv_line_send.at[k], kv_line_recv.at[spot.z],
                far_device(far),
            )

    def merge_line(k):
        far = near_first(k, spot.z)
        arrive(from_y.at[far], recv.at[2, far])
        arrive(from_x.at[far], recv.at[1, far])
        into = merge(far, 0, 0, from_y.at[far], from_x.at[far])
        if k > 0:
            push(
                into, from_z.at[spot.z], line_send.at[k], line_recv.at[spot.z], far_device(far)
            )

    def sum_kv():
        sums_kv = kv_mine[spot.z].astype(F32)
        for k in (1, 2, 3):
            source = near_first(k, spot.z)
            arrive(kv_z.at[source], kv_line_recv.at[source])
            sums_kv = sums_kv + kv_z[source].astype(F32)
        kv_own[...] = sums_kv.astype(BF16)

    produce(3)
    produce(2)
    outs.take_z(1)
    for k in (3, 2, 1, 0):
        merge_kv(k)
    queries.start()
    merge_diagonal(3)
    produce(1)
    merge_diagonal(2)
    outs.take_late_y()
    produce(0)
    merge_diagonal(1)
    sum_kv()
    kvs.start()
    kv_copy = pltpu.make_async_copy(
        kv_own, kv_all.at[pl.ds(pl.multiple_of(group * kv_rows, kv_rows), kv_rows), :],
        local_sem.at[2],
    )
    kv_copy.start()
    outs.take_z(2)
    queries.take_z(1)
    merge_diagonal(0)
    merge_yx(3)
    kvs.take_z(1)
    kvs.take_late_y()
    queries.take_late_y()
    outs.take_late_z(1)
    merge_yx(2)
    outs.take_z(3)
    queries.take_z(2)
    kvs.take_z(2)
    kvs.take_late_z(1)
    merge_line(3)
    merge_yx(1)
    queries.take_late_z(1)
    outs.take_late_z(2)
    kvs.take_z(3)
    kvs.take_late_z(2)
    merge_line(2)
    merge_yx(0)
    queries.take_z(3)
    queries.take_late_z(2)
    outs.take_late_z(3)
    merge_line(1)
    merge_line(0)
    kvs.take_late_z(3)
    queries.take_late_z(3)
    total_rows = mine[spot.z, 0, 0].astype(F32)
    for k in (1, 2, 3):
        source = near_first(k, spot.z)
        arrive(from_z.at[source], line_recv.at[source])
        total_rows = total_rows + from_z[source].astype(F32)
    reduced[...] = total_rows

    kvs.drain(kv_all.at[pl.ds(0, 2 * kv_rows), :])
    kv_copy.wait()
    outs.drain(out_all.at[pl.ds(0, 4 * dim), parts(0)])
    queries.drain(query_all.at[parts(0), pl.ds(0, 4 * dim)])
    out_copy.wait()
    query_copy.wait()
    for step in (6, 7):
        for dx in (0, 1):
            core_copy(step, near_first(0, spot.z), 0, dx).wait_send()
    arrive(from_x_diagonal, many_send.at[0])
    arrive(from_x, many_send.at[1])
    arrive(from_y, many_send.at[2])
    arrive(kv_y, kv_send)
    for k in (1, 2, 3):
        arrive(from_z.at[0], line_send.at[k])
        arrive(kv_z.at[0], kv_line_send.at[k])


def close(normed, grad_lin, w_query, w_key, w_value, head_out):
    total, width = normed.shape
    count, wide, dim = total // 32, width, w_key.shape[1]
    shape, vmem = jax.ShapeDtypeStruct, pltpu.VMEM
    line, kv_line = vmem((4, count, wide), BF16), vmem((4, 4 * count, 2 * dim), BF16)
    return pl.pallas_call(
        close_kernel,
        out_shape=(
            shape((count, wide), F32), shape((total, 2 * dim), BF16),
            shape((total, 8 * dim), BF16), shape((8 * dim, width), BF16),
        ),
        in_specs=[HBM_SPEC, VMEM_SPEC, HBM_SPEC, HBM_SPEC, HBM_SPEC, VMEM_SPEC],
        out_specs=(VMEM_SPEC, HBM_SPEC, HBM_SPEC, HBM_SPEC),
        scratch_shapes=[
            vmem((width, 3 * dim), BF16), vmem((2, 4 * count, width), BF16),
            vmem((3 * dim, width), F32), vmem((width, dim), BF16), vmem((width, 2 * dim), BF16),
            vmem((2, 4 * count, wide), BF16),
            vmem((4, 2, 2, count, wide), BF16), vmem((4, 2, 2, count, wide), BF16),
            line, line, line, line, kv_line, kv_line, kv_line,
            vmem((4 * count, 2 * dim), BF16),
        ]
        + dma_sems(
            ((2,), (3,), (3,), (2, 2), (4, 2, 2), (3,), (3, 4), (4,), (4,),
             None, (4,), (4,), (4,)) + LineGather.SEMS * 3
        ),
        compiler_params=pltpu.CompilerParams(
            collective_id=10, has_side_effects=True, vmem_limit_bytes=60 << 20
        ),
        name="close",
        cost_estimate=cost(7_000_000_000, 110),
    )(normed, grad_lin, w_query, w_key, w_value, head_out)


def cosine_sine(angles):
    lanes = lax.broadcasted_iota(jnp.int32, angles.shape, 1)
    turns = jnp.floor(angles * (2.0 / math.pi) + 0.5)
    rest = angles - turns * 1.5703125
    rest = rest - turns * 4.837512969970703125e-4
    rest = rest - turns * 7.54978995489188216e-8
    square = rest * rest
    sine = square * (8.3321608736e-3 + square * -1.9515295891e-4) - 1.6666654611e-1
    sine = rest + rest * square * sine
    cosine = -1.388731625493765e-3 + square * 2.443315711809948e-5
    cosine = 1.0 - 0.5 * square + square * square * (4.166664568298827e-2 + square * cosine)
    turns = jnp.where(lanes < angles.shape[1] // 2, turns, turns - 1.0)
    turns = turns - 4.0 * jnp.floor(turns * 0.25)
    odd = (turns == 1.0) | (turns == 3.0)
    value = jnp.where(odd, sine, cosine)
    return jnp.where((turns == 1.0) | (turns == 2.0), -value, value)


def front_kernel(
    hidden, cotangent, tag, lengths, gain, w_query, w_key, w_value, q_gain, k_gain, inverse,
    w_out, second_gain,
    normed_all, queries, keys, values, lin_out, cosine, sine, attended, log_total,
    place_row, open_row, place_column, residual, normed, chosen, kept, grad_y_all,
    rows_all, weight, out_weight, staged, tags, ranks, picks, att_rows,
    partial_sum, from_core, to_x_sum, from_x,
    weight_sem, stage_sem, tag_z, tag_y, tag_z_send, tag_y_send, tag_local,
    send_sem, recv_sem, own_sem, tensor_sems, *gather_sems,
):
    spot = Spot()
    group, part = lax.axis_index("expert"), lax.axis_index("tensor")
    count, width = residual.shape
    block = 4 * count
    total = 32 * count
    dim = w_key.shape[1]
    own = pl.ds(pl.multiple_of(part * count, count), count)

    weights = [
        pltpu.make_async_copy(
            w_query.at[:, pl.ds(pl.multiple_of(group * dim, dim), dim)],
            weight.at[:, pl.ds(0, dim)], weight_sem.at[0],
        ),
        pltpu.make_async_copy(w_key, weight.at[:, pl.ds(dim, dim)], weight_sem.at[1]),
        pltpu.make_async_copy(w_value, weight.at[:, pl.ds(2 * dim, dim)], weight_sem.at[2]),
        pltpu.make_async_copy(w_out, out_weight, weight_sem.at[3]),
    ]
    for copy in weights:
        copy.start()
    barrier = pltpu.get_barrier_semaphore()

    @pl.loop(1, 8)
    def _(step):
        pl.semaphore_signal(
            barrier, inc=1, device_id=((group + step) % 8, part), device_id_type=MESH
        )

    for device in (spot.device(0, 0, 1), spot.device(0, 0, 0, 1)):
        pl.semaphore_signal(barrier, inc=1, device_id=device, device_id_type=MESH)

    def tag_place(dz, dy):
        return tags.at[spot.device(dz, dy)[0]]

    tag_copy = pltpu.make_async_copy(tag, tag_place(0, 0), tag_local)
    tag_copy.start()
    pl.semaphore_wait(barrier, 9)

    def spread_tag(dz):
        here = tag_place(dz, 0)
        source = tag if dz == 0 else here
        for side, step in ((0, 1), (1, -1)):
            if dz * step <= 0:

                @pl.when(spot.has(step))
                def _(side=side, step=step):
                    push(
                        source, here, tag_z_send.at[dz + 3, side], tag_z.at[dz + 3 - step],
                        spot.device(step),
                    )

        push(source, here, tag_y_send.at[dz + 3], tag_y.at[dz + 3], spot.device(0, 1))

    def take_tag(dz):
        def action():
            arrive(tag_place(dz, 0), tag_z.at[dz + 3])
            spread_tag(dz)

        when_has(spot, dz, action)

    def take_tag_y(dz):
        when_has(spot, dz, lambda: arrive(tag_place(dz, 1), tag_y.at[dz + 3]))

    spread_tag(0)
    gather = Gather(spot, hidden.at[own, :], rows_all, *gather_sems[:7], full=hidden)
    gather.start()
    late = Gather(spot, cotangent.at[own, :], grad_y_all, *gather_sems[7:], full=cotangent)
    tag_copy.wait()
    gather.local.wait()
    for copy in weights:
        copy.wait()

    def group_of(step):
        far, dy = near_first(step // 2, spot.z), step % 2
        return far, dy, far * 2 + spot.y + dy * (1 - 2 * spot.y)

    def stage_copy(step):
        _, _, index = group_of(step)
        return pltpu.make_async_copy(
            staged.at[step % 2],
            normed_all.at[pl.ds(pl.multiple_of(index * block, block), block), :],
            stage_sem.at[step % 2],
        )

    experts_count = chosen.shape[0]
    names = lax.broadcasted_iota(jnp.int32, (experts_count, block), 0)
    lanes = lax.broadcasted_iota(jnp.int32, (block, dim), 1)

    def project_group(step):
        _, _, index = group_of(step)
        here = pl.ds(pl.multiple_of(index * block, block), block)
        entries = tags[index]
        place = entries[0:1, :]
        segment, opening, bound = jnp.zeros_like(place), jnp.zeros_like(place), 0
        for at in range(lengths.shape[0]):
            bound = bound + lengths[at]
            segment = segment + jnp.where(place >= bound, 1, 0)
            opening = jnp.where(place >= bound, bound, opening)
        place_row[:, here] = place.astype(F32)
        open_row[:, here] = opening.astype(F32)
        lines = jnp.concatenate(
            [place.astype(F32), (place - opening).astype(F32), entries[1:2, :].astype(F32),
             jnp.zeros((5, block), F32)],
            axis=0,
        ).T
        place_column[here, :] = lines[:, 0:1]
        ranks[here, :] = lines[:, 2:3]
        named = jnp.zeros((experts_count, block), F32)
        for at in range(2, 2 + TOPK):
            named = jnp.where(entries[at : at + 1, :] == names, 1.0, named)
        chosen[:, here] = named
        valid = segment < lengths.shape[0]
        picks[:, here] = jnp.where(valid, named, 0.0).astype(BF16)
        table = cosine_sine(lines[:, 1:2] * inverse[...])
        turned_table = pltpu.roll(table, dim // 2, 1)
        cos = jnp.where(lanes < dim // 2, table, turned_table)
        sin = jnp.where(lanes < dim // 2, -turned_table, table)
        cosine[here, :] = cos
        sine[here, :] = sin
        rows = rows_all[here, :].astype(F32)
        root = lax.rsqrt(jnp.mean(rows * rows, axis=-1, keepdims=True) + EPS)

        @pl.when(step >= 2)
        def _():
            stage_copy(step - 2).wait()

        staged[step % 2] = (rows * root * gain[...]).astype(BF16)
        stage_copy(step).start()
        lin = mxu(staged[step % 2], weight[...])
        lin_out[here, :] = lin[:, : 2 * dim]
        values[here, :] = lin[:, 2 * dim :].astype(BF16)
        for at, head_gain, scale, out in (
            (0, q_gain, dim**-0.5, queries), (dim, k_gain, 1.0, keys),
        ):
            plain, _ = head_norm(lin[:, at : at + dim])
            plain = plain * head_gain[...]
            out[here, :] = ((plain * cos + pltpu.roll(plain, dim // 2, 1) * sin) * scale).astype(
                BF16
            )

    def both_ways(take, distance):
        for dz in (distance, -distance) if distance else (0,):
            take(dz)

    def run(plans, step):
        for at, plan in plans.items():

            @pl.when(step == at)
            def _(plan=plan):
                plan()

    plans = {
        0: lambda: (both_ways(gather.take_yx, 0), both_ways(take_tag, 1),
                    both_ways(gather.take_z, 1)),
        1: lambda: (both_ways(take_tag_y, 0), both_ways(gather.take_diagonal, 0),
                    both_ways(take_tag, 2), both_ways(gather.take_z, 2),
                    both_ways(gather.take_late, 0)),
        2: lambda: (both_ways(gather.take_yx, 1), both_ways(take_tag, 3),
                    both_ways(gather.take_z, 3), both_ways(gather.take_late, 1)),
        3: lambda: (both_ways(take_tag_y, 1), both_ways(gather.take_yx, 2),
                    both_ways(gather.take_diagonal, 1), both_ways(gather.take_late, 2)),
        4: lambda: (both_ways(gather.take_yx, 3), late.start()),
        5: lambda: (both_ways(take_tag_y, 2), both_ways(gather.take_diagonal, 2),
                    both_ways(gather.take_late, 3)),
        7: lambda: (both_ways(take_tag_y, 3), both_ways(gather.take_diagonal, 3)),
    }

    @pl.loop(0, 8)
    def _(step):
        run(plans, step)
        far, dy, _ = group_of(step)

        @pl.when(step > 0)
        def _():
            for dx in (0, 1):
                gather.take_core(far, dy, dx)

        project_group(step)

    mine = att_rows.at[:, pl.ds(pl.multiple_of(group * dim, dim), dim)]

    def block_copy(step):
        target = (group + step) % 8
        return pltpu.make_async_remote_copy(
            src_ref=attended.at[pl.ds(pl.multiple_of(target * block, block), block), :],
            dst_ref=mine,
            send_sem=send_sem.at[step],
            recv_sem=recv_sem.at[step],
            device_id=(target, part),
            device_id_type=MESH,
        )

    def attend_block(step):
        here = pl.ds(pl.multiple_of((group + step) % 8 * block, block), block)
        scores = mxu(keys[...], queries[here, :], 1, 1)
        seen = (place_column[...] <= place_row[:, here]) & (place_column[...] >= open_row[:, here])
        scores = jnp.where(seen, scores, NEG)
        highest = jnp.max(scores, axis=0, keepdims=True)
        exps = jnp.exp(scores - highest)
        totals = jnp.sum(exps, axis=0, keepdims=True)
        probability = (exps * (1.0 / totals)).astype(BF16)
        attended[here, :] = mxu(values[...], probability, 0, 0).T.astype(BF16)
        log_total[:, here] = highest + jnp.log(totals)

    late_plans = {
        1: lambda: (both_ways(late.take_yx, 0), both_ways(late.take_z, 1)),
        3: lambda: (both_ways(late.take_z, 2), both_ways(late.take_diagonal, 0),
                    both_ways(late.take_late, 0)),
        5: lambda: (both_ways(late.take_yx, 1), both_ways(late.take_z, 3)),
        7: lambda: (both_ways(late.take_late, 1), both_ways(late.take_yx, 2),
                    both_ways(late.take_diagonal, 1)),
    }

    @pl.loop(1, 8)
    def _(step):
        run(late_plans, step)
        attend_block(step)
        block_copy(step).start()

    attend_block(0)
    own_copy = pltpu.make_async_copy(
        attended.at[pl.ds(pl.multiple_of(group * block, block), block), :], mine, own_sem
    )
    own_copy.start()
    both_ways(late.take_yx, 3)
    both_ways(late.take_late, 2)

    kept[...] = jnp.zeros_like(kept)

    @pl.loop(0, total // block)
    def _(step):
        here = pl.ds(pl.multiple_of(step * block, block), block)
        for at in range(0, total // block):
            columns = pl.ds(at * block, block)
            lower = jnp.where(
                ranks[here, :] < tags[at, 1:2, :].astype(F32), 1.0, 0.0
            ).astype(BF16)
            kept[:, columns] += mxu(picks[:, here], lower)

    kept[...] = jnp.where((picks[...].astype(F32) > 0.0) & (kept[...] < CAP), 1.0, 0.0)

    both_ways(late.take_diagonal, 2)
    both_ways(late.take_late, 3)

    @pl.loop(1, 8)
    def _(step):
        block_copy(step).wait_send()
        source = (group + 8 - step) % 8
        there = att_rows.at[:, pl.ds(pl.multiple_of(source * dim, dim), dim)]
        arrive(there, recv_sem.at[step])

    own_copy.wait()

    @pl.loop(0, width // 256)
    def _(step):
        columns = pl.ds(pl.multiple_of(step * 256, 256), 256)
        partial_sum[:, columns] = mxu(att_rows[...], out_weight[:, columns]).astype(BF16)

    def rows_of(dx, dc):
        _, there = spot.device(0, 0, dx, dc)
        return partial_sum.at[pl.ds(pl.multiple_of(there * count, count), count), :]

    to_x, to_c = spot.device(0, 0, 1), spot.device(0, 0, 0, 1)
    for dx in (1, 0):
        push(rows_of(dx, 1), from_core.at[dx], tensor_sems.at[dx], tensor_sems.at[2 + dx], to_c)
    arrive(from_core.at[1], tensor_sems.at[3])
    to_x_sum[...] = (rows_of(1, 0)[...].astype(F32) + from_core[1].astype(F32)).astype(BF16)
    push(to_x_sum, from_x, tensor_sems.at[4], tensor_sems.at[5], to_x)
    both_ways(late.take_diagonal, 3)
    arrive(from_core.at[0], tensor_sems.at[2])
    arrive(from_x, tensor_sems.at[5])
    branch = rows_of(0, 0)[...].astype(F32) + from_core[0].astype(F32) + from_x[...].astype(F32)
    sum_rows = hidden[own, :].astype(F32) + branch
    residual[...] = sum_rows
    root = lax.rsqrt(jnp.mean(sum_rows * sum_rows, axis=-1, keepdims=True) + EPS)
    normed[...] = (sum_rows * root * second_gain[...]).astype(BF16)
    for at, view in ((0, from_core.at[0]), (1, from_core.at[1]), (4, from_x)):
        arrive(view, tensor_sems.at[at])
    for step in (6, 7):
        stage_copy(step).wait()
    gather.drain()
    late.local.wait()
    for far in range(4):
        for dx in (0, 1):
            late.take_core(far, 1, dx)

            @pl.when(spot.z != far)
            def _(far=far, dx=dx):
                late.take_core(far, 0, dx)

    late.drain()
    for dz in range(-3, 4):

        def action(dz=dz):
            arrive(tag_place(dz, 0), tag_y_send.at[dz + 3])
            for side, step in ((0, 1), (1, -1)):
                if dz * step <= 0:

                    @pl.when(spot.has(step))
                    def _(side=side):
                        arrive(tag_place(dz, 0), tag_z_send.at[dz + 3, side])

        when_has(spot, dz, action)


def front(
    hidden, cotangent, tag, lengths, gain, w_query, w_key, w_value, q_gain, k_gain, inverse,
    w_out, second_gain, expert_count,
):
    block, width = hidden.shape
    total, count, dim = 8 * block, block // 4, w_key.shape[1]
    shape, vmem = jax.ShapeDtypeStruct, pltpu.VMEM
    smem = pl.BlockSpec(memory_space=pltpu.SMEM)
    small = (total, dim)
    return pl.pallas_call(
        front_kernel,
        out_shape=(
            shape((total, width), BF16), shape(small, BF16), shape(small, BF16),
            shape(small, BF16), shape((total, 2 * dim), F32), shape(small, F32),
            shape(small, F32), shape(small, BF16), shape((1, total), F32),
            shape((1, total), F32), shape((1, total), F32), shape((total, 1), F32),
            shape((count, width), F32), shape((count, width), BF16),
            shape((expert_count, total), F32), shape((expert_count, total), F32),
            shape((total, width), BF16),
        ),
        in_specs=[VMEM_SPEC, VMEM_SPEC, VMEM_SPEC, smem, VMEM_SPEC, HBM_SPEC, HBM_SPEC, HBM_SPEC,
                  VMEM_SPEC, VMEM_SPEC, VMEM_SPEC, HBM_SPEC, VMEM_SPEC],
        out_specs=(HBM_SPEC,) + (VMEM_SPEC,) * 15 + (HBM_SPEC,),
        scratch_shapes=[
            vmem((total, width), BF16), vmem((width, 3 * dim), BF16), vmem((8 * dim, width), BF16),
            vmem((2, block, width), BF16), vmem((8, 16, block), jnp.int32), vmem((total, 1), F32),
            vmem((expert_count, total), BF16), vmem((block, 8 * dim), BF16),
            vmem((block, width), BF16), vmem((2, count, width), BF16), vmem((count, width), BF16),
            vmem((count, width), BF16),
        ]
        + dma_sems(
            ((4,), (2,), (7,), (7,), (7, 2), (7,), None, (8,), (8,), None, (6,)) + Gather.SEMS * 2
        ),
        compiler_params=pltpu.CompilerParams(
            collective_id=1, has_side_effects=True, vmem_limit_bytes=62 << 20
        ),
        name="front",
        cost_estimate=cost(8_000_000_000, 90),
    )(
        hidden, cotangent, tag, lengths, gain, w_query, w_key, w_value, q_gain, k_gain, inverse,
        w_out, second_gain,
    )


def settle_kernel(*refs):
    half = len(refs) // 2
    for source, target in zip(refs[:half], refs[half:]):
        target[...] = source[...]


def settle(*arrays):
    width = arrays[0].shape[-1]
    flat = [v.reshape(-1, width) for v in arrays]
    steps = 6
    blocks = [pl.BlockSpec((v.shape[0] // steps, width), lambda i: (i, 0)) for v in flat]
    out = pl.pallas_call(
        settle_kernel,
        grid=(steps,),
        out_shape=tuple(jax.ShapeDtypeStruct(v.shape, v.dtype) for v in flat),
        in_specs=blocks,
        out_specs=tuple(blocks),
        cost_estimate=cost(0, 6),
        compiler_params=pltpu.CompilerParams(vmem_limit_bytes=32 << 20),
        name="settle",
    )(*flat)
    return tuple(v.reshape(w.shape) for v, w in zip(out, arrays))


def swap(value, bits):
    return lax.ppermute(
        value, ("expert", "tensor"), [(device, device ^ bits) for device in range(32)]
    )


def pair_sums(own, first, second, third):
    own, first, second, third = (v.astype(jnp.float32) for v in (own, first, second, third))
    return (own + first) + (second + third)


def in_order(rows, by_core, by_x, by_both):
    part = lax.axis_index("tensor")

    def ordered(first, second, bit):
        swapped = part // bit % 2 == 1
        return jnp.concatenate(
            [jnp.where(swapped, second, first), jnp.where(swapped, first, second)], axis=0
        )

    return ordered(ordered(rows, by_core, 1), ordered(by_x, by_both, 1), 2)


def head_device(
    hidden_in,
    cotangent,
    layout,
    seq_lengths,
    expert_ids,
    drop_rank,
    norm1_gain,
    w_query,
    key_weight,
    value_weight,
    query_gain,
    key_gain,
    w_out,
    norm2_gain,
    w_router,
    w_gate,
    w_up,
    w_down,
):
    f32, bf16 = jnp.float32, jnp.bfloat16
    tok_rows, model_width = hidden_in.shape
    head_dim = query_gain.shape[0]
    expert_count = w_router.shape[1]
    local_count, _, ff_local = w_gate.shape
    groups = lax.axis_size("expert")
    tensor_size = lax.axis_size("tensor")
    total_rows = groups * tok_rows
    own_rows = tok_rows // tensor_size
    group = lax.axis_index("expert")
    part = lax.axis_index("tensor")

    def own(rows):
        return lax.dynamic_slice_in_dim(rows, part * own_rows, own_rows, 0)

    tag = jnp.concatenate(
        [layout[None], drop_rank[None], expert_ids.T, jnp.zeros((6, tok_rows), jnp.int32)], axis=0
    )
    half_dim = head_dim // 2
    inverse = THETA ** (-(jnp.arange(half_dim, dtype=f32) * 2.0) / head_dim)
    q_gain, k_gain = query_gain[None], key_gain[None]
    (
        normed1, queries, keys, values, lin, cosine, sine, attended, log_total,
        place_row, open_row, place_column, residual, normed2, chosen, kept, grad_y_all,
    ) = front(
        hidden_in, cotangent, tag, seq_lengths, norm1_gain[None], w_query, key_weight,
        value_weight, q_gain, k_gain, jnp.concatenate([inverse, inverse])[None], w_out,
        norm2_gain[None], expert_count,
    )
    turn = lambda v: jnp.transpose(v, (0, 2, 1))
    back, grad_gate, grad_up, grad_down = experts(
        normed2, grad_y_all, turn(w_gate), turn(w_up), w_down.reshape(-1, model_width),
        w_router.T, chosen, kept,
    )
    out_own = (residual + back[:, :model_width]).astype(bf16)
    back = back[:, model_width:]

    start = group * tok_rows + part * own_rows
    chosen_own = lax.dynamic_slice_in_dim(chosen, start, own_rows, 1).T
    logits = jnp.dot(normed2, w_router, preferred_element_type=f32)
    soft_own = jax.nn.softmax(jnp.where(chosen_own > 0.0, logits, -jnp.inf), axis=1)
    grad_soft = back[:, model_width : model_width + expert_count]
    grad_logits = (
        soft_own * (grad_soft - jnp.sum(soft_own * grad_soft, axis=1, keepdims=True))
    ).astype(bf16)
    grad_router = jnp.einsum("td,te->de", normed2, grad_logits, preferred_element_type=f32)
    grad_normed2 = back[:, :model_width] + jnp.einsum(
        "te,de->td", grad_logits, w_router, preferred_element_type=f32
    )
    norm2_pull = jax.vjp(norm_rows, residual, norm2_gain)[1]
    grad_resid_norm, grad_norm2 = norm2_pull(grad_normed2)
    grad_residual = own(cotangent).astype(f32) + grad_resid_norm
    small = jnp.concatenate([grad_router.T, grad_norm2[None]], axis=0).astype(bf16)
    small = lax.optimization_barrier(small)
    far_part = swap(small, 16)

    grad_lin, grad_out, grad_qgain, grad_kgain = attend_back(
        grad_residual.astype(bf16), w_out, queries, keys, values, attended, lin, cosine, sine,
        place_column, place_row, open_row, log_total, k_gain, q_gain,
    )
    small = (small.astype(f32) + far_part.astype(f32)).astype(bf16)
    grad_lin, small, out_own = lax.optimization_barrier((grad_lin, small, out_own))
    near_part = swap(small, 8)
    out_by_x, out_by_core = swap(out_own, 2), swap(out_own, 1)
    gains = jnp.concatenate(
        [grad_qgain, grad_kgain, jnp.zeros((1, model_width - 2 * head_dim), f32)], axis=1
    )
    reduced, grad_kv, grad_query, grad_out = close(
        normed1, grad_lin, w_query, key_weight, value_weight, grad_out
    )
    reduced, near_part, out_by_x = lax.optimization_barrier((reduced, near_part, out_by_x))
    small = small.astype(f32) + near_part.astype(f32)
    norm1_pull = jax.vjp(norm_rows, own(hidden_in).astype(f32), norm1_gain)[1]
    grad_hidden_norm, grad_norm1 = norm1_pull(reduced)
    late_sums = jnp.concatenate([grad_norm1[None], gains], axis=0)
    hidden_rows = (grad_residual + grad_hidden_norm).astype(bf16)
    grad_query, hidden_rows, late_sums = lax.optimization_barrier(
        (grad_query, hidden_rows, late_sums)
    )
    by_x, by_core = swap(hidden_rows, 2), swap(hidden_rows, 1)
    moved = [swap(late_sums, 8 * step) for step in (1, 2, 3)]
    out_by_both = swap(out_by_x, 1)
    grad_query = grad_query.astype(f32)
    grad_query, grad_out, moved = lax.optimization_barrier((grad_query, grad_out, moved))
    small = jnp.concatenate([small, pair_sums(late_sums, *moved)], axis=0).astype(bf16)
    small = lax.optimization_barrier(small)
    moved = [swap(small, 2 * step) for step in (1, 2, 3)]
    grad_out, grad_kv = grad_out.astype(f32), grad_kv.astype(f32)
    out_hidden = in_order(out_own, out_by_core, out_by_x, out_by_both)
    grads = (grad_gate, grad_up, grad_down)
    grad_out, grad_kv, out_hidden, by_x, moved, grads = lax.optimization_barrier(
        (grad_out, grad_kv, out_hidden, by_x, moved, grads)
    )
    small = pair_sums(small, *moved)
    moved, by_both = swap(small, 1), swap(by_x, 1)
    grads = settle(*grads)
    grads, moved, by_both = lax.optimization_barrier((grads, moved, by_both))
    grad_gate, grad_up, grad_down = grads
    small = small + moved
    grad_hidden = in_order(hidden_rows, by_core, by_x, by_both)
    grad_norm1 = small[expert_count + 1]
    grad_router, grad_norm2 = small[:expert_count].T, small[expert_count]
    grad_qgain, grad_kgain = jnp.split(small[expert_count + 2, : 2 * head_dim], 2)
    grad_down = grad_down.reshape(local_count, ff_local, model_width)
    return (
        out_hidden,
        grad_hidden,
        grad_norm1,
        grad_query,
        grad_kv[:, :head_dim],
        grad_kv[:, head_dim:],
        grad_qgain,
        grad_kgain,
        grad_out,
        grad_norm2,
        grad_router,
        turn(grad_gate),
        turn(grad_up),
        grad_down,
    )


def solution(mesh):
    groups = mesh.shape["expert"]

    def device_fn(*operands):
        heads = operands[7].shape[1] // operands[10].shape[0]
        one_head = heads == groups == 8 and operands[8].shape[1] == operands[10].shape[0]
        one_head = one_head and mesh.shape["tensor"] == 4
        return (head_device if one_head else per_device)(*operands)

    return jax.shard_map(
        device_fn,
        mesh=mesh,
        in_specs=(
            P("expert", None),
            P("expert", None),
            P("expert"),
            P(),
            P("expert", None),
            P("expert"),
            P(),
            P(None, "tensor"),
            P(None, "tensor"),
            P(None, "tensor"),
            P(),
            P(),
            P("tensor", None),
            P(),
            P(),
            P("expert", None, "tensor"),
            P("expert", None, "tensor"),
            P("expert", "tensor", None),
        ),
        out_specs=(
            P("expert", None),
            P("expert", None),
            P(),
            P(None, "tensor"),
            P(None, "tensor"),
            P(None, "tensor"),
            P(),
            P(),
            P("tensor", None),
            P(),
            P(),
            P("expert", None, "tensor"),
            P("expert", None, "tensor"),
            P("expert", "tensor", None),
        ),
        check_vma=False,
    )
```

```python
from functools import partial
import math

import jax
import jax.numpy as jnp
from jax import lax
from jax.experimental import pallas as pl
from jax.experimental.pallas import tpu as pltpu
from jax.sharding import PartitionSpec as P

TOPK = 8
CAP = 1280


EPS = 1e-06
THETA = 1000000.0
NEG = -1e30


def norm_rows(value_matrix, gain):
    return (
        value_matrix
        * lax.rsqrt(jnp.mean(value_matrix * value_matrix, axis=-1, keepdims=True) + EPS)
        * gain
    )


def rotary(value_matrix, position):
    half_dim = value_matrix.shape[-1] // 2
    inverse = THETA ** (-(jnp.arange(half_dim, dtype=jnp.float32) * 2.0) / value_matrix.shape[-1])
    angles = position.astype(jnp.float32)[:, None] * inverse[None, :]
    cosine_table = jnp.concatenate([jnp.cos(angles), jnp.cos(angles)], axis=-1)[:, None, :]
    sine_table = jnp.concatenate([jnp.sin(angles), jnp.sin(angles)], axis=-1)[:, None, :]
    turned = jnp.concatenate([-value_matrix[..., half_dim:], value_matrix[..., :half_dim]], axis=-1)
    return value_matrix * cosine_table + turned * sine_table


def shape_queries(linear, gain, position):
    head_dim = gain.shape[0]
    shaped = linear.reshape(linear.shape[0], linear.shape[1] // head_dim, head_dim)
    return rotary(norm_rows(shaped, gain), position) * head_dim ** (-0.5)


def shape_keys(linear, gain, position):
    head_dim = gain.shape[0]
    shaped = linear.reshape(linear.shape[0], linear.shape[1] // head_dim, head_dim)
    return rotary(norm_rows(shaped, gain), position)


def token_tables(token_position, seq_lengths):
    bounds = jnp.cumsum(seq_lengths)
    passed = token_position[:, None] >= bounds[None, :]
    segment_ids = jnp.sum(passed.astype(jnp.int32), axis=1)
    opening = jnp.max(jnp.where(passed, bounds[None, :], 0), axis=1)
    return (segment_ids, (token_position - opening).astype(jnp.int32))


def visible(query_segment, query_place, key_segment, key_place):
    return (query_segment[:, None] == key_segment[None, :]) & (
        key_place[None, :] <= query_place[:, None]
    )


def deliver(payload, slot_ids):
    return (
        lax.all_to_all(payload, "expert", split_axis=0, concat_axis=0, tiled=True),
        lax.all_to_all(slot_ids, "expert", split_axis=0, concat_axis=0, tiled=True),
    )


def bring_back(payload):
    return lax.all_to_all(payload, "expert", split_axis=0, concat_axis=0, tiled=True)


def expert_forward(entry_rows, w_gate, w_up, w_down):
    gate_lin = jnp.einsum("gesd,edf->gesf", entry_rows, w_gate, preferred_element_type=jnp.float32)
    up_lin = jnp.einsum("gesd,edf->gesf", entry_rows, w_up, preferred_element_type=jnp.float32)
    activation = (jax.nn.silu(gate_lin) * up_lin).astype(jnp.bfloat16)
    expert_out = jnp.einsum(
        "gesf,efd->gesd", activation, w_down, preferred_element_type=jnp.float32
    ).astype(jnp.bfloat16)
    return (gate_lin, up_lin, activation, expert_out)


def expert_backward(entry_rows, gate_lin, up_lin, activation, grad_in, w_gate, w_up, w_down):
    grad_down = jnp.einsum(
        "gesf,gesd->efd", activation, grad_in, preferred_element_type=jnp.float32
    )
    grad_act = jnp.einsum("gesd,efd->gesf", grad_in, w_down, preferred_element_type=jnp.float32)
    sigmoid = jax.nn.sigmoid(gate_lin)
    grad_gate_lin = (grad_act * up_lin * sigmoid * (1.0 + gate_lin * (1.0 - sigmoid))).astype(
        jnp.bfloat16
    )
    grad_up_lin = (grad_act * gate_lin * sigmoid).astype(jnp.bfloat16)
    grad_w_gate = jnp.einsum(
        "gesd,gesf->edf", entry_rows, grad_gate_lin, preferred_element_type=jnp.float32
    )
    grad_w_up = jnp.einsum(
        "gesd,gesf->edf", entry_rows, grad_up_lin, preferred_element_type=jnp.float32
    )
    grad_entry = jnp.einsum(
        "gesf,edf->gesd", grad_gate_lin, w_gate, preferred_element_type=jnp.float32
    )
    grad_entry = (
        grad_entry
        + jnp.einsum("gesf,edf->gesd", grad_up_lin, w_up, preferred_element_type=jnp.float32)
    ).astype(jnp.bfloat16)
    return (grad_entry, grad_w_gate, grad_w_up, grad_down)


def per_device(
    hidden_in,
    cotangent,
    layout,
    seq_lengths,
    expert_ids,
    drop_rank,
    norm1_gain,
    w_query,
    key_weight,
    value_weight,
    query_gain,
    key_gain,
    w_out,
    norm2_gain,
    w_router,
    w_gate,
    w_up,
    w_down,
):
    tok_rows = hidden_in.shape[0]
    model_width = hidden_in.shape[1]
    head_dim = query_gain.shape[0]
    local_heads = w_query.shape[1] // head_dim
    expert_count = w_router.shape[1]
    local_count = w_gate.shape[0]
    group_count = lax.axis_size("expert")
    slot_count = 2 * tok_rows * TOPK // expert_count
    seq_count = seq_lengths.shape[0]
    expert_range = jnp.arange(expert_count, dtype=jnp.int32)
    hidden = hidden_in.astype(jnp.float32)
    segment_ids, position = token_tables(layout, seq_lengths)
    valid = segment_ids < seq_count
    first_normalized = norm_rows(hidden, norm1_gain)
    normed1_low = first_normalized.astype(jnp.bfloat16)
    query_lin = jnp.dot(normed1_low, w_query, preferred_element_type=jnp.float32)
    key_lin = jnp.dot(normed1_low, key_weight, preferred_element_type=jnp.float32)
    value_lin = jnp.dot(normed1_low, value_weight, preferred_element_type=jnp.float32)
    query_shaped = shape_queries(query_lin, query_gain, position).astype(jnp.bfloat16)
    query_total = local_heads * tok_rows
    query_rows = jnp.transpose(query_shaped, (1, 0, 2)).reshape(query_total, head_dim)
    key_rows = (
        shape_keys(key_lin, key_gain, position).astype(jnp.bfloat16).reshape(tok_rows, head_dim)
    )
    value_rows = value_lin.astype(jnp.bfloat16)
    all_keys, all_values, all_place, all_ids, all_rank = (
        lax.all_gather(key_rows, "expert", axis=0, tiled=True),
        lax.all_gather(value_rows, "expert", axis=0, tiled=True),
        lax.all_gather(layout, "expert", axis=0, tiled=True),
        lax.all_gather(expert_ids, "expert", axis=0, tiled=True),
        lax.all_gather(drop_rank, "expert", axis=0, tiled=True),
    )
    all_segment = token_tables(all_place, seq_lengths)[0]
    rows_per_block = math.gcd(512, query_total)
    count_of_blocks = query_total // rows_per_block
    query_segment = jnp.tile(segment_ids, local_heads)
    query_place = jnp.tile(layout, local_heads)

    def attend_block(operands):
        query_block, segment_block, place_block = operands
        scores = jnp.einsum("qd,kd->qk", query_block, all_keys, preferred_element_type=jnp.float32)
        scores = jnp.where(visible(segment_block, place_block, all_segment, all_place), scores, NEG)
        highest = jnp.max(scores, axis=1, keepdims=True)
        weights = jnp.exp(scores - highest)
        totals = jnp.sum(weights, axis=1, keepdims=True)
        probability = (weights / totals).astype(jnp.bfloat16)
        mixed_out = jnp.dot(probability, all_values, preferred_element_type=jnp.float32)
        return (mixed_out, (highest + jnp.log(totals))[:, 0])

    attention_output, log_totals = lax.map(
        attend_block,
        (
            query_rows.reshape(count_of_blocks, rows_per_block, head_dim),
            query_segment.reshape(count_of_blocks, rows_per_block),
            query_place.reshape(count_of_blocks, rows_per_block),
        ),
    )
    attention_output = attention_output.reshape(local_heads, tok_rows, head_dim).astype(
        jnp.bfloat16
    )
    att_cat = jnp.transpose(attention_output, (1, 0, 2)).reshape(tok_rows, local_heads * head_dim)
    branch_part = jnp.dot(att_cat, w_out, preferred_element_type=jnp.float32)
    branch = lax.psum(branch_part, "tensor")
    residual = hidden + branch
    normed2 = norm_rows(residual, norm2_gain)
    normed2_low = normed2.astype(jnp.bfloat16)
    logits = jnp.dot(normed2_low, w_router, preferred_element_type=jnp.float32)
    soft_gate = jax.nn.softmax(jnp.take_along_axis(logits, expert_ids, axis=1), axis=1)
    picks = jnp.any(expert_ids[:, :, None] == expert_range, axis=1) & valid[:, None]
    all_valid = all_segment < seq_count
    all_picks = jnp.any(all_ids[:, :, None] == expert_range, axis=1) & all_valid[:, None]
    earlier = (all_rank[None, :] < drop_rank[:, None]).astype(jnp.bfloat16)
    before_counts = jnp.dot(
        earlier, all_picks.astype(jnp.bfloat16), preferred_element_type=jnp.float32
    )
    global_slot = jnp.take_along_axis(before_counts, expert_ids, axis=1).astype(jnp.int32)
    kept_mask = (global_slot < CAP) & valid[:, None]
    gate_weight = soft_gate * kept_mask.astype(jnp.float32)
    lower_rows = (jnp.arange(tok_rows)[None, :] < jnp.arange(tok_rows)[:, None]).astype(
        jnp.bfloat16
    )
    local_counts = jnp.dot(
        lower_rows, picks.astype(jnp.bfloat16), preferred_element_type=jnp.float32
    )
    local_slot = jnp.take_along_axis(local_counts, expert_ids, axis=1).astype(jnp.int32)
    pair_count = tok_rows * TOPK
    dump_index = expert_count * slot_count
    target = jnp.where(kept_mask, expert_ids * slot_count + local_slot, dump_index)
    pair_index = jnp.arange(pair_count, dtype=jnp.int32)
    slot_pair = (
        jnp.full((dump_index,), pair_count, jnp.int32)
        .at[target.reshape(-1)]
        .set(pair_index, mode="drop")
    )
    slot_token = jnp.where(slot_pair < pair_count, slot_pair // TOPK, tok_rows)
    slot_global = (
        jnp.full((dump_index,), -1, jnp.int32)
        .at[target.reshape(-1)]
        .set(global_slot.reshape(-1), mode="drop")
    )
    padded_rows = jnp.concatenate([normed2_low, jnp.zeros((1, model_width), jnp.bfloat16)], axis=0)
    send_rows = padded_rows[slot_token].reshape(group_count, local_count, slot_count, model_width)
    send_slot = slot_global.reshape(group_count, local_count, slot_count)
    received, received_slot = deliver(send_rows, send_slot)
    gate_lin, up_lin, activation, expert_out = expert_forward(received, w_gate, w_up, w_down)
    returned = bring_back(expert_out)
    returned_flat = jnp.concatenate(
        [returned.reshape(dump_index, model_width), jnp.zeros((1, model_width), returned.dtype)],
        axis=0,
    )
    pair_out = returned_flat[target]
    moe_part = jnp.sum(gate_weight[:, :, None] * pair_out, axis=1)
    moe_branch = lax.psum(moe_part.astype(jnp.bfloat16), "tensor").astype(jnp.float32)
    out_hidden = (residual + moe_branch).astype(jnp.bfloat16)
    grad_y = cotangent.astype(jnp.float32)
    gate_dot = jnp.sum(grad_y[:, None, :] * pair_out, axis=2)
    pair_grads = (
        (gate_weight[:, :, None] * grad_y[:, None, :])
        .astype(jnp.bfloat16)
        .reshape(pair_count, model_width)
    )
    pair_grads = jnp.concatenate([pair_grads, jnp.zeros((1, model_width), jnp.bfloat16)], axis=0)
    send_grad = pair_grads[slot_pair].reshape(group_count, local_count, slot_count, model_width)
    grad_received, grad_slot = deliver(send_grad, send_slot)
    grad_entry, grad_w_gate, grad_w_up, grad_w_down = expert_backward(
        received, gate_lin, up_lin, activation, grad_received, w_gate, w_up, w_down
    )
    grad_returned = bring_back(grad_entry)
    grad_flat = jnp.concatenate(
        [
            grad_returned.reshape(dump_index, model_width),
            jnp.zeros((1, model_width), grad_returned.dtype),
        ],
        axis=0,
    )
    grad_normed2_part = jnp.sum(grad_flat[target], axis=1, dtype=jnp.float32)
    grad_normed2_exp, gate_dot = lax.psum((grad_normed2_part, gate_dot), "tensor")
    grad_soft = gate_dot * kept_mask.astype(jnp.float32)
    grad_chosen = soft_gate * (grad_soft - jnp.sum(soft_gate * grad_soft, axis=1, keepdims=True))
    grad_logits = jnp.sum(
        grad_chosen[:, :, None] * (expert_ids[:, :, None] == expert_range).astype(jnp.float32),
        axis=1,
    ).astype(jnp.bfloat16)
    grad_w_router = jnp.einsum(
        "td,te->de", normed2_low, grad_logits, preferred_element_type=jnp.float32
    )
    grad_normed2 = grad_normed2_exp + jnp.einsum(
        "te,de->td", grad_logits, w_router, preferred_element_type=jnp.float32
    )
    norm2_pull = jax.vjp(norm_rows, residual, norm2_gain)[1]
    grad_resid_norm, grad_norm2 = norm2_pull(grad_normed2)
    grad_residual = grad_y + grad_resid_norm
    grad_residual_low = grad_residual.astype(jnp.bfloat16)
    grad_w_out = jnp.einsum(
        "tc,td->cd", att_cat, grad_residual_low, preferred_element_type=jnp.float32
    )
    grad_att_cat = jnp.einsum(
        "td,cd->tc", grad_residual_low, w_out, preferred_element_type=jnp.float32
    ).astype(jnp.bfloat16)
    grad_att_rows = jnp.transpose(
        grad_att_cat.reshape(tok_rows, local_heads, head_dim), (1, 0, 2)
    ).reshape(query_total, head_dim)

    def query_grad_block(operands):
        query_block, segment_block, place_block, grad_block, log_block = operands
        scores = jnp.einsum("qd,kd->qk", query_block, all_keys, preferred_element_type=jnp.float32)
        scores = jnp.where(visible(segment_block, place_block, all_segment, all_place), scores, NEG)
        probability = jnp.exp(scores - log_block[:, None])
        grad_prob = jnp.einsum(
            "qd,kd->qk", grad_block, all_values, preferred_element_type=jnp.float32
        )
        delta_row = jnp.sum(probability * grad_prob, axis=1)
        grad_scores = (probability * (grad_prob - delta_row[:, None])).astype(jnp.bfloat16)
        return (jnp.dot(grad_scores, all_keys, preferred_element_type=jnp.float32), delta_row)

    grad_query_rows, deltas = lax.map(
        query_grad_block,
        (
            query_rows.reshape(count_of_blocks, rows_per_block, head_dim),
            query_segment.reshape(count_of_blocks, rows_per_block),
            query_place.reshape(count_of_blocks, rows_per_block),
            grad_att_rows.reshape(count_of_blocks, rows_per_block, head_dim),
            log_totals,
        ),
    )
    log_flat = log_totals.reshape(query_total)
    delta_flat = deltas.reshape(query_total)
    key_block = math.gcd(lax.axis_size("expert") * tok_rows, 2048)

    def one_block(offset):
        key_part = lax.dynamic_slice_in_dim(all_keys, offset, key_block, 0)
        value_part = lax.dynamic_slice_in_dim(all_values, offset, key_block, 0)
        segment_part = lax.dynamic_slice_in_dim(all_segment, offset, key_block, 0)
        place_part = lax.dynamic_slice_in_dim(all_place, offset, key_block, 0)
        scores = jnp.einsum("qd,kd->qk", query_rows, key_part, preferred_element_type=jnp.float32)
        scores = jnp.where(
            visible(query_segment, query_place, segment_part, place_part), scores, NEG
        )
        probability = jnp.exp(scores - log_flat[:, None])
        grad_value = jnp.einsum(
            "qk,qd->kd",
            probability.astype(jnp.bfloat16),
            grad_att_rows,
            preferred_element_type=jnp.float32,
        )
        grad_prob = jnp.einsum(
            "qd,kd->qk", grad_att_rows, value_part, preferred_element_type=jnp.float32
        )
        grad_scores = (probability * (grad_prob - delta_flat[:, None])).astype(jnp.bfloat16)
        grad_key = jnp.einsum(
            "qk,qd->kd", grad_scores, query_rows, preferred_element_type=jnp.float32
        )
        return jnp.concatenate([grad_key, grad_value], axis=1)

    stacked = lax.map(
        one_block,
        jnp.arange(lax.axis_size("expert") * tok_rows // key_block, dtype=jnp.int32) * key_block,
    )
    key_value_grad = lax.psum_scatter(
        stacked.reshape(lax.axis_size("expert") * tok_rows, 2 * head_dim).astype(jnp.bfloat16),
        "expert",
        scatter_dimension=0,
        tiled=True,
    ).astype(jnp.float32)
    grad_key_post = key_value_grad[:, :head_dim].reshape(tok_rows, 1, head_dim)
    grad_values_low = key_value_grad[:, head_dim:].astype(jnp.bfloat16)
    grad_query_tok = jnp.transpose(
        grad_query_rows.reshape(local_heads, tok_rows, head_dim), (1, 0, 2)
    )
    query_pull = jax.vjp(partial(shape_queries, position=position), query_lin, query_gain)[1]
    grad_query_lin, grad_qgain_part = query_pull(grad_query_tok)
    key_pull = jax.vjp(partial(shape_keys, position=position), key_lin, key_gain)[1]
    grad_key_lin, grad_kgain_part = key_pull(grad_key_post)
    grad_query_low = grad_query_lin.astype(jnp.bfloat16)
    grad_key_low = grad_key_lin.astype(jnp.bfloat16)
    grad_w_query = jnp.einsum(
        "td,tc->dc", normed1_low, grad_query_low, preferred_element_type=jnp.float32
    )
    grad_w_key = jnp.einsum(
        "td,tc->dc", normed1_low, grad_key_low, preferred_element_type=jnp.float32
    )
    grad_w_value = jnp.einsum(
        "td,tc->dc", normed1_low, grad_values_low, preferred_element_type=jnp.float32
    )
    grad_normed1_part = jnp.einsum(
        "tc,dc->td", grad_query_low, w_query, preferred_element_type=jnp.float32
    )
    grad_normed1_part = grad_normed1_part + jnp.einsum(
        "tc,dc->td", grad_key_low, key_weight, preferred_element_type=jnp.float32
    )
    grad_normed1_part = grad_normed1_part + jnp.einsum(
        "tc,dc->td", grad_values_low, value_weight, preferred_element_type=jnp.float32
    )
    grad_normed1, grad_qgain_part, grad_kgain_part = (
        lax.psum(grad_normed1_part.astype(jnp.bfloat16), "tensor").astype(jnp.float32),
        lax.psum(grad_qgain_part.astype(jnp.bfloat16), "tensor").astype(jnp.float32),
        lax.psum(grad_kgain_part.astype(jnp.bfloat16), "tensor").astype(jnp.float32),
    )
    norm1_pull = jax.vjp(norm_rows, hidden, norm1_gain)[1]
    grad_hidden_norm, grad_norm1 = norm1_pull(grad_normed1)
    grad_hidden = (grad_residual + grad_hidden_norm).astype(jnp.bfloat16)
    summed = (
        lax.psum(grad_norm1.astype(jnp.bfloat16), "expert").astype(jnp.float32),
        lax.psum(grad_w_query.astype(jnp.bfloat16), "expert").astype(jnp.float32),
        lax.psum(grad_w_key.astype(jnp.bfloat16), "expert").astype(jnp.float32),
        lax.psum(grad_w_value.astype(jnp.bfloat16), "expert").astype(jnp.float32),
        lax.psum(grad_qgain_part.astype(jnp.bfloat16), "expert").astype(jnp.float32),
        lax.psum(grad_kgain_part.astype(jnp.bfloat16), "expert").astype(jnp.float32),
        lax.psum(grad_w_out.astype(jnp.bfloat16), "expert").astype(jnp.float32),
        lax.psum(grad_norm2.astype(jnp.bfloat16), "expert").astype(jnp.float32),
        lax.psum(grad_w_router.astype(jnp.bfloat16), "expert").astype(jnp.float32),
    )
    return (
        out_hidden,
        grad_hidden,
        summed[0],
        summed[1],
        summed[2],
        summed[3],
        summed[4],
        summed[5],
        summed[6],
        summed[7],
        summed[8],
        grad_w_gate,
        grad_w_up,
        grad_w_down,
    )


MESH = pl.DeviceIdType.MESH
FAR_FIRST = (3, -3, 2, -2, 1, -1, 0)


class Spot:
    def __init__(self):
        group, part = lax.axis_index("expert"), lax.axis_index("tensor")
        self.z, self.y = group // 2, group % 2
        self.x, self.c = part // 2, part % 2

    def has(self, dz):
        return (self.z + dz >= 0) & (self.z + dz <= 3)

    def device(self, dz=0, dy=0, dx=0, dc=0):
        y = 1 - self.y if dy else self.y
        x = 1 - self.x if dx else self.x
        c = 1 - self.c if dc else self.c
        return ((self.z + dz) * 2 + y, x * 2 + c)

    def rows(self, dz, dy, dx, dc, count):
        group, part = self.device(dz, dy, dx, dc)
        return pl.ds(pl.multiple_of((group * 4 + part) * count, count), count)

    def greet(self, line=False):
        barrier = pltpu.get_barrier_semaphore()
        for step in ((0, 1, 0, 0), (0, 0, 1, 0), (0, 0, 0, 1)):
            pl.semaphore_signal(barrier, inc=1, device_id=self.device(*step), device_id_type=MESH)
        for dz in (1, -1, 2, -2, 3, -3) if line else (1, -1):

            @pl.when(self.has(dz))
            def _(dz=dz):
                pl.semaphore_signal(
                    barrier, inc=1, device_id=self.device(dz), device_id_type=MESH
                )

        if line:
            pl.semaphore_wait(barrier, 6)
        else:
            inner = jnp.where((self.z > 0) & (self.z < 3), 1, 0)
            pl.semaphore_wait(barrier, 4 + inner)


def when_has(spot, dz, action):
    if dz == 0:
        action()
    else:
        pl.when(spot.has(dz))(action)


def dma_sems(shapes):
    return [pltpu.SemaphoreType.DMA(shape) if shape else pltpu.SemaphoreType.DMA for shape in shapes]


def add_into(into, chunk, *terms):
    @pl.loop(0, into.shape[0] // chunk)
    def _(step):
        rows = pl.ds(pl.multiple_of(step * chunk, chunk), chunk)
        for at in range(0, into.shape[1], 1024):
            columns = pl.ds(at, min(1024, into.shape[1] - at))
            total = into[rows, columns].astype(jnp.float32)
            for term in terms:
                total = total + term[rows, columns].astype(jnp.float32)
            into[rows, columns] = total.astype(into.dtype)


def push(src, dst, send_sem, recv_sem, device):
    pltpu.make_async_remote_copy(
        src_ref=src,
        dst_ref=dst,
        send_sem=send_sem,
        recv_sem=recv_sem,
        device_id=device,
        device_id_type=MESH,
    ).start()


def arrive(view, sem):
    pltpu.make_async_copy(view, view, sem).wait()


F32, BF16 = jnp.float32, jnp.bfloat16
VMEM_SPEC = pl.BlockSpec(memory_space=pltpu.VMEM)
HBM_SPEC = pl.BlockSpec(memory_space=pl.ANY)


def cost(flops, microseconds):
    return pl.CostEstimate(
        flops=flops, bytes_accessed=microseconds * 3_000_000, transcendentals=0
    )


def mxu(left, right, left_dim=1, right_dim=0):
    return lax.dot_general(
        left, right, (((left_dim,), (right_dim,)), ((), ())), preferred_element_type=F32
    )


def head_norm(lin):
    root = lax.rsqrt(jnp.mean(lin * lin, axis=-1, keepdims=True) + EPS)
    return lin * root, root


def near_first(step, z):
    high = z // 2
    folded = z + high * (3 - 2 * z)
    place = (step + folded * (1 - step // 2)) % 2 + 2 * (step // 2)
    return place + high * (3 - 2 * place)


class Gather:
    SEMS = ((5, 7), (7, 2), (6,), (7, 2, 2), None, (7, 2), (7, 2, 2))

    def __init__(
        self, spot, src, out, recv, z_send, sends, c_recv, local_sem, late_recv, late_send, full=None, share=5
    ):
        self.spot, self.src, self.out, self.full = spot, src, out, full
        self.recv, self.z_send, self.sends, self.c_recv = recv, z_send, sends, c_recv
        self.late_recv, self.late_send = late_recv, late_send
        self.count, self.width = src.shape
        width, late = self.width, self.width * share // 16
        self.share = share
        half = width * 5 // 8 if full is not None else width // 2
        self.first, self.second = pl.ds(0, half), pl.ds(half, width - half)
        self.whole = pl.ds(0, width)
        self.early = (pl.ds(0, width - late), pl.ds(late, width - late))
        self.late = (pl.ds(width - late, late), pl.ds(0, late))
        if full is None:
            self.local = pltpu.make_async_copy(src, self.place(0, 0, 0), local_sem)
        else:
            group, _ = spot.device()
            rows = pl.ds(pl.multiple_of(group * 4 * self.count, 4 * self.count), 4 * self.count)
            self.local = pltpu.make_async_copy(full, out.at[rows, :], local_sem)

    def place(self, dz, dy, dx, dc=0, columns=None):
        rows = self.spot.rows(dz, dy, dx, dc, self.count)
        return self.out.at[rows, self.whole if columns is None else columns]

    def source(self, dz, dy, dx, columns):
        if dz == 0 and dy == 0 and dx == 0:
            return self.src.at[:, columns]
        if dz == 0 and dy == 0 and self.full is not None:
            _, part = self.spot.device(0, 0, 1)
            rows = pl.ds(pl.multiple_of(part * self.count, self.count), self.count)
            return self.full.at[rows, columns]
        return self.place(dz, dy, dx, 0, columns)

    def send(self, dz, dy, dx, columns, send_sem, recv_sem, device):
        push(
            self.source(dz, dy, dx, columns), self.place(dz, dy, dx, 0, columns), send_sem,
            recv_sem, device,
        )

    def to_core(self, dz, dy, dx):
        if dz == 0 and dy == 0 and self.full is not None:
            return
        self.send(
            dz, dy, dx, self.whole, self.sends.at[0], self.c_recv.at[dz + 3, dy, dx],
            self.spot.device(0, 0, 0, 1),
        )

    def along_z(self, dz, dy, dx, columns, send_sem, recv_sem):
        for side, step in ((0, 1), (1, -1)):
            if dz * step <= 0:

                @pl.when(self.spot.has(step))
                def _(side=side, step=step):
                    self.send(
                        dz, dy, dx, columns, send_sem(side), recv_sem(dz + 3 - step),
                        self.spot.device(step),
                    )

    def spread(self, dz):
        spot = self.spot
        self.along_z(
            dz, 0, 0, self.whole, lambda side: self.z_send.at[dz + 3, side],
            lambda at: self.recv.at[0, at],
        )
        if dz == 0:
            columns, at = (self.whole, self.whole), 0
        else:
            columns, at = self.early, 3
        self.send(
            dz, 0, 0, columns[0], self.sends.at[1 + at], self.recv.at[1, dz + 3], spot.device(0, 1)
        )
        if dz != 0 or self.full is None:
            self.send(
                dz, 0, 0, columns[1], self.sends.at[2 + at], self.recv.at[2, dz + 3],
                spot.device(0, 0, 1),
            )
        self.to_core(dz, 0, 0)

    def start(self):
        self.local.start()
        self.spread(0)

    def take_z(self, dz):
        def action():
            arrive(self.place(dz, 0, 0), self.recv.at[0, dz + 3])
            self.spread(dz)

        when_has(self.spot, dz, action)

    def take_yx(self, dz):
        spot = self.spot

        def action():
            columns = self.early if dz else (self.whole, self.whole)
            arrive(self.place(dz, 1, 0, 0, columns[0]), self.recv.at[1, dz + 3])
            self.send(
                dz, 1, 0, self.first, self.sends.at[3], self.recv.at[3, dz + 3],
                spot.device(0, 0, 1),
            )
            if dz != 0 or self.full is None:
                arrive(self.place(dz, 0, 1, 0, columns[1]), self.recv.at[2, dz + 3])
            self.send(
                dz, 0, 1, self.second, self.sends.at[3], self.recv.at[4, dz + 3],
                spot.device(0, 1),
            )

        when_has(spot, dz, action)

    def take_late(self, dz):
        def action():
            for dy, dx in ((1, 0), (0, 1)):
                columns = self.late[dx]
                if self.share and dz != 0:
                    arrive(self.place(dz, dy, dx, 0, columns), self.late_recv.at[dz + 3, dx])
                if self.share:
                    self.along_z(
                        dz, dy, dx, columns, lambda side: self.late_send.at[dz + 3, side, dx],
                        lambda at: self.late_recv.at[at, dx],
                    )
                self.to_core(dz, dy, dx)

        when_has(self.spot, dz, action)

    def take_diagonal(self, dz):
        def action():
            arrive(self.place(dz, 1, 1, 0, self.first), self.recv.at[3, dz + 3])
            arrive(self.place(dz, 1, 1, 0, self.second), self.recv.at[4, dz + 3])
            self.to_core(dz, 1, 1)

        when_has(self.spot, dz, action)

    def take_core(self, far, dy, dx):
        view = self.out.at[pl.ds(0, self.count), :]
        arrive(view, self.c_recv.at[far - self.spot.z + 3, dy, dx])

    def drain(self):
        count, spot = self.count, self.spot
        replicated = self.full is not None
        for at, pieces, columns in (
            (0, 14 if replicated else 16, self.whole), (1, 1, self.whole), (2, 1, self.whole),
            (3, 4, self.whole), (4, 3, self.early[0]), (5, 3, self.early[1]),
        ):
            if at != 2 or not replicated:
                arrive(self.out.at[pl.ds(0, pieces * count), columns], self.sends.at[at])
        for dz in range(-3, 4):
            for side, step in ((0, 1), (1, -1)):
                if dz * step <= 0:

                    @pl.when(spot.has(dz) & spot.has(step))
                    def _(dz=dz, side=side):
                        arrive(self.place(0, 0, 0), self.z_send.at[dz + 3, side])
                        for at in (0, 1) if self.share else ():
                            arrive(
                                self.place(0, 0, 0, 0, self.late[at]),
                                self.late_send.at[dz + 3, side, at],
                            )


def experts_kernel(
    normed, grad_y, w_gate, w_up, w_down, router, chosen, kept,
    reduced, grad_gate, grad_up, grad_down,
    rows_all, weight, grad_in, grad_in_down, y_block, back_block,
    mine, other, from_a, from_b, from_y, from_x, from_z,
    weight_sem, y_sem, flush_sem, core_send, core_recv, half_send, yx_send, recv,
    line_send, line_recv, *gather_sems,
):
    spot = Spot()
    count, width = normed.shape
    wide = reduced.shape[1]
    local_count, ff, _ = w_gate.shape
    both = local_count * ff
    block = 4 * count
    split = from_a.shape[2]
    first, second = pl.ds(0, split), pl.ds(split, wide - split)
    group = lax.axis_index("expert")
    to_y, to_x, to_c = spot.device(0, 1), spot.device(0, 0, 1), spot.device(0, 0, 0, 1)

    def place_of(step):
        return near_first((step // 2 + 1) % 4, spot.z), (step + (step + 6) // 8) % 2

    def group_rows(step):
        far, dy = place_of(step)
        y = spot.y + dy * (1 - 2 * spot.y)
        return pl.ds(pl.multiple_of((far * 2 + y) * block, block), block)

    def y_copy(step):
        slot = step % 2
        return pltpu.make_async_copy(
            grad_y.at[group_rows(step), :], y_block.at[slot], y_sem.at[slot]
        )

    sources = [ref.at[at] for ref in (w_gate, w_up) for at in range(local_count)]
    weights = [
        pltpu.make_async_copy(source, weight.at[pl.ds(at * ff, ff), :], weight_sem.at[at])
        for at, source in enumerate(sources)
    ]
    for copy in weights:
        copy.start()
    y_copy(0).start()
    gather = Gather(spot, normed, rows_all, *gather_sems, share=8)
    spot.greet()
    gather.start()
    grad_in[...] = jnp.zeros_like(grad_in)
    grad_in_down[...] = jnp.zeros_like(grad_in_down)
    gather.local.wait()
    for copy in weights:
        copy.wait()

    def piece(dx, dc):
        _, part = spot.device(0, 0, dx, dc)
        return pl.ds(pl.multiple_of(part * count, count), count)

    def core_copy(step, dx):
        far, dy = place_of(step)
        slot = step % 2
        return pltpu.make_async_remote_copy(
            src_ref=back_block.at[slot, piece(dx, 1), :],
            dst_ref=other.at[far, dy, dx],
            send_sem=core_send.at[slot, dx],
            recv_sem=core_recv.at[far, dy, dx],
            device_id=to_c,
            device_id_type=MESH,
        )

    def merge(far, dy, dx):
        into = mine.at[far, dy, dx]
        arrive(other.at[far, dy, dx], core_recv.at[far, dy, dx])
        return into

    def merge_diagonal(k):
        far = near_first(k, spot.z)
        into = merge(far, 1, 1)
        add_into(into, 16, other.at[far, 1, 1])
        push(into.at[:, first], from_a.at[far], half_send.at[0], recv.at[0, far], to_x)
        push(into.at[:, second], from_b.at[far], half_send.at[1], recv.at[1, far], to_y)

    def merge_yx(k):
        far = near_first(k, spot.z)
        into = merge(far, 1, 0)
        add_into(into, 16, other.at[far, 1, 0])
        arrive(from_a.at[far], recv.at[0, far])
        add_into(into.at[:, first], 16, from_a.at[far])
        push(into, from_y.at[far], yx_send.at[0], recv.at[2, far], to_y)
        into = merge(far, 0, 1)
        add_into(into, 16, other.at[far, 0, 1])
        arrive(from_b.at[far], recv.at[1, far])
        add_into(into.at[:, second], 16, from_b.at[far])
        push(into, from_x.at[far], yx_send.at[1], recv.at[3, far], to_x)

    def merge_line(k):
        far = near_first(k, spot.z)
        into = merge(far, 0, 0)
        arrive(from_y.at[far], recv.at[2, far])
        arrive(from_x.at[far], recv.at[3, far])
        add_into(into, 16, other.at[far, 0, 0], from_y.at[far], from_x.at[far])
        if k > 0:
            push(
                into, from_z.at[spot.z], line_send.at[k], line_recv.at[spot.z],
                (far * 2 + spot.y, spot.x * 2 + spot.c),
            )

    def both_ways(take, distance):
        for dz in (distance, -distance) if distance else (0,):
            take(dz)

    columns = lax.broadcasted_iota(jnp.int32, (block, both), 1)
    lower = columns < ff
    lanes = lax.broadcasted_iota(jnp.int32, (block, 128), 1)
    names = lax.broadcasted_iota(jnp.int32, (router.shape[0], block), 0)

    def compute(step):
        slot = step % 2
        here = group_rows(step)
        rows = rows_all[here, :]
        lin = mxu(rows, weight[...], 1, 1)
        gate, up = lin[:, :both], lin[:, both:]
        logits = mxu(router[...], rows, 1, 1)
        picked = chosen[:, here] > 0.0
        top = jnp.max(jnp.where(picked, logits, NEG), axis=0, keepdims=True)
        exps = jnp.where(picked, jnp.exp(logits - top), 0.0)
        soft = exps / jnp.sum(exps, axis=0, keepdims=True)
        keep = kept[:, here]
        soft = jnp.where(keep > 0.0, soft, 0.0)
        lines = []
        for table in (soft, keep):
            for at in range(local_count):
                lines.append(
                    jnp.sum(
                        jnp.where(names == group * local_count + at, table, 0.0),
                        axis=0, keepdims=True,
                    )
                )
        stack = jnp.concatenate(lines + [jnp.zeros((8 - len(lines), block), F32)], axis=0).T
        spread = jnp.where(lower, stack[:, 0:1], stack[:, 1:2])
        sigmoid = 1.0 / (1.0 + jnp.exp(-gate))
        silu = gate * sigmoid
        act = (silu * up).astype(BF16).astype(F32)
        weighted = (act * spread).astype(BF16)
        y_copy(step).wait()

        @pl.when(step >= 2)
        def _():
            for dx in (0, 1):
                core_copy(step - 2, dx).wait_send()

        back_block[slot, :, :width] = mxu(weighted, w_down[...]).astype(BF16)
        pass_on(step, 1)
        y_rows = y_block[slot]
        mid = mxu(y_rows, w_down[...], 1, 1)
        dots = act * mid
        low = jnp.sum(jnp.where(lower, dots, 0.0), axis=1, keepdims=True) * stack[:, 2:3]
        high = jnp.sum(jnp.where(lower, 0.0, dots), axis=1, keepdims=True) * stack[:, 3:4]
        mine_at = group * local_count
        tail = jnp.where(lanes == mine_at, low, jnp.where(lanes == mine_at + 1, high, 0.0))
        grad_act = mid * spread
        grad_up_lin = (grad_act * silu).astype(BF16)
        grad_gate_lin = (grad_act * up * sigmoid * (1.0 + gate * (1.0 - sigmoid))).astype(BF16)
        grad_lin = jnp.concatenate([grad_gate_lin, grad_up_lin], axis=1)
        back_block[slot, :, width : 2 * width] = mxu(grad_lin, weight[...]).astype(BF16)
        back_block[slot, :, 2 * width :] = tail.astype(BF16)
        far, dy = place_of(step)
        for dx in (1, 0):
            core_copy(step, dx).start()
            mine[far, dy, dx] = back_block[slot, piece(dx, 0), :]
        grad_in[...] += mxu(grad_lin, rows, 0, 0)
        grad_in_down[...] += mxu(weighted, y_rows, 0, 0)

    plans = {
        0: lambda: (
            both_ways(gather.take_yx, 0), both_ways(gather.take_z, 1),
            both_ways(gather.take_z, 2), both_ways(gather.take_diagonal, 0),
            both_ways(gather.take_late, 0), both_ways(gather.take_yx, 1),
            both_ways(gather.take_z, 3), both_ways(gather.take_late, 1),
        ),
        1: lambda: both_ways(gather.take_yx, 2),
        2: lambda: (both_ways(gather.take_diagonal, 1), both_ways(gather.take_late, 2)),
        3: lambda: both_ways(gather.take_yx, 3),
        4: lambda: (both_ways(gather.take_diagonal, 2), both_ways(gather.take_late, 3)),
        5: lambda: merge_diagonal(1),
        6: lambda: both_ways(gather.take_diagonal, 3),
        7: lambda: merge_diagonal(2),
        9: lambda: merge_yx(1),
        11: lambda: (merge_diagonal(3), merge_yx(2)),
        13: lambda: merge_line(1),
        15: lambda: (merge_diagonal(0), merge_yx(3)),
    }

    def pass_on(step, middle):
        for at, plan in plans.items():
            if at % 2 == middle:

                @pl.when(step == at // 2)
                def _(plan=plan):
                    plan()

    @pl.loop(0, 8)
    def _(step):
        pass_on(step, 0)

        @pl.when(step < 7)
        def _():
            y_copy(step + 1).start()

        far, dy = place_of(step)
        for dx in (0, 1):
            gather.take_core(far, dy, dx)
        compute(step)

    flush = [
        pltpu.make_async_copy(
            grad_in.at[pl.ds(at * ff, ff), :],
            (grad_gate, grad_up)[at // local_count].at[at % local_count],
            flush_sem.at[at],
        )
        for at in range(2 * local_count)
    ]
    flush.append(pltpu.make_async_copy(grad_in_down, grad_down, flush_sem.at[2 * local_count]))
    for copy in flush:
        copy.start()
    merge_line(2)
    merge_yx(0)
    merge_line(3)
    merge_line(0)
    total = mine[spot.z, 0, 0].astype(F32)
    for k in (1, 2, 3):
        source = near_first(k, spot.z)
        arrive(from_z.at[source], line_recv.at[source])
        total = total + from_z[source].astype(F32)
    reduced[...] = total
    gather.drain()
    for step in (6, 7):
        for dx in (0, 1):
            core_copy(step, dx).wait_send()
    arrive(from_a, half_send.at[0])
    arrive(from_b, half_send.at[1])
    arrive(from_y, yx_send.at[0])
    arrive(from_x, yx_send.at[1])
    for k in (1, 2, 3):
        arrive(from_z.at[0], line_send.at[k])
    for copy in flush:
        copy.wait()


def experts(normed, grad_y, w_gate, w_up, w_down, router, chosen, kept):
    count, width = normed.shape
    wide = 2 * width + 128
    total = grad_y.shape[0]
    local_count, ff, _ = w_gate.shape
    both = local_count * ff
    shape, vmem, dma = jax.ShapeDtypeStruct, pltpu.VMEM, pltpu.SemaphoreType.DMA
    line = vmem((4, count, wide), BF16)
    return pl.pallas_call(
        experts_kernel,
        out_shape=(
            shape((count, wide), F32),
            shape(w_gate.shape, F32), shape(w_up.shape, F32), shape((both, width), F32),
        ),
        in_specs=[VMEM_SPEC, HBM_SPEC, HBM_SPEC, HBM_SPEC] + [VMEM_SPEC] * 4,
        out_specs=(VMEM_SPEC,) + (HBM_SPEC,) * 3,
        scratch_shapes=[
            vmem((total, width), BF16),
            vmem((2 * both, width), BF16),
            vmem((2 * both, width), F32),
            vmem((both, width), F32),
            vmem((2, 4 * count, width), BF16),
            vmem((2, 4 * count, wide), BF16),
            vmem((4, 2, 2, count, wide), BF16),
            vmem((4, 2, 2, count, wide), BF16),
            vmem((4, count, width), BF16),
            vmem((4, count, wide - width), BF16),
            line, line, line,
        ]
        + dma_sems(
            ((2 * local_count,), (2,), (2 * local_count + 1,), (2, 2), (4, 2, 2), (2,), (2,), (4, 4),
             (4,), (4,))
            + Gather.SEMS
        ),
        compiler_params=pltpu.CompilerParams(
            collective_id=8, has_side_effects=True, vmem_limit_bytes=63 << 20
        ),
        name="experts",
        cost_estimate=cost(29_000_000_000, 120),
    )(normed, grad_y, w_gate, w_up, w_down, router, chosen, kept)


def attend_back_kernel(
    own_rows, w_out, queries, keys, values, attended, lin, cosine, sine, place_column,
    place_row, open_row, log_total, k_gain, q_gain,
    grad_lin, grad_out, grad_q_gain, grad_k_gain,
    rows_all, head_out, grad_keys, grad_values, out_sum, head_sem, *gather_sems,
):
    spot = Spot()
    count = own_rows.shape[0]
    block = 4 * count
    dim = queries.shape[1]
    group = lax.axis_index("expert")
    head_copy = pltpu.make_async_copy(
        w_out.at[pl.ds(pl.multiple_of(group * dim, dim), dim), :], head_out, head_sem
    )
    head_copy.start()
    gather = Gather(spot, own_rows, rows_all, *gather_sems, share=3)
    spot.greet()
    gather.start()
    grad_keys[...] = jnp.zeros_like(grad_keys)
    grad_values[...] = jnp.zeros_like(grad_values)
    out_sum[...] = jnp.zeros_like(out_sum)
    grad_q_gain[...] = jnp.zeros_like(grad_q_gain)
    gather.local.wait()
    head_copy.wait()

    def unshape(grad, plain, gain, cos, sin):
        grad = grad * cos + pltpu.roll(grad * sin, dim // 2, 1)
        normed, root = head_norm(plain)
        gain_part = jnp.sum(grad * normed, axis=0, keepdims=True)
        grad = grad * gain
        return root * (grad - normed * jnp.mean(grad * normed, axis=-1, keepdims=True)), gain_part

    def compute(far, dy):
        y = spot.y + dy * (1 - 2 * spot.y)
        here = pl.ds(pl.multiple_of((far * 2 + y) * block, block), block)
        rows = rows_all[here, :]
        query = queries[here, :]
        grad_att = mxu(rows, head_out[...], 1, 1).astype(BF16)
        scores = mxu(keys[...], query, 1, 1)
        seen = (place_column[...] <= place_row[:, here]) & (place_column[...] >= open_row[:, here])
        probability = jnp.exp(jnp.where(seen, scores - log_total[:, here], NEG))
        grad_prob = mxu(values[...], grad_att, 1, 1)
        delta = jnp.sum(probability * grad_prob, axis=0, keepdims=True)
        grad_scores = (probability * (grad_prob - delta)).astype(BF16)
        grad_values[...] += mxu(probability.astype(BF16), grad_att)
        grad_keys[...] += mxu(grad_scores, query)
        grad_query = mxu(grad_scores, keys[...], 0, 0) * dim**-0.5
        grad_query, gain_part = unshape(
            grad_query, lin[here, :dim], q_gain[...], cosine[here, :], sine[here, :]
        )
        grad_q_gain[...] += gain_part
        grad_lin[here, :dim] = grad_query.astype(BF16)
        out_sum[...] += mxu(attended[here, :], rows, 0, 0)

    def both_ways(take, distance):
        for dz in (distance, -distance) if distance else (0,):
            take(dz)

    plans = {
        0: lambda: (both_ways(gather.take_yx, 0), both_ways(gather.take_late, 0),
                    both_ways(gather.take_z, 1)),
        1: lambda: (both_ways(gather.take_diagonal, 0), both_ways(gather.take_z, 2)),
        2: lambda: (both_ways(gather.take_yx, 1), both_ways(gather.take_late, 1),
                    both_ways(gather.take_z, 3)),
        3: lambda: (both_ways(gather.take_yx, 2), both_ways(gather.take_late, 2),
                    both_ways(gather.take_diagonal, 1)),
        4: lambda: (both_ways(gather.take_yx, 3), both_ways(gather.take_late, 3)),
        5: lambda: both_ways(gather.take_diagonal, 2),
        7: lambda: both_ways(gather.take_diagonal, 3),
    }

    @pl.loop(0, 8)
    def _(step):
        for at, plan in plans.items():

            @pl.when(step == at)
            def _(plan=plan):
                plan()

        far, dy = near_first(step // 2, spot.z), step % 2
        for dx in (0, 1):
            gather.take_core(far, dy, dx)
        compute(far, dy)

    grad_out[...] = out_sum[...].astype(BF16)
    grad_key, key_part = unshape(grad_keys[...], lin[:, dim:], k_gain[...], cosine[...], sine[...])
    grad_lin[:, dim : 2 * dim] = grad_key.astype(BF16)
    grad_lin[:, 2 * dim :] = grad_values[...].astype(BF16)
    grad_k_gain[...] = key_part
    gather.drain()


def attend_back(
    own_rows, w_out, queries, keys, values, attended, lin, cosine, sine, place_column,
    place_row, open_row, log_total, k_gain, q_gain,
):
    count, width = own_rows.shape
    total, dim = keys.shape
    shape, vmem = jax.ShapeDtypeStruct, pltpu.VMEM
    return pl.pallas_call(
        attend_back_kernel,
        out_shape=[
            shape((total, 3 * dim), BF16), shape((dim, width), BF16),
            shape((1, dim), F32), shape((1, dim), F32),
        ],
        in_specs=[VMEM_SPEC, HBM_SPEC] + [VMEM_SPEC] * 13,
        out_specs=[VMEM_SPEC] * 4,
        scratch_shapes=[
            vmem((total, width), BF16), vmem((dim, width), BF16),
            vmem((total, dim), F32), vmem((total, dim), F32), vmem((dim, width), F32),
        ]
        + dma_sems((None,) + Gather.SEMS),
        compiler_params=pltpu.CompilerParams(
            collective_id=9, has_side_effects=True, vmem_limit_bytes=60 << 20
        ),
        name="attend_back",
        cost_estimate=cost(9_000_000_000, 50),
    )(
        own_rows, w_out, queries, keys, values, attended, lin, cosine, sine, place_column,
        place_row, open_row, log_total, k_gain, q_gain,
    )


class LineGather:
    SEMS = ((7,), (7,), (7, 2), None, None, (7, 2), (7, 2, 2), None)

    def __init__(self, spot, place, own, sems):
        self.spot, self.place, self.own = spot, place, own
        self.z_recv, self.y_recv, self.z_send, self.y_send = sems[:4]
        self.late_y_recv, self.late_z_recv, self.late_z_send, self.late_y_send = sems[4:]

    def source(self, dz, dy, part):
        return self.own(part) if dz == 0 and dy == 0 else self.place(dz, dy, part)

    def along_z(self, dz, dy, part):
        for side, step in ((0, 1), (1, -1)):
            if dz * step <= 0:

                @pl.when(self.spot.has(step))
                def _(side=side, step=step):
                    if part:
                        send = self.late_z_send.at[dz + 3, side, dy]
                        recv = self.late_z_recv.at[dz + 3 - step, dy]
                    else:
                        send = self.z_send.at[dz + 3, side]
                        recv = self.z_recv.at[dz + 3 - step]
                    push(
                        self.source(dz, dy, part), self.place(dz, dy, part), send, recv,
                        self.spot.device(step),
                    )

    def along_y(self, dz):
        push(
            self.source(dz, 0, 0), self.place(dz, 0, 0), self.y_send, self.y_recv.at[dz + 3],
            self.spot.device(0, 1),
        )

    def start(self):
        self.along_z(0, 0, 0)
        push(
            self.own(1), self.place(0, 0, 1), self.late_y_send, self.late_y_recv,
            self.spot.device(0, 1),
        )
        self.along_y(0)
        self.along_z(0, 0, 1)

    def take_z(self, distance):
        for dz in (distance, -distance):

            def action(dz=dz):
                arrive(self.place(dz, 0, 0), self.z_recv.at[dz + 3])
                self.along_z(dz, 0, 0)
                self.along_y(dz)

            when_has(self.spot, dz, action)

    def take_late_y(self):
        arrive(self.place(0, 1, 1), self.late_y_recv)
        self.along_z(0, 1, 1)

    def take_late_z(self, distance):
        for dz in (distance, -distance):

            def action(dz=dz):
                for dy in (0, 1):
                    arrive(self.place(dz, dy, 1), self.late_z_recv.at[dz + 3, dy])
                    self.along_z(dz, dy, 1)

            when_has(self.spot, dz, action)

    def drain(self, four):
        for dz in (0, 1, -1, 2, -2, 3, -3):

            def action(dz=dz):
                arrive(self.place(dz, 1, 0), self.y_recv.at[dz + 3])
                for side, step in ((0, 1), (1, -1)):
                    if dz * step <= 0:

                        @pl.when(self.spot.has(step))
                        def _(side=side):
                            arrive(self.place(dz, 0, 0), self.z_send.at[dz + 3, side])
                            for dy in (0, 1):
                                arrive(
                                    self.place(dz, dy, 1), self.late_z_send.at[dz + 3, side, dy]
                                )

            when_has(self.spot, dz, action)
        arrive(four, self.y_send)
        arrive(self.place(0, 0, 1), self.late_y_send)


def close_kernel(
    normed, grad_lin, w_query, w_key, w_value, head_out,
    reduced, kv_all, query_all, out_all,
    weight, rows, sums, query_own, kv_part, back, mine, other, from_x_diagonal, from_y, from_x,
    from_z, kv_mine, kv_y, kv_z, kv_own, row_sem, weight_sem, local_sem,
    core_send, core_recv, many_send, recv, line_send, line_recv,
    kv_send, kv_y_recv, kv_line_send, kv_line_recv, *gather_sems,
):
    spot = Spot()
    total, width = normed.shape
    count, wide = reduced.shape
    block = 4 * count
    dim = w_key.shape[1]
    group = lax.axis_index("expert")
    to_y, to_x, to_c = spot.device(0, 1), spot.device(0, 0, 1), spot.device(0, 0, 0, 1)
    cut = 1664

    def parts(part):
        return pl.ds(cut, total - cut) if part else pl.ds(0, cut)

    def lane_block(dz, dy):
        return pl.ds(pl.multiple_of(spot.device(dz, dy)[0] * dim, dim), dim)

    weights = [
        pltpu.make_async_copy(
            w_query.at[:, pl.ds(pl.multiple_of(group * dim, dim), dim)],
            weight.at[:, pl.ds(0, dim)], weight_sem.at[0],
        ),
        pltpu.make_async_copy(w_key, weight.at[:, pl.ds(dim, dim)], weight_sem.at[1]),
        pltpu.make_async_copy(w_value, weight.at[:, pl.ds(2 * dim, dim)], weight_sem.at[2]),
    ]

    def row_copy(step):
        return pltpu.make_async_copy(
            normed.at[pl.ds(pl.multiple_of(step * block, block), block), :],
            rows.at[step % 2], row_sem.at[step % 2],
        )

    for copy in weights:
        copy.start()
    row_copy(0).start()
    outs = LineGather(
        spot,
        lambda dz, dy, part: out_all.at[lane_block(dz, dy), parts(part)],
        lambda part: head_out.at[:, parts(part)],
        gather_sems[:8],
    )
    queries = LineGather(
        spot,
        lambda dz, dy, part: query_all.at[parts(part), lane_block(dz, dy)],
        lambda part: query_own.at[parts(part), :],
        gather_sems[8:16],
    )
    kv_rows = total // 8

    def kv_span(start, part):
        return pl.ds(pl.multiple_of(start + part * (kv_rows // 2), kv_rows // 2), kv_rows // 2)

    kvs = LineGather(
        spot,
        lambda dz, dy, part: kv_all.at[kv_span(spot.device(dz, dy)[0] * kv_rows, part), :],
        lambda part: kv_own.at[kv_span(0, part), :],
        gather_sems[16:],
    )
    out_copy = pltpu.make_async_copy(head_out, out_all.at[lane_block(0, 0), :], local_sem.at[0])
    out_copy.start()
    spot.greet(line=True)
    outs.start()

    sums[...] = jnp.zeros_like(sums)

    @pl.loop(0, total // block)
    def _(step):
        @pl.when(step < total // block - 1)
        def _():
            row_copy(step + 1).start()

        row_copy(step).wait()
        here = pl.ds(pl.multiple_of(step * block, block), block)
        sums[...] += mxu(grad_lin[here, :], rows[step % 2], 0, 0)

    query_own[...] = sums[:dim, :].T.astype(BF16)
    kv_part[...] = sums[dim:, :].T.astype(BF16)
    query_copy = pltpu.make_async_copy(query_own, query_all.at[:, lane_block(0, 0)], local_sem.at[1])
    query_copy.start()

    def group_rows(far, dy):
        y = spot.y + dy * (1 - 2 * spot.y)
        return pl.ds(pl.multiple_of((far * 2 + y) * block, block), block)

    for k in (3, 2, 1, 0):
        far = near_first(k, spot.z)
        push(
            kv_part.at[group_rows(far, 1), :], kv_y.at[far], kv_send, kv_y_recv.at[far], to_y
        )
    for copy in weights:
        copy.wait()

    def piece(dx, dc):
        _, part = spot.device(0, 0, dx, dc)
        return pl.ds(pl.multiple_of(part * count, count), count)

    def core_copy(step, far, dy, dx):
        return pltpu.make_async_remote_copy(
            src_ref=back.at[step % 2, piece(dx, 1), :],
            dst_ref=other.at[far, dy, dx],
            send_sem=core_send.at[step % 2, dx],
            recv_sem=core_recv.at[far, dy, dx],
            device_id=to_c,
            device_id_type=MESH,
        )

    def produce(k):
        far = near_first(k, spot.z)
        for dy in (1, 0):
            step = 2 * (3 - k) + 1 - dy
            if step >= 2:
                for dx in (1, 0):
                    core_copy(step, far, dy, dx).wait_send()
            here = group_rows(far, dy)
            back[step % 2] = mxu(grad_lin[here, :], weight[...], 1, 1).astype(BF16)
            for dx in (1, 0):
                core_copy(step, far, dy, dx).start()
                mine[far, dy, dx] = back[step % 2, piece(dx, 0), :]

    def merge(far, dy, dx, *terms):
        arrive(other.at[far, dy, dx], core_recv.at[far, dy, dx])
        add_into(mine.at[far, dy, dx], 16, other.at[far, dy, dx], *terms)
        return mine.at[far, dy, dx]

    def merge_diagonal(k):
        far = near_first(k, spot.z)
        push(
            merge(far, 1, 1), from_x_diagonal.at[far], many_send.at[0], recv.at[0, far], to_x
        )

    def merge_yx(k):
        far = near_first(k, spot.z)
        push(merge(far, 0, 1), from_x.at[far], many_send.at[1], recv.at[1, far], to_x)
        arrive(from_x_diagonal.at[far], recv.at[0, far])
        push(
            merge(far, 1, 0, from_x_diagonal.at[far]), from_y.at[far], many_send.at[2],
            recv.at[2, far], to_y,
        )

    def far_device(far):
        return (far * 2 + spot.y, spot.x * 2 + spot.c)

    def merge_kv(k):
        far = near_first(k, spot.z)
        kv_mine[far] = kv_part[group_rows(far, 0), :]
        arrive(kv_y.at[far], kv_y_recv.at[far])
        add_into(kv_mine.at[far], 64, kv_y.at[far])
        if k > 0:
            push(
                kv_mine.at[far], kv_z.at[spot.z], kv_line_send.at[k], kv_line_recv.at[spot.z],
                far_device(far),
            )

    def merge_line(k):
        far = near_first(k, spot.z)
        arrive(from_y.at[far], recv.at[2, far])
        arrive(from_x.at[far], recv.at[1, far])
        into = merge(far, 0, 0, from_y.at[far], from_x.at[far])
        if k > 0:
            push(
                into, from_z.at[spot.z], line_send.at[k], line_recv.at[spot.z], far_device(far)
            )

    def sum_kv():
        sums_kv = kv_mine[spot.z].astype(F32)
        for k in (1, 2, 3):
            source = near_first(k, spot.z)
            arrive(kv_z.at[source], kv_line_recv.at[source])
            sums_kv = sums_kv + kv_z[source].astype(F32)
        kv_own[...] = sums_kv.astype(BF16)

    produce(3)
    produce(2)
    outs.take_z(1)
    for k in (3, 2, 1, 0):
        merge_kv(k)
    queries.start()
    merge_diagonal(3)
    produce(1)
    merge_diagonal(2)
    outs.take_late_y()
    produce(0)
    merge_diagonal(1)
    sum_kv()
    kvs.start()
    kv_copy = pltpu.make_async_copy(
        kv_own, kv_all.at[pl.ds(pl.multiple_of(group * kv_rows, kv_rows), kv_rows), :],
        local_sem.at[2],
    )
    kv_copy.start()
    outs.take_z(2)
    queries.take_z(1)
    merge_diagonal(0)
    merge_yx(3)
    kvs.take_z(1)
    kvs.take_late_y()
    queries.take_late_y()
    outs.take_late_z(1)
    merge_yx(2)
    outs.take_z(3)
    queries.take_z(2)
    kvs.take_z(2)
    kvs.take_late_z(1)
    merge_line(3)
    merge_yx(1)
    queries.take_late_z(1)
    outs.take_late_z(2)
    kvs.take_z(3)
    kvs.take_late_z(2)
    merge_line(2)
    merge_yx(0)
    queries.take_z(3)
    queries.take_late_z(2)
    outs.take_late_z(3)
    merge_line(1)
    merge_line(0)
    kvs.take_late_z(3)
    queries.take_late_z(3)
    total_rows = mine[spot.z, 0, 0].astype(F32)
    for k in (1, 2, 3):
        source = near_first(k, spot.z)
        arrive(from_z.at[source], line_recv.at[source])
        total_rows = total_rows + from_z[source].astype(F32)
    reduced[...] = total_rows

    kvs.drain(kv_all.at[pl.ds(0, 2 * kv_rows), :])
    kv_copy.wait()
    outs.drain(out_all.at[pl.ds(0, 4 * dim), parts(0)])
    queries.drain(query_all.at[parts(0), pl.ds(0, 4 * dim)])
    out_copy.wait()
    query_copy.wait()
    for step in (6, 7):
        for dx in (0, 1):
            core_copy(step, near_first(0, spot.z), 0, dx).wait_send()
    arrive(from_x_diagonal, many_send.at[0])
    arrive(from_x, many_send.at[1])
    arrive(from_y, many_send.at[2])
    arrive(kv_y, kv_send)
    for k in (1, 2, 3):
        arrive(from_z.at[0], line_send.at[k])
        arrive(kv_z.at[0], kv_line_send.at[k])


def close(normed, grad_lin, w_query, w_key, w_value, head_out):
    total, width = normed.shape
    count, wide, dim = total // 32, width, w_key.shape[1]
    shape, vmem = jax.ShapeDtypeStruct, pltpu.VMEM
    line, kv_line = vmem((4, count, wide), BF16), vmem((4, 4 * count, 2 * dim), BF16)
    return pl.pallas_call(
        close_kernel,
        out_shape=(
            shape((count, wide), F32), shape((total, 2 * dim), BF16),
            shape((total, 8 * dim), BF16), shape((8 * dim, width), BF16),
        ),
        in_specs=[HBM_SPEC, VMEM_SPEC, HBM_SPEC, HBM_SPEC, HBM_SPEC, VMEM_SPEC],
        out_specs=(VMEM_SPEC, HBM_SPEC, HBM_SPEC, HBM_SPEC),
        scratch_shapes=[
            vmem((width, 3 * dim), BF16), vmem((2, 4 * count, width), BF16),
            vmem((3 * dim, width), F32), vmem((width, dim), BF16), vmem((width, 2 * dim), BF16),
            vmem((2, 4 * count, wide), BF16),
            vmem((4, 2, 2, count, wide), BF16), vmem((4, 2, 2, count, wide), BF16),
            line, line, line, line, kv_line, kv_line, kv_line,
            vmem((4 * count, 2 * dim), BF16),
        ]
        + dma_sems(
            ((2,), (3,), (3,), (2, 2), (4, 2, 2), (3,), (3, 4), (4,), (4,),
             None, (4,), (4,), (4,)) + LineGather.SEMS * 3
        ),
        compiler_params=pltpu.CompilerParams(
            collective_id=10, has_side_effects=True, vmem_limit_bytes=60 << 20
        ),
        name="close",
        cost_estimate=cost(7_000_000_000, 110),
    )(normed, grad_lin, w_query, w_key, w_value, head_out)


def cosine_sine(angles):
    lanes = lax.broadcasted_iota(jnp.int32, angles.shape, 1)
    turns = jnp.floor(angles * (2.0 / math.pi) + 0.5)
    rest = angles - turns * 1.5703125
    rest = rest - turns * 4.837512969970703125e-4
    rest = rest - turns * 7.54978995489188216e-8
    square = rest * rest
    sine = square * (8.3321608736e-3 + square * -1.9515295891e-4) - 1.6666654611e-1
    sine = rest + rest * square * sine
    cosine = -1.388731625493765e-3 + square * 2.443315711809948e-5
    cosine = 1.0 - 0.5 * square + square * square * (4.166664568298827e-2 + square * cosine)
    turns = jnp.where(lanes < angles.shape[1] // 2, turns, turns - 1.0)
    turns = turns - 4.0 * jnp.floor(turns * 0.25)
    odd = (turns == 1.0) | (turns == 3.0)
    value = jnp.where(odd, sine, cosine)
    return jnp.where((turns == 1.0) | (turns == 2.0), -value, value)


def front_kernel(
    hidden, cotangent, tag, lengths, gain, w_query, w_key, w_value, q_gain, k_gain, inverse,
    w_out, second_gain,
    normed_all, queries, keys, values, lin_out, cosine, sine, attended, log_total,
    place_row, open_row, place_column, residual, normed, chosen, kept, grad_y_all,
    rows_all, weight, out_weight, staged, tags, ranks, picks, att_rows,
    partial_sum, from_core, to_x_sum, from_x,
    weight_sem, stage_sem, tag_z, tag_y, tag_z_send, tag_y_send, tag_local,
    send_sem, recv_sem, own_sem, tensor_sems, *gather_sems,
):
    spot = Spot()
    group, part = lax.axis_index("expert"), lax.axis_index("tensor")
    count, width = residual.shape
    block = 4 * count
    total = 32 * count
    dim = w_key.shape[1]
    own = pl.ds(pl.multiple_of(part * count, count), count)

    weights = [
        pltpu.make_async_copy(
            w_query.at[:, pl.ds(pl.multiple_of(group * dim, dim), dim)],
            weight.at[:, pl.ds(0, dim)], weight_sem.at[0],
        ),
        pltpu.make_async_copy(w_key, weight.at[:, pl.ds(dim, dim)], weight_sem.at[1]),
        pltpu.make_async_copy(w_value, weight.at[:, pl.ds(2 * dim, dim)], weight_sem.at[2]),
        pltpu.make_async_copy(w_out, out_weight, weight_sem.at[3]),
    ]
    for copy in weights:
        copy.start()
    barrier = pltpu.get_barrier_semaphore()

    @pl.loop(1, 8)
    def _(step):
        pl.semaphore_signal(
            barrier, inc=1, device_id=((group + step) % 8, part), device_id_type=MESH
        )

    for device in (spot.device(0, 0, 1), spot.device(0, 0, 0, 1)):
        pl.semaphore_signal(barrier, inc=1, device_id=device, device_id_type=MESH)

    def tag_place(dz, dy):
        return tags.at[spot.device(dz, dy)[0]]

    tag_copy = pltpu.make_async_copy(tag, tag_place(0, 0), tag_local)
    tag_copy.start()
    pl.semaphore_wait(barrier, 9)

    def spread_tag(dz):
        here = tag_place(dz, 0)
        source = tag if dz == 0 else here
        for side, step in ((0, 1), (1, -1)):
            if dz * step <= 0:

                @pl.when(spot.has(step))
                def _(side=side, step=step):
                    push(
                        source, here, tag_z_send.at[dz + 3, side], tag_z.at[dz + 3 - step],
                        spot.device(step),
                    )

        push(source, here, tag_y_send.at[dz + 3], tag_y.at[dz + 3], spot.device(0, 1))

    def take_tag(dz):
        def action():
            arrive(tag_place(dz, 0), tag_z.at[dz + 3])
            spread_tag(dz)

        when_has(spot, dz, action)

    def take_tag_y(dz):
        when_has(spot, dz, lambda: arrive(tag_place(dz, 1), tag_y.at[dz + 3]))

    spread_tag(0)
    gather = Gather(spot, hidden.at[own, :], rows_all, *gather_sems[:7], full=hidden)
    gather.start()
    late = Gather(spot, cotangent.at[own, :], grad_y_all, *gather_sems[7:], full=cotangent)
    tag_copy.wait()
    gather.local.wait()
    for copy in weights:
        copy.wait()

    def group_of(step):
        far, dy = near_first(step // 2, spot.z), step % 2
        return far, dy, far * 2 + spot.y + dy * (1 - 2 * spot.y)

    def stage_copy(step):
        _, _, index = group_of(step)
        return pltpu.make_async_copy(
            staged.at[step % 2],
            normed_all.at[pl.ds(pl.multiple_of(index * block, block), block), :],
            stage_sem.at[step % 2],
        )

    experts_count = chosen.shape[0]
    names = lax.broadcasted_iota(jnp.int32, (experts_count, block), 0)
    lanes = lax.broadcasted_iota(jnp.int32, (block, dim), 1)

    def project_group(step):
        _, _, index = group_of(step)
        here = pl.ds(pl.multiple_of(index * block, block), block)
        entries = tags[index]
        place = entries[0:1, :]
        segment, opening, bound = jnp.zeros_like(place), jnp.zeros_like(place), 0
        for at in range(lengths.shape[0]):
            bound = bound + lengths[at]
            segment = segment + jnp.where(place >= bound, 1, 0)
            opening = jnp.where(place >= bound, bound, opening)
        place_row[:, here] = place.astype(F32)
        open_row[:, here] = opening.astype(F32)
        lines = jnp.concatenate(
            [place.astype(F32), (place - opening).astype(F32), entries[1:2, :].astype(F32),
             jnp.zeros((5, block), F32)],
            axis=0,
        ).T
        place_column[here, :] = lines[:, 0:1]
        ranks[here, :] = lines[:, 2:3]
        named = jnp.zeros((experts_count, block), F32)
        for at in range(2, 2 + TOPK):
            named = jnp.where(entries[at : at + 1, :] == names, 1.0, named)
        chosen[:, here] = named
        valid = segment < lengths.shape[0]
        picks[:, here] = jnp.where(valid, named, 0.0).astype(BF16)
        table = cosine_sine(lines[:, 1:2] * inverse[...])
        turned_table = pltpu.roll(table, dim // 2, 1)
        cos = jnp.where(lanes < dim // 2, table, turned_table)
        sin = jnp.where(lanes < dim // 2, -turned_table, table)
        cosine[here, :] = cos
        sine[here, :] = sin
        rows = rows_all[here, :].astype(F32)
        root = lax.rsqrt(jnp.mean(rows * rows, axis=-1, keepdims=True) + EPS)

        @pl.when(step >= 2)
        def _():
            stage_copy(step - 2).wait()

        staged[step % 2] = (rows * root * gain[...]).astype(BF16)
        stage_copy(step).start()
        lin = mxu(staged[step % 2], weight[...])
        lin_out[here, :] = lin[:, : 2 * dim]
        values[here, :] = lin[:, 2 * dim :].astype(BF16)
        for at, head_gain, scale, out in (
            (0, q_gain, dim**-0.5, queries), (dim, k_gain, 1.0, keys),
        ):
            plain, _ = head_norm(lin[:, at : at + dim])
            plain = plain * head_gain[...]
            out[here, :] = ((plain * cos + pltpu.roll(plain, dim // 2, 1) * sin) * scale).astype(
                BF16
            )

    def both_ways(take, distance):
        for dz in (distance, -distance) if distance else (0,):
            take(dz)

    def run(plans, step):
        for at, plan in plans.items():

            @pl.when(step == at)
            def _(plan=plan):
                plan()

    plans = {
        0: lambda: (both_ways(gather.take_yx, 0), both_ways(take_tag, 1),
                    both_ways(gather.take_z, 1)),
        1: lambda: (both_ways(take_tag_y, 0), both_ways(gather.take_diagonal, 0),
                    both_ways(take_tag, 2), both_ways(gather.take_z, 2),
                    both_ways(gather.take_late, 0)),
        2: lambda: (both_ways(gather.take_yx, 1), both_ways(take_tag, 3),
                    both_ways(gather.take_z, 3), both_ways(gather.take_late, 1)),
        3: lambda: (both_ways(take_tag_y, 1), both_ways(gather.take_yx, 2),
                    both_ways(gather.take_diagonal, 1), both_ways(gather.take_late, 2)),
        4: lambda: (both_ways(gather.take_yx, 3), late.start()),
        5: lambda: (both_ways(take_tag_y, 2), both_ways(gather.take_diagonal, 2),
                    both_ways(gather.take_late, 3)),
        7: lambda: (both_ways(take_tag_y, 3), both_ways(gather.take_diagonal, 3)),
    }

    @pl.loop(0, 8)
    def _(step):
        run(plans, step)
        far, dy, _ = group_of(step)

        @pl.when(step > 0)
        def _():
            for dx in (0, 1):
                gather.take_core(far, dy, dx)

        project_group(step)

    mine = att_rows.at[:, pl.ds(pl.multiple_of(group * dim, dim), dim)]

    def block_copy(step):
        target = (group + step) % 8
        return pltpu.make_async_remote_copy(
            src_ref=attended.at[pl.ds(pl.multiple_of(target * block, block), block), :],
            dst_ref=mine,
            send_sem=send_sem.at[step],
            recv_sem=recv_sem.at[step],
            device_id=(target, part),
            device_id_type=MESH,
        )

    def attend_block(step):
        here = pl.ds(pl.multiple_of((group + step) % 8 * block, block), block)
        scores = mxu(keys[...], queries[here, :], 1, 1)
        seen = (place_column[...] <= place_row[:, here]) & (place_column[...] >= open_row[:, here])
        scores = jnp.where(seen, scores, NEG)
        highest = jnp.max(scores, axis=0, keepdims=True)
        exps = jnp.exp(scores - highest)
        totals = jnp.sum(exps, axis=0, keepdims=True)
        probability = (exps * (1.0 / totals)).astype(BF16)
        attended[here, :] = mxu(values[...], probability, 0, 0).T.astype(BF16)
        log_total[:, here] = highest + jnp.log(totals)

    late_plans = {
        1: lambda: (both_ways(late.take_yx, 0), both_ways(late.take_z, 1)),
        3: lambda: (both_ways(late.take_z, 2), both_ways(late.take_diagonal, 0),
                    both_ways(late.take_late, 0)),
        5: lambda: (both_ways(late.take_yx, 1), both_ways(late.take_z, 3)),
        7: lambda: (both_ways(late.take_late, 1), both_ways(late.take_yx, 2),
                    both_ways(late.take_diagonal, 1)),
    }

    @pl.loop(1, 8)
    def _(step):
        run(late_plans, step)
        attend_block(step)
        block_copy(step).start()

    attend_block(0)
    own_copy = pltpu.make_async_copy(
        attended.at[pl.ds(pl.multiple_of(group * block, block), block), :], mine, own_sem
    )
    own_copy.start()
    both_ways(late.take_yx, 3)
    both_ways(late.take_late, 2)

    kept[...] = jnp.zeros_like(kept)

    @pl.loop(0, total // block)
    def _(step):
        here = pl.ds(pl.multiple_of(step * block, block), block)
        for at in range(0, total // block):
            columns = pl.ds(at * block, block)
            lower = jnp.where(
                ranks[here, :] < tags[at, 1:2, :].astype(F32), 1.0, 0.0
            ).astype(BF16)
            kept[:, columns] += mxu(picks[:, here], lower)

    kept[...] = jnp.where((picks[...].astype(F32) > 0.0) & (kept[...] < CAP), 1.0, 0.0)

    both_ways(late.take_diagonal, 2)
    both_ways(late.take_late, 3)

    @pl.loop(1, 8)
    def _(step):
        block_copy(step).wait_send()
        source = (group + 8 - step) % 8
        there = att_rows.at[:, pl.ds(pl.multiple_of(source * dim, dim), dim)]
        arrive(there, recv_sem.at[step])

    own_copy.wait()

    @pl.loop(0, width // 256)
    def _(step):
        columns = pl.ds(pl.multiple_of(step * 256, 256), 256)
        partial_sum[:, columns] = mxu(att_rows[...], out_weight[:, columns]).astype(BF16)

    def rows_of(dx, dc):
        _, there = spot.device(0, 0, dx, dc)
        return partial_sum.at[pl.ds(pl.multiple_of(there * count, count), count), :]

    to_x, to_c = spot.device(0, 0, 1), spot.device(0, 0, 0, 1)
    for dx in (1, 0):
        push(rows_of(dx, 1), from_core.at[dx], tensor_sems.at[dx], tensor_sems.at[2 + dx], to_c)
    arrive(from_core.at[1], tensor_sems.at[3])
    to_x_sum[...] = (rows_of(1, 0)[...].astype(F32) + from_core[1].astype(F32)).astype(BF16)
    push(to_x_sum, from_x, tensor_sems.at[4], tensor_sems.at[5], to_x)
    both_ways(late.take_diagonal, 3)
    arrive(from_core.at[0], tensor_sems.at[2])
    arrive(from_x, tensor_sems.at[5])
    branch = rows_of(0, 0)[...].astype(F32) + from_core[0].astype(F32) + from_x[...].astype(F32)
    sum_rows = hidden[own, :].astype(F32) + branch
    residual[...] = sum_rows
    root = lax.rsqrt(jnp.mean(sum_rows * sum_rows, axis=-1, keepdims=True) + EPS)
    normed[...] = (sum_rows * root * second_gain[...]).astype(BF16)
    for at, view in ((0, from_core.at[0]), (1, from_core.at[1]), (4, from_x)):
        arrive(view, tensor_sems.at[at])
    for step in (6, 7):
        stage_copy(step).wait()
    gather.drain()
    late.local.wait()
    for far in range(4):
        for dx in (0, 1):
            late.take_core(far, 1, dx)

            @pl.when(spot.z != far)
            def _(far=far, dx=dx):
                late.take_core(far, 0, dx)

    late.drain()
    for dz in range(-3, 4):

        def action(dz=dz):
            arrive(tag_place(dz, 0), tag_y_send.at[dz + 3])
            for side, step in ((0, 1), (1, -1)):
                if dz * step <= 0:

                    @pl.when(spot.has(step))
                    def _(side=side):
                        arrive(tag_place(dz, 0), tag_z_send.at[dz + 3, side])

        when_has(spot, dz, action)


def front(
    hidden, cotangent, tag, lengths, gain, w_query, w_key, w_value, q_gain, k_gain, inverse,
    w_out, second_gain, expert_count,
):
    block, width = hidden.shape
    total, count, dim = 8 * block, block // 4, w_key.shape[1]
    shape, vmem = jax.ShapeDtypeStruct, pltpu.VMEM
    smem = pl.BlockSpec(memory_space=pltpu.SMEM)
    small = (total, dim)
    return pl.pallas_call(
        front_kernel,
        out_shape=(
            shape((total, width), BF16), shape(small, BF16), shape(small, BF16),
            shape(small, BF16), shape((total, 2 * dim), F32), shape(small, F32),
            shape(small, F32), shape(small, BF16), shape((1, total), F32),
            shape((1, total), F32), shape((1, total), F32), shape((total, 1), F32),
            shape((count, width), F32), shape((count, width), BF16),
            shape((expert_count, total), F32), shape((expert_count, total), F32),
            shape((total, width), BF16),
        ),
        in_specs=[VMEM_SPEC, VMEM_SPEC, VMEM_SPEC, smem, VMEM_SPEC, HBM_SPEC, HBM_SPEC, HBM_SPEC,
                  VMEM_SPEC, VMEM_SPEC, VMEM_SPEC, HBM_SPEC, VMEM_SPEC],
        out_specs=(HBM_SPEC,) + (VMEM_SPEC,) * 15 + (HBM_SPEC,),
        scratch_shapes=[
            vmem((total, width), BF16), vmem((width, 3 * dim), BF16), vmem((8 * dim, width), BF16),
            vmem((2, block, width), BF16), vmem((8, 16, block), jnp.int32), vmem((total, 1), F32),
            vmem((expert_count, total), BF16), vmem((block, 8 * dim), BF16),
            vmem((block, width), BF16), vmem((2, count, width), BF16), vmem((count, width), BF16),
            vmem((count, width), BF16),
        ]
        + dma_sems(
            ((4,), (2,), (7,), (7,), (7, 2), (7,), None, (8,), (8,), None, (6,)) + Gather.SEMS * 2
        ),
        compiler_params=pltpu.CompilerParams(
            collective_id=1, has_side_effects=True, vmem_limit_bytes=62 << 20
        ),
        name="front",
        cost_estimate=cost(8_000_000_000, 90),
    )(
        hidden, cotangent, tag, lengths, gain, w_query, w_key, w_value, q_gain, k_gain, inverse,
        w_out, second_gain,
    )


def settle_kernel(*refs):
    half = len(refs) // 2
    for source, target in zip(refs[:half], refs[half:]):
        target[...] = source[...]


def settle(*arrays):
    width = arrays[0].shape[-1]
    flat = [v.reshape(-1, width) for v in arrays]
    steps = 6
    blocks = [pl.BlockSpec((v.shape[0] // steps, width), lambda i: (i, 0)) for v in flat]
    out = pl.pallas_call(
        settle_kernel,
        grid=(steps,),
        out_shape=tuple(jax.ShapeDtypeStruct(v.shape, v.dtype) for v in flat),
        in_specs=blocks,
        out_specs=tuple(blocks),
        cost_estimate=cost(0, 6),
        compiler_params=pltpu.CompilerParams(vmem_limit_bytes=32 << 20),
        name="settle",
    )(*flat)
    return tuple(v.reshape(w.shape) for v, w in zip(out, arrays))


def swap(value, bits):
    return lax.ppermute(
        value, ("expert", "tensor"), [(device, device ^ bits) for device in range(32)]
    )


def pair_sums(own, first, second, third):
    own, first, second, third = (v.astype(jnp.float32) for v in (own, first, second, third))
    return (own + first) + (second + third)


def in_order(rows, by_core, by_x, by_both):
    part = lax.axis_index("tensor")

    def ordered(first, second, bit):
        swapped = part // bit % 2 == 1
        return jnp.concatenate(
            [jnp.where(swapped, second, first), jnp.where(swapped, first, second)], axis=0
        )

    return ordered(ordered(rows, by_core, 1), ordered(by_x, by_both, 1), 2)


def head_device(
    hidden_in,
    cotangent,
    layout,
    seq_lengths,
    expert_ids,
    drop_rank,
    norm1_gain,
    w_query,
    key_weight,
    value_weight,
    query_gain,
    key_gain,
    w_out,
    norm2_gain,
    w_router,
    w_gate,
    w_up,
    w_down,
):
    f32, bf16 = jnp.float32, jnp.bfloat16
    tok_rows, model_width = hidden_in.shape
    head_dim = query_gain.shape[0]
    expert_count = w_router.shape[1]
    local_count, _, ff_local = w_gate.shape
    groups = lax.axis_size("expert")
    tensor_size = lax.axis_size("tensor")
    total_rows = groups * tok_rows
    own_rows = tok_rows // tensor_size
    group = lax.axis_index("expert")
    part = lax.axis_index("tensor")

    def own(rows):
        return lax.dynamic_slice_in_dim(rows, part * own_rows, own_rows, 0)

    tag = jnp.concatenate(
        [layout[None], drop_rank[None], expert_ids.T, jnp.zeros((6, tok_rows), jnp.int32)], axis=0
    )
    half_dim = head_dim // 2
    inverse = THETA ** (-(jnp.arange(half_dim, dtype=f32) * 2.0) / head_dim)
    q_gain, k_gain = query_gain[None], key_gain[None]
    (
        normed1, queries, keys, values, lin, cosine, sine, attended, log_total,
        place_row, open_row, place_column, residual, normed2, chosen, kept, grad_y_all,
    ) = front(
        hidden_in, cotangent, tag, seq_lengths, norm1_gain[None], w_query, key_weight,
        value_weight, q_gain, k_gain, jnp.concatenate([inverse, inverse])[None], w_out,
        norm2_gain[None], expert_count,
    )
    turn = lambda v: jnp.transpose(v, (0, 2, 1))
    back, grad_gate, grad_up, grad_down = experts(
        normed2, grad_y_all, turn(w_gate), turn(w_up), w_down.reshape(-1, model_width),
        w_router.T, chosen, kept,
    )
    out_own = (residual + back[:, :model_width]).astype(bf16)
    back = back[:, model_width:]

    start = group * tok_rows + part * own_rows
    chosen_own = lax.dynamic_slice_in_dim(chosen, start, own_rows, 1).T
    logits = jnp.dot(normed2, w_router, preferred_element_type=f32)
    soft_own = jax.nn.softmax(jnp.where(chosen_own > 0.0, logits, -jnp.inf), axis=1)
    grad_soft = back[:, model_width : model_width + expert_count]
    grad_logits = (
        soft_own * (grad_soft - jnp.sum(soft_own * grad_soft, axis=1, keepdims=True))
    ).astype(bf16)
    grad_router = jnp.einsum("td,te->de", normed2, grad_logits, preferred_element_type=f32)
    grad_normed2 = back[:, :model_width] + jnp.einsum(
        "te,de->td", grad_logits, w_router, preferred_element_type=f32
    )
    norm2_pull = jax.vjp(norm_rows, residual, norm2_gain)[1]
    grad_resid_norm, grad_norm2 = norm2_pull(grad_normed2)
    grad_residual = own(cotangent).astype(f32) + grad_resid_norm
    small = jnp.concatenate([grad_router.T, grad_norm2[None]], axis=0).astype(bf16)
    small = lax.optimization_barrier(small)
    far_part = swap(small, 16)

    grad_lin, grad_out, grad_qgain, grad_kgain = attend_back(
        grad_residual.astype(bf16), w_out, queries, keys, values, attended, lin, cosine, sine,
        place_column, place_row, open_row, log_total, k_gain, q_gain,
    )
    small = (small.astype(f32) + far_part.astype(f32)).astype(bf16)
    grad_lin, small, out_own = lax.optimization_barrier((grad_lin, small, out_own))
    near_part = swap(small, 8)
    out_by_x, out_by_core = swap(out_own, 2), swap(out_own, 1)
    gains = jnp.concatenate(
        [grad_qgain, grad_kgain, jnp.zeros((1, model_width - 2 * head_dim), f32)], axis=1
    )
    reduced, grad_kv, grad_query, grad_out = close(
        normed1, grad_lin, w_query, key_weight, value_weight, grad_out
    )
    reduced, near_part, out_by_x = lax.optimization_barrier((reduced, near_part, out_by_x))
    small = small.astype(f32) + near_part.astype(f32)
    norm1_pull = jax.vjp(norm_rows, own(hidden_in).astype(f32), norm1_gain)[1]
    grad_hidden_norm, grad_norm1 = norm1_pull(reduced)
    late_sums = jnp.concatenate([grad_norm1[None], gains], axis=0)
    hidden_rows = (grad_residual + grad_hidden_norm).astype(bf16)
    grad_query, hidden_rows, late_sums = lax.optimization_barrier(
        (grad_query, hidden_rows, late_sums)
    )
    by_x, by_core = swap(hidden_rows, 2), swap(hidden_rows, 1)
    moved = [swap(late_sums, 8 * step) for step in (1, 2, 3)]
    out_by_both = swap(out_by_x, 1)
    grad_query = grad_query.astype(f32)
    grad_query, grad_out, moved = lax.optimization_barrier((grad_query, grad_out, moved))
    small = jnp.concatenate([small, pair_sums(late_sums, *moved)], axis=0).astype(bf16)
    small = lax.optimization_barrier(small)
    moved = [swap(small, 2 * step) for step in (1, 2, 3)]
    grad_out, grad_kv = grad_out.astype(f32), grad_kv.astype(f32)
    out_hidden = in_order(out_own, out_by_core, out_by_x, out_by_both)
    grads = (grad_gate, grad_up, grad_down)
    grad_out, grad_kv, out_hidden, by_x, moved, grads = lax.optimization_barrier(
        (grad_out, grad_kv, out_hidden, by_x, moved, grads)
    )
    small = pair_sums(small, *moved)
    moved, by_both = swap(small, 1), swap(by_x, 1)
    grads = settle(*grads)
    grads, moved, by_both = lax.optimization_barrier((grads, moved, by_both))
    grad_gate, grad_up, grad_down = grads
    small = small + moved
    grad_hidden = in_order(hidden_rows, by_core, by_x, by_both)
    grad_norm1 = small[expert_count + 1]
    grad_router, grad_norm2 = small[:expert_count].T, small[expert_count]
    grad_qgain, grad_kgain = jnp.split(small[expert_count + 2, : 2 * head_dim], 2)
    grad_down = grad_down.reshape(local_count, ff_local, model_width)
    return (
        out_hidden,
        grad_hidden,
        grad_norm1,
        grad_query,
        grad_kv[:, :head_dim],
        grad_kv[:, head_dim:],
        grad_qgain,
        grad_kgain,
        grad_out,
        grad_norm2,
        grad_router,
        turn(grad_gate),
        turn(grad_up),
        grad_down,
    )


def solution(mesh):
    groups = mesh.shape["expert"]

    def device_fn(*operands):
        heads = operands[7].shape[1] // operands[10].shape[0]
        one_head = heads == groups == 8 and operands[8].shape[1] == operands[10].shape[0]
        one_head = one_head and mesh.shape["tensor"] == 4
        return (head_device if one_head else per_device)(*operands)

    return jax.shard_map(
        device_fn,
        mesh=mesh,
        in_specs=(
            P("expert", None),
            P("expert", None),
            P("expert"),
            P(),
            P("expert", None),
            P("expert"),
            P(),
            P(None, "tensor"),
            P(None, "tensor"),
            P(None, "tensor"),
            P(),
            P(),
            P("tensor", None),
            P(),
            P(),
            P("expert", None, "tensor"),
            P("expert", None, "tensor"),
            P("expert", "tensor", None),
        ),
        out_specs=(
            P("expert", None),
            P("expert", None),
            P(),
            P(None, "tensor"),
            P(None, "tensor"),
            P(None, "tensor"),
            P(),
            P(),
            P("tensor", None),
            P(),
            P(),
            P("expert", None, "tensor"),
            P("expert", None, "tensor"),
            P("expert", "tensor", None),
        ),
        check_vma=False,
    )
```
